32 devices in a mesh: dp: 8 (over y, x, core), tensor: 4 (over z).
Axes of the slice: x: 2, y: 2, z: 4, core: 2. Of those that a mesh axis runs over, the one named last changes fastest.
Arguments:
- tokens: bfloat16 [32768, 1024], P(('dp', 'tensor')), may hold values from -6 to 6
- first_values: bfloat16 [32768, 1024], P('dp', 'tensor'), may hold values from -6 to 6
- doc_lengths: int32 [16, 8], P('dp'), may hold values from 1 to 1024, 2048 in all within a row
- cotangent: bfloat16 [32768, 1024], P(('dp', 'tensor')), may hold values from -6 to 6
- w_query: bfloat16 [1024, 1024], P('dp', 'tensor'), may hold values from -0.1875 to 0.1875
- w_key: bfloat16 [1024, 1024], P('dp', 'tensor'), may hold values from -0.1875 to 0.1875
- w_value: bfloat16 [1024, 1024], P('dp', 'tensor'), may hold values from -0.1875 to 0.1875
- w_out: bfloat16 [1024, 1024], P('tensor', 'dp'), may hold values from -1 to 1
- w_gate: bfloat16 [1024, 2816], P('dp', 'tensor'), may hold values from -0.1875 to 0.1875
- w_up: bfloat16 [1024, 2816], P('dp', 'tensor'), may hold values from -0.1875 to 0.1875
- w_down: bfloat16 [2816, 1024], P('tensor', 'dp'), may hold values from -0.109375 to 0.109375
- gain_attn: float32 [1024], replicated, may hold values from 0.1 to 1.9
- gain_mlp: float32 [1024], replicated, may hold values from 0.1 to 1.9
Outputs:
- layer_out: bfloat16 [32768, 1024], P(('dp', 'tensor'))
- grad_tokens: float32 [32768, 1024], P(('dp', 'tensor'))
- grad_first_values: float32 [32768, 1024], P('dp', 'tensor')
- grad_w_query: float32 [1024, 1024], P('dp', 'tensor')
- grad_w_key: float32 [1024, 1024], P('dp', 'tensor')
- grad_w_value: float32 [1024, 1024], P('dp', 'tensor')
- grad_w_out: float32 [1024, 1024], P('tensor', 'dp')
- grad_w_gate: float32 [1024, 2816], P('dp', 'tensor')
- grad_w_up: float32 [1024, 2816], P('dp', 'tensor')
- grad_w_down: float32 [2816, 1024], P('tensor', 'dp')
- grad_gain_attn: float32 [1024], replicated
- grad_gain_mlp: float32 [1024], replicated
The draws below stay inside these ranges and needn't reach their ends.
Inputs may be any that keep to these rules, and one draw needn't show every extreme that they name: `doc_lengths`: each row's 8 lengths sum to 2048, and the largest in each row is 1024.
All inputs are finite; a program needn't handle non-finite values.
Results may differ from the reference program's by a relative error of at most 0.013.
Values may be sent and summed in bfloat16 or wider, within the bound.
A program may use at most 256 MiB of HBM per device.

```python
import math
import jax
import jax.numpy as jnp
import numpy as np
from jax import lax

D = 1024
HEADS = 16
HEAD = 64
FF = 2816
SEQ = 2048
DOCS = 8
MOST_DOC = 1024
ROWS = 16
TOKENS = 32768


def level_of(stream_key, dims, shards, low, top_value):
    def one(dim, shards_of):
        heights = jax.random.uniform(jax.random.fold_in(jax.random.fold_in(stream_key, 6), dim), (shards_of,), jnp.float32, low / len(shards), top_value / len(shards))
        return jnp.repeat(jnp.exp(heights), dims[dim] // shards_of).reshape((-1,) + (1,) * (len(dims) - dim - 1))

    level = one(*shards[0])
    for cut in shards[1:]:
        level = level * one(*cut)
    return level


def profile(number_of, total, reach, slope):
    loads = [(1 << 20) // math.isqrt(rank ** slope) + 1 for rank in range(2, number_of + 1)]
    rest, holding = total - reach - (number_of - 1), [1] * (number_of - 1)
    while rest > 0:
        movable = [i for i in range(number_of - 1) if holding[i] < reach]
        mass, remaining = sum([loads[i] for i in movable]), rest
        for i in movable:
            extra = min(reach - holding[i], max(1, remaining * loads[i] // mass), rest)
            holding[i] = holding[i] + extra
            rest = rest - extra
    return np.array([reach] + holding)


def ragged_sizes(own_key, amount, total, limit, skew):
    if amount == 2:
        one = jax.random.randint(own_key, (), max(1, total - limit), min(limit, total - 1) + 1)
        return jnp.stack([one, total - one])
    sizes = jnp.asarray(profile(amount, total, limit, skew), jnp.int32)
    pairs = (amount - 1) // 2
    donor, sink = sizes[1:1 + 2 * pairs:2], sizes[2:2 + 2 * pairs:2]
    room = jnp.minimum(donor - 1, limit - sink)
    shifted = jax.random.randint(jax.random.fold_in(own_key, 1), (pairs,), 0, 1 << 20) % (room + 1)
    sizes = sizes.at[1:1 + 2 * pairs:2].set(donor - shifted).at[2:2 + 2 * pairs:2].set(sink + shifted)
    return sizes[jax.random.permutation(jax.random.fold_in(own_key, 2), amount)]


def centred(own_key, extent, deviation, reach, shards=(), held_as=jnp.bfloat16):
    array = deviation * jax.random.normal(own_key, extent, jnp.float32)
    if shards:
        array = array * level_of(own_key, extent, shards, -0.22, 0.18)
    return jnp.clip(array, -reach, reach).astype(held_as)


def setup_inputs(seed: int = 0) -> dict:
    streams_of = jax.random.split(jax.random.key(seed), 14)
    tokens = centred(streams_of[0], (TOKENS, D), 1.0, 6.0, ((0, 32),))
    first_values = centred(streams_of[1], (TOKENS, D), 1.0, 6.0, ((0, 8), (1, 4)))
    doc_lengths = jax.vmap(lambda own: ragged_sizes(own, DOCS, SEQ, MOST_DOC, 2))(jax.random.split(streams_of[2], ROWS)).reshape((ROWS, DOCS)).astype(jnp.int32)
    cotangent = centred(streams_of[3], (TOKENS, D), 1.0, 6.0, ((0, 32),))
    w_query = centred(streams_of[4], (D, D), D ** -0.5, 0.1875, ((0, 8), (1, 4)))
    w_key = centred(streams_of[5], (D, D), D ** -0.5, 0.1875, ((0, 8), (1, 4)))
    w_value = centred(streams_of[6], (D, D), D ** -0.5, 0.1875, ((0, 8), (1, 4)))
    w_out = centred(streams_of[7], (D, D), (D // 32) ** -0.5, 1.0, ((0, 4), (1, 8)))
    w_gate = centred(streams_of[8], (D, FF), D ** -0.5, 0.1875, ((0, 8), (1, 4)))
    w_up = centred(streams_of[9], (D, FF), D ** -0.5, 0.1875, ((0, 8), (1, 4)))
    w_down = centred(streams_of[10], (FF, D), FF ** -0.5, 0.109375, ((0, 4), (1, 8)))
    gain_attn = jnp.clip(1.0 + 0.18 * jax.random.normal(streams_of[11], (D,), jnp.float32), 0.1, 1.9)
    gain_mlp = jnp.clip(1.0 + 0.18 * jax.random.normal(streams_of[12], (D,), jnp.float32), 0.1, 1.9)
    return {"tokens": tokens, "first_values": first_values, "doc_lengths": doc_lengths, "cotangent": cotangent, "w_query": w_query, "w_key": w_key, "w_value": w_value, "w_out": w_out, "w_gate": w_gate, "w_up": w_up, "w_down": w_down, "gain_attn": gain_attn, "gain_mlp": gain_mlp}


EPSILON = 1e-05
HIGHEST = lax.Precision.HIGHEST

@jax.custom_vjp
def low(v):
    return lax.optimization_barrier(v.astype(jnp.bfloat16)).astype(jnp.float32)

@jax.custom_vjp
def low_back(v):
    return v

def low_keep(v):
    return (low(v), None)

def low_pass(kept, grad):
    return (grad,)

def back_keep(v):
    return (v, None)

def back_low(kept, grad):
    return (low(grad),)
low.defvjp(low_keep, low_pass)
low_back.defvjp(back_keep, back_low)

def matmul(left, right):
    return jnp.dot(left, right, precision=HIGHEST, preferred_element_type=jnp.float32)

def rms_norm(values, gain):
    factor = lax.rsqrt(lax.optimization_barrier(jnp.mean(values * values, axis=1, keepdims=True)) + EPSILON)
    return values * factor * gain

def documents(doc_lengths):
    ends = jnp.cumsum(doc_lengths, axis=1).astype(jnp.int32)
    starts = ends - doc_lengths
    places = jnp.arange(SEQ, dtype=jnp.int32)
    segment = lax.optimization_barrier(jnp.sum((places[None, :, None] >= ends[:, None, :]).astype(jnp.int32), axis=2))
    member = segment[:, :, None] == jnp.arange(DOCS, dtype=jnp.int32)[None, None, :]
    offset = lax.optimization_barrier(jnp.sum(jnp.where(member, starts[:, None, :], 0), axis=2))
    return (segment, (places[None, :] - offset).astype(jnp.float32))

def rotation(positions):
    half = HEAD // 2
    freqs = 10000.0 ** (-(jnp.arange(half, dtype=jnp.float32) * 2.0 / HEAD))
    angles = positions[:, None] * freqs[None, :]
    return (jnp.cos(angles), jnp.sin(angles))

def rotate(values, cosine, sine):
    shaped = values.reshape(values.shape[0], -1, HEAD)
    half = HEAD // 2
    first = shaped[:, :, :half]
    second = shaped[:, :, half:]
    cos_rows = cosine[:, None, :]
    sin_rows = sine[:, None, :]
    turned = jnp.concatenate([first * cos_rows - second * sin_rows, second * cos_rows + first * sin_rows], axis=2)
    return turned.reshape(values.shape)

def attend_row(pieces):
    queries, keys, values, segment = pieces
    scores = jnp.einsum('qhd,khd->hqk', queries, keys, precision=HIGHEST)
    scores = low_back(scores * 0.125)
    places = jnp.arange(SEQ, dtype=jnp.int32)
    allowed = (segment[:, None] == segment[None, :]) & (places[None, :] <= places[:, None])
    scores = jnp.where(allowed[None], scores, -1e+30)
    weights = low(jax.nn.softmax(scores, axis=-1))
    return jnp.einsum('hqk,khd->qhd', weights, values, precision=HIGHEST)

def reference(tokens, first_values, doc_lengths, cotangent, w_query, w_key, w_value, w_out, w_gate, w_up, w_down, gain_attn, gain_mlp):
    segment, positions = documents(doc_lengths)
    cosine, sine = rotation(positions.reshape(-1))

    def heads(matrix):
        return matrix.reshape(ROWS, SEQ, HEADS, HEAD)

    def layer(inputs, first_layer, query_mat, key_mat, value_mat, out_mat, gate_mat, up_mat, down_mat, gain_one, gain_two):
        normed_one = low(rms_norm(inputs, gain_one))
        query_raw = low_back(matmul(normed_one, query_mat))
        key_raw = low_back(matmul(normed_one, key_mat))
        value_raw = low_back(matmul(normed_one, value_mat))
        queries = low(rotate(query_raw, cosine, sine))
        keys = low(rotate(key_raw, cosine, sine))
        mixed = low(0.5 * value_raw + 0.5 * first_layer)
        attended = lax.map(jax.checkpoint(attend_row), (heads(queries), heads(keys), heads(mixed), segment))
        attended = low(low_back(attended.reshape(TOKENS, D)))
        hidden = inputs + low_back(matmul(attended, out_mat))
        normed_two = low(rms_norm(hidden, gain_two))
        gate = low_back(matmul(normed_two, gate_mat))
        up_val = low_back(matmul(normed_two, up_mat))
        act = low(jax.nn.silu(gate) * up_val)
        return hidden + low_back(matmul(act, down_mat))
    primal = tuple((item.astype(jnp.float32) for item in (tokens, first_values, w_query, w_key, w_value, w_out, w_gate, w_up, w_down, gain_attn, gain_mlp)))
    output, backward = jax.vjp(layer, *primal)
    grads = backward(cotangent.astype(jnp.float32))
    return (output.astype(jnp.bfloat16), grads[0], grads[1], grads[2], grads[3], grads[4], grads[5], grads[6], grads[7], grads[8], grads[9], grads[10])
```

```python
import functools

import jax
import jax.numpy as jnp
from jax import lax
from jax.experimental import pallas as pl
from jax.experimental.pallas import tpu as pltpu
from jax.sharding import PartitionSpec as P

HEAD = 64
SEQ = 2048
DOCS = 8
EPSILON = 1e-05


def rms_norm(values, gain):
    factor = lax.rsqrt(jnp.mean(values * values, axis=1, keepdims=True) + EPSILON)
    return values * factor * gain


def documents(doc_lengths):
    ends = jnp.cumsum(doc_lengths, axis=1)
    starts = ends - doc_lengths
    places = jnp.arange(SEQ, dtype=jnp.int32)
    segment = jnp.sum((places[None, :, None] >= ends[:, None, :]).astype(jnp.int32), axis=2)
    member = segment[:, :, None] == jnp.arange(DOCS, dtype=jnp.int32)[None, None, :]
    offset = jnp.sum(jnp.where(member, starts[:, None, :], 0), axis=2)
    return (segment, (places[None, :] - offset).astype(jnp.float32))


def rotation(positions):
    half = HEAD // 2
    freqs = 10000.0 ** (-(jnp.arange(half, dtype=jnp.float32) * 2.0 / HEAD))
    angles = positions[:, None] * freqs[None, :]
    return (jnp.cos(angles), jnp.sin(angles))


def rotate(values, cosine, sine):
    shaped = values.reshape(values.shape[0], -1, HEAD)
    half = HEAD // 2
    first = shaped[:, :, :half]
    second = shaped[:, :, half:]
    cos_rows = cosine[:, None, :]
    sin_rows = sine[:, None, :]
    turned = jnp.concatenate(
        [first * cos_rows - second * sin_rows, second * cos_rows + first * sin_rows], axis=2
    )
    return turned.reshape(values.shape)


def rotate_back(grads, cosine, sine):
    shaped = grads.reshape(grads.shape[0], -1, HEAD)
    half = HEAD // 2
    first = shaped[:, :, :half]
    second = shaped[:, :, half:]
    cos_rows = cosine[:, None, :]
    sin_rows = sine[:, None, :]
    turned = jnp.concatenate(
        [first * cos_rows + second * sin_rows, second * cos_rows - first * sin_rows], axis=2
    )
    return turned.reshape(grads.shape)


def swiglu(gate, up_val):
    return jax.nn.silu(gate) * up_val


def product(left, right):
    return jnp.dot(left, right, preferred_element_type=jnp.float32)


def inner(left, right):
    return lax.dot_general(
        left, right, (((0,), (0,)), ((), ())), preferred_element_type=jnp.float32
    )


def outer(left, right):
    return lax.dot_general(
        left, right, (((1,), (1,)), ((), ())), preferred_element_type=jnp.float32
    )


def block_scores(queries, keys_all, segment, start, width):
    query_block = lax.dynamic_slice_in_dim(queries, start, width, 0)
    query_seg = lax.dynamic_slice_in_dim(segment, start, width, 0)
    scores = (
        jnp.einsum("qhd,khd->hqk", query_block, keys_all, preferred_element_type=jnp.float32)
        * 0.125
    )
    places = jnp.arange(SEQ, dtype=jnp.int32)
    rows_at = start + jnp.arange(width, dtype=jnp.int32)
    allowed = (query_seg[:, None] == segment[None, :]) & (places[None, :] <= rows_at[:, None])
    return (query_block, jnp.where(allowed[None], scores, -1e30))


def forward_row(pieces):
    queries, keys_all, values_all, segment = pieces
    width = min(512, SEQ)
    count = SEQ // width

    def forward_one_block(index):
        unused, scores = block_scores(queries, keys_all, segment, index * width, width)
        top = jnp.max(scores, axis=2, keepdims=True)
        expo = jnp.exp(scores - top)
        total = jnp.sum(expo, axis=2, keepdims=True)
        weights = (expo / total).astype(jnp.bfloat16)
        result = jnp.einsum("hqk,khd->qhd", weights, values_all, preferred_element_type=jnp.float32)
        return (result, (top + jnp.log(total))[:, :, 0])

    results, logsums = lax.map(forward_one_block, jnp.arange(count, dtype=jnp.int32))
    return (results.reshape(SEQ, queries.shape[1], HEAD), logsums)


def backward_row(pieces):
    queries, keys_all, values_all, segment, grad_rows, logsums = pieces
    width = min(512, SEQ)
    count = SEQ // width

    def backward_one_block(carry, extra):
        index, logsum = extra
        start = index * width
        query_block, scores = block_scores(queries, keys_all, segment, start, width)
        probs = jnp.exp(scores - logsum[:, :, None])
        grad_block = lax.dynamic_slice_in_dim(grad_rows, start, width, 0)
        grad_probs = jnp.einsum(
            "qhd,khd->hqk", grad_block, values_all, preferred_element_type=jnp.float32
        )
        delta = jnp.sum(probs * grad_probs, axis=2, keepdims=True)
        grad_scores = (probs * (grad_probs - delta)).astype(jnp.bfloat16)
        grad_query = (
            jnp.einsum("hqk,khd->qhd", grad_scores, keys_all, preferred_element_type=jnp.float32)
            * 0.125
        )
        grad_keys = (
            carry[0]
            + jnp.einsum(
                "hqk,qhd->khd", grad_scores, query_block, preferred_element_type=jnp.float32
            )
            * 0.125
        )
        grad_values = carry[1] + jnp.einsum(
            "hqk,qhd->khd",
            probs.astype(jnp.bfloat16),
            grad_block,
            preferred_element_type=jnp.float32,
        )
        return ((grad_keys, grad_values), grad_query)

    zeros = jnp.zeros(keys_all.shape, jnp.float32)
    sums, grad_queries = lax.scan(
        backward_one_block, (zeros, zeros), (jnp.arange(count, dtype=jnp.int32), logsums)
    )
    return (grad_queries.reshape(SEQ, queries.shape[1], HEAD), sums[0], sums[1])


def general_body(
    tokens,
    first_values,
    doc_lengths,
    cotangent,
    w_query,
    w_key,
    w_value,
    w_out,
    w_gate,
    w_up,
    w_down,
    gain_attn,
    gain_mlp,
):
    query_mat, key_mat, value_mat, out_mat, gate_mat, up_mat, down_mat = (
        lax.all_gather(w_query, "dp", axis=0, tiled=True),
        lax.all_gather(w_key, "dp", axis=0, tiled=True),
        lax.all_gather(w_value, "dp", axis=0, tiled=True),
        lax.all_gather(w_out, "dp", axis=1, tiled=True),
        lax.all_gather(w_gate, "dp", axis=0, tiled=True),
        lax.all_gather(w_up, "dp", axis=0, tiled=True),
        lax.all_gather(w_down, "dp", axis=1, tiled=True),
    )
    local_heads = query_mat.shape[1] // HEAD
    row_count = doc_lengths.shape[0]
    group = row_count * SEQ
    segment, positions = documents(doc_lengths)
    cosine, sine = rotation(positions.reshape(-1))

    def heads(matrix):
        return matrix.reshape(row_count, SEQ, local_heads, HEAD)

    inputs = tokens.astype(jnp.float32)
    normed_one, norm_one_back = jax.vjp(rms_norm, inputs, gain_attn)
    gathered_one = lax.all_gather(normed_one.astype(jnp.bfloat16), "tensor", axis=0, tiled=True)
    query_raw = product(gathered_one, query_mat)
    key_raw = product(gathered_one, key_mat)
    value_raw = product(gathered_one, value_mat)
    queries = rotate(query_raw, cosine, sine).astype(jnp.bfloat16)
    keys_low = rotate(key_raw, cosine, sine).astype(jnp.bfloat16)
    mixed_values = (0.5 * value_raw + 0.5 * first_values.astype(jnp.float32)).astype(jnp.bfloat16)
    attended, logsums = lax.map(
        forward_row, (heads(queries), heads(keys_low), heads(mixed_values), segment)
    )
    attended_low = attended.reshape(group, -1).astype(jnp.bfloat16)
    hidden_in = inputs + lax.psum_scatter(
        product(attended_low, out_mat), "tensor", scatter_dimension=0, tiled=True
    )
    normed_two, norm_two_back = jax.vjp(rms_norm, hidden_in, gain_mlp)
    normed_low_two = normed_two.astype(jnp.bfloat16)
    grad_out = cotangent.astype(jnp.float32)
    gathered_two = lax.all_gather(normed_low_two, "tensor", axis=0, tiled=True)
    activated, swiglu_back = jax.vjp(
        swiglu, product(gathered_two, gate_mat), product(gathered_two, up_mat)
    )
    act_low = activated.astype(jnp.bfloat16)
    layer_out = hidden_in + lax.psum_scatter(
        product(act_low, down_mat).astype(jnp.bfloat16), "tensor", scatter_dimension=0, tiled=True
    ).astype(jnp.float32)
    grad_rows = lax.all_gather(cotangent, "tensor", axis=0, tiled=True)
    grad_gate, grad_up = swiglu_back(outer(grad_rows, down_mat))
    gate_low = grad_gate.astype(jnp.bfloat16)
    up_low = grad_up.astype(jnp.bfloat16)
    grad_normed_two = lax.psum_scatter(
        outer(gate_low, gate_mat) + outer(up_low, up_mat), "tensor", scatter_dimension=0, tiled=True
    )
    grad_gate_mat = inner(gathered_two, gate_low)
    grad_up_mat = inner(gathered_two, up_low)
    grad_down_mat = inner(act_low, grad_rows)
    grad_hidden_two, grad_gain_two = norm_two_back(grad_normed_two)
    grad_hidden = grad_out + grad_hidden_two
    grad_branch = lax.all_gather(grad_hidden.astype(jnp.bfloat16), "tensor", axis=0, tiled=True)
    grad_attended = outer(grad_branch, out_mat).astype(jnp.bfloat16)
    grad_out_mat = inner(attended_low, grad_branch)
    grad_rot_query, grad_rot_key, grad_mixed = lax.map(
        backward_row,
        (
            heads(queries),
            heads(keys_low),
            heads(mixed_values),
            segment,
            heads(grad_attended),
            logsums,
        ),
    )
    grad_query_low = rotate_back(grad_rot_query.reshape(group, -1), cosine, sine).astype(
        jnp.bfloat16
    )
    grad_key_low = rotate_back(grad_rot_key.reshape(group, -1), cosine, sine).astype(jnp.bfloat16)
    grad_first = 0.5 * grad_mixed.reshape(group, -1)
    grad_value_low = grad_first.astype(jnp.bfloat16)
    grad_normed_one = lax.psum_scatter(
        outer(grad_query_low, query_mat)
        + outer(grad_key_low, key_mat)
        + outer(grad_value_low, value_mat),
        "tensor",
        scatter_dimension=0,
        tiled=True,
    )
    grad_query_mat = inner(gathered_one, grad_query_low)
    grad_key_mat = inner(gathered_one, grad_key_low)
    grad_value_mat = inner(gathered_one, grad_value_low)
    grad_inputs_one, grad_gain_one = norm_one_back(grad_normed_one)
    grad_tokens = grad_hidden + grad_inputs_one
    summed = (
        lax.psum_scatter(grad_query_mat, "dp", scatter_dimension=0, tiled=True),
        lax.psum_scatter(grad_key_mat, "dp", scatter_dimension=0, tiled=True),
        lax.psum_scatter(grad_value_mat, "dp", scatter_dimension=0, tiled=True),
        lax.psum_scatter(grad_out_mat, "dp", scatter_dimension=1, tiled=True),
        lax.psum_scatter(grad_gate_mat, "dp", scatter_dimension=0, tiled=True),
        lax.psum_scatter(grad_up_mat, "dp", scatter_dimension=0, tiled=True),
        lax.psum_scatter(grad_down_mat, "dp", scatter_dimension=1, tiled=True),
    )
    gain_sums = lax.psum((grad_gain_one, grad_gain_two), ("dp", "tensor"))
    return (
        layer_out.astype(jnp.bfloat16),
        grad_tokens,
        grad_first,
        summed[0],
        summed[1],
        summed[2],
        summed[3],
        summed[4],
        summed[5],
        summed[6],
        gain_sums[0],
        gain_sums[1],
    )


AXES = ("dp", "tensor")
TILE = 256
NEG = -1e30
F32 = jnp.float32
BF16 = jnp.bfloat16


def flat(y, x, c, t):
    return ((y * 2 + x) * 2 + c) * 4 + t


def move(values, to):
    pairs = []
    for y in range(2):
        for x in range(2):
            for c in range(2):
                for t in range(4):
                    pairs.append((flat(y, x, c, t), flat(*to(y, x, c, t))))
    return lax.ppermute(values, AXES, pairs)


def across_x(values):
    return move(values, lambda y, x, c, t: (y, 1 - x, c, t))


def across_y(values):
    return move(values, lambda y, x, c, t: (1 - y, x, c, t))


def across_c(values):
    return move(values, lambda y, x, c, t: (y, x, 1 - c, t))


def along_t(values, step):
    return move(values, lambda y, x, c, t: (y, x, c, (t + step) % 4))


def swap_halves(values):
    return move(values, lambda y, x, c, t: (y, x, t % 2, (t // 2) * 2 + c))


PIECES = []
for _c in range(2):
    PIECES += [
        [[(_c + 2 * i, j) for j in range(2)] for i in range(2)],
        [[(_c + 4 + 2 * i, j) for j in range(2)] for i in range(2)],
        [[(_c + 4 * i, 2 + j) for j in range(2)] for i in range(2)],
        [[(_c + 2 + 4 * i, 2 + j) for j in range(2)] for i in range(2)],
    ]


def gather_pieces(shard):
    along = [shard] + [along_t(shard, d) for d in (1, 2, 3)]
    first = jnp.stack(along[:2])
    second = jnp.stack(along[2:])
    first = jnp.stack([first, across_x(first)])
    second = jnp.stack([second, across_y(second)])
    own = [first, across_y(first), second, across_x(second)]
    return own + [across_c(piece) for piece in own]


def start_loads(pieces, which, held, sem, me, t):
    for array, places in zip(pieces, PIECES, strict=True):
        for i in range(2):
            for j in range(2):
                rel, dist = places[i][j]
                block = (me ^ rel) * 128
                pltpu.make_async_copy(
                    array.at[i, j, which],
                    held.at[(t - dist) & 3, pl.ds(pl.multiple_of(block, 128), 128), :],
                    sem,
                ).start()


def wait_loads(held, sem):
    pltpu.make_async_copy(held, held, sem).wait()


def dot(left, right):
    return jnp.dot(left, right, preferred_element_type=F32)


def dot_nt(left, right):
    return lax.dot_general(left, right, (((1,), (1,)), ((), ())), preferred_element_type=F32)


def dot_tn(left, right):
    return lax.dot_general(left, right, (((0,), (0,)), ((), ())), preferred_element_type=F32)


def any_spec():
    return pl.BlockSpec(memory_space=pl.ANY)


def params(**more):
    return pltpu.CompilerParams(vmem_limit_bytes=62 * 1024 * 1024, **more)


def cost(flops, size, exps=0):
    return pl.CostEstimate(flops=int(flops), bytes_accessed=int(size), transcendentals=int(exps))


def project_kernel(at, own, other, fv0, fv1, cosine, sine, gain, *rest):
    pieces, (normed_out, q_out, k_out, v_out, wq, wk, wv, sems) = rest[:8], rest[8:]
    step = pl.program_id(0)
    me, t = at[0], at[1]
    c, pair = me & 1, t >> 1

    @pl.when(step == 0)
    def _():
        for n, held in enumerate((wq, wk, wv)):
            start_loads(pieces, n, held, sems.at[n], me, t)
        for n, held in enumerate((wq, wk, wv)):
            wait_loads(held, sems.at[n])

    values = jnp.where(step < 2, own[...], other[...]).astype(F32)
    factor = lax.rsqrt(jnp.mean(values * values, axis=1, keepdims=True) + EPSILON)
    normed = (values * factor * gain[...]).astype(BF16)
    normed_out[...] = normed
    cos, sin = cosine[...], sine[...]
    for u in range(2):
        shard = 2 * c + u
        for held, out, scale in ((wq, q_out, 0.125), (wk, k_out, 1.0)):
            raw = dot(normed, held[shard])
            a, b = raw[:, :128], raw[:, 128:]
            out[:, u * 256 : u * 256 + 128] = ((a * cos - b * sin) * scale).astype(BF16)
            out[:, u * 256 + 128 : u * 256 + 256] = ((b * cos + a * sin) * scale).astype(BF16)
        raw = dot(normed, wv[shard])
        first = jnp.where(pair == u, fv0[...], fv1[...]).astype(F32)
        v_out[:, u * 256 : u * 256 + 256] = (0.5 * raw + 0.5 * first).astype(BF16)


def project(at, own, other, fv, cosine, sine, gain, pieces):
    rows, wide = 512, own.shape[1]

    def place(i, at):
        half = jnp.where(i < 2, at[0] & 1, 1 - (at[0] & 1))
        return half * 2 + (i & 1)

    row = lambda width: pl.BlockSpec((rows, width), lambda i, at: (place(i, at), 0))
    grid = pltpu.PrefetchScalarGridSpec(
        num_scalar_prefetch=1,
        grid=(4,),
        in_specs=[
            pl.BlockSpec((rows, wide), lambda i, at: (jnp.minimum(i, 1), 0)),
            pl.BlockSpec((rows, wide), lambda i, at: (jnp.maximum(i - 2, 0), 0)),
            row(256),
            row(256),
            row(128),
            row(128),
            pl.BlockSpec((1, wide), lambda i, at: (0, 0)),
        ]
        + [any_spec()] * 8,
        out_specs=[row(wide), row(512), row(512), row(512)],
        scratch_shapes=[pltpu.VMEM((4, wide, 256), BF16)] * 3 + [pltpu.SemaphoreType.DMA((3,))],
    )
    return pl.pallas_call(
        project_kernel,
        out_shape=[jax.ShapeDtypeStruct((SEQ, wide), BF16)]
        + [jax.ShapeDtypeStruct((SEQ, 512), BF16)] * 3,
        grid_spec=grid,
        compiler_params=params(),
        cost_estimate=cost(2 * SEQ * wide * 1536, 24e6),
        name="project",
    )(at, own, other, fv[0], fv[1], cosine, sine, gain, *pieces)


def head_masks(rows):
    lane = lax.broadcasted_iota(jnp.int32, (rows, 256), 1)
    return (lane & 127) >> 5, lane >> 6


def attend_kernel(bounds, q_ref, k_ref, v_ref, starts, o_ref, lse_ref, kept, top, total, acc):
    of_qk, of_v = head_masks(TILE)
    row = lax.broadcasted_iota(jnp.int32, (TILE, TILE), 0)
    lane = lax.broadcasted_iota(jnp.int32, (TILE, TILE), 1)

    def query_tile(i, carry):
        here = pl.ds(pl.multiple_of(i * TILE, TILE), TILE)
        q = q_ref[here, :]
        zero = jnp.zeros_like(q)
        q4 = jnp.concatenate([jnp.where(of_qk == h, q, zero) for h in range(4)], axis=0)
        begin = starts[here, :]
        begin = jnp.concatenate([begin, begin], axis=1)
        at_row = row + i * TILE
        low = bounds[i]
        top[...] = jnp.full_like(top, NEG)

        def score(j, carry):
            keys = k_ref[pl.ds(pl.multiple_of(j * TILE, TILE), TILE), :]
            s = dot_nt(q4, keys)
            at_lane = lane + j * TILE
            ok = (at_lane >= begin) & (at_lane <= at_row)
            for h in range(4):
                part = slice(h * TILE, (h + 1) * TILE)
                one = jnp.where(ok, s[part], NEG)
                kept[j - low, part, :] = one
                top[part] = jnp.maximum(top[part], jnp.maximum(one[:, :128], one[:, 128:]))
            return carry

        lax.fori_loop(low, i + 1, score, 0)
        highest = jnp.max(top[...], axis=1, keepdims=True)
        top[...] = jnp.broadcast_to(highest, top.shape)
        total[...] = jnp.zeros_like(total)
        acc[...] = jnp.zeros_like(acc)

        def weigh(j, carry):
            values = v_ref[pl.ds(pl.multiple_of(j * TILE, TILE), TILE), :]
            zero = jnp.zeros_like(values)
            exps, parts = [], []
            for h in range(4):
                part = slice(h * TILE, (h + 1) * TILE)
                peak = top[part]
                e = jnp.exp(kept[j - low, part, :] - jnp.concatenate([peak, peak], axis=1))
                total[part] += e[:, :128] + e[:, 128:]
                exps.append(e.astype(BF16))
                parts.append(jnp.where(of_v == h, values, zero))
            acc[...] += dot(jnp.concatenate(exps, axis=1), jnp.concatenate(parts, axis=0))
            return carry

        lax.fori_loop(low, i + 1, weigh, 0)
        sums = jnp.sum(total[...], axis=1, keepdims=True)
        inverse = 1.0 / sums
        scale = jnp.broadcast_to(inverse[:TILE], (TILE, 256))
        for h in range(1, 4):
            scale = jnp.where(of_v == h, inverse[h * TILE : (h + 1) * TILE], scale)
        o_ref[here, :] = (acc[...] * scale).astype(BF16)
        logs = top[...] + jnp.log(jnp.broadcast_to(sums, top.shape))
        for h in range(4):
            turned = logs[h * TILE : (h + 1) * TILE].T
            lse_ref[0, pl.ds(i, 1), h * TILE : (h + 1) * TILE] = turned[:1]
        return carry

    lax.fori_loop(0, SEQ // TILE, query_tile, 0)


def attend(bounds, q, k, v, starts):
    slab = pl.BlockSpec((SEQ, 256), lambda u, b: (0, u))
    tiles = SEQ // TILE
    grid = pltpu.PrefetchScalarGridSpec(
        num_scalar_prefetch=1,
        grid=(2,),
        in_specs=[slab, slab, slab, pl.BlockSpec((SEQ, 128), lambda u, b: (0, 0))],
        out_specs=[slab, pl.BlockSpec((1, tiles, 4 * TILE), lambda u, b: (u, 0, 0))],
        scratch_shapes=[
            pltpu.VMEM((tiles, 4 * TILE, TILE), F32),
            pltpu.VMEM((4 * TILE, 128), F32),
            pltpu.VMEM((4 * TILE, 128), F32),
            pltpu.VMEM((TILE, 256), F32),
        ],
    )
    return pl.pallas_call(
        attend_kernel,
        out_shape=[
            jax.ShapeDtypeStruct((SEQ, 512), BF16),
            jax.ShapeDtypeStruct((2, tiles, 4 * TILE), F32),
        ],
        grid_spec=grid,
        compiler_params=params(),
        cost_estimate=cost(20e9, 12e6, 1e7),
        name="attend",
    )(bounds, q, k, v, starts)


def attend_back_kernel(
    bounds, q_ref, k_ref, v_ref, do_ref, o_ref, lse_ref, starts, cosine, sine, dq_ref, dk_ref, dv_ref, dq_acc, delta, dk_acc, dv_acc
):
    tiles = SEQ // TILE
    of_qk, of_v = head_masks(TILE)
    row = lax.broadcasted_iota(jnp.int32, (TILE, TILE), 0)
    lane = lax.broadcasted_iota(jnp.int32, (TILE, TILE), 1)
    pick = (lax.broadcasted_iota(jnp.int32, (8, 256), 1) >> 6) == lax.broadcasted_iota(
        jnp.int32, (8, 256), 0
    )
    pick = pick.astype(F32)
    dq_acc[...] = jnp.zeros_like(dq_acc)

    def prepare(i, carry):
        here = pl.ds(pl.multiple_of(i * TILE, TILE), TILE)
        both = do_ref[here, :].astype(F32) * o_ref[here, :].astype(F32)
        sums = lax.dot_general(
            pick, both, (((1,), (1,)), ((), ())), precision=lax.Precision.HIGHEST, preferred_element_type=F32
        )
        for h in range(4):
            delta[pl.ds(i, 1), h * TILE : (h + 1) * TILE] = sums[h : h + 1]
        return carry

    lax.fori_loop(0, tiles, prepare, 0)

    def rotate_out(values, here, out, scale):
        a, b = values[:, :128], values[:, 128:]
        cos, sin = cosine[here, :], sine[here, :]
        out[here, :128] = ((a * cos + b * sin) * scale).astype(BF16)
        out[here, 128:] = ((b * cos - a * sin) * scale).astype(BF16)

    def split(values, of):
        zero = jnp.zeros_like(values)
        return jnp.concatenate([jnp.where(of == h, values, zero) for h in range(4)], axis=0)

    def key_tile(j, carry):
        there = pl.ds(pl.multiple_of(j * TILE, TILE), TILE)
        keys, values = k_ref[there, :], v_ref[there, :]
        k4 = split(keys, of_qk)
        at_row = row + j * TILE
        dk_acc[...] = jnp.zeros_like(dk_acc)
        dv_acc[...] = jnp.zeros_like(dv_acc)

        def query_tile(i, carry):
            here = pl.ds(pl.multiple_of(i * TILE, TILE), TILE)
            q4 = split(q_ref[here, :], of_qk)
            do4 = split(do_ref[here, :], of_v)
            s = dot_nt(keys, q4)
            dp = dot_nt(values, do4)
            at_lane = lane + i * TILE
            ok = (at_row >= starts[pl.ds(i, 1), :]) & (at_row <= at_lane)
            lse, shift = lse_ref[0, pl.ds(i, 1), :], delta[pl.ds(i, 1), :]
            ps, dss = [], []
            for h in range(4):
                part = slice(h * TILE, (h + 1) * TILE)
                p = jnp.exp(jnp.where(ok, s[:, part] - lse[:, part], NEG))
                ds = p * (dp[:, part] - shift[:, part])
                ps.append(p.astype(BF16))
                dss.append(ds.astype(BF16))
            dv_acc[...] += dot(jnp.concatenate(ps, axis=1), do4)
            dk_acc[...] += dot(jnp.concatenate(dss, axis=1), q4)
            dq_acc[here, :] += dot_tn(jnp.concatenate(dss, axis=0), k4)
            return carry

        lax.fori_loop(j, bounds[tiles + j] + 1, query_tile, 0)
        rotate_out(dk_acc[...], there, dk_ref, 1.0)
        dv_ref[there, :] = (0.5 * dv_acc[...]).astype(BF16)
        return carry

    lax.fori_loop(0, tiles, key_tile, 0)

    def finish(i, carry):
        here = pl.ds(pl.multiple_of(i * TILE, TILE), TILE)
        rotate_out(dq_acc[here, :], here, dq_ref, 0.125)
        return carry

    lax.fori_loop(0, tiles, finish, 0)


def attend_back(bounds, q, k, v, do, o, lse, starts, cosine, sine):
    slab = pl.BlockSpec((SEQ, 256), lambda u, b: (0, u))
    whole = lambda shape: pl.BlockSpec(shape, lambda u, b: (0,) * len(shape))
    tiles = SEQ // TILE
    grid = pltpu.PrefetchScalarGridSpec(
        num_scalar_prefetch=1,
        grid=(2,),
        in_specs=[slab] * 5
        + [
            pl.BlockSpec((1, tiles, 4 * TILE), lambda u, b: (u, 0, 0)),
            whole((tiles, TILE)),
            whole((SEQ, 128)),
            whole((SEQ, 128)),
        ],
        out_specs=[slab] * 3,
        scratch_shapes=[
            pltpu.VMEM((SEQ, 256), F32),
            pltpu.VMEM((tiles, 4 * TILE), F32),
            pltpu.VMEM((TILE, 256), F32),
            pltpu.VMEM((TILE, 256), F32),
        ],
    )
    return pl.pallas_call(
        attend_back_kernel,
        out_shape=[jax.ShapeDtypeStruct((SEQ, 512), BF16)] * 3,
        grid_spec=grid,
        compiler_params=params(),
        cost_estimate=cost(50e9, 20e6, 1e7),
        name="attend_back",
    )(bounds, q, k, v, do, o, lse, starts, cosine, sine)


def mlp_kernel(at, att_own, att_other, tok, cot, gain, *rest):
    small, big, rest = rest[:8], rest[8:16], rest[16:]
    (out, gh_out, gb_out, n2_out, hid_out, ga_own, ga_other, gg_out) = rest[:8]
    (wo, wg, wu, wd, sems) = rest[8:]
    step = pl.program_id(0)
    me, t = at[0], at[1]
    c = me & 1

    @pl.when(step == 0)
    def _():
        start_loads(small, 3, wo, sems.at[0], me, t)
        for n, held in enumerate((wg, wu, wd)):
            start_loads(big, n, held, sems.at[1 + n], me, t)
        wait_loads(wo, sems.at[0])
        gg_out[...] = jnp.zeros_like(gg_out)

    hidden = tok[...].astype(F32)
    for e, att in enumerate((att_own, att_other)):
        for u in range(2):
            hidden += dot_nt(att[:, u * 256 : u * 256 + 256], wo[2 * (c ^ e) + u])
    factor = lax.rsqrt(jnp.mean(hidden * hidden, axis=1, keepdims=True) + EPSILON)
    gains = gain[...]
    normed = (hidden * factor * gains).astype(BF16)
    n2_out[...] = normed
    g = cot[...]

    @pl.when(step == 0)
    def _():
        for n, held in enumerate((wg, wu, wd)):
            wait_loads(held, sems.at[1 + n])

    down = jnp.zeros_like(hidden)
    back = jnp.zeros_like(hidden)
    for k in range(4):
        gate, up, grad_act = dot(normed, wg[k]), dot(normed, wu[k]), dot(g, wd[k])
        sig = 1.0 / (1.0 + jnp.exp(-gate))
        silu = gate * sig
        act = (silu * up).astype(BF16)
        grad_up = (grad_act * silu).astype(BF16)
        grad_gate = (grad_act * up * (sig * (1.0 + gate * (1.0 - sig)))).astype(BF16)
        hid_out[0, k], hid_out[1, k], hid_out[2, k] = grad_gate, grad_up, act
        down += dot_nt(act, wd[k])
        back += dot_nt(grad_gate, wg[k]) + dot_nt(grad_up, wu[k])
    out[...] = (hidden + down).astype(BF16)
    gg_out[...] += jnp.sum((back * hidden * factor).reshape(-1, 8, back.shape[1]), axis=0)
    scaled = back * gains
    mean = jnp.mean(scaled * hidden, axis=1, keepdims=True)
    grad_hidden = g.astype(F32) + factor * scaled - hidden * (factor * factor * factor * mean)
    gh_out[...] = grad_hidden
    branch = grad_hidden.astype(BF16)
    gb_out[...] = branch
    for e, ga in enumerate((ga_own, ga_other)):
        for u in range(2):
            ga[:, u * 256 : u * 256 + 256] = dot(branch, wo[2 * (c ^ e) + u]).astype(BF16)


def mlp(at, att_own, att_other, tok, cot, gain, small, big):
    count, wide = tok.shape
    rows, part = 256, big[0].shape[-1]
    row = lambda width: pl.BlockSpec((rows, width), lambda i, at: (i, 0))
    one = pl.BlockSpec((1, wide), lambda i, at: (0, 0))
    grid = pltpu.PrefetchScalarGridSpec(
        num_scalar_prefetch=1,
        grid=(count // rows,),
        in_specs=[row(512), row(512), row(wide), row(wide), one] + [any_spec()] * 16,
        out_specs=[
            row(wide),
            row(wide),
            row(wide),
            row(wide),
            pl.BlockSpec((3, 4, rows, part), lambda i, at: (0, 0, i, 0)),
            row(512),
            row(512),
            pl.BlockSpec((8, wide), lambda i, at: (0, 0)),
        ],
        scratch_shapes=[pltpu.VMEM((4, wide, 256), BF16)]
        + [pltpu.VMEM((4, wide, part), BF16)] * 3
        + [pltpu.SemaphoreType.DMA((4,))],
    )
    tokens = lambda width, kind=BF16: jax.ShapeDtypeStruct((count, width), kind)
    return pl.pallas_call(
        mlp_kernel,
        out_shape=[
            tokens(wide),
            tokens(wide, F32),
            tokens(wide),
            tokens(wide),
            jax.ShapeDtypeStruct((3, 4, count, part), BF16),
            tokens(512),
            tokens(512),
            jax.ShapeDtypeStruct((8, wide), F32),
        ],
        grid_spec=grid,
        compiler_params=params(),
        cost_estimate=cost(2 * count * wide * (6 * 4 * part + 2 * wide), 60e6, 3e6),
        name="mlp",
    )(at, att_own, att_other, tok, cot, gain, *small, *big)


def turn_rows(source, parity, held):
    for r in range(4):
        block = source[:, pl.ds(pl.multiple_of((r * 2 + parity) * 128, 128), 128)]
        held[r * 128 : (r + 1) * 128, :] = block.T


def weight_send_kernel(at, n2, g, hid, out, turned):
    n, k = pl.program_id(0), pl.program_id(1)
    parity = 1 - (at[0] & 1)

    @pl.when((n == 0) & (k == 0))
    def _():
        turn_rows(n2, parity, turned)

    @pl.when((n == 2) & (k == 0))
    def _():
        turn_rows(g, parity, turned)

    out[0, 0] = dot(turned[...], hid[0, 0]).astype(BF16).reshape(out.shape[2:])


def weight_send(at, n2, g, hid):
    count, wide = n2.shape
    part = hid.shape[-1]
    whole = pl.BlockSpec((count, wide), lambda n, k, at: (0, 0))
    grid = pltpu.PrefetchScalarGridSpec(
        num_scalar_prefetch=1,
        grid=(3, 4),
        in_specs=[whole, whole, pl.BlockSpec((1, 1, count, part), lambda n, k, at: (n, k, 0, 0))],
        out_specs=pl.BlockSpec((1, 1, 4, 128, part), lambda n, k, at: (n, k, 0, 0, 0)),
        scratch_shapes=[pltpu.VMEM((512, count), BF16)],
    )
    return pl.pallas_call(
        weight_send_kernel,
        out_shape=jax.ShapeDtypeStruct((3, 4, 4, 128, part), BF16),
        grid_spec=grid,
        compiler_params=params(),
        cost_estimate=cost(2 * count * 512 * part * 12, 30e6),
        name="weight_send",
    )(at, n2, g, hid)


def weight_keep_kernel(at, n2, g, hid, got, first_send, first_keep, second_send, second_keep, turned):
    n, d = pl.program_id(0), pl.program_id(1)
    me = at[0]

    @pl.when((n == 0) & (d == 0))
    def _():
        turn_rows(n2, me & 1, turned)

    @pl.when((n == 2) & (d == 0))
    def _():
        turn_rows(g, me & 1, turned)

    def block(rel):
        index = (me >> 1) ^ rel
        rows = turned[pl.ds(pl.multiple_of(index * 128, 128), 128), :]
        return rows, got[0, 0, index].astype(F32)

    rows, extra = zip(*[block(rel) for rel in range(4)], strict=True)
    product = dot(jnp.concatenate(rows, axis=0), hid[0, 0])
    done = [(product[r * 128 : (r + 1) * 128] + extra[r]).astype(BF16) for r in range(4)]

    @pl.when(d < 2)
    def _():
        first_send[0, 0, 0], first_send[0, 1, 0] = done[1], done[3]
        first_keep[0, 0, 0], first_keep[0, 1, 0] = done[0], done[2]

    @pl.when(d >= 2)
    def _():
        second_send[0, 0, 0], second_send[0, 1, 0] = done[2], done[3]
        second_keep[0, 0, 0], second_keep[0, 1, 0] = done[0], done[1]


def weight_keep(at, n2, g, hid, got):
    count, wide = n2.shape
    part = hid.shape[-1]
    whole = pl.BlockSpec((count, wide), lambda n, d, at: (0, 0))
    first = pl.BlockSpec((1, 2, 1, 128, part), lambda n, d, at: (jnp.minimum(d, 1), 0, n, 0, 0))
    second = pl.BlockSpec((1, 2, 1, 128, part), lambda n, d, at: (jnp.maximum(d - 2, 0), 0, n, 0, 0))
    grid = pltpu.PrefetchScalarGridSpec(
        num_scalar_prefetch=1,
        grid=(3, 4),
        in_specs=[
            whole,
            whole,
            pl.BlockSpec((1, 1, count, part), lambda n, d, at: (n, (at[1] + d) & 3, 0, 0)),
            pl.BlockSpec((1, 1, 4, 128, part), lambda n, d, at: (n, (at[1] + d) & 3, 0, 0, 0)),
        ],
        out_specs=[first, first, second, second],
        scratch_shapes=[pltpu.VMEM((512, count), BF16)],
    )
    return pl.pallas_call(
        weight_keep_kernel,
        out_shape=[jax.ShapeDtypeStruct((2, 2, 3, 128, part), BF16)] * 4,
        grid_spec=grid,
        compiler_params=params(),
        cost_estimate=cost(2 * count * 512 * part * 12, 40e6),
        name="weight_keep",
    )(at, n2, g, hid, got)


def add(left, right):
    return (left.astype(F32) + right.astype(F32)).astype(BF16)


def scatter_xy(first_send, first_keep, second_send, second_keep):
    got = across_x(first_send)
    send, keep = add(first_keep[:, 1], got[:, 1]), add(first_keep[:, 0], got[:, 0])
    first = add(keep, across_y(send))
    got = across_y(second_send)
    send, keep = add(second_keep[:, 1], got[:, 1]), add(second_keep[:, 0], got[:, 0])
    return first, add(keep, across_x(send))


def scatter_t(pieces):
    total = pieces[0].astype(F32)
    for d in (1, 2, 3):
        total = total + along_t(pieces[d], d).astype(F32)
    return total


def project_back_kernel(at, dq, dk, dv, *rest):
    pieces, (out, wq, wk, wv, sems) = rest[:8], rest[8:]
    me, t = at[0], at[1]
    c = me & 1

    @pl.when(pl.program_id(0) == 0)
    def _():
        for n, held in enumerate((wq, wk, wv)):
            start_loads(pieces, n, held, sems.at[n], me, t)
        for n, held in enumerate((wq, wk, wv)):
            wait_loads(held, sems.at[n])

    total = None
    for u in range(2):
        for grad, held in ((dq, wq), (dk, wk), (dv, wv)):
            term = dot_nt(grad[:, u * 256 : u * 256 + 256], held[2 * c + u])
            total = term if total is None else total + term
    out[...] = total.astype(out.dtype)


def project_back(at, dq, dk, dv, pieces, other, kind):
    rows, wide = 512, 1024
    row = pl.BlockSpec((rows, 512), lambda i, at: (((at[0] & 1) ^ other) * 2 + i, 0))
    grid = pltpu.PrefetchScalarGridSpec(
        num_scalar_prefetch=1,
        grid=(2,),
        in_specs=[row] * 3 + [any_spec()] * 8,
        out_specs=pl.BlockSpec((rows, wide), lambda i, at: (i, 0)),
        scratch_shapes=[pltpu.VMEM((4, wide, 256), BF16)] * 3 + [pltpu.SemaphoreType.DMA((3,))],
    )
    return pl.pallas_call(
        project_back_kernel,
        out_shape=jax.ShapeDtypeStruct((SEQ // 2, wide), kind),
        grid_spec=grid,
        compiler_params=params(),
        cost_estimate=cost(SEQ * wide * 1536, 14e6),
        name="project_back",
    )(at, dq, dk, dv, *pieces)


def parity_columns(values, parity):
    shaped = values.reshape(values.shape[0], 4, 2, 128)
    return lax.dynamic_index_in_dim(shaped, parity, 2, keepdims=False).reshape(values.shape[0], 512)


def fast_body(tokens, first_values, doc_lengths, cotangent, w_query, w_key, w_value, w_out, w_gate, w_up, w_down, gain_attn, gain_mlp):
    me, t = lax.axis_index("dp"), lax.axis_index("tensor")
    y, x, c = me // 4, (me // 2) % 2, me % 2
    pair, side = t // 2, t % 2
    wide = tokens.shape[1]
    tiles = SEQ // TILE
    at = jnp.where(jnp.arange(8, dtype=jnp.int32) == 0, me, t).astype(jnp.int32)

    def halves_apart(matrix):
        return matrix.reshape(-1, 4, 2, 32).swapaxes(1, 2).reshape(-1, 256)

    small_shard = jnp.stack([halves_apart(w_query), halves_apart(w_key), w_value, w_out.T])
    big_shard = jnp.stack([w_gate, w_up, w_down.T])

    own = swap_halves(tokens)
    small = gather_pieces(small_shard)
    other = across_c(own)
    blocks = first_values.reshape(2, SEQ, 256)

    def first_round(r):
        block = lax.dynamic_index_in_dim(blocks, r ^ (t % 2), 0, keepdims=False)
        return move(block, lambda y, x, c, t: (y, x, t // 2, 2 * (r ^ (t % 2)) + c))

    fv = [first_round(0), first_round(1)]
    big = gather_pieces(big_shard)
    cot = swap_halves(cotangent)

    lengths = jnp.where(c == side, doc_lengths, across_c(doc_lengths))
    lengths = lax.dynamic_index_in_dim(lengths, pair, 0, keepdims=False)
    order = jnp.arange(DOCS, dtype=jnp.int32)
    ends = jnp.sum(jnp.where(order[None, :] <= order[:, None], lengths[None, :], 0), axis=1)
    places = jnp.arange(SEQ, dtype=jnp.int32)
    starts = jnp.max(jnp.where(ends[None, :] <= places[:, None], ends[None, :], 0), axis=1)
    last = jnp.arange(tiles, dtype=jnp.int32) * TILE + (TILE - 1)
    finish = jnp.min(jnp.where(ends[None, :] > last[:, None], ends[None, :], SEQ), axis=1)
    bounds = jnp.concatenate([starts.reshape(tiles, TILE)[:, 0] // TILE, (finish - 1) // TILE])
    starts_wide = jnp.broadcast_to(starts[:, None], (SEQ, 128))
    freqs = 10000.0 ** (-(jnp.arange(32, dtype=F32) * 2.0 / HEAD))
    angles = (places - starts).astype(F32)[:, None] * jnp.tile(freqs, 4)[None, :]
    cosine, sine = jnp.cos(angles), jnp.sin(angles)

    normed_one, q, k, v = project(at, own, other, fv, cosine, sine, gain_attn[None], small)
    attended, lse = attend(bounds, q, k, v, starts_wide)
    by_half = attended.reshape(2, SEQ // 2, 512)
    att_own = lax.dynamic_index_in_dim(by_half, c, 0, keepdims=False)
    att_other = across_c(lax.dynamic_index_in_dim(by_half, 1 - c, 0, keepdims=False))
    out, grad_hidden, branch, normed_two, hid, ga_own, ga_other, gain_two = mlp(
        at, att_own, att_other, own, cot, gain_mlp[None], small, big
    )
    layer_out = swap_halves(out)

    ga_got = across_c(ga_other)
    do = jnp.where(c == 0, jnp.concatenate([ga_own, ga_got]), jnp.concatenate([ga_got, ga_own]))

    got = across_c(weight_send(at, normed_two, cot, hid))
    kept = weight_keep(at, normed_two, cot, hid, got)
    first, second = scatter_xy(*kept)
    grads = scatter_t([first[0], first[1], second[0], second[1]])

    att_all = jnp.where(c == 0, jnp.concatenate([att_own, att_other], 1), jnp.concatenate([att_other, att_own], 1))
    shape = (2, 2, 128, 4, 256)
    sent = dot_tn(parity_columns(branch, 1 - c), att_all).astype(BF16)
    held = (dot_tn(parity_columns(branch, c), att_all) + across_c(sent).astype(F32)).astype(BF16)
    held = held.reshape(shape).transpose(3, 0, 1, 2, 4)

    def pick(values, axis, index):
        return lax.dynamic_index_in_dim(values, index, axis, keepdims=False)

    def relative(values, axis):
        order = jnp.stack([pick(values, axis, (t + d) % 4) for d in range(4)])
        return order

    held = relative(held, 0)

    def by_neighbour(values, rows):
        if rows == "x":
            send, keep = pick(values, 2, 1 - x), pick(values, 2, x)
            flip = y
        else:
            send, keep = pick(values, 1, 1 - y), pick(values, 1, y)
            flip = x
        turn = lambda item: jnp.where(flip == 0, item, item[:, ::-1])
        return turn(send), turn(keep)

    first, second = scatter_xy(*by_neighbour(held[:2], "x"), *by_neighbour(held[2:], "y"))
    grad_out = scatter_t([first[0], first[1], second[0], second[1]])

    dq, dk, dv = attend_back(bounds, q, k, v, do, attended, lse, starts.reshape(tiles, TILE), cosine, sine)

    def first_back(r):
        slab = jnp.where(pair == r, dv[:, :256], dv[:, 256:])
        return move(slab, lambda y, x, c, t: (y, x, t % 2, 2 * c + ((t // 2) ^ r)))

    fb = [first_back(0), first_back(1)]
    odd = t % 2
    grad_first = jnp.concatenate(
        [jnp.where(odd == 0, fb[0], fb[1]), jnp.where(odd == 0, fb[1], fb[0])]
    ).astype(F32)

    gn_got = across_c(project_back(at, dq, dk, dv, small, 1, BF16))
    stacked = jnp.concatenate([dq, dk, dv], axis=1)
    sent = dot_tn(parity_columns(normed_one, 1 - c), stacked).astype(BF16)
    mine = dot_tn(parity_columns(normed_one, c), stacked).astype(BF16)
    got = across_c(sent)

    def arrange(values):
        return values.reshape(2, 2, 128, 3, 2, 256).transpose(4, 0, 1, 3, 2, 5)

    first, second = scatter_xy(*by_neighbour(arrange(mine), "x"), *by_neighbour(arrange(got), "y"))
    all_four = jnp.where(c == 0, jnp.concatenate([first, second]), jnp.concatenate([second, first]))
    gq, gk, gv = scatter_t(list(relative(all_four, 0)))

    def halves_together(matrix):
        return matrix.reshape(-1, 2, 4, 32).swapaxes(1, 2).reshape(-1, 256)

    gn_keep = project_back(at, dq, dk, dv, small, 0, F32)
    grad_normed = gn_keep + gn_got.astype(F32)
    values = own.astype(F32)
    factor = lax.rsqrt(jnp.mean(values * values, axis=1, keepdims=True) + EPSILON)
    scaled = grad_normed * gain_attn[None]
    mean = jnp.mean(scaled * values, axis=1, keepdims=True)
    grad_tokens = grad_hidden + factor * scaled - values * (factor * factor * factor * mean)
    grad_tokens = swap_halves(grad_tokens.astype(BF16)).astype(F32)
    gain_one = jnp.sum(grad_normed * values * factor, axis=0)
    gains = jnp.stack([gain_one, jnp.sum(gain_two, axis=0)]).reshape(16, 128)
    gains = gains + across_c(gains)
    gains = gains + across_x(gains)
    gains = gains + across_y(gains)
    gains = gains + move(gains, lambda y, x, c, t: (y, x, c, t ^ 1))
    gains = gains + move(gains, lambda y, x, c, t: (y, x, c, t ^ 2))
    gains = gains.reshape(2, wide)
    return (
        layer_out,
        grad_tokens,
        grad_first,
        halves_together(gq),
        halves_together(gk),
        gv,
        grad_out.T,
        grads[0],
        grads[1],
        grads[2].T,
        gains[0],
        gains[1],
    )


def solution(mesh):
    fits = dict(mesh.shape) == {"dp": 8, "tensor": 4}
    placed = (
        P(("dp", "tensor"), None),
        P("dp", "tensor"),
        P("dp", None),
        P(("dp", "tensor"), None),
        P("dp", "tensor"),
        P("dp", "tensor"),
        P("dp", "tensor"),
        P("tensor", "dp"),
        P("dp", "tensor"),
        P("dp", "tensor"),
        P("tensor", "dp"),
        P(),
        P(),
    )
    return jax.shard_map(
        fast_body if fits else general_body,
        mesh=mesh,
        in_specs=placed,
        out_specs=(
            P(("dp", "tensor"), None),
            P(("dp", "tensor"), None),
            P("dp", "tensor"),
            P("dp", "tensor"),
            P("dp", "tensor"),
            P("dp", "tensor"),
            P("tensor", "dp"),
            P("dp", "tensor"),
            P("dp", "tensor"),
            P("tensor", "dp"),
            P(),
            P(),
        ),
        check_vma=False,
    )
```

```python
import functools

import jax
import jax.numpy as jnp
from jax import lax
from jax.experimental import pallas as pl
from jax.experimental.pallas import tpu as pltpu
from jax.sharding import PartitionSpec as P

HEAD = 64
SEQ = 2048
DOCS = 8
EPSILON = 1e-05


def rms_norm(values, gain):
    factor = lax.rsqrt(jnp.mean(values * values, axis=1, keepdims=True) + EPSILON)
    return values * factor * gain


def documents(doc_lengths):
    ends = jnp.cumsum(doc_lengths, axis=1)
    starts = ends - doc_lengths
    places = jnp.arange(SEQ, dtype=jnp.int32)
    segment = jnp.sum((places[None, :, None] >= ends[:, None, :]).astype(jnp.int32), axis=2)
    member = segment[:, :, None] == jnp.arange(DOCS, dtype=jnp.int32)[None, None, :]
    offset = jnp.sum(jnp.where(member, starts[:, None, :], 0), axis=2)
    return (segment, (places[None, :] - offset).astype(jnp.float32))


def rotation(positions):
    half = HEAD // 2
    freqs = 10000.0 ** (-(jnp.arange(half, dtype=jnp.float32) * 2.0 / HEAD))
    angles = positions[:, None] * freqs[None, :]
    return (jnp.cos(angles), jnp.sin(angles))


def rotate(values, cosine, sine):
    shaped = values.reshape(values.shape[0], -1, HEAD)
    half = HEAD // 2
    first = shaped[:, :, :half]
    second = shaped[:, :, half:]
    cos_rows = cosine[:, None, :]
    sin_rows = sine[:, None, :]
    turned = jnp.concatenate(
        [first * cos_rows - second * sin_rows, second * cos_rows + first * sin_rows], axis=2
    )
    return turned.reshape(values.shape)


def rotate_back(grads, cosine, sine):
    shaped = grads.reshape(grads.shape[0], -1, HEAD)
    half = HEAD // 2
    first = shaped[:, :, :half]
    second = shaped[:, :, half:]
    cos_rows = cosine[:, None, :]
    sin_rows = sine[:, None, :]
    turned = jnp.concatenate(
        [first * cos_rows + second * sin_rows, second * cos_rows - first * sin_rows], axis=2
    )
    return turned.reshape(grads.shape)


def swiglu(gate, up_val):
    return jax.nn.silu(gate) * up_val


def product(left, right):
    return jnp.dot(left, right, preferred_element_type=jnp.float32)


def inner(left, right):
    return lax.dot_general(
        left, right, (((0,), (0,)), ((), ())), preferred_element_type=jnp.float32
    )


def outer(left, right):
    return lax.dot_general(
        left, right, (((1,), (1,)), ((), ())), preferred_element_type=jnp.float32
    )


def block_scores(queries, keys_all, segment, start, width):
    query_block = lax.dynamic_slice_in_dim(queries, start, width, 0)
    query_seg = lax.dynamic_slice_in_dim(segment, start, width, 0)
    scores = (
        jnp.einsum("qhd,khd->hqk", query_block, keys_all, preferred_element_type=jnp.float32)
        * 0.125
    )
    places = jnp.arange(SEQ, dtype=jnp.int32)
    rows_at = start + jnp.arange(width, dtype=jnp.int32)
    allowed = (query_seg[:, None] == segment[None, :]) & (places[None, :] <= rows_at[:, None])
    return (query_block, jnp.where(allowed[None], scores, -1e30))


def forward_row(pieces):
    queries, keys_all, values_all, segment = pieces
    width = min(512, SEQ)
    count = SEQ // width

    def forward_one_block(index):
        unused, scores = block_scores(queries, keys_all, segment, index * width, width)
        top = jnp.max(scores, axis=2, keepdims=True)
        expo = jnp.exp(scores - top)
        total = jnp.sum(expo, axis=2, keepdims=True)
        weights = (expo / total).astype(jnp.bfloat16)
        result = jnp.einsum("hqk,khd->qhd", weights, values_all, preferred_element_type=jnp.float32)
        return (result, (top + jnp.log(total))[:, :, 0])

    results, logsums = lax.map(forward_one_block, jnp.arange(count, dtype=jnp.int32))
    return (results.reshape(SEQ, queries.shape[1], HEAD), logsums)


def backward_row(pieces):
    queries, keys_all, values_all, segment, grad_rows, logsums = pieces
    width = min(512, SEQ)
    count = SEQ // width

    def backward_one_block(carry, extra):
        index, logsum = extra
        start = index * width
        query_block, scores = block_scores(queries, keys_all, segment, start, width)
        probs = jnp.exp(scores - logsum[:, :, None])
        grad_block = lax.dynamic_slice_in_dim(grad_rows, start, width, 0)
        grad_probs = jnp.einsum(
            "qhd,khd->hqk", grad_block, values_all, preferred_element_type=jnp.float32
        )
        delta = jnp.sum(probs * grad_probs, axis=2, keepdims=True)
        grad_scores = (probs * (grad_probs - delta)).astype(jnp.bfloat16)
        grad_query = (
            jnp.einsum("hqk,khd->qhd", grad_scores, keys_all, preferred_element_type=jnp.float32)
            * 0.125
        )
        grad_keys = (
            carry[0]
            + jnp.einsum(
                "hqk,qhd->khd", grad_scores, query_block, preferred_element_type=jnp.float32
            )
            * 0.125
        )
        grad_values = carry[1] + jnp.einsum(
            "hqk,qhd->khd",
            probs.astype(jnp.bfloat16),
            grad_block,
            preferred_element_type=jnp.float32,
        )
        return ((grad_keys, grad_values), grad_query)

    zeros = jnp.zeros(keys_all.shape, jnp.float32)
    sums, grad_queries = lax.scan(
        backward_one_block, (zeros, zeros), (jnp.arange(count, dtype=jnp.int32), logsums)
    )
    return (grad_queries.reshape(SEQ, queries.shape[1], HEAD), sums[0], sums[1])


def general_body(
    tokens,
    first_values,
    doc_lengths,
    cotangent,
    w_query,
    w_key,
    w_value,
    w_out,
    w_gate,
    w_up,
    w_down,
    gain_attn,
    gain_mlp,
):
    query_mat, key_mat, value_mat, out_mat, gate_mat, up_mat, down_mat = (
        lax.all_gather(w_query, "dp", axis=0, tiled=True),
        lax.all_gather(w_key, "dp", axis=0, tiled=True),
        lax.all_gather(w_value, "dp", axis=0, tiled=True),
        lax.all_gather(w_out, "dp", axis=1, tiled=True),
        lax.all_gather(w_gate, "dp", axis=0, tiled=True),
        lax.all_gather(w_up, "dp", axis=0, tiled=True),
        lax.all_gather(w_down, "dp", axis=1, tiled=True),
    )
    local_heads = query_mat.shape[1] // HEAD
    row_count = doc_lengths.shape[0]
    group = row_count * SEQ
    segment, positions = documents(doc_lengths)
    cosine, sine = rotation(positions.reshape(-1))

    def heads(matrix):
        return matrix.reshape(row_count, SEQ, local_heads, HEAD)

    inputs = tokens.astype(jnp.float32)
    normed_one, norm_one_back = jax.vjp(rms_norm, inputs, gain_attn)
    gathered_one = lax.all_gather(normed_one.astype(jnp.bfloat16), "tensor", axis=0, tiled=True)
    query_raw = product(gathered_one, query_mat)
    key_raw = product(gathered_one, key_mat)
    value_raw = product(gathered_one, value_mat)
    queries = rotate(query_raw, cosine, sine).astype(jnp.bfloat16)
    keys_low = rotate(key_raw, cosine, sine).astype(jnp.bfloat16)
    mixed_values = (0.5 * value_raw + 0.5 * first_values.astype(jnp.float32)).astype(jnp.bfloat16)
    attended, logsums = lax.map(
        forward_row, (heads(queries), heads(keys_low), heads(mixed_values), segment)
    )
    attended_low = attended.reshape(group, -1).astype(jnp.bfloat16)
    hidden_in = inputs + lax.psum_scatter(
        product(attended_low, out_mat), "tensor", scatter_dimension=0, tiled=True
    )
    normed_two, norm_two_back = jax.vjp(rms_norm, hidden_in, gain_mlp)
    normed_low_two = normed_two.astype(jnp.bfloat16)
    grad_out = cotangent.astype(jnp.float32)
    gathered_two = lax.all_gather(normed_low_two, "tensor", axis=0, tiled=True)
    activated, swiglu_back = jax.vjp(
        swiglu, product(gathered_two, gate_mat), product(gathered_two, up_mat)
    )
    act_low = activated.astype(jnp.bfloat16)
    layer_out = hidden_in + lax.psum_scatter(
        product(act_low, down_mat).astype(jnp.bfloat16), "tensor", scatter_dimension=0, tiled=True
    ).astype(jnp.float32)
    grad_rows = lax.all_gather(cotangent, "tensor", axis=0, tiled=True)
    grad_gate, grad_up = swiglu_back(outer(grad_rows, down_mat))
    gate_low = grad_gate.astype(jnp.bfloat16)
    up_low = grad_up.astype(jnp.bfloat16)
    grad_normed_two = lax.psum_scatter(
        outer(gate_low, gate_mat) + outer(up_low, up_mat), "tensor", scatter_dimension=0, tiled=True
    )
    grad_gate_mat = inner(gathered_two, gate_low)
    grad_up_mat = inner(gathered_two, up_low)
    grad_down_mat = inner(act_low, grad_rows)
    grad_hidden_two, grad_gain_two = norm_two_back(grad_normed_two)
    grad_hidden = grad_out + grad_hidden_two
    grad_branch = lax.all_gather(grad_hidden.astype(jnp.bfloat16), "tensor", axis=0, tiled=True)
    grad_attended = outer(grad_branch, out_mat).astype(jnp.bfloat16)
    grad_out_mat = inner(attended_low, grad_branch)
    grad_rot_query, grad_rot_key, grad_mixed = lax.map(
        backward_row,
        (
            heads(queries),
            heads(keys_low),
            heads(mixed_values),
            segment,
            heads(grad_attended),
            logsums,
        ),
    )
    grad_query_low = rotate_back(grad_rot_query.reshape(group, -1), cosine, sine).astype(
        jnp.bfloat16
    )
    grad_key_low = rotate_back(grad_rot_key.reshape(group, -1), cosine, sine).astype(jnp.bfloat16)
    grad_first = 0.5 * grad_mixed.reshape(group, -1)
    grad_value_low = grad_first.astype(jnp.bfloat16)
    grad_normed_one = lax.psum_scatter(
        outer(grad_query_low, query_mat)
        + outer(grad_key_low, key_mat)
        + outer(grad_value_low, value_mat),
        "tensor",
        scatter_dimension=0,
        tiled=True,
    )
    grad_query_mat = inner(gathered_one, grad_query_low)
    grad_key_mat = inner(gathered_one, grad_key_low)
    grad_value_mat = inner(gathered_one, grad_value_low)
    grad_inputs_one, grad_gain_one = norm_one_back(grad_normed_one)
    grad_tokens = grad_hidden + grad_inputs_one
    summed = (
        lax.psum_scatter(grad_query_mat, "dp", scatter_dimension=0, tiled=True),
        lax.psum_scatter(grad_key_mat, "dp", scatter_dimension=0, tiled=True),
        lax.psum_scatter(grad_value_mat, "dp", scatter_dimension=0, tiled=True),
        lax.psum_scatter(grad_out_mat, "dp", scatter_dimension=1, tiled=True),
        lax.psum_scatter(grad_gate_mat, "dp", scatter_dimension=0, tiled=True),
        lax.psum_scatter(grad_up_mat, "dp", scatter_dimension=0, tiled=True),
        lax.psum_scatter(grad_down_mat, "dp", scatter_dimension=1, tiled=True),
    )
    gain_sums = lax.psum((grad_gain_one, grad_gain_two), ("dp", "tensor"))
    return (
        layer_out.astype(jnp.bfloat16),
        grad_tokens,
        grad_first,
        summed[0],
        summed[1],
        summed[2],
        summed[3],
        summed[4],
        summed[5],
        summed[6],
        gain_sums[0],
        gain_sums[1],
    )


AXES = ("dp", "tensor")
MESH = pl.DeviceIdType.MESH
TILE = 256
NEG = -1e30
F32 = jnp.float32
BF16 = jnp.bfloat16


def flat(y, x, c, t):
    return ((y * 2 + x) * 2 + c) * 4 + t


def move(values, to):
    pairs = []
    for y in range(2):
        for x in range(2):
            for c in range(2):
                for t in range(4):
                    pair = (flat(y, x, c, t), flat(*to(y, x, c, t)))
                    if pair[0] != pair[1]:
                        pairs.append(pair)
    return lax.ppermute(values, AXES, pairs)


def across_x(values):
    return move(values, lambda y, x, c, t: (y, 1 - x, c, t))


def across_y(values):
    return move(values, lambda y, x, c, t: (1 - y, x, c, t))


def across_c(values):
    return move(values, lambda y, x, c, t: (y, x, 1 - c, t))


def along_t(values, step):
    return move(values, lambda y, x, c, t: (y, x, c, (t + step) % 4))


def swap_halves(values):
    return move(values, lambda y, x, c, t: (y, x, t % 2, (t // 2) * 2 + c))


def pack_kernel(wq, wk, wv, wo, wg, wu, wd, halves, small, big):
    small[0] = dot(wq[...], halves[...]).astype(BF16)
    small[1] = dot(wk[...], halves[...]).astype(BF16)
    small[2] = wv[...]
    small[3] = wo[...].T
    for n, turned in enumerate((wg[...].T, wu[...].T, wd[...])):
        big[n] = turned.reshape(big.shape[1:])


def pack(wq, wk, wv, wo, wg, wu, wd):
    rows, part = wg.shape
    lane = jnp.arange(256, dtype=jnp.int32)
    source = ((lane & 127) >> 5) * 64 + (lane >> 7) * 32 + (lane & 31)
    halves = (lane[:, None] == source[None, :]).astype(BF16)
    return pl.pallas_call(
        pack_kernel,
        out_shape=[
            jax.ShapeDtypeStruct((4, rows, 256), BF16),
            jax.ShapeDtypeStruct((3, 2, part // 2, rows), BF16),
        ],
        compiler_params=params(),
        name="pack",
    )(wq, wk, wv, wo, wg, wu, wd, halves)


def gather_kernel(tok, fv, small, big, row, first, g_small, g_big, send, recv, swap, fsend, frecv, here):
    dp, t = lax.axis_index("dp"), lax.axis_index("tensor")
    c, x, y = lax.rem(dp, 2), lax.rem(lax.div(dp, 2), 2), lax.div(dp, 4)
    pair, side = lax.div(t, 2), lax.rem(t, 2)
    plane = dp - c
    dpx, dpy, dpc = dp + 2 - 4 * x, dp + 4 - 8 * y, dp + 1 - 2 * c
    dpxy = dpx + 4 - 8 * y

    barrier = pltpu.get_barrier_semaphore()
    for e in range(2):
        for d in range(4):
            if e or d:
                other = plane + (c + e) - 2 * lax.div(c + e, 2)
                pl.semaphore_signal(barrier, inc=1, device_id=(other, lax.rem(t + d, 4)), device_id_type=MESH)
    pl.semaphore_signal(barrier, inc=1, device_id=(dpx, t), device_id_type=MESH)
    pl.semaphore_signal(barrier, inc=1, device_id=(dpy, t), device_id_type=MESH)
    pl.semaphore_wait(barrier, 9)

    dist = [lax.rem(t + 4 - d, 4) for d in range(4)]

    def slot(k, at, owner, h):
        if k == 0:
            return g_small.at[pl.ds(2 * h, 2), at, pl.ds(owner * 128, 128), :]
        return g_big.at[k - 1, owner, h, at]

    def column(k, owner, h):
        if k == 0:
            return g_small.at[pl.ds(2 * h, 2), :, pl.ds(owner * 128, 128), :]
        return g_big.at[k - 1, owner, h]

    def both(k, at, owner):
        if k == 0:
            return g_small.at[:, at, pl.ds(owner * 128, 128), :]
        return g_big.at[k - 1, owner, :, at]

    def all_of(k, owner):
        if k == 0:
            return g_small.at[:, :, pl.ds(owner * 128, 128), :]
        return g_big.at[k - 1, owner]

    def shard(k):
        return small if k == 0 else big.at[k - 1]

    def part_of(k, h):
        return small.at[pl.ds(2 * h, 2)] if k == 0 else big.at[k - 1, h]

    def copy(k, n, src, dst, to, at):
        return pltpu.make_async_remote_copy(
            src_ref=src,
            dst_ref=dst,
            send_sem=send.at[k, n],
            recv_sem=recv.at[k, n],
            device_id=(to, at),
            device_id_type=MESH,
        )

    chunks = 4
    near, far = (dpx, dpy), (dpy, dpx)
    along = [[copy(k, d - 1, shard(k), both(k, t, dp), dp, lax.rem(t + d, 4)) for d in (1, 2, 3)] for k in range(chunks)]
    onward = [[[copy(k, 3 + h, part_of(k, h), slot(k, t, dp, h), near[h], t) for h in range(2)]] for k in range(chunks)]
    kept = [pltpu.make_async_copy(shard(k), both(k, t, dp), here.at[k]) for k in range(chunks)]
    for k in range(chunks):
        onward[k] += [
            [copy(k, 3 + 2 * d + h, slot(k, dist[d], dp, h), slot(k, dist[d], dp, h), near[h], t) for h in range(2)]
            for d in (1, 2, 3)
        ]
    across = [
        [
            copy(k, 11 + 2 * h + i, column(k, owner, h), column(k, owner, h), far[h], t)
            for h in range(2)
            for i, owner in enumerate((dp, near[h]))
        ]
        for k in range(chunks)
    ]
    over = [
        [copy(k, 15 + i, all_of(k, owner), all_of(k, owner), dpc, t) for i, owner in enumerate((dp, dpx, dpy, dpxy))]
        for k in range(chunks)
    ]

    for item in along[0] + onward[0][0] + kept:
        item.start()
    for k in range(1, chunks):
        for item in onward[k][0]:
            item.start()

    moved = side != c
    to_own = pltpu.make_async_copy(tok, row.at[c], here.at[4])
    swapped = pltpu.make_async_remote_copy(
        src_ref=tok,
        dst_ref=row.at[side],
        send_sem=swap.at[0],
        recv_sem=swap.at[1],
        device_id=(plane + side, 2 * pair + c),
        device_id_type=MESH,
    )

    def start_tokens():
        @pl.when(moved)
        def _():
            swapped.start()

        @pl.when(jnp.logical_not(moved))
        def _():
            to_own.start()

    heads_core, slab = pair, side

    def first_copy(p):
        return pltpu.make_async_remote_copy(
            src_ref=fv.at[pl.ds(p * SEQ, SEQ), :],
            dst_ref=first.at[slab],
            send_sem=fsend.at[p],
            recv_sem=frecv.at[slab],
            device_id=(plane + heads_core, 2 * p + c),
            device_id_type=MESH,
        )

    def first_local(p):
        return pltpu.make_async_copy(fv.at[pl.ds(p * SEQ, SEQ), :], first.at[slab], here.at[5])

    stays = [(heads_core == c) & (t == 2 * p + c) for p in range(2)]

    def start_first():
        for p in range(2):

            @pl.when(stays[p])
            def _():
                first_local(p).start()

            @pl.when(jnp.logical_not(stays[p]))
            def _():
                first_copy(p).start()

    for step in range(chunks + 2):
        if step < chunks:
            for item in along[step]:
                item.wait_recv()
            kept[step].wait()
            if step + 1 < chunks:
                for item in along[step + 1]:
                    item.start()
            if step == 0:
                start_tokens()
            if step == 1:
                start_first()
            for pair_of in onward[step][1:]:
                for item in pair_of:
                    item.start()
            over[step][0].start()
        if 0 <= step - 1 < chunks:
            for pair_of in onward[step - 1]:
                for item in pair_of:
                    item.wait_recv()
            for item in across[step - 1]:
                item.start()
        if 0 <= step - 2 < chunks:
            for item in across[step - 2]:
                item.wait_recv()
            for item in over[step - 2][1:]:
                item.start()

    @pl.when(moved)
    def _():
        swapped.wait_send()
        swapped.wait_recv()

    @pl.when(jnp.logical_not(moved))
    def _():
        to_own.wait()

    given = pltpu.make_async_remote_copy(
        src_ref=row.at[c],
        dst_ref=row.at[c],
        send_sem=swap.at[2],
        recv_sem=swap.at[3],
        device_id=(dpc, t),
        device_id_type=MESH,
    )
    given.start()
    for p in range(2):

        @pl.when(stays[p])
        def _():
            first_local(p).wait()

        @pl.when(jnp.logical_not(stays[p]))
        def _():
            first_copy(p).wait_send()

    for u in range(2):
        came = pltpu.make_async_remote_copy(
            src_ref=first.at[u],
            dst_ref=first.at[u],
            send_sem=fsend.at[u],
            recv_sem=frecv.at[u],
            device_id=(dpc, t),
            device_id_type=MESH,
        )

        @pl.when((side != c) | (t != 2 * c + u))
        def _():
            came.wait_recv()

    given.wait()
    for k in range(chunks):
        for item in over[k]:
            item.wait_recv()
        for item in along[k] + across[k] + over[k]:
            item.wait_send()
        for pair_of in onward[k]:
            for item in pair_of:
                item.wait_send()


def gather(tok, fv, small, big):
    part, rows = big.shape[2:]
    wide = tok.shape[1]
    vmem = pl.BlockSpec(memory_space=pltpu.VMEM)
    sems = pltpu.SemaphoreType.DMA
    return pl.pallas_call(
        gather_kernel,
        out_shape=[
            jax.ShapeDtypeStruct((2, SEQ // 2, wide), BF16),
            jax.ShapeDtypeStruct((2, SEQ, 256), BF16),
            jax.ShapeDtypeStruct((4, 4, wide, 256), BF16),
            jax.ShapeDtypeStruct((3, 8, 2, 4, part, rows), BF16),
        ],
        in_specs=[vmem] * 4,
        out_specs=[any_spec()] * 4,
        scratch_shapes=[sems((4, 19)), sems((4, 19)), sems((4,)), sems((2,)), sems((2,)), sems((6,))],
        compiler_params=params(collective_id=0, has_side_effects=True),
        name="gather",
    )(tok, fv, small, big)


def dot(left, right):
    return jnp.dot(left, right, preferred_element_type=F32)


def dot_nt(left, right):
    return lax.dot_general(left, right, (((1,), (1,)), ((), ())), preferred_element_type=F32)


def dot_tn(left, right):
    return lax.dot_general(left, right, (((0,), (0,)), ((), ())), preferred_element_type=F32)


def any_spec():
    return pl.BlockSpec(memory_space=pl.ANY)


def params(**more):
    return pltpu.CompilerParams(vmem_limit_bytes=62 * 1024 * 1024, **more)


def cost(flops, size, exps=0):
    return pl.CostEstimate(flops=int(flops), bytes_accessed=int(size), transcendentals=int(exps))


def project_kernel(at, tok, first, cosine, sine, gain, held, normed_out, q_out, k_out, v_out):
    values = tok[0].astype(F32)
    factor = lax.rsqrt(jnp.mean(values * values, axis=1, keepdims=True) + EPSILON)
    normed = (values * factor * gain[...]).astype(BF16)
    normed_out[...] = normed
    cos, sin = cosine[...], sine[...]
    for u in range(2):
        for n, out, scale in ((0, q_out, 0.125), (1, k_out, 1.0)):
            raw = dot(normed, held[n, u])
            a, b = raw[:, :128], raw[:, 128:]
            out[:, u * 256 : u * 256 + 128] = ((a * cos - b * sin) * scale).astype(BF16)
            out[:, u * 256 + 128 : u * 256 + 256] = ((b * cos + a * sin) * scale).astype(BF16)
        raw = dot(normed, held[2, u])
        v_out[:, u * 256 : u * 256 + 256] = (0.5 * raw + 0.5 * first[u].astype(F32)).astype(BF16)


def once(shape, place):
    return pl.BlockSpec(shape, place, pipeline_mode=pl.Buffered(1))


def project(at, tok, first, cosine, sine, gain, small):
    rows, wide = 512, tok.shape[2]
    row = lambda width: pl.BlockSpec((rows, width), lambda i, at: (i, 0))
    grid = pltpu.PrefetchScalarGridSpec(
        num_scalar_prefetch=1,
        grid=(4,),
        in_specs=[
            pl.BlockSpec((1, rows, wide), lambda i, at: (i // 2, i % 2, 0)),
            pl.BlockSpec((2, rows, 256), lambda i, at: (0, i, 0)),
            row(128),
            row(128),
            pl.BlockSpec((1, wide), lambda i, at: (0, 0)),
            once((4, 2, wide, 256), lambda i, at: (0, at[0] & 1, 0, 0)),
        ],
        out_specs=[row(wide), row(512), row(512), row(512)],
    )
    return pl.pallas_call(
        project_kernel,
        out_shape=[jax.ShapeDtypeStruct((SEQ, wide), BF16)]
        + [jax.ShapeDtypeStruct((SEQ, 512), BF16)] * 3,
        grid_spec=grid,
        compiler_params=params(),
        cost_estimate=cost(2 * SEQ * wide * 1536, 24e6),
        name="project",
    )(at, tok, first, cosine, sine, gain, small)


def head_masks(rows):
    lane = lax.broadcasted_iota(jnp.int32, (rows, 256), 1)
    return (lane & 127) >> 5, lane >> 6


def attend_kernel(bounds, q_ref, k_ref, v_ref, starts, o_ref, lse_ref, kept, top, total, acc):
    of_qk, of_v = head_masks(TILE)
    row = lax.broadcasted_iota(jnp.int32, (TILE, TILE), 0)
    lane = lax.broadcasted_iota(jnp.int32, (TILE, TILE), 1)

    def query_tile(i, carry):
        here = pl.ds(pl.multiple_of(i * TILE, TILE), TILE)
        q = q_ref[here, :]
        zero = jnp.zeros_like(q)
        q4 = jnp.concatenate([jnp.where(of_qk == h, q, zero) for h in range(4)], axis=0)
        begin = starts[here, :]
        begin = jnp.concatenate([begin, begin], axis=1)
        at_row = row + i * TILE
        low = bounds[i]
        top[...] = jnp.full_like(top, NEG)

        def score(j, carry):
            keys = k_ref[pl.ds(pl.multiple_of(j * TILE, TILE), TILE), :]
            s = dot_nt(q4, keys)
            at_lane = lane + j * TILE
            ok = (at_lane >= begin) & (at_lane <= at_row)
            for h in range(4):
                part = slice(h * TILE, (h + 1) * TILE)
                one = jnp.where(ok, s[part], NEG)
                kept[j - low, part, :] = one
                top[part] = jnp.maximum(top[part], jnp.maximum(one[:, :128], one[:, 128:]))
            return carry

        lax.fori_loop(low, i + 1, score, 0)
        highest = jnp.max(top[...], axis=1, keepdims=True)
        top[...] = jnp.broadcast_to(highest, top.shape)
        total[...] = jnp.zeros_like(total)
        acc[...] = jnp.zeros_like(acc)

        def weigh(j, carry):
            values = v_ref[pl.ds(pl.multiple_of(j * TILE, TILE), TILE), :]
            zero = jnp.zeros_like(values)
            exps, parts = [], []
            for h in range(4):
                part = slice(h * TILE, (h + 1) * TILE)
                peak = top[part]
                e = jnp.exp(kept[j - low, part, :] - jnp.concatenate([peak, peak], axis=1))
                total[part] += e[:, :128] + e[:, 128:]
                exps.append(e.astype(BF16))
                parts.append(jnp.where(of_v == h, values, zero))
            acc[...] += dot(jnp.concatenate(exps, axis=1), jnp.concatenate(parts, axis=0))
            return carry

        lax.fori_loop(low, i + 1, weigh, 0)
        sums = jnp.sum(total[...], axis=1, keepdims=True)
        inverse = 1.0 / sums
        scale = jnp.broadcast_to(inverse[:TILE], (TILE, 256))
        for h in range(1, 4):
            scale = jnp.where(of_v == h, inverse[h * TILE : (h + 1) * TILE], scale)
        o_ref[here, :] = (acc[...] * scale).astype(BF16)
        logs = top[...] + jnp.log(jnp.broadcast_to(sums, top.shape))
        for h in range(4):
            turned = logs[h * TILE : (h + 1) * TILE].T
            lse_ref[0, pl.ds(i, 1), h * TILE : (h + 1) * TILE] = turned[:1]
        return carry

    lax.fori_loop(0, SEQ // TILE, query_tile, 0)


def attend(bounds, q, k, v, starts):
    slab = pl.BlockSpec((SEQ, 256), lambda u, b: (0, u))
    tiles = SEQ // TILE
    grid = pltpu.PrefetchScalarGridSpec(
        num_scalar_prefetch=1,
        grid=(2,),
        in_specs=[slab, slab, slab, pl.BlockSpec((SEQ, 128), lambda u, b: (0, 0))],
        out_specs=[slab, pl.BlockSpec((1, tiles, 4 * TILE), lambda u, b: (u, 0, 0))],
        scratch_shapes=[
            pltpu.VMEM((tiles, 4 * TILE, TILE), F32),
            pltpu.VMEM((4 * TILE, 128), F32),
            pltpu.VMEM((4 * TILE, 128), F32),
            pltpu.VMEM((TILE, 256), F32),
        ],
    )
    return pl.pallas_call(
        attend_kernel,
        out_shape=[
            jax.ShapeDtypeStruct((SEQ, 512), BF16),
            jax.ShapeDtypeStruct((2, tiles, 4 * TILE), F32),
        ],
        grid_spec=grid,
        compiler_params=params(),
        cost_estimate=cost(20e9, 12e6, 1e7),
        name="attend",
    )(bounds, q, k, v, starts)


def attend_back_kernel(
    bounds, q_ref, k_ref, v_ref, do_ref, o_ref, lse_ref, starts, cosine, sine, dq_ref, dk_ref, dv_ref, dq_acc, delta, dk_acc, dv_acc
):
    tiles = SEQ // TILE
    of_qk, of_v = head_masks(TILE)
    row = lax.broadcasted_iota(jnp.int32, (TILE, TILE), 0)
    lane = lax.broadcasted_iota(jnp.int32, (TILE, TILE), 1)
    pick = (lax.broadcasted_iota(jnp.int32, (8, 256), 1) >> 6) == lax.broadcasted_iota(
        jnp.int32, (8, 256), 0
    )
    pick = pick.astype(F32)
    dq_acc[...] = jnp.zeros_like(dq_acc)

    def prepare(i, carry):
        here = pl.ds(pl.multiple_of(i * TILE, TILE), TILE)
        both = do_ref[here, :].astype(F32) * o_ref[here, :].astype(F32)
        sums = lax.dot_general(
            pick, both, (((1,), (1,)), ((), ())), precision=lax.Precision.HIGHEST, preferred_element_type=F32
        )
        for h in range(4):
            delta[pl.ds(i, 1), h * TILE : (h + 1) * TILE] = sums[h : h + 1]
        return carry

    lax.fori_loop(0, tiles, prepare, 0)

    def rotate_out(values, here, out, scale):
        a, b = values[:, :128], values[:, 128:]
        cos, sin = cosine[here, :], sine[here, :]
        out[here, :128] = ((a * cos + b * sin) * scale).astype(BF16)
        out[here, 128:] = ((b * cos - a * sin) * scale).astype(BF16)

    def split(values, of):
        zero = jnp.zeros_like(values)
        return jnp.concatenate([jnp.where(of == h, values, zero) for h in range(4)], axis=0)

    def key_tile(j, carry):
        there = pl.ds(pl.multiple_of(j * TILE, TILE), TILE)
        keys, values = k_ref[there, :], v_ref[there, :]
        k4 = split(keys, of_qk)
        at_row = row + j * TILE
        dk_acc[...] = jnp.zeros_like(dk_acc)
        dv_acc[...] = jnp.zeros_like(dv_acc)

        def query_tile(i, carry):
            here = pl.ds(pl.multiple_of(i * TILE, TILE), TILE)
            q4 = split(q_ref[here, :], of_qk)
            do4 = split(do_ref[here, :], of_v)
            s = dot_nt(keys, q4)
            dp = dot_nt(values, do4)
            at_lane = lane + i * TILE
            ok = (at_row >= starts[pl.ds(i, 1), :]) & (at_row <= at_lane)
            lse, shift = lse_ref[0, pl.ds(i, 1), :], delta[pl.ds(i, 1), :]
            ps, dss = [], []
            for h in range(4):
                part = slice(h * TILE, (h + 1) * TILE)
                p = jnp.exp(jnp.where(ok, s[:, part] - lse[:, part], NEG))
                ds = p * (dp[:, part] - shift[:, part])
                ps.append(p.astype(BF16))
                dss.append(ds.astype(BF16))
            dv_acc[...] += dot(jnp.concatenate(ps, axis=1), do4)
            dk_acc[...] += dot(jnp.concatenate(dss, axis=1), q4)
            dq_acc[here, :] += dot_tn(jnp.concatenate(dss, axis=0), k4)
            return carry

        lax.fori_loop(j, bounds[tiles + j] + 1, query_tile, 0)
        rotate_out(dk_acc[...], there, dk_ref, 1.0)
        dv_ref[there, :] = (0.5 * dv_acc[...]).astype(BF16)
        return carry

    lax.fori_loop(0, tiles, key_tile, 0)

    def finish(i, carry):
        here = pl.ds(pl.multiple_of(i * TILE, TILE), TILE)
        rotate_out(dq_acc[here, :], here, dq_ref, 0.125)
        return carry

    lax.fori_loop(0, tiles, finish, 0)


def attend_back(bounds, q, k, v, do, o, lse, starts, cosine, sine):
    slab = pl.BlockSpec((SEQ, 256), lambda u, b: (0, u))
    whole = lambda shape: pl.BlockSpec(shape, lambda u, b: (0,) * len(shape))
    tiles = SEQ // TILE
    grid = pltpu.PrefetchScalarGridSpec(
        num_scalar_prefetch=1,
        grid=(2,),
        in_specs=[slab] * 5
        + [
            pl.BlockSpec((1, tiles, 4 * TILE), lambda u, b: (u, 0, 0)),
            whole((tiles, TILE)),
            whole((SEQ, 128)),
            whole((SEQ, 128)),
        ],
        out_specs=[slab] * 3,
        scratch_shapes=[
            pltpu.VMEM((SEQ, 256), F32),
            pltpu.VMEM((tiles, 4 * TILE), F32),
            pltpu.VMEM((TILE, 256), F32),
            pltpu.VMEM((TILE, 256), F32),
        ],
    )
    return pl.pallas_call(
        attend_back_kernel,
        out_shape=[jax.ShapeDtypeStruct((SEQ, 512), BF16)] * 3,
        grid_spec=grid,
        compiler_params=params(),
        cost_estimate=cost(50e9, 20e6, 1e7),
        name="attend_back",
    )(bounds, q, k, v, do, o, lse, starts, cosine, sine)


def mlp_kernel(at, att_own, att_other, tok, cot_here, cot_moved, gain, wo, big, *rest):
    (out, gh_out, gb_out, n2_out, hid_out, ga_own, ga_other, gg_out, cot_out) = rest[:9]
    (wg, wu, wd, sems) = rest[9:]
    step = pl.program_id(0)
    c = at[0] & 1

    @pl.when(step == 0)
    def _():
        for n, held in enumerate((wg, wu, wd)):
            for owner in range(8):
                pltpu.make_async_copy(
                    big.at[n, owner], held.at[:, owner * 128 : owner * 128 + 128], sems.at[n]
                ).start()
        gg_out[...] = jnp.zeros_like(gg_out)

    hidden = tok[0].astype(F32)
    for e, att in enumerate((att_own, att_other)):
        for u in range(2):
            hidden += dot_nt(att[:, u * 256 : u * 256 + 256], wo[0, 2 * (c ^ e) + u])
    factor = lax.rsqrt(jnp.mean(hidden * hidden, axis=1, keepdims=True) + EPSILON)
    gains = gain[...]
    normed = (hidden * factor * gains).astype(BF16)
    n2_out[...] = normed
    g = jnp.where((at[1] & 1) == c, cot_here[...], cot_moved[...])
    cot_out[...] = g

    @pl.when(step == 0)
    def _():
        for n, held in enumerate((wg, wu, wd)):
            pltpu.make_async_copy(held, held, sems.at[n]).wait()

    down = jnp.zeros_like(hidden)
    back = jnp.zeros_like(hidden)
    units = wg.shape[0]
    for low in range(0, units, 768):
        part = slice(low, min(low + 768, units))
        gate, up, grad_act = dot_nt(normed, wg[part]), dot_nt(normed, wu[part]), dot_nt(g, wd[part])
        sig = 1.0 / (1.0 + jnp.exp(-gate))
        silu = gate * sig
        act = (silu * up).astype(BF16)
        grad_up = (grad_act * silu).astype(BF16)
        grad_gate = (grad_act * up * (sig * (1.0 + gate * (1.0 - sig)))).astype(BF16)
        hid_out[0, :, part], hid_out[1, :, part], hid_out[2, :, part] = grad_gate, grad_up, act
        down += dot(act, wd[part])
        back += dot(grad_gate, wg[part]) + dot(grad_up, wu[part])
    out[...] = (hidden + down).astype(BF16)
    gg_out[...] += jnp.sum((back * hidden * factor).reshape(-1, 8, back.shape[1]), axis=0)
    scaled = back * gains
    mean = jnp.mean(scaled * hidden, axis=1, keepdims=True)
    grad_hidden = g.astype(F32) + factor * scaled - hidden * (factor * factor * factor * mean)
    gh_out[...] = grad_hidden
    branch = grad_hidden.astype(BF16)
    gb_out[...] = branch
    for e, ga in enumerate((ga_own, ga_other)):
        for u in range(2):
            ga[:, u * 256 : u * 256 + 256] = dot(branch, wo[0, 2 * (c ^ e) + u]).astype(BF16)


def mlp(at, att_own, att_other, tok, cot_here, cot_moved, gain, small, big):
    _, count, wide = tok.shape
    big = big.reshape(3, 8, -1, 128)
    rows, units = 256, big.shape[2]
    row = lambda width: pl.BlockSpec((rows, width), lambda i, at: (i, 0))
    grid = pltpu.PrefetchScalarGridSpec(
        num_scalar_prefetch=1,
        grid=(count // rows,),
        in_specs=[
            row(512),
            row(512),
            pl.BlockSpec((1, rows, wide), lambda i, at: (at[0] & 1, i, 0)),
            row(wide),
            row(wide),
            pl.BlockSpec((1, wide), lambda i, at: (0, 0)),
            once((1, 4, wide, 256), lambda i, at: (3, 0, 0, 0)),
            any_spec(),
        ],
        out_specs=[
            row(wide),
            row(wide),
            row(wide),
            row(wide),
            pl.BlockSpec((3, rows, units), lambda i, at: (0, i, 0)),
            row(512),
            row(512),
            pl.BlockSpec((8, wide), lambda i, at: (0, 0)),
            row(wide),
        ],
        scratch_shapes=[pltpu.VMEM((units, wide), BF16)] * 3 + [pltpu.SemaphoreType.DMA((3,))],
    )
    tokens = lambda width, kind=BF16: jax.ShapeDtypeStruct((count, width), kind)
    return pl.pallas_call(
        mlp_kernel,
        out_shape=[
            tokens(wide),
            tokens(wide, F32),
            tokens(wide),
            tokens(wide),
            jax.ShapeDtypeStruct((3, count, units), BF16),
            tokens(512),
            tokens(512),
            jax.ShapeDtypeStruct((8, wide), F32),
            tokens(wide),
        ],
        grid_spec=grid,
        compiler_params=params(),
        cost_estimate=cost(2 * count * wide * (6 * units + 2 * wide), 60e6, 3e6),
        name="mlp",
    )(at, att_own, att_other, tok, cot_here, cot_moved, gain, small, big)


def turn_rows(source, plane, parity, held):
    for rel in range(4):
        block = ((plane ^ rel) * 2 + parity) * 128
        held[rel * 128 : rel * 128 + 128, :] = source[:, pl.ds(pl.multiple_of(block, 128), 128)].T


def place_first(send, keep, done, lanes):
    for yr in range(2):
        keep[yr, :, lanes] = done[2 * yr]
        send[yr, :, lanes] = done[2 * yr + 1]


def place_second(send, keep, done, lanes):
    for xr in range(2):
        keep[xr, :, lanes] = done[xr]
        send[xr, :, lanes] = done[2 + xr]


def weights_kernel(n2, g, branch, hid, own, other, send1, keep1, send2, keep2, turned, given, got, out_sem, in_sem):
    step = pl.program_id(0)
    dp, t = lax.axis_index("dp"), lax.axis_index("tensor")
    c = lax.rem(dp, 2)
    plane = lax.div(dp, 2)
    n = lax.rem(step, 4)
    units = hid.shape[2] // 2

    @pl.when(step == 0)
    def _():
        barrier = pltpu.get_barrier_semaphore()
        pl.semaphore_signal(barrier, inc=1, device_id=(dp + 1 - 2 * c, t), device_id_type=MESH)
        pl.semaphore_wait(barrier, 1)

    def exchange(k):
        lanes = pl.ds(k * units, units if k < 3 else 512)
        return pltpu.make_async_remote_copy(
            src_ref=given.at[:, :, :, lanes],
            dst_ref=got.at[:, :, :, lanes],
            send_sem=out_sem.at[k],
            recv_sem=in_sem.at[k],
            device_id=(dp + 1 - 2 * c, t),
            device_id_type=MESH,
        )

    for phase, parity in ((0, 1 - c), (1, c)):
        for at_n, source in ((0, n2), (2, g), (3, branch)):

            @pl.when(step == 4 * phase + at_n)
            def _():
                x = lax.rem(plane, 2)
                y = lax.div(plane, 2)
                for rel in range(4):
                    yy, xx = (y, 1 - y)[rel // 2], (x, 1 - x)[rel % 2]
                    block = pl.multiple_of((yy * 4 + xx * 2 + parity) * 128, 128)
                    turned[rel * 128 : rel * 128 + 128, :] = source[:, pl.ds(block, 128)].T

    def heads(h):
        return jnp.where(c == h, own[...], other[...])

    @pl.when(step < 3)
    def _():
        for h in range(2):
            product = dot(turned[...], hid[0, :, h * units : h * units + units]).astype(BF16)
            given[:, h, :, pl.ds(pl.multiple_of(n * units, 128), units)] = product.reshape(4, 128, units)

    @pl.when(step == 3)
    def _():
        for h in range(2):
            product = dot(turned[...], heads(h)).astype(BF16)
            given[:, h, :, 3 * units : 3 * units + 512] = product.reshape(4, 128, 512)

    for k in range(4):

        @pl.when(step == k + 1)
        def _():
            exchange(k).start()

        @pl.when(step == k + 4)
        def _():
            exchange(k).wait_recv()

    def keep(product, h, lanes):
        done = [(product[r * 128 : r * 128 + 128] + got[r, h, :, lanes].astype(F32)).astype(BF16) for r in range(4)]
        (place_first, place_second)[h](*((send1, keep1), (send2, keep2))[h], done, lanes)

    @pl.when((step >= 4) & (step < 7))
    def _():
        for h in range(2):
            product = dot(turned[...], hid[0, :, h * units : h * units + units])
            keep(product, h, pl.ds(pl.multiple_of(n * units, 128), units))

    @pl.when(step == 7)
    def _():
        for h in range(2):
            keep(dot(turned[...], heads(h)), h, pl.ds(3 * units, 512))
        for k in range(4):
            exchange(k).wait_send()


def weights(n2, g, branch, hid, own, other):
    count, wide = n2.shape
    units = hid.shape[2] // 2
    full = lambda *shape: pl.BlockSpec(shape, lambda s: (0,) * len(shape), pipeline_mode=pl.Buffered(1))
    length = 3 * units + 512
    grid = pl.GridSpec(
        grid=(8,),
        in_specs=[
            full(count, wide),
            full(count, wide),
            full(count, wide),
            pl.BlockSpec((1, count, 2 * units), lambda s: (jnp.minimum(lax.rem(s, 4), 2), 0, 0)),
            full(count, 512),
            full(count, 512),
        ],
        out_specs=[full(2, 128, length)] * 4,
        scratch_shapes=[
            pltpu.VMEM((512, count), BF16),
            pltpu.VMEM((4, 2, 128, length), BF16),
            pltpu.VMEM((4, 2, 128, length), BF16),
            pltpu.SemaphoreType.DMA((4,)),
            pltpu.SemaphoreType.DMA((4,)),
        ],
    )
    return pl.pallas_call(
        weights_kernel,
        out_shape=[jax.ShapeDtypeStruct((2, 128, length), BF16)] * 4,
        grid_spec=grid,
        compiler_params=params(collective_id=1, has_side_effects=True),
        cost_estimate=cost(2 * count * 1024 * length * 2, 50e6),
        name="weights",
    )(n2, g, branch, hid, own, other)


def add(left, right):
    return (left.astype(F32) + right.astype(F32)).astype(BF16)


def scatter_xy(keep1, got1, keep2, got2):
    last1, last2 = across_y(add(keep1[1], got1[1])), across_x(add(keep2[1], got2[1]))
    return add(keep1[0], got1[0]), last1, add(keep2[0], got2[0]), last2


def turn_kernel(at, kept1, got1, kept2, got2, out, *, units):
    t = at[1]
    sums = [kept1[...].astype(F32) + got1[...].astype(F32), kept2[...].astype(F32) + got2[...].astype(F32)]
    part = units // 4
    for h in range(2):
        for n in range(3):
            turned = sums[h][:, n * units : n * units + units].T.astype(BF16)
            for i in range(4):
                rows = slice((2 * n + h) * part, (2 * n + h + 1) * part)
                out[(i - t) & 3, rows, :] = turned[i * part : (i + 1) * part]
        turned = sums[h][:, 3 * units :].T.astype(BF16)
        for i in range(2):
            out[(2 * h + i - t) & 3, 6 * part :, :] = turned[i * 256 : i * 256 + 256]


def turn(at, arrays, units):
    vmem = pl.BlockSpec(memory_space=pltpu.VMEM)
    rows = 3 * (units // 2) + 256
    return pl.pallas_call(
        functools.partial(turn_kernel, units=units),
        out_shape=jax.ShapeDtypeStruct((4, rows, 128), BF16),
        in_specs=[pl.BlockSpec(memory_space=pltpu.SMEM)] + [vmem] * 4,
        out_specs=vmem,
        compiler_params=params(),
        cost_estimate=cost(1e6, 8e6),
        name="turn",
    )(at, *arrays)


def final_kernel(a, b, c, d, gate, up, down, out):
    total = a[...].astype(F32) + b[...].astype(F32) + c[...].astype(F32) + d[...].astype(F32)
    part = down.shape[0]
    gate[...] = total[:part].T
    up[...] = total[part : 2 * part].T
    down[...] = total[2 * part : 3 * part]
    out[...] = total[3 * part :]


def scatter_t(pieces):
    return [pieces[0]] + [along_t(pieces[d], d) for d in (1, 2, 3)]


def final(pieces, part):
    return pl.pallas_call(
        final_kernel,
        out_shape=[
            jax.ShapeDtypeStruct((128, part), F32),
            jax.ShapeDtypeStruct((128, part), F32),
            jax.ShapeDtypeStruct((part, 128), F32),
            jax.ShapeDtypeStruct((256, 128), F32),
        ],
        compiler_params=params(),
        cost_estimate=cost(1e6, 4e6),
        name="final",
    )(*pieces)


def project_back_kernel(at, dq, dk, dv, held, out):
    out[...] = back_product(dq, dk, dv, held).astype(out.dtype)


def back_product(dq, dk, dv, held):
    total = None
    for u in range(2):
        for n, grad in enumerate((dq, dk, dv)):
            term = dot_nt(grad[:, u * 256 : u * 256 + 256], held[n, u])
            total = term if total is None else total + term
    return total


def back_specs(rows, other, wide):
    half = SEQ // 2 // rows
    row = pl.BlockSpec((rows, 512), lambda i, at: (((at[0] & 1) ^ other) * half + i, 0))
    return [row] * 3 + [once((4, 2, wide, 256), lambda i, at: (0, at[0] & 1, 0, 0))]


def project_back_send(at, dq, dk, dv, small):
    rows, wide = 512, small.shape[2]
    grid = pltpu.PrefetchScalarGridSpec(
        num_scalar_prefetch=1,
        grid=(SEQ // 2 // rows,),
        in_specs=back_specs(rows, 1, wide),
        out_specs=pl.BlockSpec((rows, wide), lambda i, at: (i, 0)),
    )
    return pl.pallas_call(
        project_back_kernel,
        out_shape=jax.ShapeDtypeStruct((SEQ // 2, wide), BF16),
        grid_spec=grid,
        compiler_params=params(),
        cost_estimate=cost(SEQ * wide * 1536, 10e6),
        name="project_back_send",
    )(at, dq, dk, dv, small)


def project_back_keep_kernel(at, dq, dk, dv, held, got, tok, grad_hidden, gain, out, gain_out):
    @pl.when(pl.program_id(0) == 0)
    def _():
        gain_out[...] = jnp.zeros_like(gain_out)

    grad = back_product(dq, dk, dv, held) + got[...].astype(F32)
    values = tok[0].astype(F32)
    factor = lax.rsqrt(jnp.mean(values * values, axis=1, keepdims=True) + EPSILON)
    gain_out[...] += jnp.sum((grad * values * factor).reshape(-1, 8, grad.shape[1]), axis=0)
    scaled = grad * gain[...]
    mean = jnp.mean(scaled * values, axis=1, keepdims=True)
    out[...] = (grad_hidden[...] + factor * scaled - values * (factor * factor * factor * mean)).astype(BF16)


def project_back_keep(at, dq, dk, dv, small, got, tok, grad_hidden, gain):
    rows, wide = 512, small.shape[2]
    row = pl.BlockSpec((rows, wide), lambda i, at: (i, 0))
    grid = pltpu.PrefetchScalarGridSpec(
        num_scalar_prefetch=1,
        grid=(SEQ // 2 // rows,),
        in_specs=back_specs(rows, 0, wide)
        + [
            row,
            pl.BlockSpec((1, rows, wide), lambda i, at: (at[0] & 1, i, 0)),
            row,
            pl.BlockSpec((1, wide), lambda i, at: (0, 0)),
        ],
        out_specs=[row, pl.BlockSpec((8, wide), lambda i, at: (0, 0))],
    )
    return pl.pallas_call(
        project_back_keep_kernel,
        out_shape=[jax.ShapeDtypeStruct((SEQ // 2, wide), BF16), jax.ShapeDtypeStruct((8, wide), F32)],
        grid_spec=grid,
        compiler_params=params(),
        cost_estimate=cost(SEQ * wide * 1536, 20e6),
        name="project_back_keep",
    )(at, dq, dk, dv, small, got, tok, grad_hidden, gain)


def heads_send_kernel(at, left, dq, dk, dv, send, keep, turned):
    n = pl.program_id(0)

    @pl.when(n == 0)
    def _():
        turn_rows(left, at[0] >> 1, 1 - (at[0] & 1), turned)

    for k, right in enumerate((dq, dk, dv)):

        @pl.when(n == k)
        def _():
            product = dot(turned[...], right[...]).astype(BF16)
            done = [product[r * 128 : r * 128 + 128] for r in range(4)]
            place_second(send, keep, done, slice(k * 512, k * 512 + 512))


def heads_keep_kernel(at, left, dq, dk, dv, send, keep, turned):
    n = pl.program_id(0)

    @pl.when(n == 0)
    def _():
        turn_rows(left, at[0] >> 1, at[0] & 1, turned)

    for k, right in enumerate((dq, dk, dv)):

        @pl.when(n == k)
        def _():
            product = dot(turned[...], right[...]).astype(BF16)
            done = [product[r * 128 : r * 128 + 128] for r in range(4)]
            place_first(send, keep, done, slice(k * 512, k * 512 + 512))


def heads_gradient(kernel, name, at, left, dq, dk, dv):
    count, wide = left.shape
    full = lambda *shape: pl.BlockSpec(shape, lambda n, at: (0,) * len(shape), pipeline_mode=pl.Buffered(1))
    grid = pltpu.PrefetchScalarGridSpec(
        num_scalar_prefetch=1,
        grid=(3,),
        in_specs=[full(count, wide)] + [full(count, 512)] * 3,
        out_specs=[full(2, 128, 1536)] * 2,
        scratch_shapes=[pltpu.VMEM((512, count), BF16)],
    )
    return pl.pallas_call(
        kernel,
        out_shape=[jax.ShapeDtypeStruct((2, 128, 1536), BF16)] * 2,
        grid_spec=grid,
        compiler_params=params(),
        cost_estimate=cost(2 * count * 512 * 1536, 12e6),
        name=name,
    )(at, left, dq, dk, dv)


def heads_turn_kernel(at, kept1, got1, kept2, got2, out):
    c, t = at[0] & 1, at[1]
    for e, (kept, got) in enumerate(((kept1, got1), (kept2, got2))):
        total = (kept[...].astype(F32) + got[...].astype(F32)).astype(BF16)
        for u in range(2):
            d = (2 * (c ^ e) + u - t) & 3
            for n in range(3):
                out[d, n] = total[:, n * 512 + u * 256 : n * 512 + u * 256 + 256]


def heads_turn(at, arrays):
    vmem = pl.BlockSpec(memory_space=pltpu.VMEM)
    return pl.pallas_call(
        heads_turn_kernel,
        out_shape=jax.ShapeDtypeStruct((4, 3, 128, 256), BF16),
        in_specs=[pl.BlockSpec(memory_space=pltpu.SMEM)] + [vmem] * 4,
        out_specs=vmem,
        compiler_params=params(),
        cost_estimate=cost(1e6, 3e6),
        name="heads_turn",
    )(at, *arrays)


def heads_final_kernel(a, b, c, d, query, key, value):
    total = a[...].astype(F32) + b[...].astype(F32) + c[...].astype(F32) + d[...].astype(F32)
    for n, out in enumerate((query, key)):
        parts = []
        for h in range(4):
            parts += [total[n, :, h * 32 : h * 32 + 32], total[n, :, 128 + h * 32 : 160 + h * 32]]
        out[...] = jnp.concatenate(parts, axis=1)
    value[...] = total[2]


def heads_final(pieces):
    return pl.pallas_call(
        heads_final_kernel,
        out_shape=[jax.ShapeDtypeStruct((128, 256), F32)] * 3,
        compiler_params=params(),
        cost_estimate=cost(1e6, 2e6),
        name="heads_final",
    )(*pieces)


def fast_body(tokens, first_values, doc_lengths, cotangent, w_query, w_key, w_value, w_out, w_gate, w_up, w_down, gain_attn, gain_mlp):
    me, t = lax.axis_index("dp"), lax.axis_index("tensor")
    c = me % 2
    pair, side = t // 2, t % 2
    wide = tokens.shape[1]
    tiles = SEQ // TILE
    at = jnp.where(jnp.arange(8, dtype=jnp.int32) == 0, me, t).astype(jnp.int32)

    small_shard, big_shard = pack(w_query, w_key, w_value, w_out, w_gate, w_up, w_down)
    row, first, small, big = gather(tokens, first_values, small_shard, big_shard)

    lengths = jnp.where(c == side, doc_lengths, across_c(doc_lengths))
    lengths = lax.dynamic_index_in_dim(lengths, pair, 0, keepdims=False)
    order = jnp.arange(DOCS, dtype=jnp.int32)
    ends = jnp.sum(jnp.where(order[None, :] <= order[:, None], lengths[None, :], 0), axis=1)
    places = jnp.arange(SEQ, dtype=jnp.int32)
    starts = jnp.max(jnp.where(ends[None, :] <= places[:, None], ends[None, :], 0), axis=1)
    last = jnp.arange(tiles, dtype=jnp.int32) * TILE + (TILE - 1)
    finish = jnp.min(jnp.where(ends[None, :] > last[:, None], ends[None, :], SEQ), axis=1)
    bounds = jnp.concatenate([starts.reshape(tiles, TILE)[:, 0] // TILE, (finish - 1) // TILE])
    starts_wide = jnp.broadcast_to(starts[:, None], (SEQ, 128))
    freqs = 10000.0 ** (-(jnp.arange(32, dtype=F32) * 2.0 / HEAD))
    angles = (places - starts).astype(F32)[:, None] * jnp.tile(freqs, 4)[None, :]
    cosine, sine = jnp.cos(angles), jnp.sin(angles)

    row, cotangent = lax.optimization_barrier((row, cotangent))
    moved_cot = swap_halves(cotangent)
    normed_one, q, k, v = project(at, row, first, cosine, sine, gain_attn[None], small)
    attended, lse = attend(bounds, q, k, v, starts_wide)
    by_half = attended.reshape(2, SEQ // 2, 512)
    att_own = lax.dynamic_index_in_dim(by_half, c, 0, keepdims=False)
    att_other = across_c(lax.dynamic_index_in_dim(by_half, 1 - c, 0, keepdims=False))
    out, grad_hidden, branch, normed_two, hid, ga_own, ga_other, gain_two, cot = mlp(
        at, att_own, att_other, row, cotangent, moved_cot, gain_mlp[None], small, big
    )
    stays = c == side
    layer_out = jnp.where(stays, out, swap_halves(out))

    ga_got = across_c(ga_other)
    do = jnp.where(c == 0, jnp.concatenate([ga_own, ga_got]), jnp.concatenate([ga_got, ga_own]))

    kept = weights(normed_two, cot, branch, hid, att_own, att_other)
    kept, do = lax.optimization_barrier((kept, do))
    got1, got2 = across_x(kept[0]), across_y(kept[2])

    dq, dk, dv = attend_back(bounds, q, k, v, do, attended, lse, starts.reshape(tiles, TILE), cosine, sine)

    dq, dk, dv, got1, got2 = lax.optimization_barrier((dq, dk, dv, got1, got2))
    sums = scatter_xy(kept[1], got1, kept[3], got2)

    def first_back(r):
        slab = jnp.where(pair == r, dv[:, :256], dv[:, 256:])
        came = move(slab, lambda y, x, c, t: (y, x, t % 2, 2 * c + ((t // 2) ^ r)))
        return jnp.where(stays & (t == 2 * c + (pair ^ r)), slab, came)

    fb = [first_back(0), first_back(1)]
    odd = side
    grad_first = jnp.concatenate(
        [jnp.where(odd == 0, fb[0], fb[1]), jnp.where(odd == 0, fb[1], fb[0])]
    ).astype(F32)

    gn_got = across_c(project_back_send(at, dq, dk, dv, small))
    send2, keep2 = heads_gradient(heads_send_kernel, "heads_send", at, normed_one, dq, dk, dv)
    send2, keep2 = across_c(send2), across_c(keep2)
    send1, keep1 = heads_gradient(heads_keep_kernel, "heads_keep", at, normed_one, dq, dk, dv)
    grad_gate, grad_up, grad_down, grad_out = final(scatter_t(turn(at, sums, hid.shape[2] // 2)), w_gate.shape[1])
    head_sums = scatter_xy(keep1, across_x(send1), keep2, across_y(send2))
    grad_tokens, gain_one = project_back_keep(at, dq, dk, dv, small, gn_got, row, grad_hidden, gain_attn[None])
    grad_tokens = jnp.where(stays, grad_tokens, swap_halves(grad_tokens)).astype(F32)
    gq, gk, gv = heads_final(scatter_t(heads_turn(at, head_sums)))

    gains = jnp.stack([jnp.sum(gain_one, axis=0), jnp.sum(gain_two, axis=0)]).reshape(16, 128)
    gains = gains + across_c(gains)
    gains = gains + across_x(gains)
    gains = gains + across_y(gains)
    gains = gains + move(gains, lambda y, x, c, t: (y, x, c, t ^ 1))
    gains = gains + move(gains, lambda y, x, c, t: (y, x, c, t ^ 2))
    gains = gains.reshape(2, wide)
    return (
        layer_out,
        grad_tokens,
        grad_first,
        gq,
        gk,
        gv,
        grad_out,
        grad_gate,
        grad_up,
        grad_down,
        gains[0],
        gains[1],
    )


def solution(mesh):
    fits = dict(mesh.shape) == {"dp": 8, "tensor": 4}
    placed = (
        P(("dp", "tensor"), None),
        P("dp", "tensor"),
        P("dp", None),
        P(("dp", "tensor"), None),
        P("dp", "tensor"),
        P("dp", "tensor"),
        P("dp", "tensor"),
        P("tensor", "dp"),
        P("dp", "tensor"),
        P("dp", "tensor"),
        P("tensor", "dp"),
        P(),
        P(),
    )
    return jax.shard_map(
        fast_body if fits else general_body,
        mesh=mesh,
        in_specs=placed,
        out_specs=(
            P(("dp", "tensor"), None),
            P(("dp", "tensor"), None),
            P("dp", "tensor"),
            P("dp", "tensor"),
            P("dp", "tensor"),
            P("dp", "tensor"),
            P("tensor", "dp"),
            P("dp", "tensor"),
            P("dp", "tensor"),
            P("tensor", "dp"),
            P(),
            P(),
        ),
        check_vma=False,
    )
```

```python
import functools

import jax
import jax.numpy as jnp
from jax import lax
from jax.experimental import pallas as pl
from jax.experimental.pallas import tpu as pltpu
from jax.sharding import PartitionSpec as P

HEAD = 64
SEQ = 2048
DOCS = 8
EPSILON = 1e-05


def rms_norm(values, gain):
    factor = lax.rsqrt(jnp.mean(values * values, axis=1, keepdims=True) + EPSILON)
    return values * factor * gain


def documents(doc_lengths):
    ends = jnp.cumsum(doc_lengths, axis=1)
    starts = ends - doc_lengths
    places = jnp.arange(SEQ, dtype=jnp.int32)
    segment = jnp.sum((places[None, :, None] >= ends[:, None, :]).astype(jnp.int32), axis=2)
    member = segment[:, :, None] == jnp.arange(DOCS, dtype=jnp.int32)[None, None, :]
    offset = jnp.sum(jnp.where(member, starts[:, None, :], 0), axis=2)
    return (segment, (places[None, :] - offset).astype(jnp.float32))


def rotation(positions):
    half = HEAD // 2
    freqs = 10000.0 ** (-(jnp.arange(half, dtype=jnp.float32) * 2.0 / HEAD))
    angles = positions[:, None] * freqs[None, :]
    return (jnp.cos(angles), jnp.sin(angles))


def rotate(values, cosine, sine):
    shaped = values.reshape(values.shape[0], -1, HEAD)
    half = HEAD // 2
    first = shaped[:, :, :half]
    second = shaped[:, :, half:]
    cos_rows = cosine[:, None, :]
    sin_rows = sine[:, None, :]
    turned = jnp.concatenate(
        [first * cos_rows - second * sin_rows, second * cos_rows + first * sin_rows], axis=2
    )
    return turned.reshape(values.shape)


def rotate_back(grads, cosine, sine):
    shaped = grads.reshape(grads.shape[0], -1, HEAD)
    half = HEAD // 2
    first = shaped[:, :, :half]
    second = shaped[:, :, half:]
    cos_rows = cosine[:, None, :]
    sin_rows = sine[:, None, :]
    turned = jnp.concatenate(
        [first * cos_rows + second * sin_rows, second * cos_rows - first * sin_rows], axis=2
    )
    return turned.reshape(grads.shape)


def swiglu(gate, up_val):
    return jax.nn.silu(gate) * up_val


def product(left, right):
    return jnp.dot(left, right, preferred_element_type=jnp.float32)


def inner(left, right):
    return lax.dot_general(
        left, right, (((0,), (0,)), ((), ())), preferred_element_type=jnp.float32
    )


def outer(left, right):
    return lax.dot_general(
        left, right, (((1,), (1,)), ((), ())), preferred_element_type=jnp.float32
    )


def block_scores(queries, keys_all, segment, start, width):
    query_block = lax.dynamic_slice_in_dim(queries, start, width, 0)
    query_seg = lax.dynamic_slice_in_dim(segment, start, width, 0)
    scores = (
        jnp.einsum("qhd,khd->hqk", query_block, keys_all, preferred_element_type=jnp.float32)
        * 0.125
    )
    places = jnp.arange(SEQ, dtype=jnp.int32)
    rows_at = start + jnp.arange(width, dtype=jnp.int32)
    allowed = (query_seg[:, None] == segment[None, :]) & (places[None, :] <= rows_at[:, None])
    return (query_block, jnp.where(allowed[None], scores, -1e30))


def forward_row(pieces):
    queries, keys_all, values_all, segment = pieces
    width = min(512, SEQ)
    count = SEQ // width

    def forward_one_block(index):
        unused, scores = block_scores(queries, keys_all, segment, index * width, width)
        top = jnp.max(scores, axis=2, keepdims=True)
        expo = jnp.exp(scores - top)
        total = jnp.sum(expo, axis=2, keepdims=True)
        weights = (expo / total).astype(jnp.bfloat16)
        result = jnp.einsum("hqk,khd->qhd", weights, values_all, preferred_element_type=jnp.float32)
        return (result, (top + jnp.log(total))[:, :, 0])

    results, logsums = lax.map(forward_one_block, jnp.arange(count, dtype=jnp.int32))
    return (results.reshape(SEQ, queries.shape[1], HEAD), logsums)


def backward_row(pieces):
    queries, keys_all, values_all, segment, grad_rows, logsums = pieces
    width = min(512, SEQ)
    count = SEQ // width

    def backward_one_block(carry, extra):
        index, logsum = extra
        start = index * width
        query_block, scores = block_scores(queries, keys_all, segment, start, width)
        probs = jnp.exp(scores - logsum[:, :, None])
        grad_block = lax.dynamic_slice_in_dim(grad_rows, start, width, 0)
        grad_probs = jnp.einsum(
            "qhd,khd->hqk", grad_block, values_all, preferred_element_type=jnp.float32
        )
        delta = jnp.sum(probs * grad_probs, axis=2, keepdims=True)
        grad_scores = (probs * (grad_probs - delta)).astype(jnp.bfloat16)
        grad_query = (
            jnp.einsum("hqk,khd->qhd", grad_scores, keys_all, preferred_element_type=jnp.float32)
            * 0.125
        )
        grad_keys = (
            carry[0]
            + jnp.einsum(
                "hqk,qhd->khd", grad_scores, query_block, preferred_element_type=jnp.float32
            )
            * 0.125
        )
        grad_values = carry[1] + jnp.einsum(
            "hqk,qhd->khd",
            probs.astype(jnp.bfloat16),
            grad_block,
            preferred_element_type=jnp.float32,
        )
        return ((grad_keys, grad_values), grad_query)

    zeros = jnp.zeros(keys_all.shape, jnp.float32)
    sums, grad_queries = lax.scan(
        backward_one_block, (zeros, zeros), (jnp.arange(count, dtype=jnp.int32), logsums)
    )
    return (grad_queries.reshape(SEQ, queries.shape[1], HEAD), sums[0], sums[1])


def general_body(
    tokens,
    first_values,
    doc_lengths,
    cotangent,
    w_query,
    w_key,
    w_value,
    w_out,
    w_gate,
    w_up,
    w_down,
    gain_attn,
    gain_mlp,
):
    query_mat, key_mat, value_mat, out_mat, gate_mat, up_mat, down_mat = (
        lax.all_gather(w_query, "dp", axis=0, tiled=True),
        lax.all_gather(w_key, "dp", axis=0, tiled=True),
        lax.all_gather(w_value, "dp", axis=0, tiled=True),
        lax.all_gather(w_out, "dp", axis=1, tiled=True),
        lax.all_gather(w_gate, "dp", axis=0, tiled=True),
        lax.all_gather(w_up, "dp", axis=0, tiled=True),
        lax.all_gather(w_down, "dp", axis=1, tiled=True),
    )
    local_heads = query_mat.shape[1] // HEAD
    row_count = doc_lengths.shape[0]
    group = row_count * SEQ
    segment, positions = documents(doc_lengths)
    cosine, sine = rotation(positions.reshape(-1))

    def heads(matrix):
        return matrix.reshape(row_count, SEQ, local_heads, HEAD)

    inputs = tokens.astype(jnp.float32)
    normed_one, norm_one_back = jax.vjp(rms_norm, inputs, gain_attn)
    gathered_one = lax.all_gather(normed_one.astype(jnp.bfloat16), "tensor", axis=0, tiled=True)
    query_raw = product(gathered_one, query_mat)
    key_raw = product(gathered_one, key_mat)
    value_raw = product(gathered_one, value_mat)
    queries = rotate(query_raw, cosine, sine).astype(jnp.bfloat16)
    keys_low = rotate(key_raw, cosine, sine).astype(jnp.bfloat16)
    mixed_values = (0.5 * value_raw + 0.5 * first_values.astype(jnp.float32)).astype(jnp.bfloat16)
    attended, logsums = lax.map(
        forward_row, (heads(queries), heads(keys_low), heads(mixed_values), segment)
    )
    attended_low = attended.reshape(group, -1).astype(jnp.bfloat16)
    hidden_in = inputs + lax.psum_scatter(
        product(attended_low, out_mat), "tensor", scatter_dimension=0, tiled=True
    )
    normed_two, norm_two_back = jax.vjp(rms_norm, hidden_in, gain_mlp)
    normed_low_two = normed_two.astype(jnp.bfloat16)
    grad_out = cotangent.astype(jnp.float32)
    gathered_two = lax.all_gather(normed_low_two, "tensor", axis=0, tiled=True)
    activated, swiglu_back = jax.vjp(
        swiglu, product(gathered_two, gate_mat), product(gathered_two, up_mat)
    )
    act_low = activated.astype(jnp.bfloat16)
    layer_out = hidden_in + lax.psum_scatter(
        product(act_low, down_mat).astype(jnp.bfloat16), "tensor", scatter_dimension=0, tiled=True
    ).astype(jnp.float32)
    grad_rows = lax.all_gather(cotangent, "tensor", axis=0, tiled=True)
    grad_gate, grad_up = swiglu_back(outer(grad_rows, down_mat))
    gate_low = grad_gate.astype(jnp.bfloat16)
    up_low = grad_up.astype(jnp.bfloat16)
    grad_normed_two = lax.psum_scatter(
        outer(gate_low, gate_mat) + outer(up_low, up_mat), "tensor", scatter_dimension=0, tiled=True
    )
    grad_gate_mat = inner(gathered_two, gate_low)
    grad_up_mat = inner(gathered_two, up_low)
    grad_down_mat = inner(act_low, grad_rows)
    grad_hidden_two, grad_gain_two = norm_two_back(grad_normed_two)
    grad_hidden = grad_out + grad_hidden_two
    grad_branch = lax.all_gather(grad_hidden.astype(jnp.bfloat16), "tensor", axis=0, tiled=True)
    grad_attended = outer(grad_branch, out_mat).astype(jnp.bfloat16)
    grad_out_mat = inner(attended_low, grad_branch)
    grad_rot_query, grad_rot_key, grad_mixed = lax.map(
        backward_row,
        (
            heads(queries),
            heads(keys_low),
            heads(mixed_values),
            segment,
            heads(grad_attended),
            logsums,
        ),
    )
    grad_query_low = rotate_back(grad_rot_query.reshape(group, -1), cosine, sine).astype(
        jnp.bfloat16
    )
    grad_key_low = rotate_back(grad_rot_key.reshape(group, -1), cosine, sine).astype(jnp.bfloat16)
    grad_first = 0.5 * grad_mixed.reshape(group, -1)
    grad_value_low = grad_first.astype(jnp.bfloat16)
    grad_normed_one = lax.psum_scatter(
        outer(grad_query_low, query_mat)
        + outer(grad_key_low, key_mat)
        + outer(grad_value_low, value_mat),
        "tensor",
        scatter_dimension=0,
        tiled=True,
    )
    grad_query_mat = inner(gathered_one, grad_query_low)
    grad_key_mat = inner(gathered_one, grad_key_low)
    grad_value_mat = inner(gathered_one, grad_value_low)
    grad_inputs_one, grad_gain_one = norm_one_back(grad_normed_one)
    grad_tokens = grad_hidden + grad_inputs_one
    summed = (
        lax.psum_scatter(grad_query_mat, "dp", scatter_dimension=0, tiled=True),
        lax.psum_scatter(grad_key_mat, "dp", scatter_dimension=0, tiled=True),
        lax.psum_scatter(grad_value_mat, "dp", scatter_dimension=0, tiled=True),
        lax.psum_scatter(grad_out_mat, "dp", scatter_dimension=1, tiled=True),
        lax.psum_scatter(grad_gate_mat, "dp", scatter_dimension=0, tiled=True),
        lax.psum_scatter(grad_up_mat, "dp", scatter_dimension=0, tiled=True),
        lax.psum_scatter(grad_down_mat, "dp", scatter_dimension=1, tiled=True),
    )
    gain_sums = lax.psum((grad_gain_one, grad_gain_two), ("dp", "tensor"))
    return (
        layer_out.astype(jnp.bfloat16),
        grad_tokens,
        grad_first,
        summed[0],
        summed[1],
        summed[2],
        summed[3],
        summed[4],
        summed[5],
        summed[6],
        gain_sums[0],
        gain_sums[1],
    )


AXES = ("dp", "tensor")
MESH = pl.DeviceIdType.MESH
TILE = 256
NEG = -1e30
F32 = jnp.float32
BF16 = jnp.bfloat16


def flat(y, x, c, t):
    return ((y * 2 + x) * 2 + c) * 4 + t


def move(values, to):
    pairs = []
    for y in range(2):
        for x in range(2):
            for c in range(2):
                for t in range(4):
                    pair = (flat(y, x, c, t), flat(*to(y, x, c, t)))
                    if pair[0] != pair[1]:
                        pairs.append(pair)
    return lax.ppermute(values, AXES, pairs)


def across_x(values):
    return move(values, lambda y, x, c, t: (y, 1 - x, c, t))


def across_y(values):
    return move(values, lambda y, x, c, t: (1 - y, x, c, t))


def across_c(values):
    return move(values, lambda y, x, c, t: (y, x, 1 - c, t))


def along_t(values, step):
    return move(values, lambda y, x, c, t: (y, x, c, (t + step) % 4))


def swap_halves(values):
    return move(values, lambda y, x, c, t: (y, x, t % 2, (t // 2) * 2 + c))


def pack_kernel(wq, wk, wv, wo, wg, wu, wd, halves, small, big):
    small[0] = dot(wq[...], halves[...]).astype(BF16)
    small[1] = dot(wk[...], halves[...]).astype(BF16)
    small[2] = wv[...]
    small[3] = wo[...].T
    for n, units in enumerate((wg, wu, wd)):
        big[n] = units[...].reshape(big.shape[1:])


def pack(wq, wk, wv, wo, wg, wu, wd):
    wg, wu = wg.T, wu.T
    part, rows = wg.shape
    lane = jnp.arange(256, dtype=jnp.int32)
    source = ((lane & 127) >> 5) * 64 + (lane >> 7) * 32 + (lane & 31)
    halves = (lane[:, None] == source[None, :]).astype(BF16)
    return pl.pallas_call(
        pack_kernel,
        out_shape=[
            jax.ShapeDtypeStruct((4, rows, 256), BF16),
            jax.ShapeDtypeStruct((3, 2, part // 2, rows), BF16),
        ],
        compiler_params=params(),
        name="pack",
    )(wq, wk, wv, wo, wg, wu, wd, halves)


def meet(plane, c, t, dpx, dpy):
    barrier = pltpu.get_barrier_semaphore()
    for e in range(2):
        for d in range(4):
            if e or d:
                other = plane + lax.rem(c + e, 2)
                pl.semaphore_signal(barrier, inc=1, device_id=(other, lax.rem(t + d, 4)), device_id_type=MESH)
    pl.semaphore_signal(barrier, inc=1, device_id=(dpx, t), device_id_type=MESH)
    pl.semaphore_signal(barrier, inc=1, device_id=(dpy, t), device_id_type=MESH)
    pl.semaphore_wait(barrier, 9)


def gather_kernel(tok, fv, small, big, row, first, g_small, g_big, send, recv, relay_send, along_recv, next_send, next_recv, swap, fsend, frecv, here):
    dp, t = lax.axis_index("dp"), lax.axis_index("tensor")
    c, x, y = lax.rem(dp, 2), lax.rem(lax.div(dp, 2), 2), lax.div(dp, 4)
    pair, side = lax.div(t, 2), lax.rem(t, 2)
    plane = dp - c
    dpx, dpy, dpc = dp + 2 - 4 * x, dp + 4 - 8 * y, dp + 1 - 2 * c
    dpxy = dpx + 4 - 8 * y

    meet(plane, c, t, dpx, dpy)
    def slot(k, at, owner, h):
        if k == 0:
            return g_small.at[pl.ds(2 * h, 2), at, pl.ds(owner * 128, 128), :]
        return g_big.at[k - 1, owner, h, at]

    def column(k, owner, h):
        if k == 0:
            return g_small.at[pl.ds(2 * h, 2), :, pl.ds(owner * 128, 128), :]
        return g_big.at[k - 1, owner, h]

    def both(k, at, owner):
        if k == 0:
            return g_small.at[:, at, pl.ds(owner * 128, 128), :]
        return g_big.at[k - 1, owner, :, at]

    def all_of(k, owner):
        if k == 0:
            return g_small.at[:, :, pl.ds(owner * 128, 128), :]
        return g_big.at[k - 1, owner]

    def shard(k):
        return small if k == 0 else big.at[k - 1]

    def part_of(k, h):
        return small.at[pl.ds(2 * h, 2)] if k == 0 else big.at[k - 1, h]

    def copy(k, n, src, dst, to, at):
        return pltpu.make_async_remote_copy(
            src_ref=src,
            dst_ref=dst,
            send_sem=send.at[k, n],
            recv_sem=recv.at[k, n],
            device_id=(to, at),
            device_id_type=MESH,
        )

    chunks = 4
    near, far = (dpx, dpy), (dpy, dpx)
    kept = [pltpu.make_async_copy(shard(k), both(k, t, dp), here.at[k]) for k in range(chunks)]

    def relay(k, at, side, src):
        return pltpu.make_async_remote_copy(
            src_ref=src,
            dst_ref=both(k, at, dp),
            send_sem=relay_send.at[k, at, side],
            recv_sem=along_recv.at[k, at],
            device_id=(dp, t + 2 * side - 1),
            device_id_type=MESH,
        )

    def onward(k, at, h, src):
        return pltpu.make_async_remote_copy(
            src_ref=src,
            dst_ref=slot(k, at, dp, h),
            send_sem=next_send.at[k, at, h],
            recv_sem=next_recv.at[k, at, h],
            device_id=(near[h], t),
            device_id_type=MESH,
        )

    def start_along(k):
        @pl.when(t < 3)
        def _():
            relay(k, t, 1, shard(k)).start()

        @pl.when(t > 0)
        def _():
            relay(k, t, 0, shard(k)).start()

    def pass_along(k, level):
        for side, at in ((1, t - level), (0, t + level)):

            @pl.when((at >= 0) & (at < 4))
            def _():
                block = both(k, at, dp)
                move = relay(k, at, side, block)
                move.wait_recv()

                @pl.when((t < 3) if side else (t > 0))
                def _():
                    move.start()

                for h in range(2):
                    onward(k, at, h, slot(k, at, dp, h)).start()

    def end_along(k):
        for level in range(4):
            for side, at in ((1, t - level), (0, t + level)):

                @pl.when((at >= 0) & (at < 4) & ((t < 3) if side else (t > 0)))
                def _():
                    relay(k, at, side, both(k, at, dp)).wait_send()

    across = [
        [
            copy(k, 2 * h + i, column(k, owner, h), column(k, owner, h), far[h], t)
            for h in range(2)
            for i, owner in enumerate((dp, near[h]))
        ]
        for k in range(chunks)
    ]
    over = [
        [copy(k, 4 + i, all_of(k, owner), all_of(k, owner), dpc, t) for i, owner in enumerate((dp, dpx, dpy, dpxy))]
        for k in range(chunks)
    ]

    order = (1, 0, 2, 3)
    start_along(order[0])
    for item in kept:
        item.start()
    for k in order:
        for h in range(2):
            onward(k, t, h, part_of(k, h)).start()
        if k == order[0]:
            start_along(order[1])

    moved = side != c
    to_own = pltpu.make_async_copy(tok, row.at[c], here.at[4])
    swapped = pltpu.make_async_remote_copy(
        src_ref=tok,
        dst_ref=row.at[side],
        send_sem=swap.at[0],
        recv_sem=swap.at[1],
        device_id=(plane + side, 2 * pair + c),
        device_id_type=MESH,
    )

    def start_tokens():
        @pl.when(moved)
        def _():
            swapped.start()

        @pl.when(jnp.logical_not(moved))
        def _():
            to_own.start()

    heads_core, slab = pair, side

    def first_copy(p):
        return pltpu.make_async_remote_copy(
            src_ref=fv.at[pl.ds(p * SEQ, SEQ), :],
            dst_ref=first.at[slab],
            send_sem=fsend.at[p],
            recv_sem=frecv.at[slab],
            device_id=(plane + heads_core, 2 * p + c),
            device_id_type=MESH,
        )

    def first_local(p):
        return pltpu.make_async_copy(fv.at[pl.ds(p * SEQ, SEQ), :], first.at[slab], here.at[5])

    stays = [(heads_core == c) & (t == 2 * p + c) for p in range(2)]

    def start_first():
        for p in range(2):

            @pl.when(stays[p])
            def _():
                first_local(p).start()

            @pl.when(jnp.logical_not(stays[p]))
            def _():
                first_copy(p).start()

    def pass_over(k):
        for item in across[k]:
            item.wait_recv()
        for item in over[k][1:]:
            item.start()

    def pass_next(k):
        for at in range(4):
            for h in range(2):
                onward(k, at, h, slot(k, at, dp, h)).wait_recv()
        for item in across[k]:
            item.start()

    for i, k in enumerate(order):
        pass_along(k, 1)
        if i + 2 < chunks:
            start_along(order[i + 2])
        if i:
            pass_next(order[i - 1])
        pass_along(k, 2)
        pass_along(k, 3)
        kept[k].wait()
        over[k][0].start()
        if i == 2:
            start_tokens()
        if i == 3:
            start_first()
        if i >= 2:
            pass_over(order[i - 2])
    pass_next(order[3])
    for k in order[2:]:
        pass_over(k)

    @pl.when(moved)
    def _():
        swapped.wait_send()
        swapped.wait_recv()

    @pl.when(jnp.logical_not(moved))
    def _():
        to_own.wait()

    given = pltpu.make_async_remote_copy(
        src_ref=row.at[c],
        dst_ref=row.at[c],
        send_sem=swap.at[2],
        recv_sem=swap.at[3],
        device_id=(dpc, t),
        device_id_type=MESH,
    )
    given.start()
    for p in range(2):

        @pl.when(stays[p])
        def _():
            first_local(p).wait()

        @pl.when(jnp.logical_not(stays[p]))
        def _():
            first_copy(p).wait_send()

    for u in range(2):
        came = pltpu.make_async_remote_copy(
            src_ref=first.at[u],
            dst_ref=first.at[u],
            send_sem=fsend.at[u],
            recv_sem=frecv.at[u],
            device_id=(dpc, t),
            device_id_type=MESH,
        )

        @pl.when((side != c) | (t != 2 * c + u))
        def _():
            came.wait_recv()

    given.wait()
    for k in range(chunks):
        for item in over[k]:
            item.wait_recv()
        end_along(k)
        for item in across[k] + over[k]:
            item.wait_send()
        for at in range(4):
            for h in range(2):
                onward(k, at, h, slot(k, at, dp, h)).wait_send()


def gather(tok, fv, small, big):
    part, rows = big.shape[2:]
    wide = tok.shape[1]
    vmem = pl.BlockSpec(memory_space=pltpu.VMEM)
    sems = pltpu.SemaphoreType.DMA
    return pl.pallas_call(
        gather_kernel,
        out_shape=[
            jax.ShapeDtypeStruct((2, SEQ // 2, wide), BF16),
            jax.ShapeDtypeStruct((2, SEQ, 256), BF16),
            jax.ShapeDtypeStruct((4, 4, wide, 256), BF16),
            jax.ShapeDtypeStruct((3, 8, 2, 4, part, rows), BF16),
        ],
        in_specs=[vmem] * 4,
        out_specs=[any_spec()] * 4,
        scratch_shapes=[
            sems((4, 8)),
            sems((4, 8)),
            sems((4, 4, 2)),
            sems((4, 4)),
            sems((4, 4, 2)),
            sems((4, 4, 2)),
            sems((4,)), sems((2,)), sems((2,)), sems((6,))],
        compiler_params=params(collective_id=0, has_side_effects=True),
        name="gather",
    )(tok, fv, small, big)


def dot(left, right):
    return jnp.dot(left, right, preferred_element_type=F32)


def dot_nt(left, right):
    return lax.dot_general(left, right, (((1,), (1,)), ((), ())), preferred_element_type=F32)


def dot_tn(left, right):
    return lax.dot_general(left, right, (((0,), (0,)), ((), ())), preferred_element_type=F32)


def any_spec():
    return pl.BlockSpec(memory_space=pl.ANY)


def params(**more):
    return pltpu.CompilerParams(vmem_limit_bytes=62 * 1024 * 1024, **more)


def cost(flops, size, exps=0):
    return pl.CostEstimate(flops=int(flops), bytes_accessed=int(size), transcendentals=int(exps))


def project_kernel(at, tok, first, cosine, sine, gain, held, normed_out, q_out, k_out, v_out):
    values = tok[0].astype(F32)
    factor = lax.rsqrt(jnp.mean(values * values, axis=1, keepdims=True) + EPSILON)
    normed = (values * factor * gain[...]).astype(BF16)
    normed_out[...] = normed
    cos, sin = cosine[...], sine[...]
    for u in range(2):
        for n, out, scale in ((0, q_out, 0.125), (1, k_out, 1.0)):
            raw = dot(normed, held[n, u])
            a, b = raw[:, :128], raw[:, 128:]
            out[:, u * 256 : u * 256 + 128] = ((a * cos - b * sin) * scale).astype(BF16)
            out[:, u * 256 + 128 : u * 256 + 256] = ((b * cos + a * sin) * scale).astype(BF16)
        raw = dot(normed, held[2, u])
        v_out[:, u * 256 : u * 256 + 256] = (0.5 * raw + 0.5 * first[u].astype(F32)).astype(BF16)


def once(shape, place):
    return pl.BlockSpec(shape, place, pipeline_mode=pl.Buffered(1))


def project(at, tok, first, cosine, sine, gain, small):
    rows, wide = 512, tok.shape[2]
    row = lambda width: pl.BlockSpec((rows, width), lambda i, at: (i, 0))
    grid = pltpu.PrefetchScalarGridSpec(
        num_scalar_prefetch=1,
        grid=(4,),
        in_specs=[
            pl.BlockSpec((1, rows, wide), lambda i, at: (i // 2, i % 2, 0)),
            pl.BlockSpec((2, rows, 256), lambda i, at: (0, i, 0)),
            row(128),
            row(128),
            pl.BlockSpec((1, wide), lambda i, at: (0, 0)),
            once((4, 2, wide, 256), lambda i, at: (0, at[0] & 1, 0, 0)),
        ],
        out_specs=[row(wide), row(512), row(512), row(512)],
    )
    return pl.pallas_call(
        project_kernel,
        out_shape=[jax.ShapeDtypeStruct((SEQ, wide), BF16)]
        + [jax.ShapeDtypeStruct((SEQ, 512), BF16)] * 3,
        grid_spec=grid,
        compiler_params=params(),
        cost_estimate=cost(2 * SEQ * wide * 1536, 24e6),
        name="project",
    )(at, tok, first, cosine, sine, gain, small)


def head_masks(rows):
    lane = lax.broadcasted_iota(jnp.int32, (rows, 256), 1)
    return (lane & 127) >> 5, lane >> 6


def attend_kernel(bounds, q_ref, k_ref, v_ref, starts, o_ref, lse_ref, kept, turned, acc):
    tiles = SEQ // TILE
    of_qk, _ = head_masks(TILE)
    row = lax.broadcasted_iota(jnp.int32, (TILE, TILE), 0)
    lane = lax.broadcasted_iota(jnp.int32, (TILE, TILE), 1)
    slabs = [slice(0, 256), slice(256, 512)]

    def turn_values(j, carry):
        there = pl.ds(pl.multiple_of(j * TILE, TILE), TILE)
        turned[j] = v_ref[there, :].T
        return carry

    lax.fori_loop(0, tiles, turn_values, 0)

    def eighths(values, reduce):
        return reduce(values.reshape(TILE // 8, 8, 4 * TILE), axis=0)

    def query_tile(i, carry):
        here = pl.ds(pl.multiple_of(i * TILE, TILE), TILE)
        q4 = []
        for slab in slabs:
            q = q_ref[here, slab]
            zero = jnp.zeros_like(q)
            q4.append(jnp.concatenate([jnp.where(of_qk == h, q, zero) for h in range(4)], axis=0))
        low = bounds[i]
        begin = starts[pl.ds(i, 1), :]
        limit = lane + i * TILE

        def score(j, tops):
            there = pl.ds(pl.multiple_of(j * TILE, TILE), TILE)
            at_row = row + j * TILE
            ok = (at_row >= begin) & (at_row <= limit)
            ok = jnp.concatenate([ok] * 4, axis=1)
            new = []
            for u, slab in enumerate(slabs):
                s = jnp.where(ok, dot_nt(k_ref[there, slab], q4[u]), NEG)
                kept[j - low, u] = s
                new.append(jnp.maximum(tops[u], eighths(s, jnp.max)))
            return tuple(new)

        start = jnp.full((8, 4 * TILE), NEG, F32)
        tops = lax.fori_loop(low, i + 1, score, (start, start))
        tops = [jnp.max(top, axis=0, keepdims=True) for top in tops]
        acc[...] = jnp.zeros_like(acc)

        def weigh(j, totals):
            new = []
            for u in range(2):
                e = jnp.exp(kept[j - low, u] - tops[u])
                p = e.astype(BF16)
                for h in range(4):
                    part = slice(u * 256 + h * 64, u * 256 + h * 64 + 64)
                    acc[part] += dot(turned[j, part, :], p[:, h * TILE : (h + 1) * TILE])
                new.append(totals[u] + eighths(e, jnp.sum))
            return tuple(new)

        zero = jnp.zeros((8, 4 * TILE), F32)
        totals = lax.fori_loop(low, i + 1, weigh, (zero, zero))
        for u, slab in enumerate(slabs):
            total = jnp.sum(totals[u], axis=0, keepdims=True)
            inverse = 1.0 / total
            scaled = [
                acc[u * 256 + h * 64 : u * 256 + h * 64 + 64] * inverse[:, h * TILE : (h + 1) * TILE] for h in range(4)
            ]
            o_ref[here, slab] = jnp.concatenate(scaled, axis=0).T.astype(BF16)
            lse_ref[u, pl.ds(i, 1), :] = tops[u] + jnp.log(total)
        return carry

    lax.fori_loop(0, tiles, query_tile, 0)


def attend(bounds, q, k, v, starts):
    tiles = SEQ // TILE
    vmem = pl.BlockSpec(memory_space=pltpu.VMEM)
    return pl.pallas_call(
        attend_kernel,
        out_shape=[
            jax.ShapeDtypeStruct((SEQ, 512), BF16),
            jax.ShapeDtypeStruct((2, tiles, 4 * TILE), F32),
        ],
        in_specs=[pl.BlockSpec(memory_space=pltpu.SMEM)] + [vmem] * 4,
        out_specs=[vmem] * 2,
        scratch_shapes=[
            pltpu.VMEM((tiles, 2, TILE, 4 * TILE), F32),
            pltpu.VMEM((tiles, 512, TILE), BF16),
            pltpu.VMEM((512, TILE), F32),
        ],
        compiler_params=params(),
        cost_estimate=cost(20e9, 12e6, 1e7),
        name="attend",
    )(bounds, q, k, v, starts)


def attend_back_kernel(
    bounds, q_ref, k_ref, v_ref, do_ref, o_ref, lse_ref, starts, cosine, sine, dq_ref, dk_ref, dv_ref, dq_acc, delta, dk_acc, dv_acc
):
    tiles = SEQ // TILE
    of_qk, of_v = head_masks(TILE)
    row = lax.broadcasted_iota(jnp.int32, (TILE, TILE), 0)
    lane = lax.broadcasted_iota(jnp.int32, (TILE, TILE), 1)
    slabs = [slice(0, 256), slice(256, 512)]
    pick = (lax.broadcasted_iota(jnp.int32, (8, 256), 1) >> 6) == lax.broadcasted_iota(
        jnp.int32, (8, 256), 0
    )
    pick = pick.astype(F32)
    dq_acc[...] = jnp.zeros_like(dq_acc)

    def prepare(i, carry):
        here = pl.ds(pl.multiple_of(i * TILE, TILE), TILE)
        for u, slab in enumerate(slabs):
            both = do_ref[here, slab].astype(F32) * o_ref[here, slab].astype(F32)
            sums = lax.dot_general(
                pick, both, (((1,), (1,)), ((), ())), precision=lax.Precision.HIGHEST, preferred_element_type=F32
            )
            for h in range(4):
                delta[u, pl.ds(i, 1), h * TILE : (h + 1) * TILE] = sums[h : h + 1]
        return carry

    lax.fori_loop(0, tiles, prepare, 0)

    def rotate_out(values, here, out, low, scale):
        a, b = values[:, :128], values[:, 128:]
        cos, sin = cosine[here, :], sine[here, :]
        out[here, low : low + 128] = ((a * cos + b * sin) * scale).astype(BF16)
        out[here, low + 128 : low + 256] = ((b * cos - a * sin) * scale).astype(BF16)

    def split(values, of):
        zero = jnp.zeros_like(values)
        return jnp.concatenate([jnp.where(of == h, values, zero) for h in range(4)], axis=0)

    def key_tile(j, carry):
        there = pl.ds(pl.multiple_of(j * TILE, TILE), TILE)
        at_row = row + j * TILE
        dk_acc[...] = jnp.zeros_like(dk_acc)
        dv_acc[...] = jnp.zeros_like(dv_acc)

        def query_tile(i, carry):
            here = pl.ds(pl.multiple_of(i * TILE, TILE), TILE)
            at_lane = lane + i * TILE
            ok = (at_row >= starts[pl.ds(i, 1), :]) & (at_row <= at_lane)
            ok = jnp.concatenate([ok] * 4, axis=1)
            for u, slab in enumerate(slabs):
                q4 = split(q_ref[here, slab], of_qk)
                do4 = split(do_ref[here, slab], of_v)
                s = dot_nt(k_ref[there, slab], q4)
                dp = dot_nt(v_ref[there, slab], do4)
                p = jnp.exp(jnp.where(ok, s - lse_ref[u, pl.ds(i, 1), :], NEG))
                ds = (p * (dp - delta[u, pl.ds(i, 1), :])).astype(BF16)
                dv_acc[u] += dot(p.astype(BF16), do4)
                dk_acc[u] += dot(ds, q4)
                ds4 = jnp.concatenate([ds[:, h * TILE : (h + 1) * TILE] for h in range(4)], axis=0)
                dq_acc[i, u] += dot_tn(ds4, split(k_ref[there, slab], of_qk))
            return carry

        lax.fori_loop(j, bounds[tiles + j] + 1, query_tile, 0)
        for u, slab in enumerate(slabs):
            rotate_out(dk_acc[u], there, dk_ref, u * 256, 1.0)
            dv_ref[there, slab] = (0.5 * dv_acc[u]).astype(BF16)
        return carry

    lax.fori_loop(0, tiles, key_tile, 0)

    def finish_tile(i, carry):
        here = pl.ds(pl.multiple_of(i * TILE, TILE), TILE)
        for u in range(2):
            rotate_out(dq_acc[i, u], here, dq_ref, u * 256, 0.125)
        return carry

    lax.fori_loop(0, tiles, finish_tile, 0)


def attend_back(bounds, q, k, v, do, o, lse, starts, cosine, sine):
    tiles = SEQ // TILE
    vmem = pl.BlockSpec(memory_space=pltpu.VMEM)
    return pl.pallas_call(
        attend_back_kernel,
        out_shape=[jax.ShapeDtypeStruct((SEQ, 512), BF16)] * 3,
        in_specs=[pl.BlockSpec(memory_space=pltpu.SMEM)] + [vmem] * 9,
        out_specs=[vmem] * 3,
        scratch_shapes=[
            pltpu.VMEM((tiles, 2, TILE, 256), F32),
            pltpu.VMEM((2, tiles, 4 * TILE), F32),
            pltpu.VMEM((2, TILE, 256), F32),
            pltpu.VMEM((2, TILE, 256), F32),
        ],
        compiler_params=params(),
        cost_estimate=cost(50e9, 20e6, 1e7),
        name="attend_back",
    )(bounds, q, k, v, do, o, lse, starts, cosine, sine)


def mlp_kernel(at, att_own, att_other, tok, cot_here, cot_moved, gain, wo, big, *rest):
    (out, gh_out, gb_out, n2_out, hid_out, ga_own, ga_other, gg_out, cot_out) = rest[:9]
    (wg, wu, wd, sems) = rest[9:]
    step = pl.program_id(0)
    c = at[0] & 1

    @pl.when(step == 0)
    def _():
        for n, held in enumerate((wg, wu, wd)):
            for owner in range(8):
                pltpu.make_async_copy(
                    big.at[n, owner], held.at[:, owner * 128 : owner * 128 + 128], sems.at[n]
                ).start()
        gg_out[...] = jnp.zeros_like(gg_out)

    hidden = tok[0].astype(F32)
    for e, att in enumerate((att_own, att_other)):
        for u in range(2):
            hidden += dot_nt(att[:, u * 256 : u * 256 + 256], wo[0, 2 * (c ^ e) + u])
    factor = lax.rsqrt(jnp.mean(hidden * hidden, axis=1, keepdims=True) + EPSILON)
    gains = gain[...]
    normed = (hidden * factor * gains).astype(BF16)
    n2_out[...] = normed
    g = jnp.where((at[1] & 1) == c, cot_here[...], cot_moved[...])
    cot_out[...] = g

    @pl.when(step == 0)
    def _():
        for n, held in enumerate((wg, wu, wd)):
            pltpu.make_async_copy(held, held, sems.at[n]).wait()

    down = jnp.zeros_like(hidden)
    back = jnp.zeros_like(hidden)
    units = wg.shape[0]
    for low in range(0, units, 768):
        part = slice(low, min(low + 768, units))
        gate, up, grad_act = dot_nt(normed, wg[part]), dot_nt(normed, wu[part]), dot_nt(g, wd[part])
        sig = 1.0 / (1.0 + jnp.exp(-gate))
        silu = gate * sig
        act = (silu * up).astype(BF16)
        grad_up = (grad_act * silu).astype(BF16)
        grad_gate = (grad_act * up * (sig * (1.0 + gate * (1.0 - sig)))).astype(BF16)
        hid_out[0, :, part], hid_out[1, :, part], hid_out[2, :, part] = grad_gate, grad_up, act
        down += dot(act, wd[part])
        back += dot(grad_gate, wg[part]) + dot(grad_up, wu[part])
    out[...] = (hidden + down).astype(BF16)
    gg_out[...] += jnp.sum((back * hidden * factor).reshape(-1, 8, back.shape[1]), axis=0)
    scaled = back * gains
    mean = jnp.mean(scaled * hidden, axis=1, keepdims=True)
    grad_hidden = g.astype(F32) + factor * scaled - hidden * (factor * factor * factor * mean)
    gh_out[...] = grad_hidden
    branch = grad_hidden.astype(BF16)
    gb_out[...] = branch
    for e, ga in enumerate((ga_own, ga_other)):
        for u in range(2):
            ga[:, u * 256 : u * 256 + 256] = dot(branch, wo[0, 2 * (c ^ e) + u]).astype(BF16)


def mlp(at, att_own, att_other, tok, cot_here, cot_moved, gain, small, big):
    _, count, wide = tok.shape
    big = big.reshape(3, 8, -1, 128)
    rows, units = 256, big.shape[2]
    row = lambda width: pl.BlockSpec((rows, width), lambda i, at: (i, 0))
    grid = pltpu.PrefetchScalarGridSpec(
        num_scalar_prefetch=1,
        grid=(count // rows,),
        in_specs=[
            row(512),
            row(512),
            pl.BlockSpec((1, rows, wide), lambda i, at: (at[0] & 1, i, 0)),
            row(wide),
            row(wide),
            pl.BlockSpec((1, wide), lambda i, at: (0, 0)),
            once((1, 4, wide, 256), lambda i, at: (3, 0, 0, 0)),
            any_spec(),
        ],
        out_specs=[
            row(wide),
            row(wide),
            row(wide),
            row(wide),
            pl.BlockSpec((3, rows, units), lambda i, at: (0, i, 0)),
            row(512),
            row(512),
            pl.BlockSpec((8, wide), lambda i, at: (0, 0)),
            row(wide),
        ],
        scratch_shapes=[pltpu.VMEM((units, wide), BF16)] * 3 + [pltpu.SemaphoreType.DMA((3,))],
    )
    tokens = lambda width, kind=BF16: jax.ShapeDtypeStruct((count, width), kind)
    return pl.pallas_call(
        mlp_kernel,
        out_shape=[
            tokens(wide),
            tokens(wide, F32),
            tokens(wide),
            tokens(wide),
            jax.ShapeDtypeStruct((3, count, units), BF16),
            tokens(512),
            tokens(512),
            jax.ShapeDtypeStruct((8, wide), F32),
            tokens(wide),
        ],
        grid_spec=grid,
        compiler_params=params(),
        cost_estimate=cost(2 * count * wide * (6 * units + 2 * wide), 60e6, 3e6),
        name="mlp",
    )(at, att_own, att_other, tok, cot_here, cot_moved, gain, small, big)


def turn_rows(source, plane, parity, held):
    for rel in range(4):
        block = ((plane ^ rel) * 2 + parity) * 128
        held[rel * 128 : rel * 128 + 128, :] = source[:, pl.ds(pl.multiple_of(block, 128), 128)].T


def place_first(send, keep, done, lanes):
    for yr in range(2):
        keep[yr, :, lanes] = done[2 * yr]
        send[yr, :, lanes] = done[2 * yr + 1]


def place_second(send, keep, done, lanes):
    for xr in range(2):
        keep[xr, :, lanes] = done[xr]
        send[xr, :, lanes] = done[2 + xr]


def weights_kernel(n2, g, branch, hid, own, other, send1, keep1, send2, keep2, turned, given, got, out_sem, in_sem):
    step = pl.program_id(0)
    dp, t = lax.axis_index("dp"), lax.axis_index("tensor")
    c = lax.rem(dp, 2)
    plane = lax.div(dp, 2)
    n = lax.rem(step, 4)
    units = hid.shape[2] // 2

    @pl.when(step == 0)
    def _():
        barrier = pltpu.get_barrier_semaphore()
        pl.semaphore_signal(barrier, inc=1, device_id=(dp + 1 - 2 * c, t), device_id_type=MESH)
        pl.semaphore_wait(barrier, 1)

    def exchange(k):
        lanes = pl.ds(k * units, units if k < 3 else 512)
        return pltpu.make_async_remote_copy(
            src_ref=given.at[:, :, :, lanes],
            dst_ref=got.at[:, :, :, lanes],
            send_sem=out_sem.at[k],
            recv_sem=in_sem.at[k],
            device_id=(dp + 1 - 2 * c, t),
            device_id_type=MESH,
        )

    for phase, parity in ((0, 1 - c), (1, c)):
        for at_n, source in ((0, n2), (2, g), (3, branch)):

            @pl.when(step == 4 * phase + at_n)
            def _():
                x = lax.rem(plane, 2)
                y = lax.div(plane, 2)
                for rel in range(4):
                    yy, xx = (y, 1 - y)[rel // 2], (x, 1 - x)[rel % 2]
                    block = pl.multiple_of((yy * 4 + xx * 2 + parity) * 128, 128)
                    turned[rel * 128 : rel * 128 + 128, :] = source[:, pl.ds(block, 128)].T

    def heads(h):
        return jnp.where(c == h, own[...], other[...])

    @pl.when(step < 3)
    def _():
        for h in range(2):
            product = dot(turned[...], hid[0, :, h * units : h * units + units]).astype(BF16)
            given[:, h, :, pl.ds(pl.multiple_of(n * units, 128), units)] = product.reshape(4, 128, units)

    @pl.when(step == 3)
    def _():
        for h in range(2):
            product = dot(turned[...], heads(h)).astype(BF16)
            given[:, h, :, 3 * units : 3 * units + 512] = product.reshape(4, 128, 512)

    for k in range(4):

        @pl.when(step == k + 1)
        def _():
            exchange(k).start()

        @pl.when(step == k + 4)
        def _():
            exchange(k).wait_recv()

    def keep(product, h, lanes):
        done = [(product[r * 128 : r * 128 + 128] + got[r, h, :, lanes].astype(F32)).astype(BF16) for r in range(4)]
        (place_first, place_second)[h](*((send1, keep1), (send2, keep2))[h], done, lanes)

    @pl.when((step >= 4) & (step < 7))
    def _():
        for h in range(2):
            product = dot(turned[...], hid[0, :, h * units : h * units + units])
            keep(product, h, pl.ds(pl.multiple_of(n * units, 128), units))

    @pl.when(step == 7)
    def _():
        for h in range(2):
            keep(dot(turned[...], heads(h)), h, pl.ds(3 * units, 512))
        for k in range(4):
            exchange(k).wait_send()


def weights(n2, g, branch, hid, own, other):
    count, wide = n2.shape
    units = hid.shape[2] // 2
    full = lambda *shape: pl.BlockSpec(shape, lambda s: (0,) * len(shape), pipeline_mode=pl.Buffered(1))
    length = 3 * units + 512
    grid = pl.GridSpec(
        grid=(8,),
        in_specs=[
            full(count, wide),
            full(count, wide),
            full(count, wide),
            pl.BlockSpec((1, count, 2 * units), lambda s: (jnp.minimum(lax.rem(s, 4), 2), 0, 0)),
            full(count, 512),
            full(count, 512),
        ],
        out_specs=[full(2, 128, length)] * 4,
        scratch_shapes=[
            pltpu.VMEM((512, count), BF16),
            pltpu.VMEM((4, 2, 128, length), BF16),
            pltpu.VMEM((4, 2, 128, length), BF16),
            pltpu.SemaphoreType.DMA((4,)),
            pltpu.SemaphoreType.DMA((4,)),
        ],
    )
    return pl.pallas_call(
        weights_kernel,
        out_shape=[jax.ShapeDtypeStruct((2, 128, length), BF16)] * 4,
        grid_spec=grid,
        compiler_params=params(collective_id=1, has_side_effects=True),
        cost_estimate=cost(2 * count * 1024 * length * 2, 50e6),
        name="weights",
    )(n2, g, branch, hid, own, other)


def add(left, right):
    return (left.astype(F32) + right.astype(F32)).astype(BF16)


def turn_kernel(at, kept1, got1, last1, kept2, got2, last2, out, *, units):
    t = at[1]
    sums = [
        kept[0].astype(F32) + got[0].astype(F32) + last[...].astype(F32)
        for kept, got, last in ((kept1, got1, last1), (kept2, got2, last2))
    ]
    part = units // 4
    for h in range(2):
        for n in range(3):
            turned = sums[h][:, n * units : n * units + units].T.astype(BF16)
            for i in range(4):
                rows = slice((2 * n + h) * part, (2 * n + h + 1) * part)
                out[(i - t) & 3, rows, :] = turned[i * part : (i + 1) * part]
        turned = sums[h][:, 3 * units :].T.astype(BF16)
        for i in range(2):
            out[(2 * h + i - t) & 3, 6 * part :, :] = turned[i * 256 : i * 256 + 256]


def turn(at, arrays, units):
    length = arrays[0].shape[2]
    rows = 3 * (units // 2) + 256
    half = pl.BlockSpec((1, 128, length), lambda i, at: (0, 0, 0))
    last = pl.BlockSpec((128, length), lambda i, at: (0, 0))
    grid = pltpu.PrefetchScalarGridSpec(
        num_scalar_prefetch=1,
        grid=(1,),
        in_specs=[half, half, last] * 2,
        out_specs=pl.BlockSpec((4, rows, 128), lambda i, at: (0, 0, 0)),
    )
    return pl.pallas_call(
        functools.partial(turn_kernel, units=units),
        out_shape=jax.ShapeDtypeStruct((4, rows, 128), BF16),
        grid_spec=grid,
        compiler_params=params(),
        cost_estimate=cost(1e6, 10e6),
        name="turn",
    )(at, *arrays)


def last_kernel(pieces, send1, keep1, send2, keep2, tok, gains, got_pieces, own_heads, got_heads, got_tok, sums, *rest):
    (got1, got2, part1, part2, last1, last2, heads, held, came, p_sem, h_sem, one_sem, two_sem, swap, g_sem) = rest
    dp, t = lax.axis_index("dp"), lax.axis_index("tensor")
    c, x, y = lax.rem(dp, 2), lax.rem(lax.div(dp, 2), 2), lax.div(dp, 4)
    pair, side = lax.div(t, 2), lax.rem(t, 2)
    plane = dp - c
    dpx, dpy, dpc = dp + 2 - 4 * x, dp + 4 - 8 * y, dp + 1 - 2 * c
    meet(plane, c, t, dpx, dpy)

    def copy(src, dst, sems, n, to):
        return pltpu.make_async_remote_copy(
            src_ref=src,
            dst_ref=dst,
            send_sem=sems.at[0, n],
            recv_sem=sems.at[1, n],
            device_id=to,
            device_id_type=MESH,
        )

    ones = [copy(send1, got1, one_sem, 0, (dpx, t)), copy(send2, got2, one_sem, 1, (dpy, t))]
    for item in ones:
        item.start()
    turns = (dpc, t), (dpx, t), (dpy, t), (dp, t + 1 - 2 * side), (dp, lax.rem(t + 2, 4))
    held[0] = gains[...]
    zs = [copy(pieces.at[d], got_pieces.at[d - 1], p_sem, d - 1, (dp, lax.rem(t + d, 4))) for d in (1, 2, 3)]
    for item in zs:
        item.start()
    moved = side != c
    swapped = copy(tok, got_tok, swap, 0, (plane + side, 2 * pair + c))

    @pl.when(moved)
    def _():
        swapped.start()

    def gain_step(n):
        return copy(held.at[n], came.at[n], g_sem, n, turns[n])

    def gain_next(n):
        gain_step(n).wait_recv()
        held[n + 1] = held[n] + came[n]

    gain_step(0).start()
    for item in ones:
        item.wait_recv()
    part1[...] = add(keep1[1], got1[1])
    part2[...] = add(keep2[1], got2[1])
    gain_next(0)
    first1 = keep1[0].astype(F32) + got1[0].astype(F32)
    first2 = keep2[0].astype(F32) + got2[0].astype(F32)
    twos = [copy(part1, last1, two_sem, 0, (dpy, t)), copy(part2, last2, two_sem, 1, (dpx, t))]
    for item in twos:
        item.start()
    gain_step(1).start()
    gain_next(1)
    for item in twos:
        item.wait_recv()
    totals = ((first1 + last1[...].astype(F32)).astype(BF16), (first2 + last2[...].astype(F32)).astype(BF16))
    for e, total in enumerate(totals):
        core = (c, 1 - c)[e]
        for u in range(2):
            d = lax.rem(2 * core + u + 4 - t, 4)
            for n in range(3):
                heads[d, n] = total[:, n * 512 + u * 256 : n * 512 + u * 256 + 256]
    gain_step(2).start()
    gain_next(2)
    own_heads[...] = heads[0]
    hs = [copy(heads.at[d], got_heads.at[d - 1], h_sem, d - 1, (dp, lax.rem(t + d, 4))) for d in (1, 2, 3)]
    for item in hs:
        item.start()
    for n in (3, 4):
        gain_step(n).start()
        gain_next(n)
    sums[...] = held[5]
    for item in ones + twos:
        item.wait_send()
    for n in range(5):
        gain_step(n).wait_send()
    for item in zs + hs:
        item.wait()

    @pl.when(moved)
    def _():
        swapped.wait()


def last_exchanges(pieces, send1, keep1, send2, keep2, tok, gains):
    vmem = pl.BlockSpec(memory_space=pltpu.VMEM)
    sems = pltpu.SemaphoreType.DMA
    rows = pieces.shape[1]
    half = send1.shape
    return pl.pallas_call(
        last_kernel,
        out_shape=[
            jax.ShapeDtypeStruct((3, rows, 128), BF16),
            jax.ShapeDtypeStruct((3, 128, 256), BF16),
            jax.ShapeDtypeStruct((3, 3, 128, 256), BF16),
            jax.ShapeDtypeStruct(tok.shape, BF16),
            jax.ShapeDtypeStruct(gains.shape, F32),
        ],
        in_specs=[vmem] * 7,
        out_specs=[any_spec(), vmem, any_spec(), any_spec(), vmem],
        scratch_shapes=[pltpu.VMEM(half, BF16)] * 2
        + [pltpu.VMEM(half[1:], BF16)] * 4
        + [pltpu.VMEM((4, 3, 128, 256), BF16), pltpu.VMEM((6,) + gains.shape, F32), pltpu.VMEM((5,) + gains.shape, F32)]
        + [sems((2, 3)), sems((2, 3)), sems((2, 2)), sems((2, 2)), sems((2, 1)), sems((2, 5))],
        compiler_params=params(collective_id=2, has_side_effects=True),
        name="last_exchanges",
    )(pieces, send1, keep1, send2, keep2, tok, gains)


def finish_kernel(at, own, got, own_heads, got_heads, tok, got_tok, gate, up, down, out, query, key, value, tok_out):
    @pl.when(pl.program_id(0) == 0)
    def _():
        part = down.shape[0]
        for n, ref in enumerate((gate, up, down, out)):
            rows = slice(n * part, n * part + ref.shape[0])
            total = own[0, rows, :].astype(F32)
            for d in range(3):
                total += got[d, rows, :].astype(F32)
            ref[...] = total
        heads = own_heads[...].astype(F32)
        for d in range(3):
            heads += got_heads[d].astype(F32)
        for n, ref in enumerate((query, key)):
            parts = []
            for h in range(4):
                parts += [heads[n, :, h * 32 : h * 32 + 32], heads[n, :, 128 + h * 32 : 160 + h * 32]]
            ref[...] = jnp.concatenate(parts, axis=1)
        value[...] = heads[2]

    stays = (at[0] & 1) == (at[1] & 1)
    tok_out[...] = jnp.where(stays, tok[...], got_tok[...]).astype(F32)


def finish(at, pieces, got, own_heads, got_heads, tok, got_tok, part):
    count, wide = tok.shape
    rows = 256
    row = pl.BlockSpec((rows, wide), lambda i, at: (i, 0))
    whole = lambda *shape: pl.BlockSpec(shape, lambda i, at: (0,) * len(shape))
    shapes = [(part, 128)] * 3 + [(256, 128)] + [(128, 256)] * 3
    grid = pltpu.PrefetchScalarGridSpec(
        num_scalar_prefetch=1,
        grid=(count // rows,),
        in_specs=[
            whole(1, pieces.shape[1], 128),
            whole(*got.shape),
            whole(*own_heads.shape),
            whole(*got_heads.shape),
            row,
            row,
        ],
        out_specs=[whole(*shape) for shape in shapes] + [row],
    )
    return pl.pallas_call(
        finish_kernel,
        out_shape=[jax.ShapeDtypeStruct(shape, F32) for shape in shapes + [(count, wide)]],
        grid_spec=grid,
        compiler_params=params(),
        cost_estimate=cost(1e6, 18e6),
        name="finish",
    )(at, pieces, got, own_heads, got_heads, tok, got_tok)


def project_back_kernel(at, dq, dk, dv, held, out):
    out[...] = back_product(dq, dk, dv, held).astype(out.dtype)


def back_product(dq, dk, dv, held):
    total = None
    for u in range(2):
        for n, grad in enumerate((dq, dk, dv)):
            term = dot_nt(grad[:, u * 256 : u * 256 + 256], held[n, u])
            total = term if total is None else total + term
    return total


def back_specs(rows, other, wide):
    half = SEQ // 2 // rows
    row = pl.BlockSpec((rows, 512), lambda i, at: (((at[0] & 1) ^ other) * half + i, 0))
    return [row] * 3 + [once((4, 2, wide, 256), lambda i, at: (0, at[0] & 1, 0, 0))]


def project_back_send(at, dq, dk, dv, small):
    rows, wide = 512, small.shape[2]
    grid = pltpu.PrefetchScalarGridSpec(
        num_scalar_prefetch=1,
        grid=(SEQ // 2 // rows,),
        in_specs=back_specs(rows, 1, wide),
        out_specs=pl.BlockSpec((rows, wide), lambda i, at: (i, 0)),
    )
    return pl.pallas_call(
        project_back_kernel,
        out_shape=jax.ShapeDtypeStruct((SEQ // 2, wide), BF16),
        grid_spec=grid,
        compiler_params=params(),
        cost_estimate=cost(SEQ * wide * 1536, 10e6),
        name="project_back_send",
    )(at, dq, dk, dv, small)


def project_back_keep_kernel(at, dq, dk, dv, held, got, tok, grad_hidden, gain, out, gain_out):
    @pl.when(pl.program_id(0) == 0)
    def _():
        gain_out[...] = jnp.zeros_like(gain_out)

    grad = back_product(dq, dk, dv, held) + got[...].astype(F32)
    values = tok[0].astype(F32)
    factor = lax.rsqrt(jnp.mean(values * values, axis=1, keepdims=True) + EPSILON)
    gain_out[...] += jnp.sum((grad * values * factor).reshape(-1, 8, grad.shape[1]), axis=0)
    scaled = grad * gain[...]
    mean = jnp.mean(scaled * values, axis=1, keepdims=True)
    out[...] = (grad_hidden[...] + factor * scaled - values * (factor * factor * factor * mean)).astype(BF16)


def project_back_keep(at, dq, dk, dv, small, got, tok, grad_hidden, gain):
    rows, wide = 512, small.shape[2]
    row = pl.BlockSpec((rows, wide), lambda i, at: (i, 0))
    grid = pltpu.PrefetchScalarGridSpec(
        num_scalar_prefetch=1,
        grid=(SEQ // 2 // rows,),
        in_specs=back_specs(rows, 0, wide)
        + [
            row,
            pl.BlockSpec((1, rows, wide), lambda i, at: (at[0] & 1, i, 0)),
            row,
            pl.BlockSpec((1, wide), lambda i, at: (0, 0)),
        ],
        out_specs=[row, pl.BlockSpec((8, wide), lambda i, at: (0, 0))],
    )
    return pl.pallas_call(
        project_back_keep_kernel,
        out_shape=[jax.ShapeDtypeStruct((SEQ // 2, wide), BF16), jax.ShapeDtypeStruct((8, wide), F32)],
        grid_spec=grid,
        compiler_params=params(),
        cost_estimate=cost(SEQ * wide * 1536, 20e6),
        name="project_back_keep",
    )(at, dq, dk, dv, small, got, tok, grad_hidden, gain)


def heads_send_kernel(at, left, dq, dk, dv, send, keep, turned):
    n = pl.program_id(0)

    @pl.when(n == 0)
    def _():
        turn_rows(left, at[0] >> 1, 1 - (at[0] & 1), turned)

    for k, right in enumerate((dq, dk, dv)):

        @pl.when(n == k)
        def _():
            product = dot(turned[...], right[...]).astype(BF16)
            done = [product[r * 128 : r * 128 + 128] for r in range(4)]
            place_second(send, keep, done, slice(k * 512, k * 512 + 512))


def heads_keep_kernel(at, left, dq, dk, dv, send, keep, turned):
    n = pl.program_id(0)

    @pl.when(n == 0)
    def _():
        turn_rows(left, at[0] >> 1, at[0] & 1, turned)

    for k, right in enumerate((dq, dk, dv)):

        @pl.when(n == k)
        def _():
            product = dot(turned[...], right[...]).astype(BF16)
            done = [product[r * 128 : r * 128 + 128] for r in range(4)]
            place_first(send, keep, done, slice(k * 512, k * 512 + 512))


def heads_gradient(kernel, name, at, left, dq, dk, dv):
    count, wide = left.shape
    full = lambda *shape: pl.BlockSpec(shape, lambda n, at: (0,) * len(shape), pipeline_mode=pl.Buffered(1))
    grid = pltpu.PrefetchScalarGridSpec(
        num_scalar_prefetch=1,
        grid=(3,),
        in_specs=[full(count, wide)] + [full(count, 512)] * 3,
        out_specs=[full(2, 128, 1536)] * 2,
        scratch_shapes=[pltpu.VMEM((512, count), BF16)],
    )
    return pl.pallas_call(
        kernel,
        out_shape=[jax.ShapeDtypeStruct((2, 128, 1536), BF16)] * 2,
        grid_spec=grid,
        compiler_params=params(),
        cost_estimate=cost(2 * count * 512 * 1536, 12e6),
        name=name,
    )(at, left, dq, dk, dv)


def fast_body(tokens, first_values, doc_lengths, cotangent, w_query, w_key, w_value, w_out, w_gate, w_up, w_down, gain_attn, gain_mlp):
    me, t = lax.axis_index("dp"), lax.axis_index("tensor")
    c = me % 2
    pair, side = t // 2, t % 2
    wide = tokens.shape[1]
    tiles = SEQ // TILE
    at = jnp.where(jnp.arange(8, dtype=jnp.int32) == 0, me, t).astype(jnp.int32)

    small_shard, big_shard = pack(w_query, w_key, w_value, w_out, w_gate, w_up, w_down)
    row, first, small, big = gather(tokens, first_values, small_shard, big_shard)

    lengths = jnp.where(c == side, doc_lengths, across_c(doc_lengths))
    lengths = lax.dynamic_index_in_dim(lengths, pair, 0, keepdims=False)
    order = jnp.arange(DOCS, dtype=jnp.int32)
    ends = jnp.sum(jnp.where(order[None, :] <= order[:, None], lengths[None, :], 0), axis=1)
    places = jnp.arange(SEQ, dtype=jnp.int32)
    starts = jnp.max(jnp.where(ends[None, :] <= places[:, None], ends[None, :], 0), axis=1)
    last = jnp.arange(tiles, dtype=jnp.int32) * TILE + (TILE - 1)
    stop = jnp.min(jnp.where(ends[None, :] > last[:, None], ends[None, :], SEQ), axis=1)
    bounds = jnp.concatenate([starts.reshape(tiles, TILE)[:, 0] // TILE, (stop - 1) // TILE])
    starts_by_tile = starts.reshape(tiles, TILE)
    freqs = 10000.0 ** (-(jnp.arange(32, dtype=F32) * 2.0 / HEAD))
    angles = (places - starts).astype(F32)[:, None] * jnp.tile(freqs, 4)[None, :]
    cosine, sine = jnp.cos(angles), jnp.sin(angles)

    row, cotangent = lax.optimization_barrier((row, cotangent))
    moved_cot = swap_halves(cotangent)
    normed_one, q, k, v = project(at, row, first, cosine, sine, gain_attn[None], small)
    attended, lse = attend(bounds, q, k, v, starts_by_tile)
    by_half = attended.reshape(2, SEQ // 2, 512)
    att_own = lax.dynamic_index_in_dim(by_half, c, 0, keepdims=False)
    att_other = across_c(lax.dynamic_index_in_dim(by_half, 1 - c, 0, keepdims=False))
    out, grad_hidden, branch, normed_two, hid, ga_own, ga_other, gain_two, cot = mlp(
        at, att_own, att_other, row, cotangent, moved_cot, gain_mlp[None], small, big
    )
    stays = c == side
    layer_out = jnp.where(stays, out, swap_halves(out))

    ga_got = across_c(ga_other)
    do = jnp.where(c == 0, jnp.concatenate([ga_own, ga_got]), jnp.concatenate([ga_got, ga_own]))

    kept = weights(normed_two, cot, branch, hid, att_own, att_other)
    kept, do = lax.optimization_barrier((kept, do))
    got1, got2 = across_x(kept[0]), across_y(kept[2])

    dq, dk, dv = attend_back(bounds, q, k, v, do, attended, lse, starts_by_tile, cosine, sine)

    dq, dk, dv, got1, got2 = lax.optimization_barrier((dq, dk, dv, got1, got2))
    last1, last2 = across_y(add(kept[1][1], got1[1])), across_x(add(kept[3][1], got2[1]))

    def first_back(r):
        slab = jnp.where(pair == r, dv[:, :256], dv[:, 256:])
        came = move(slab, lambda y, x, c, t: (y, x, t % 2, 2 * c + ((t // 2) ^ r)))
        return jnp.where(stays & (t == 2 * c + (pair ^ r)), slab, came)

    fb = [first_back(0), first_back(1)]
    odd = side
    grad_first = jnp.concatenate(
        [jnp.where(odd == 0, fb[0], fb[1]), jnp.where(odd == 0, fb[1], fb[0])]
    ).astype(F32)

    gn_got = across_c(project_back_send(at, dq, dk, dv, small))
    send2, keep2 = heads_gradient(heads_send_kernel, "heads_send", at, normed_one, dq, dk, dv)
    send2, keep2 = across_c(send2), across_c(keep2)
    send1, keep1 = heads_gradient(heads_keep_kernel, "heads_keep", at, normed_one, dq, dk, dv)
    grad_tokens, gain_one = project_back_keep(at, dq, dk, dv, small, gn_got, row, grad_hidden, gain_attn[None])
    pieces = turn(at, (kept[1], got1, last1, kept[3], got2, last2), hid.shape[2] // 2)
    gains = jnp.stack([jnp.sum(gain_one, axis=0), jnp.sum(gain_two, axis=0)]).reshape(16, 128)
    pieces, grad_first = lax.optimization_barrier((pieces, grad_first))
    got, own_heads, got_heads, got_tokens, gains = last_exchanges(pieces, send1, keep1, send2, keep2, grad_tokens, gains)
    grad_gate, grad_up, grad_down, grad_out, gq, gk, gv, grad_tokens = finish(
        at, pieces, got, own_heads, got_heads, grad_tokens, got_tokens, w_gate.shape[1]
    )
    gains = gains.reshape(2, wide)
    return (
        layer_out,
        grad_tokens,
        grad_first,
        gq,
        gk,
        gv,
        grad_out,
        grad_gate.T,
        grad_up.T,
        grad_down,
        gains[0],
        gains[1],
    )


def solution(mesh):
    fits = dict(mesh.shape) == {"dp": 8, "tensor": 4}
    placed = (
        P(("dp", "tensor"), None),
        P("dp", "tensor"),
        P("dp", None),
        P(("dp", "tensor"), None),
        P("dp", "tensor"),
        P("dp", "tensor"),
        P("dp", "tensor"),
        P("tensor", "dp"),
        P("dp", "tensor"),
        P("dp", "tensor"),
        P("tensor", "dp"),
        P(),
        P(),
    )
    return jax.shard_map(
        fast_body if fits else general_body,
        mesh=mesh,
        in_specs=placed,
        out_specs=(
            P(("dp", "tensor"), None),
            P(("dp", "tensor"), None),
            P("dp", "tensor"),
            P("dp", "tensor"),
            P("dp", "tensor"),
            P("dp", "tensor"),
            P("tensor", "dp"),
            P("dp", "tensor"),
            P("dp", "tensor"),
            P("tensor", "dp"),
            P(),
            P(),
        ),
        check_vma=False,
    )
```

```python
import functools

import jax
import jax.numpy as jnp
from jax import lax
from jax.experimental import pallas as pl
from jax.experimental.pallas import tpu as pltpu
from jax.sharding import PartitionSpec as P

HEAD = 64
SEQ = 2048
DOCS = 8
EPSILON = 1e-05


def rms_norm(values, gain):
    factor = lax.rsqrt(jnp.mean(values * values, axis=1, keepdims=True) + EPSILON)
    return values * factor * gain


def documents(doc_lengths):
    ends = jnp.cumsum(doc_lengths, axis=1)
    starts = ends - doc_lengths
    places = jnp.arange(SEQ, dtype=jnp.int32)
    segment = jnp.sum((places[None, :, None] >= ends[:, None, :]).astype(jnp.int32), axis=2)
    member = segment[:, :, None] == jnp.arange(DOCS, dtype=jnp.int32)[None, None, :]
    offset = jnp.sum(jnp.where(member, starts[:, None, :], 0), axis=2)
    return (segment, (places[None, :] - offset).astype(jnp.float32))


def rotation(positions):
    half = HEAD // 2
    freqs = 10000.0 ** (-(jnp.arange(half, dtype=jnp.float32) * 2.0 / HEAD))
    angles = positions[:, None] * freqs[None, :]
    return (jnp.cos(angles), jnp.sin(angles))


def rotate(values, cosine, sine):
    shaped = values.reshape(values.shape[0], -1, HEAD)
    half = HEAD // 2
    first = shaped[:, :, :half]
    second = shaped[:, :, half:]
    cos_rows = cosine[:, None, :]
    sin_rows = sine[:, None, :]
    turned = jnp.concatenate(
        [first * cos_rows - second * sin_rows, second * cos_rows + first * sin_rows], axis=2
    )
    return turned.reshape(values.shape)


def rotate_back(grads, cosine, sine):
    shaped = grads.reshape(grads.shape[0], -1, HEAD)
    half = HEAD // 2
    first = shaped[:, :, :half]
    second = shaped[:, :, half:]
    cos_rows = cosine[:, None, :]
    sin_rows = sine[:, None, :]
    turned = jnp.concatenate(
        [first * cos_rows + second * sin_rows, second * cos_rows - first * sin_rows], axis=2
    )
    return turned.reshape(grads.shape)


def swiglu(gate, up_val):
    return jax.nn.silu(gate) * up_val


def product(left, right):
    return jnp.dot(left, right, preferred_element_type=jnp.float32)


def inner(left, right):
    return lax.dot_general(
        left, right, (((0,), (0,)), ((), ())), preferred_element_type=jnp.float32
    )


def outer(left, right):
    return lax.dot_general(
        left, right, (((1,), (1,)), ((), ())), preferred_element_type=jnp.float32
    )


def block_scores(queries, keys_all, segment, start, width):
    query_block = lax.dynamic_slice_in_dim(queries, start, width, 0)
    query_seg = lax.dynamic_slice_in_dim(segment, start, width, 0)
    scores = (
        jnp.einsum("qhd,khd->hqk", query_block, keys_all, preferred_element_type=jnp.float32)
        * 0.125
    )
    places = jnp.arange(SEQ, dtype=jnp.int32)
    rows_at = start + jnp.arange(width, dtype=jnp.int32)
    allowed = (query_seg[:, None] == segment[None, :]) & (places[None, :] <= rows_at[:, None])
    return (query_block, jnp.where(allowed[None], scores, -1e30))


def forward_row(pieces):
    queries, keys_all, values_all, segment = pieces
    width = min(512, SEQ)
    count = SEQ // width

    def forward_one_block(index):
        unused, scores = block_scores(queries, keys_all, segment, index * width, width)
        top = jnp.max(scores, axis=2, keepdims=True)
        expo = jnp.exp(scores - top)
        total = jnp.sum(expo, axis=2, keepdims=True)
        weights = (expo / total).astype(jnp.bfloat16)
        result = jnp.einsum("hqk,khd->qhd", weights, values_all, preferred_element_type=jnp.float32)
        return (result, (top + jnp.log(total))[:, :, 0])

    results, logsums = lax.map(forward_one_block, jnp.arange(count, dtype=jnp.int32))
    return (results.reshape(SEQ, queries.shape[1], HEAD), logsums)


def backward_row(pieces):
    queries, keys_all, values_all, segment, grad_rows, logsums = pieces
    width = min(512, SEQ)
    count = SEQ // width

    def backward_one_block(carry, extra):
        index, logsum = extra
        start = index * width
        query_block, scores = block_scores(queries, keys_all, segment, start, width)
        probs = jnp.exp(scores - logsum[:, :, None])
        grad_block = lax.dynamic_slice_in_dim(grad_rows, start, width, 0)
        grad_probs = jnp.einsum(
            "qhd,khd->hqk", grad_block, values_all, preferred_element_type=jnp.float32
        )
        delta = jnp.sum(probs * grad_probs, axis=2, keepdims=True)
        grad_scores = (probs * (grad_probs - delta)).astype(jnp.bfloat16)
        grad_query = (
            jnp.einsum("hqk,khd->qhd", grad_scores, keys_all, preferred_element_type=jnp.float32)
            * 0.125
        )
        grad_keys = (
            carry[0]
            + jnp.einsum(
                "hqk,qhd->khd", grad_scores, query_block, preferred_element_type=jnp.float32
            )
            * 0.125
        )
        grad_values = carry[1] + jnp.einsum(
            "hqk,qhd->khd",
            probs.astype(jnp.bfloat16),
            grad_block,
            preferred_element_type=jnp.float32,
        )
        return ((grad_keys, grad_values), grad_query)

    zeros = jnp.zeros(keys_all.shape, jnp.float32)
    sums, grad_queries = lax.scan(
        backward_one_block, (zeros, zeros), (jnp.arange(count, dtype=jnp.int32), logsums)
    )
    return (grad_queries.reshape(SEQ, queries.shape[1], HEAD), sums[0], sums[1])


def general_body(
    tokens,
    first_values,
    doc_lengths,
    cotangent,
    w_query,
    w_key,
    w_value,
    w_out,
    w_gate,
    w_up,
    w_down,
    gain_attn,
    gain_mlp,
):
    query_mat, key_mat, value_mat, out_mat, gate_mat, up_mat, down_mat = (
        lax.all_gather(w_query, "dp", axis=0, tiled=True),
        lax.all_gather(w_key, "dp", axis=0, tiled=True),
        lax.all_gather(w_value, "dp", axis=0, tiled=True),
        lax.all_gather(w_out, "dp", axis=1, tiled=True),
        lax.all_gather(w_gate, "dp", axis=0, tiled=True),
        lax.all_gather(w_up, "dp", axis=0, tiled=True),
        lax.all_gather(w_down, "dp", axis=1, tiled=True),
    )
    local_heads = query_mat.shape[1] // HEAD
    row_count = doc_lengths.shape[0]
    group = row_count * SEQ
    segment, positions = documents(doc_lengths)
    cosine, sine = rotation(positions.reshape(-1))

    def heads(matrix):
        return matrix.reshape(row_count, SEQ, local_heads, HEAD)

    inputs = tokens.astype(jnp.float32)
    normed_one, norm_one_back = jax.vjp(rms_norm, inputs, gain_attn)
    gathered_one = lax.all_gather(normed_one.astype(jnp.bfloat16), "tensor", axis=0, tiled=True)
    query_raw = product(gathered_one, query_mat)
    key_raw = product(gathered_one, key_mat)
    value_raw = product(gathered_one, value_mat)
    queries = rotate(query_raw, cosine, sine).astype(jnp.bfloat16)
    keys_low = rotate(key_raw, cosine, sine).astype(jnp.bfloat16)
    mixed_values = (0.5 * value_raw + 0.5 * first_values.astype(jnp.float32)).astype(jnp.bfloat16)
    attended, logsums = lax.map(
        forward_row, (heads(queries), heads(keys_low), heads(mixed_values), segment)
    )
    attended_low = attended.reshape(group, -1).astype(jnp.bfloat16)
    hidden_in = inputs + lax.psum_scatter(
        product(attended_low, out_mat), "tensor", scatter_dimension=0, tiled=True
    )
    normed_two, norm_two_back = jax.vjp(rms_norm, hidden_in, gain_mlp)
    normed_low_two = normed_two.astype(jnp.bfloat16)
    grad_out = cotangent.astype(jnp.float32)
    gathered_two = lax.all_gather(normed_low_two, "tensor", axis=0, tiled=True)
    activated, swiglu_back = jax.vjp(
        swiglu, product(gathered_two, gate_mat), product(gathered_two, up_mat)
    )
    act_low = activated.astype(jnp.bfloat16)
    layer_out = hidden_in + lax.psum_scatter(
        product(act_low, down_mat).astype(jnp.bfloat16), "tensor", scatter_dimension=0, tiled=True
    ).astype(jnp.float32)
    grad_rows = lax.all_gather(cotangent, "tensor", axis=0, tiled=True)
    grad_gate, grad_up = swiglu_back(outer(grad_rows, down_mat))
    gate_low = grad_gate.astype(jnp.bfloat16)
    up_low = grad_up.astype(jnp.bfloat16)
    grad_normed_two = lax.psum_scatter(
        outer(gate_low, gate_mat) + outer(up_low, up_mat), "tensor", scatter_dimension=0, tiled=True
    )
    grad_gate_mat = inner(gathered_two, gate_low)
    grad_up_mat = inner(gathered_two, up_low)
    grad_down_mat = inner(act_low, grad_rows)
    grad_hidden_two, grad_gain_two = norm_two_back(grad_normed_two)
    grad_hidden = grad_out + grad_hidden_two
    grad_branch = lax.all_gather(grad_hidden.astype(jnp.bfloat16), "tensor", axis=0, tiled=True)
    grad_attended = outer(grad_branch, out_mat).astype(jnp.bfloat16)
    grad_out_mat = inner(attended_low, grad_branch)
    grad_rot_query, grad_rot_key, grad_mixed = lax.map(
        backward_row,
        (
            heads(queries),
            heads(keys_low),
            heads(mixed_values),
            segment,
            heads(grad_attended),
            logsums,
        ),
    )
    grad_query_low = rotate_back(grad_rot_query.reshape(group, -1), cosine, sine).astype(
        jnp.bfloat16
    )
    grad_key_low = rotate_back(grad_rot_key.reshape(group, -1), cosine, sine).astype(jnp.bfloat16)
    grad_first = 0.5 * grad_mixed.reshape(group, -1)
    grad_value_low = grad_first.astype(jnp.bfloat16)
    grad_normed_one = lax.psum_scatter(
        outer(grad_query_low, query_mat)
        + outer(grad_key_low, key_mat)
        + outer(grad_value_low, value_mat),
        "tensor",
        scatter_dimension=0,
        tiled=True,
    )
    grad_query_mat = inner(gathered_one, grad_query_low)
    grad_key_mat = inner(gathered_one, grad_key_low)
    grad_value_mat = inner(gathered_one, grad_value_low)
    grad_inputs_one, grad_gain_one = norm_one_back(grad_normed_one)
    grad_tokens = grad_hidden + grad_inputs_one
    summed = (
        lax.psum_scatter(grad_query_mat, "dp", scatter_dimension=0, tiled=True),
        lax.psum_scatter(grad_key_mat, "dp", scatter_dimension=0, tiled=True),
        lax.psum_scatter(grad_value_mat, "dp", scatter_dimension=0, tiled=True),
        lax.psum_scatter(grad_out_mat, "dp", scatter_dimension=1, tiled=True),
        lax.psum_scatter(grad_gate_mat, "dp", scatter_dimension=0, tiled=True),
        lax.psum_scatter(grad_up_mat, "dp", scatter_dimension=0, tiled=True),
        lax.psum_scatter(grad_down_mat, "dp", scatter_dimension=1, tiled=True),
    )
    gain_sums = lax.psum((grad_gain_one, grad_gain_two), ("dp", "tensor"))
    return (
        layer_out.astype(jnp.bfloat16),
        grad_tokens,
        grad_first,
        summed[0],
        summed[1],
        summed[2],
        summed[3],
        summed[4],
        summed[5],
        summed[6],
        gain_sums[0],
        gain_sums[1],
    )


AXES = ("dp", "tensor")
MESH = pl.DeviceIdType.MESH
TILE = 256
NEG = -1e30
F32 = jnp.float32
BF16 = jnp.bfloat16


def flat(y, x, c, t):
    return ((y * 2 + x) * 2 + c) * 4 + t


def move(values, to):
    pairs = []
    for y in range(2):
        for x in range(2):
            for c in range(2):
                for t in range(4):
                    pair = (flat(y, x, c, t), flat(*to(y, x, c, t)))
                    if pair[0] != pair[1]:
                        pairs.append(pair)
    return lax.ppermute(values, AXES, pairs)


def across_x(values):
    return move(values, lambda y, x, c, t: (y, 1 - x, c, t))


def across_y(values):
    return move(values, lambda y, x, c, t: (1 - y, x, c, t))


def across_c(values):
    return move(values, lambda y, x, c, t: (y, x, 1 - c, t))


def along_t(values, step):
    return move(values, lambda y, x, c, t: (y, x, c, (t + step) % 4))


def swap_halves(values):
    return move(values, lambda y, x, c, t: (y, x, t % 2, (t // 2) * 2 + c))


def pack_kernel(wq, wk, wv, wo, wg, wu, wd, halves, small, big):
    small[0] = dot(wq[...], halves[...]).astype(BF16)
    small[1] = dot(wk[...], halves[...]).astype(BF16)
    small[2] = wv[...]
    small[3] = wo[...].T
    for n, units in enumerate((wg, wu, wd)):
        big[n] = units[...].reshape(big.shape[1:])


def pack(wq, wk, wv, wo, wg, wu, wd):
    wg, wu = wg.T, wu.T
    part, rows = wg.shape
    lane = jnp.arange(256, dtype=jnp.int32)
    source = ((lane & 127) >> 5) * 64 + (lane >> 7) * 32 + (lane & 31)
    halves = (lane[:, None] == source[None, :]).astype(BF16)
    return pl.pallas_call(
        pack_kernel,
        out_shape=[
            jax.ShapeDtypeStruct((4, rows, 256), BF16),
            jax.ShapeDtypeStruct((3, 2, part // 2, rows), BF16),
        ],
        compiler_params=params(),
        name="pack",
    )(wq, wk, wv, wo, wg, wu, wd, halves)


def meet(plane, c, t, dpx, dpy):
    barrier = pltpu.get_barrier_semaphore()
    for e in range(2):
        for d in range(4):
            if e or d:
                other = plane + lax.rem(c + e, 2)
                pl.semaphore_signal(barrier, inc=1, device_id=(other, lax.rem(t + d, 4)), device_id_type=MESH)
    pl.semaphore_signal(barrier, inc=1, device_id=(dpx, t), device_id_type=MESH)
    pl.semaphore_signal(barrier, inc=1, device_id=(dpy, t), device_id_type=MESH)
    pl.semaphore_wait(barrier, 9)


def gather_kernel(tok, fv, small, big, row, first, g_small, g_big, send, recv, relay_send, along_recv, next_send, next_recv, swap, fsend, frecv, here):
    dp, t = lax.axis_index("dp"), lax.axis_index("tensor")
    c, x, y = lax.rem(dp, 2), lax.rem(lax.div(dp, 2), 2), lax.div(dp, 4)
    pair, side = lax.div(t, 2), lax.rem(t, 2)
    plane = dp - c
    dpx, dpy, dpc = dp + 2 - 4 * x, dp + 4 - 8 * y, dp + 1 - 2 * c
    dpxy = dpx + 4 - 8 * y

    meet(plane, c, t, dpx, dpy)
    def slot(k, at, owner, h):
        if k == 0:
            return g_small.at[pl.ds(2 * h, 2), at, pl.ds(owner * 128, 128), :]
        return g_big.at[k - 1, owner, h, at]

    def column(k, owner, h):
        if k == 0:
            return g_small.at[pl.ds(2 * h, 2), :, pl.ds(owner * 128, 128), :]
        return g_big.at[k - 1, owner, h]

    def both(k, at, owner):
        if k == 0:
            return g_small.at[:, at, pl.ds(owner * 128, 128), :]
        return g_big.at[k - 1, owner, :, at]

    def all_of(k, owner):
        if k == 0:
            return g_small.at[:, :, pl.ds(owner * 128, 128), :]
        return g_big.at[k - 1, owner]

    def shard(k):
        return small if k == 0 else big.at[k - 1]

    def part_of(k, h):
        return small.at[pl.ds(2 * h, 2)] if k == 0 else big.at[k - 1, h]

    def copy(k, n, src, dst, to, at):
        return pltpu.make_async_remote_copy(
            src_ref=src,
            dst_ref=dst,
            send_sem=send.at[k, n],
            recv_sem=recv.at[k, n],
            device_id=(to, at),
            device_id_type=MESH,
        )

    chunks = 4
    near, far = (dpx, dpy), (dpy, dpx)
    kept = [pltpu.make_async_copy(shard(k), both(k, t, dp), here.at[k]) for k in range(chunks)]

    def relay(k, at, side, src):
        return pltpu.make_async_remote_copy(
            src_ref=src,
            dst_ref=both(k, at, dp),
            send_sem=relay_send.at[k, at, side],
            recv_sem=along_recv.at[k, at],
            device_id=(dp, t + 2 * side - 1),
            device_id_type=MESH,
        )

    def onward(k, at, h, src):
        return pltpu.make_async_remote_copy(
            src_ref=src,
            dst_ref=slot(k, at, dp, h),
            send_sem=next_send.at[k, at, h],
            recv_sem=next_recv.at[k, at, h],
            device_id=(near[h], t),
            device_id_type=MESH,
        )

    def start_along(k):
        @pl.when(t < 3)
        def _():
            relay(k, t, 1, shard(k)).start()

        @pl.when(t > 0)
        def _():
            relay(k, t, 0, shard(k)).start()

    def pass_along(k, level):
        for side, at in ((1, t - level), (0, t + level)):

            @pl.when((at >= 0) & (at < 4))
            def _():
                block = both(k, at, dp)
                move = relay(k, at, side, block)
                move.wait_recv()

                @pl.when((t < 3) if side else (t > 0))
                def _():
                    move.start()

                for h in range(2):
                    onward(k, at, h, slot(k, at, dp, h)).start()

    def end_along(k):
        for level in range(4):
            for side, at in ((1, t - level), (0, t + level)):

                @pl.when((at >= 0) & (at < 4) & ((t < 3) if side else (t > 0)))
                def _():
                    relay(k, at, side, both(k, at, dp)).wait_send()

    across = [
        [
            copy(k, 2 * h + i, column(k, owner, h), column(k, owner, h), far[h], t)
            for h in range(2)
            for i, owner in enumerate((dp, near[h]))
        ]
        for k in range(chunks)
    ]
    over = [
        [copy(k, 4 + i, all_of(k, owner), all_of(k, owner), dpc, t) for i, owner in enumerate((dp, dpx, dpy, dpxy))]
        for k in range(chunks)
    ]

    order = (1, 0, 2, 3)
    start_along(order[0])
    for item in kept:
        item.start()
    for k in order:
        for h in range(2):
            onward(k, t, h, part_of(k, h)).start()
        if k == order[0]:
            start_along(order[1])

    moved = side != c
    to_own = pltpu.make_async_copy(tok, row.at[c], here.at[4])
    swapped = pltpu.make_async_remote_copy(
        src_ref=tok,
        dst_ref=row.at[side],
        send_sem=swap.at[0],
        recv_sem=swap.at[1],
        device_id=(plane + side, 2 * pair + c),
        device_id_type=MESH,
    )

    def start_tokens():
        @pl.when(moved)
        def _():
            swapped.start()

        @pl.when(jnp.logical_not(moved))
        def _():
            to_own.start()

    heads_core, slab = pair, side

    def first_copy(p):
        return pltpu.make_async_remote_copy(
            src_ref=fv.at[pl.ds(p * SEQ, SEQ), :],
            dst_ref=first.at[slab],
            send_sem=fsend.at[p],
            recv_sem=frecv.at[slab],
            device_id=(plane + heads_core, 2 * p + c),
            device_id_type=MESH,
        )

    def first_local(p):
        return pltpu.make_async_copy(fv.at[pl.ds(p * SEQ, SEQ), :], first.at[slab], here.at[5])

    stays = [(heads_core == c) & (t == 2 * p + c) for p in range(2)]

    def start_first():
        for p in range(2):

            @pl.when(stays[p])
            def _():
                first_local(p).start()

            @pl.when(jnp.logical_not(stays[p]))
            def _():
                first_copy(p).start()

    def pass_over(k):
        for item in across[k]:
            item.wait_recv()
        for item in over[k][1:]:
            item.start()

    def pass_next(k):
        for at in range(4):
            for h in range(2):
                onward(k, at, h, slot(k, at, dp, h)).wait_recv()
        for item in across[k]:
            item.start()

    for i, k in enumerate(order):
        pass_along(k, 1)
        if i + 2 < chunks:
            start_along(order[i + 2])
        if i:
            pass_next(order[i - 1])
        pass_along(k, 2)
        pass_along(k, 3)
        kept[k].wait()
        over[k][0].start()
        if i == 2:
            start_tokens()
        if i == 3:
            start_first()
        if i >= 2:
            pass_over(order[i - 2])
    pass_next(order[3])
    for k in order[2:]:
        pass_over(k)

    @pl.when(moved)
    def _():
        swapped.wait_send()
        swapped.wait_recv()

    @pl.when(jnp.logical_not(moved))
    def _():
        to_own.wait()

    given = pltpu.make_async_remote_copy(
        src_ref=row.at[c],
        dst_ref=row.at[c],
        send_sem=swap.at[2],
        recv_sem=swap.at[3],
        device_id=(dpc, t),
        device_id_type=MESH,
    )
    given.start()
    for p in range(2):

        @pl.when(stays[p])
        def _():
            first_local(p).wait()

        @pl.when(jnp.logical_not(stays[p]))
        def _():
            first_copy(p).wait_send()

    for u in range(2):
        came = pltpu.make_async_remote_copy(
            src_ref=first.at[u],
            dst_ref=first.at[u],
            send_sem=fsend.at[u],
            recv_sem=frecv.at[u],
            device_id=(dpc, t),
            device_id_type=MESH,
        )

        @pl.when((side != c) | (t != 2 * c + u))
        def _():
            came.wait_recv()

    given.wait()
    for k in range(chunks):
        for item in over[k]:
            item.wait_recv()
        end_along(k)
        for item in across[k] + over[k]:
            item.wait_send()
        for at in range(4):
            for h in range(2):
                onward(k, at, h, slot(k, at, dp, h)).wait_send()


def gather(tok, fv, small, big):
    part, rows = big.shape[2:]
    wide = tok.shape[1]
    vmem = pl.BlockSpec(memory_space=pltpu.VMEM)
    sems = pltpu.SemaphoreType.DMA
    return pl.pallas_call(
        gather_kernel,
        out_shape=[
            jax.ShapeDtypeStruct((2, SEQ // 2, wide), BF16),
            jax.ShapeDtypeStruct((2, SEQ, 256), BF16),
            jax.ShapeDtypeStruct((4, 4, wide, 256), BF16),
            jax.ShapeDtypeStruct((3, 8, 2, 4, part, rows), BF16),
        ],
        in_specs=[vmem] * 4,
        out_specs=[any_spec()] * 4,
        scratch_shapes=[
            sems((4, 8)),
            sems((4, 8)),
            sems((4, 4, 2)),
            sems((4, 4)),
            sems((4, 4, 2)),
            sems((4, 4, 2)),
            sems((4,)), sems((2,)), sems((2,)), sems((6,))],
        compiler_params=params(collective_id=0, has_side_effects=True),
        name="gather",
    )(tok, fv, small, big)


def dot(left, right):
    return jnp.dot(left, right, preferred_element_type=F32)


def dot_nt(left, right):
    return lax.dot_general(left, right, (((1,), (1,)), ((), ())), preferred_element_type=F32)


def dot_tn(left, right):
    return lax.dot_general(left, right, (((0,), (0,)), ((), ())), preferred_element_type=F32)


def any_spec():
    return pl.BlockSpec(memory_space=pl.ANY)


def params(**more):
    return pltpu.CompilerParams(vmem_limit_bytes=62 * 1024 * 1024, **more)


def cost(flops, size, exps=0):
    return pl.CostEstimate(flops=int(flops), bytes_accessed=int(size), transcendentals=int(exps))


def project_kernel(at, tok, first, cosine, sine, gain, held, normed_out, q_out, k_out, v_out):
    values = tok[0].astype(F32)
    factor = lax.rsqrt(jnp.mean(values * values, axis=1, keepdims=True) + EPSILON)
    normed = (values * factor * gain[...]).astype(BF16)
    normed_out[...] = normed
    cos, sin = cosine[...], sine[...]
    for u in range(2):
        for n, out, scale in ((0, q_out, 0.125), (1, k_out, 1.0)):
            raw = dot(normed, held[n, u])
            a, b = raw[:, :128], raw[:, 128:]
            out[:, u * 256 : u * 256 + 128] = ((a * cos - b * sin) * scale).astype(BF16)
            out[:, u * 256 + 128 : u * 256 + 256] = ((b * cos + a * sin) * scale).astype(BF16)
        raw = dot(normed, held[2, u])
        v_out[:, u * 256 : u * 256 + 256] = (0.5 * raw + 0.5 * first[u].astype(F32)).astype(BF16)


def once(shape, place):
    return pl.BlockSpec(shape, place, pipeline_mode=pl.Buffered(1))


def project(at, tok, first, cosine, sine, gain, small):
    rows, wide = 512, tok.shape[2]
    row = lambda width: pl.BlockSpec((rows, width), lambda i, at: (i, 0))
    grid = pltpu.PrefetchScalarGridSpec(
        num_scalar_prefetch=1,
        grid=(4,),
        in_specs=[
            pl.BlockSpec((1, rows, wide), lambda i, at: (i // 2, i % 2, 0)),
            pl.BlockSpec((2, rows, 256), lambda i, at: (0, i, 0)),
            row(128),
            row(128),
            pl.BlockSpec((1, wide), lambda i, at: (0, 0)),
            once((4, 2, wide, 256), lambda i, at: (0, at[0] & 1, 0, 0)),
        ],
        out_specs=[row(wide), row(512), row(512), row(512)],
    )
    return pl.pallas_call(
        project_kernel,
        out_shape=[jax.ShapeDtypeStruct((SEQ, wide), BF16)]
        + [jax.ShapeDtypeStruct((SEQ, 512), BF16)] * 3,
        grid_spec=grid,
        compiler_params=params(),
        cost_estimate=cost(2 * SEQ * wide * 1536, 24e6),
        name="project",
    )(at, tok, first, cosine, sine, gain, small)


def head_masks(rows):
    lane = lax.broadcasted_iota(jnp.int32, (rows, 256), 1)
    return (lane & 127) >> 5, lane >> 6


def attend_kernel(bounds, q_ref, k_ref, v_ref, starts, o_ref, lse_ref, kept, turned, acc):
    tiles = SEQ // TILE
    of_qk, _ = head_masks(TILE)
    row = lax.broadcasted_iota(jnp.int32, (TILE, TILE), 0)
    lane = lax.broadcasted_iota(jnp.int32, (TILE, TILE), 1)
    slabs = [slice(0, 256), slice(256, 512)]

    def turn_values(j, carry):
        there = pl.ds(pl.multiple_of(j * TILE, TILE), TILE)
        turned[j] = v_ref[there, :].T
        return carry

    lax.fori_loop(0, tiles, turn_values, 0)

    def eighths(values, reduce):
        return reduce(values.reshape(TILE // 8, 8, 4 * TILE), axis=0)

    def query_tile(i, carry):
        here = pl.ds(pl.multiple_of(i * TILE, TILE), TILE)
        q4 = []
        for slab in slabs:
            q = q_ref[here, slab]
            zero = jnp.zeros_like(q)
            q4.append(jnp.concatenate([jnp.where(of_qk == h, q, zero) for h in range(4)], axis=0))
        low = bounds[i]
        begin = starts[pl.ds(i, 1), :]
        limit = lane + i * TILE

        def score(j, tops):
            there = pl.ds(pl.multiple_of(j * TILE, TILE), TILE)
            at_row = row + j * TILE
            ok = (at_row >= begin) & (at_row <= limit)
            ok = jnp.concatenate([ok] * 4, axis=1)
            new = []
            for u, slab in enumerate(slabs):
                s = jnp.where(ok, dot_nt(k_ref[there, slab], q4[u]), NEG)
                kept[j - low, u] = s
                new.append(jnp.maximum(tops[u], eighths(s, jnp.max)))
            return tuple(new)

        start = jnp.full((8, 4 * TILE), NEG, F32)
        tops = lax.fori_loop(low, i + 1, score, (start, start))
        tops = [jnp.max(top, axis=0, keepdims=True) for top in tops]
        acc[...] = jnp.zeros_like(acc)

        def weigh(j, totals):
            new = []
            for u in range(2):
                e = jnp.exp(kept[j - low, u] - tops[u])
                p = e.astype(BF16)
                for h in range(4):
                    part = slice(u * 256 + h * 64, u * 256 + h * 64 + 64)
                    acc[part] += dot(turned[j, part, :], p[:, h * TILE : (h + 1) * TILE])
                new.append(totals[u] + eighths(e, jnp.sum))
            return tuple(new)

        zero = jnp.zeros((8, 4 * TILE), F32)
        totals = lax.fori_loop(low, i + 1, weigh, (zero, zero))
        for u, slab in enumerate(slabs):
            total = jnp.sum(totals[u], axis=0, keepdims=True)
            inverse = 1.0 / total
            scaled = [
                acc[u * 256 + h * 64 : u * 256 + h * 64 + 64] * inverse[:, h * TILE : (h + 1) * TILE] for h in range(4)
            ]
            o_ref[here, slab] = jnp.concatenate(scaled, axis=0).T.astype(BF16)
            lse_ref[u, pl.ds(i, 1), :] = tops[u] + jnp.log(total)
        return carry

    lax.fori_loop(0, tiles, query_tile, 0)


def attend(bounds, q, k, v, starts):
    tiles = SEQ // TILE
    vmem = pl.BlockSpec(memory_space=pltpu.VMEM)
    return pl.pallas_call(
        attend_kernel,
        out_shape=[
            jax.ShapeDtypeStruct((SEQ, 512), BF16),
            jax.ShapeDtypeStruct((2, tiles, 4 * TILE), F32),
        ],
        in_specs=[pl.BlockSpec(memory_space=pltpu.SMEM)] + [vmem] * 4,
        out_specs=[vmem] * 2,
        scratch_shapes=[
            pltpu.VMEM((tiles, 2, TILE, 4 * TILE), F32),
            pltpu.VMEM((tiles, 512, TILE), BF16),
            pltpu.VMEM((512, TILE), F32),
        ],
        compiler_params=params(),
        cost_estimate=cost(20e9, 12e6, 1e7),
        name="attend",
    )(bounds, q, k, v, starts)


def attend_back_kernel(
    bounds, q_ref, k_ref, v_ref, do_ref, o_ref, lse_ref, starts, cosine, sine, dq_ref, dk_ref, dv_ref, dq_acc, delta, dk_acc, dv_acc
):
    tiles = SEQ // TILE
    of_qk, of_v = head_masks(TILE)
    row = lax.broadcasted_iota(jnp.int32, (TILE, TILE), 0)
    lane = lax.broadcasted_iota(jnp.int32, (TILE, TILE), 1)
    slabs = [slice(0, 256), slice(256, 512)]
    pick = (lax.broadcasted_iota(jnp.int32, (8, 256), 1) >> 6) == lax.broadcasted_iota(
        jnp.int32, (8, 256), 0
    )
    pick = pick.astype(F32)
    dq_acc[...] = jnp.zeros_like(dq_acc)

    def prepare(i, carry):
        here = pl.ds(pl.multiple_of(i * TILE, TILE), TILE)
        for u, slab in enumerate(slabs):
            both = do_ref[here, slab].astype(F32) * o_ref[here, slab].astype(F32)
            sums = lax.dot_general(
                pick, both, (((1,), (1,)), ((), ())), precision=lax.Precision.HIGHEST, preferred_element_type=F32
            )
            for h in range(4):
                delta[u, pl.ds(i, 1), h * TILE : (h + 1) * TILE] = sums[h : h + 1]
        return carry

    lax.fori_loop(0, tiles, prepare, 0)

    def rotate_out(values, here, out, low, scale):
        a, b = values[:, :128], values[:, 128:]
        cos, sin = cosine[here, :], sine[here, :]
        out[here, low : low + 128] = ((a * cos + b * sin) * scale).astype(BF16)
        out[here, low + 128 : low + 256] = ((b * cos - a * sin) * scale).astype(BF16)

    def split(values, of):
        zero = jnp.zeros_like(values)
        return jnp.concatenate([jnp.where(of == h, values, zero) for h in range(4)], axis=0)

    def key_tile(j, carry):
        there = pl.ds(pl.multiple_of(j * TILE, TILE), TILE)
        at_row = row + j * TILE
        dk_acc[...] = jnp.zeros_like(dk_acc)
        dv_acc[...] = jnp.zeros_like(dv_acc)

        def query_tile(i, carry):
            here = pl.ds(pl.multiple_of(i * TILE, TILE), TILE)
            at_lane = lane + i * TILE
            ok = (at_row >= starts[pl.ds(i, 1), :]) & (at_row <= at_lane)
            ok = jnp.concatenate([ok] * 4, axis=1)
            for u, slab in enumerate(slabs):
                q4 = split(q_ref[here, slab], of_qk)
                do4 = split(do_ref[here, slab], of_v)
                s = dot_nt(k_ref[there, slab], q4)
                dp = dot_nt(v_ref[there, slab], do4)
                p = jnp.exp(jnp.where(ok, s - lse_ref[u, pl.ds(i, 1), :], NEG))
                ds = (p * (dp - delta[u, pl.ds(i, 1), :])).astype(BF16)
                dv_acc[u] += dot(p.astype(BF16), do4)
                dk_acc[u] += dot(ds, q4)
                ds4 = jnp.concatenate([ds[:, h * TILE : (h + 1) * TILE] for h in range(4)], axis=0)
                dq_acc[i, u] += dot_tn(ds4, split(k_ref[there, slab], of_qk))
            return carry

        lax.fori_loop(j, bounds[tiles + j] + 1, query_tile, 0)
        for u, slab in enumerate(slabs):
            rotate_out(dk_acc[u], there, dk_ref, u * 256, 1.0)
            dv_ref[there, slab] = (0.5 * dv_acc[u]).astype(BF16)
        return carry

    lax.fori_loop(0, tiles, key_tile, 0)

    def finish_tile(i, carry):
        here = pl.ds(pl.multiple_of(i * TILE, TILE), TILE)
        for u in range(2):
            rotate_out(dq_acc[i, u], here, dq_ref, u * 256, 0.125)
        return carry

    lax.fori_loop(0, tiles, finish_tile, 0)


def attend_back(bounds, q, k, v, do, o, lse, starts, cosine, sine):
    tiles = SEQ // TILE
    vmem = pl.BlockSpec(memory_space=pltpu.VMEM)
    return pl.pallas_call(
        attend_back_kernel,
        out_shape=[jax.ShapeDtypeStruct((SEQ, 512), BF16)] * 3,
        in_specs=[pl.BlockSpec(memory_space=pltpu.SMEM)] + [vmem] * 9,
        out_specs=[vmem] * 3,
        scratch_shapes=[
            pltpu.VMEM((tiles, 2, TILE, 256), F32),
            pltpu.VMEM((2, tiles, 4 * TILE), F32),
            pltpu.VMEM((2, TILE, 256), F32),
            pltpu.VMEM((2, TILE, 256), F32),
        ],
        compiler_params=params(),
        cost_estimate=cost(50e9, 20e6, 1e7),
        name="attend_back",
    )(bounds, q, k, v, do, o, lse, starts, cosine, sine)


def mlp_kernel(at, att_own, att_other, tok, cot_here, cot_moved, gain, wo, big, *rest):
    (out, gh_out, gb_out, n2_out, hid_out, ga_own, ga_other, gg_out, cot_out) = rest[:9]
    (wg, wu, wd, sems) = rest[9:]
    step = pl.program_id(0)
    c = at[0] & 1

    @pl.when(step == 0)
    def _():
        for n, held in enumerate((wg, wu, wd)):
            for owner in range(8):
                pltpu.make_async_copy(
                    big.at[n, owner], held.at[:, owner * 128 : owner * 128 + 128], sems.at[n]
                ).start()
        gg_out[...] = jnp.zeros_like(gg_out)

    hidden = tok[0].astype(F32)
    for e, att in enumerate((att_own, att_other)):
        for u in range(2):
            hidden += dot_nt(att[:, u * 256 : u * 256 + 256], wo[0, 2 * (c ^ e) + u])
    factor = lax.rsqrt(jnp.mean(hidden * hidden, axis=1, keepdims=True) + EPSILON)
    gains = gain[...]
    normed = (hidden * factor * gains).astype(BF16)
    n2_out[...] = normed
    g = jnp.where((at[1] & 1) == c, cot_here[...], cot_moved[...])
    cot_out[...] = g

    @pl.when(step == 0)
    def _():
        for n, held in enumerate((wg, wu, wd)):
            pltpu.make_async_copy(held, held, sems.at[n]).wait()

    down = jnp.zeros_like(hidden)
    back = jnp.zeros_like(hidden)
    units = wg.shape[0]
    for low in range(0, units, 768):
        part = slice(low, min(low + 768, units))
        gate, up, grad_act = dot_nt(normed, wg[part]), dot_nt(normed, wu[part]), dot_nt(g, wd[part])
        sig = 1.0 / (1.0 + jnp.exp(-gate))
        silu = gate * sig
        act = (silu * up).astype(BF16)
        grad_up = (grad_act * silu).astype(BF16)
        grad_gate = (grad_act * up * (sig * (1.0 + gate * (1.0 - sig)))).astype(BF16)
        hid_out[0, :, part], hid_out[1, :, part], hid_out[2, :, part] = grad_gate, grad_up, act
        down += dot(act, wd[part])
        back += dot(grad_gate, wg[part]) + dot(grad_up, wu[part])
    out[...] = (hidden + down).astype(BF16)
    gg_out[...] += jnp.sum((back * hidden * factor).reshape(-1, 8, back.shape[1]), axis=0)
    scaled = back * gains
    mean = jnp.mean(scaled * hidden, axis=1, keepdims=True)
    grad_hidden = g.astype(F32) + factor * scaled - hidden * (factor * factor * factor * mean)
    gh_out[...] = grad_hidden
    branch = grad_hidden.astype(BF16)
    gb_out[...] = branch
    for e, ga in enumerate((ga_own, ga_other)):
        for u in range(2):
            ga[:, u * 256 : u * 256 + 256] = dot(branch, wo[0, 2 * (c ^ e) + u]).astype(BF16)


def mlp(at, att_own, att_other, tok, cot_here, cot_moved, gain, small, big):
    _, count, wide = tok.shape
    big = big.reshape(3, 8, -1, 128)
    rows, units = 256, big.shape[2]
    row = lambda width: pl.BlockSpec((rows, width), lambda i, at: (i, 0))
    grid = pltpu.PrefetchScalarGridSpec(
        num_scalar_prefetch=1,
        grid=(count // rows,),
        in_specs=[
            row(512),
            row(512),
            pl.BlockSpec((1, rows, wide), lambda i, at: (at[0] & 1, i, 0)),
            row(wide),
            row(wide),
            pl.BlockSpec((1, wide), lambda i, at: (0, 0)),
            once((1, 4, wide, 256), lambda i, at: (3, 0, 0, 0)),
            any_spec(),
        ],
        out_specs=[
            row(wide),
            row(wide),
            row(wide),
            row(wide),
            pl.BlockSpec((3, rows, units), lambda i, at: (0, i, 0)),
            row(512),
            row(512),
            pl.BlockSpec((8, wide), lambda i, at: (0, 0)),
            row(wide),
        ],
        scratch_shapes=[pltpu.VMEM((units, wide), BF16)] * 3 + [pltpu.SemaphoreType.DMA((3,))],
    )
    tokens = lambda width, kind=BF16: jax.ShapeDtypeStruct((count, width), kind)
    return pl.pallas_call(
        mlp_kernel,
        out_shape=[
            tokens(wide),
            tokens(wide, F32),
            tokens(wide),
            tokens(wide),
            jax.ShapeDtypeStruct((3, count, units), BF16),
            tokens(512),
            tokens(512),
            jax.ShapeDtypeStruct((8, wide), F32),
            tokens(wide),
        ],
        grid_spec=grid,
        compiler_params=params(),
        cost_estimate=cost(2 * count * wide * (6 * units + 2 * wide), 60e6, 3e6),
        name="mlp",
    )(at, att_own, att_other, tok, cot_here, cot_moved, gain, small, big)


def turn_rows(source, plane, parity, held):
    for rel in range(4):
        block = ((plane ^ rel) * 2 + parity) * 128
        held[rel * 128 : rel * 128 + 128, :] = source[:, pl.ds(pl.multiple_of(block, 128), 128)].T


def place_first(send, keep, done, lanes):
    for yr in range(2):
        keep[yr, :, lanes] = done[2 * yr]
        send[yr, :, lanes] = done[2 * yr + 1]


def place_second(send, keep, done, lanes):
    for xr in range(2):
        keep[xr, :, lanes] = done[xr]
        send[xr, :, lanes] = done[2 + xr]


def weights_kernel(n2, g, branch, hid, own, other, send1, keep1, send2, keep2, turned, given, got, out_sem, in_sem):
    step = pl.program_id(0)
    dp, t = lax.axis_index("dp"), lax.axis_index("tensor")
    c = lax.rem(dp, 2)
    plane = lax.div(dp, 2)
    n = lax.rem(step, 4)
    units = hid.shape[2] // 2

    @pl.when(step == 0)
    def _():
        barrier = pltpu.get_barrier_semaphore()
        pl.semaphore_signal(barrier, inc=1, device_id=(dp + 1 - 2 * c, t), device_id_type=MESH)
        pl.semaphore_wait(barrier, 1)

    def exchange(k):
        lanes = pl.ds(k * units, units if k < 3 else 512)
        return pltpu.make_async_remote_copy(
            src_ref=given.at[:, :, :, lanes],
            dst_ref=got.at[:, :, :, lanes],
            send_sem=out_sem.at[k],
            recv_sem=in_sem.at[k],
            device_id=(dp + 1 - 2 * c, t),
            device_id_type=MESH,
        )

    for phase, parity in ((0, 1 - c), (1, c)):
        for at_n, source in ((0, n2), (2, g), (3, branch)):

            @pl.when(step == 4 * phase + at_n)
            def _():
                x = lax.rem(plane, 2)
                y = lax.div(plane, 2)
                for rel in range(4):
                    yy, xx = (y, 1 - y)[rel // 2], (x, 1 - x)[rel % 2]
                    block = pl.multiple_of((yy * 4 + xx * 2 + parity) * 128, 128)
                    turned[rel * 128 : rel * 128 + 128, :] = source[:, pl.ds(block, 128)].T

    def heads(h):
        return jnp.where(c == h, own[...], other[...])

    @pl.when(step < 3)
    def _():
        for h in range(2):
            product = dot(turned[...], hid[0, :, h * units : h * units + units]).astype(BF16)
            given[:, h, :, pl.ds(pl.multiple_of(n * units, 128), units)] = product.reshape(4, 128, units)

    @pl.when(step == 3)
    def _():
        for h in range(2):
            product = dot(turned[...], heads(h)).astype(BF16)
            given[:, h, :, 3 * units : 3 * units + 512] = product.reshape(4, 128, 512)

    for k in range(4):

        @pl.when(step == k + 1)
        def _():
            exchange(k).start()

        @pl.when(step == k + 4)
        def _():
            exchange(k).wait_recv()

    def keep(product, h, lanes):
        done = [(product[r * 128 : r * 128 + 128] + got[r, h, :, lanes].astype(F32)).astype(BF16) for r in range(4)]
        (place_first, place_second)[h](*((send1, keep1), (send2, keep2))[h], done, lanes)

    @pl.when((step >= 4) & (step < 7))
    def _():
        for h in range(2):
            product = dot(turned[...], hid[0, :, h * units : h * units + units])
            keep(product, h, pl.ds(pl.multiple_of(n * units, 128), units))

    @pl.when(step == 7)
    def _():
        for h in range(2):
            keep(dot(turned[...], heads(h)), h, pl.ds(3 * units, 512))
        for k in range(4):
            exchange(k).wait_send()


def weights(n2, g, branch, hid, own, other):
    count, wide = n2.shape
    units = hid.shape[2] // 2
    full = lambda *shape: pl.BlockSpec(shape, lambda s: (0,) * len(shape), pipeline_mode=pl.Buffered(1))
    length = 3 * units + 512
    grid = pl.GridSpec(
        grid=(8,),
        in_specs=[
            full(count, wide),
            full(count, wide),
            full(count, wide),
            pl.BlockSpec((1, count, 2 * units), lambda s: (jnp.minimum(lax.rem(s, 4), 2), 0, 0)),
            full(count, 512),
            full(count, 512),
        ],
        out_specs=[full(2, 128, length)] * 4,
        scratch_shapes=[
            pltpu.VMEM((512, count), BF16),
            pltpu.VMEM((4, 2, 128, length), BF16),
            pltpu.VMEM((4, 2, 128, length), BF16),
            pltpu.SemaphoreType.DMA((4,)),
            pltpu.SemaphoreType.DMA((4,)),
        ],
    )
    return pl.pallas_call(
        weights_kernel,
        out_shape=[jax.ShapeDtypeStruct((2, 128, length), BF16)] * 4,
        grid_spec=grid,
        compiler_params=params(collective_id=1, has_side_effects=True),
        cost_estimate=cost(2 * count * 1024 * length * 2, 50e6),
        name="weights",
    )(n2, g, branch, hid, own, other)


def add(left, right):
    return (left.astype(F32) + right.astype(F32)).astype(BF16)


def finish_kernel(at, own, got, own_heads, got_heads, tok, got_tok, first, gate, up, down, out, query, key, value, tok_out, first_out):
    @pl.when(pl.program_id(0) == 0)
    def _():
        part = down.shape[0]
        for n, ref in enumerate((gate, up, down, out)):
            rows = slice(n * part, n * part + ref.shape[0])
            total = own[rows, :].astype(F32)
            for d in range(3):
                total += got[d, rows, :].astype(F32)
            ref[...] = total
        heads = own_heads[...].astype(F32)
        for d in range(3):
            heads += got_heads[d].astype(F32)
        for n, ref in enumerate((query, key)):
            parts = []
            for h in range(4):
                parts += [heads[n, :, h * 32 : h * 32 + 32], heads[n, :, 128 + h * 32 : 160 + h * 32]]
            ref[...] = jnp.concatenate(parts, axis=1)
        value[...] = heads[2]

    stays = (at[0] & 1) == (at[1] & 1)
    tok_out[...] = jnp.where(stays, tok[...], got_tok[...]).astype(F32)
    first_out[...] = first[...].astype(F32)


def finish(at, pieces, got, own_heads, got_heads, tok, got_tok, first, part):
    count, wide = tok.shape
    rows = 256
    row = pl.BlockSpec((rows, wide), lambda i, at: (i, 0))
    wider = pl.BlockSpec((first.shape[0] * rows // count, first.shape[1]), lambda i, at: (i, 0))
    whole = lambda *shape: pl.BlockSpec(shape, lambda i, at: (0,) * len(shape))
    shapes = [(part, 128)] * 3 + [(256, 128)] + [(128, 256)] * 3
    grid = pltpu.PrefetchScalarGridSpec(
        num_scalar_prefetch=1,
        grid=(count // rows,),
        in_specs=[
            whole(*pieces.shape),
            whole(*got.shape),
            whole(*own_heads.shape),
            whole(*got_heads.shape),
            row,
            row,
            wider,
        ],
        out_specs=[whole(*shape) for shape in shapes] + [row, wider],
    )
    return pl.pallas_call(
        finish_kernel,
        out_shape=[jax.ShapeDtypeStruct(shape, F32) for shape in shapes + [(count, wide), first.shape]],
        grid_spec=grid,
        compiler_params=params(),
        cost_estimate=cost(1e6, 18e6),
        name="finish",
    )(at, pieces, got, own_heads, got_heads, tok, got_tok, first)


def tail_kernel(
    dq, dk, dv, small, normed, row, grad_hidden, keep1, got1, keep2, got2, gain, gain_two,
    first, own_pieces, got_pieces, own_heads, got_heads, tok, got_tok, sums,
    q_s, k_s, v_s, w_s, n_s, x_s, gh_s, ks1, gs1, ks2, gs2, last1, last2, pieces, gn_send, gn_got, turned,
    h_send, h_got, s1, k1, a1, a2, part1, part2, rest1, rest2, heads, held, came,
    load, f_sem, m_sem, p_sem, n_sem, c_sem, one_sem, two_sem, h_sem, swap, g_sem,
):
    dp, t = lax.axis_index("dp"), lax.axis_index("tensor")
    c, x, y = lax.rem(dp, 2), lax.rem(lax.div(dp, 2), 2), lax.div(dp, 4)
    pair, side = lax.div(t, 2), lax.rem(t, 2)
    plane = dp - c
    dpx, dpy, dpc = dp + 2 - 4 * x, dp + 4 - 8 * y, dp + 1 - 2 * c
    half = SEQ // 2
    units = (ks1.shape[2] - 512) // 3

    def copy(src, dst, sems, n, to):
        return pltpu.make_async_remote_copy(
            src_ref=src,
            dst_ref=dst,
            send_sem=sems.at[0, n],
            recv_sem=sems.at[1, n],
            device_id=to,
            device_id_type=MESH,
        )

    sources = [(keep1, ks1), (got1, gs1), (keep2, ks2), (got2, gs2), (dq, q_s), (dk, k_s), (dv, v_s)]
    sources += [(small.at[pl.ds(0, 3), pl.ds(2 * c, 2)], w_s), (normed, n_s), (row.at[c], x_s), (grad_hidden, gh_s)]
    loads = [pltpu.make_async_copy(src, dst, load.at[n]) for n, (src, dst) in enumerate(sources)]
    for item in loads:
        item.start()
    meet(plane, c, t, dpx, dpy)

    def value_copy(u):
        src = dv.at[:, pl.ds(u * 256, 256)]
        return pltpu.make_async_remote_copy(
            src_ref=src,
            dst_ref=first.at[pair],
            send_sem=f_sem.at[0, u],
            recv_sem=f_sem.at[1, pair],
            device_id=(plane + side, 2 * c + u),
            device_id_type=MESH,
        )

    def value_local(u):
        return pltpu.make_async_copy(dv.at[:, pl.ds(u * 256, 256)], first.at[pair], load.at[11])

    for u in range(2):
        stay = (side == c) & (t == 2 * c + u)

        @pl.when(stay)
        def _():
            value_local(u).start()

        @pl.when(jnp.logical_not(stay))
        def _():
            value_copy(u).start()

    for item in loads[:4]:
        item.wait()
    gs1[1] = add(ks1[1], gs1[1])
    gs2[1] = add(ks2[1], gs2[1])
    seconds = [copy(gs1.at[1], last1, m_sem, 0, (dpy, t)), copy(gs2.at[1], last2, m_sem, 1, (dpx, t))]
    for item in loads[4:8]:
        item.wait()
    for item in seconds:
        item.start()

    def back_product(rows):
        total = None
        for u in range(2):
            for n, grad in enumerate((q_s, k_s, v_s)):
                term = dot_nt(grad[rows, u * 256 : u * 256 + 256], w_s[n, u])
                total = term if total is None else total + term
        return total

    ns = []
    for i in range(2):
        rows = pl.ds(pl.multiple_of((1 - c) * half + i * 512, 512), 512)
        gn_send[i] = back_product(rows).astype(BF16)
        ns.append(copy(gn_send.at[i], gn_got.at[i], n_sem, i, (dpc, t)))

    def turn(parity):
        for rel in range(4):
            yy, xx = (y, 1 - y)[rel // 2], (x, 1 - x)[rel % 2]
            block = pl.multiple_of((yy * 4 + xx * 2 + parity) * 128, 128)
            turned[rel * 128 : rel * 128 + 128, :] = n_s[:, pl.ds(block, 128)].T

    loads[8].wait()
    turn(1 - c)
    for item in ns:
        item.start()
    cs = []
    for n, right in enumerate((q_s, k_s, v_s)):
        product = dot(turned[...], right[...]).astype(BF16)
        lanes = slice(n * 512, n * 512 + 512)
        place_second(h_send.at[0], h_send.at[1], [product[r * 128 : r * 128 + 128] for r in range(4)], lanes)
        cs.append(copy(h_send.at[:, :, :, pl.ds(n * 512, 512)], h_got.at[:, :, :, pl.ds(n * 512, 512)], c_sem, n, (dpc, t)))
        if n:
            cs[n - 1].start()
    turn(c)
    cs[2].start()
    for n, right in enumerate((q_s, k_s, v_s)):
        product = dot(turned[...], right[...]).astype(BF16)
        lanes = slice(n * 512, n * 512 + 512)
        place_first(s1, k1, [product[r * 128 : r * 128 + 128] for r in range(4)], lanes)
    for item in cs:
        item.wait_recv()
    ones = [copy(h_got.at[0], a2, one_sem, 1, (dpy, t)), copy(s1, a1, one_sem, 0, (dpx, t))]
    for item in ones:
        item.start()

    for item in seconds:
        item.wait_recv()
    part = units // 4
    for h, (kept, got, last) in enumerate(((ks1, gs1, last1), (ks2, gs2, last2))):
        for n in range(4):
            lanes = slice(n * units, n * units + (units if n < 3 else 512))
            total = kept[0, :, lanes].astype(F32) + got[0, :, lanes].astype(F32) + last[:, lanes].astype(F32)
            flipped = total.T.astype(BF16)
            if n < 3:
                for i in range(4):
                    rows = slice((2 * n + h) * part, (2 * n + h + 1) * part)
                    pieces[lax.rem(i + 4 - t, 4), rows, :] = flipped[i * part : (i + 1) * part]
            else:
                for i in range(2):
                    pieces[lax.rem(2 * h + i + 4 - t, 4), 6 * part :, :] = flipped[i * 256 : i * 256 + 256]
    own_pieces[...] = pieces[0]
    zs = [copy(pieces.at[d], got_pieces.at[d - 1], p_sem, d - 1, (dp, lax.rem(t + d, 4))) for d in (1, 2, 3)]
    for item in zs:
        item.start()

    for item in loads[9:11]:
        item.wait()
    moved = side != c
    gained = jnp.zeros((8, tok.shape[2]), F32)
    for i in range(2):
        ns[i].wait_recv()
        rows = pl.ds(pl.multiple_of(c * half + i * 512, 512), 512)
        here = slice(i * 512, i * 512 + 512)
        grad = back_product(rows) + gn_got[i].astype(F32)
        values = x_s[here, :].astype(F32)
        factor = lax.rsqrt(jnp.mean(values * values, axis=1, keepdims=True) + EPSILON)
        gained += jnp.sum((grad * values * factor).reshape(-1, 8, grad.shape[1]), axis=0)
        scaled = grad * gain[...]
        mean = jnp.mean(scaled * values, axis=1, keepdims=True)
        tok[i] = (gh_s[here, :] + factor * scaled - values * (factor * factor * factor * mean)).astype(BF16)
    swaps = [copy(tok.at[i], got_tok.at[i], swap, i, (plane + side, 2 * pair + c)) for i in range(2)]

    for item in ones:
        item.wait_recv()
    part1[...] = add(k1[1], a1[1])
    part2[...] = add(h_got[1, 1], a2[1])

    @pl.when(moved)
    def _():
        for item in swaps:
            item.start()

    twos = [copy(part1, rest1, two_sem, 0, (dpy, t)), copy(part2, rest2, two_sem, 1, (dpx, t))]
    for item in twos:
        item.start()

    turns = (dpc, t), (dpx, t), (dpy, t), (dp, t + 1 - 2 * side), (dp, lax.rem(t + 2, 4))
    line = lax.broadcasted_iota(jnp.int32, gained.shape, 0)
    total_one = jnp.sum(gained, axis=0, keepdims=True)
    total_two = jnp.sum(gain_two[...], axis=0, keepdims=True)
    held[0] = jnp.where(line == 0, total_one, jnp.where(line == 1, total_two, 0.0))

    def gain_step(n):
        return copy(held.at[n], came.at[n], g_sem, n, turns[n])

    def gain_next(n):
        gain_step(n).wait_recv()
        held[n + 1] = held[n] + came[n]

    total1 = k1[0].astype(F32) + a1[0].astype(F32)
    total2 = h_got[1, 0].astype(F32) + a2[0].astype(F32)
    gain_step(0).start()
    gain_next(0)
    gain_step(1).start()
    gain_next(1)
    for item in twos:
        item.wait_recv()
    totals = ((total1 + rest1[...].astype(F32)).astype(BF16), (total2 + rest2[...].astype(F32)).astype(BF16))
    for e, total in enumerate(totals):
        core = (c, 1 - c)[e]
        for u in range(2):
            d = lax.rem(2 * core + u + 4 - t, 4)
            for n in range(3):
                heads[d, n] = total[:, n * 512 + u * 256 : n * 512 + u * 256 + 256]
    gain_step(2).start()
    gain_next(2)
    own_heads[...] = heads[0]
    hs = [copy(heads.at[d], got_heads.at[d - 1], h_sem, d - 1, (dp, lax.rem(t + d, 4))) for d in (1, 2, 3)]
    for item in hs:
        item.start()
    for n in (3, 4):
        gain_step(n).start()
        gain_next(n)
    sums[...] = held[5]

    for item in seconds + ns + cs + ones + twos:
        item.wait_send()
    for n in range(5):
        gain_step(n).wait_send()
    for u in range(2):
        stay = (side == c) & (t == 2 * c + u)

        @pl.when(stay)
        def _():
            value_local(u).wait()

        @pl.when(jnp.logical_not(stay))
        def _():
            value_copy(u).wait_send()

    for p in range(2):

        @pl.when((pair != c) | (t != 2 * p + c))
        def _():
            pltpu.make_async_remote_copy(
                src_ref=first.at[p],
                dst_ref=first.at[p],
                send_sem=f_sem.at[0, p],
                recv_sem=f_sem.at[1, p],
                device_id=(dpc, t),
                device_id_type=MESH,
            ).wait_recv()

    for item in zs + hs:
        item.wait()

    @pl.when(moved)
    def _():
        for item in swaps:
            item.wait()


def tail(dq, dk, dv, small, normed, row, grad_hidden, keep1, got1, keep2, got2, gain, gain_two):
    vmem = pl.BlockSpec(memory_space=pltpu.VMEM)
    sems = pltpu.SemaphoreType.DMA
    wide = normed.shape[1]
    length = keep1.shape[2]
    rows = (length - 512) // 2 + 256
    half = SEQ // 2
    low = lambda *shape: pltpu.VMEM(shape, BF16)
    return pl.pallas_call(
        tail_kernel,
        out_shape=[
            jax.ShapeDtypeStruct((2, SEQ, 256), BF16),
            jax.ShapeDtypeStruct((rows, 128), BF16),
            jax.ShapeDtypeStruct((3, rows, 128), BF16),
            jax.ShapeDtypeStruct((3, 128, 256), BF16),
            jax.ShapeDtypeStruct((3, 3, 128, 256), BF16),
            jax.ShapeDtypeStruct((2, half // 2, wide), BF16),
            jax.ShapeDtypeStruct((2, half // 2, wide), BF16),
            jax.ShapeDtypeStruct((8, wide), F32),
        ],
        in_specs=[any_spec()] * 11 + [vmem] * 2,
        out_specs=[any_spec(), vmem, any_spec(), vmem, any_spec(), vmem, any_spec(), vmem],
        scratch_shapes=[low(SEQ, 512)] * 3
        + [low(3, 2, wide, 256), low(SEQ, wide), low(half, wide), pltpu.VMEM((half, wide), F32)]
        + [low(2, 128, length)] * 4
        + [low(128, length)] * 2
        + [low(4, rows, 128), low(2, half // 2, wide), low(2, half // 2, wide), low(512, SEQ)]
        + [low(2, 2, 128, 1536)] * 2
        + [low(2, 128, 1536)] * 4
        + [low(128, 1536)] * 4
        + [low(4, 3, 128, 256), pltpu.VMEM((6, 8, wide), F32), pltpu.VMEM((5, 8, wide), F32)]
        + [sems((12,)), sems((2, 2)), sems((2, 2)), sems((2, 3)), sems((2, 2)), sems((2, 3)), sems((2, 2)), sems((2, 2))]
        + [sems((2, 3)), sems((2, 2)), sems((2, 5))],
        compiler_params=params(collective_id=2, has_side_effects=True),
        name="tail",
    )(dq, dk, dv, small, normed, row, grad_hidden, keep1, got1, keep2, got2, gain, gain_two)


def fast_body(tokens, first_values, doc_lengths, cotangent, w_query, w_key, w_value, w_out, w_gate, w_up, w_down, gain_attn, gain_mlp):
    me, t = lax.axis_index("dp"), lax.axis_index("tensor")
    c = me % 2
    pair, side = t // 2, t % 2
    wide = tokens.shape[1]
    tiles = SEQ // TILE
    at = jnp.where(jnp.arange(8, dtype=jnp.int32) == 0, me, t).astype(jnp.int32)

    small_shard, big_shard = pack(w_query, w_key, w_value, w_out, w_gate, w_up, w_down)
    row, first, small, big = gather(tokens, first_values, small_shard, big_shard)

    lengths = jnp.where(c == side, doc_lengths, across_c(doc_lengths))
    lengths = lax.dynamic_index_in_dim(lengths, pair, 0, keepdims=False)
    order = jnp.arange(DOCS, dtype=jnp.int32)
    ends = jnp.sum(jnp.where(order[None, :] <= order[:, None], lengths[None, :], 0), axis=1)
    places = jnp.arange(SEQ, dtype=jnp.int32)
    starts = jnp.max(jnp.where(ends[None, :] <= places[:, None], ends[None, :], 0), axis=1)
    last = jnp.arange(tiles, dtype=jnp.int32) * TILE + (TILE - 1)
    stop = jnp.min(jnp.where(ends[None, :] > last[:, None], ends[None, :], SEQ), axis=1)
    bounds = jnp.concatenate([starts.reshape(tiles, TILE)[:, 0] // TILE, (stop - 1) // TILE])
    starts_by_tile = starts.reshape(tiles, TILE)
    freqs = 10000.0 ** (-(jnp.arange(32, dtype=F32) * 2.0 / HEAD))
    angles = (places - starts).astype(F32)[:, None] * jnp.tile(freqs, 4)[None, :]
    cosine, sine = jnp.cos(angles), jnp.sin(angles)

    row, cotangent = lax.optimization_barrier((row, cotangent))
    moved_cot = swap_halves(cotangent)
    normed_one, q, k, v = project(at, row, first, cosine, sine, gain_attn[None], small)
    attended, lse = attend(bounds, q, k, v, starts_by_tile)
    by_half = attended.reshape(2, SEQ // 2, 512)
    att_own = lax.dynamic_index_in_dim(by_half, c, 0, keepdims=False)
    att_other = across_c(lax.dynamic_index_in_dim(by_half, 1 - c, 0, keepdims=False))
    out, grad_hidden, branch, normed_two, hid, ga_own, ga_other, gain_two, cot = mlp(
        at, att_own, att_other, row, cotangent, moved_cot, gain_mlp[None], small, big
    )
    stays = c == side
    layer_out = jnp.where(stays, out, swap_halves(out))

    ga_got = across_c(ga_other)
    do = jnp.where(c == 0, jnp.concatenate([ga_own, ga_got]), jnp.concatenate([ga_got, ga_own]))

    kept = weights(normed_two, cot, branch, hid, att_own, att_other)
    kept, do = lax.optimization_barrier((kept, do))
    got1, got2 = across_x(kept[0]), across_y(kept[2])

    dq, dk, dv = attend_back(bounds, q, k, v, do, attended, lse, starts_by_tile, cosine, sine)

    first_back, pieces, got, own_heads, got_heads, grad_tokens, got_tokens, gains = tail(
        dq, dk, dv, small, normed_one, row, grad_hidden, kept[1], got1, kept[3], got2, gain_attn[None], gain_two
    )
    shape = (SEQ // 2, wide)
    grad_gate, grad_up, grad_down, grad_out, gq, gk, gv, grad_tokens, grad_first = finish(
        at, pieces, got, own_heads, got_heads, grad_tokens.reshape(shape), got_tokens.reshape(shape), first_back.reshape(2 * SEQ, 256), w_gate.shape[1]
    )
    return (
        layer_out,
        grad_tokens,
        grad_first,
        gq,
        gk,
        gv,
        grad_out,
        grad_gate.T,
        grad_up.T,
        grad_down,
        gains[0],
        gains[1],
    )


def solution(mesh):
    fits = dict(mesh.shape) == {"dp": 8, "tensor": 4}
    placed = (
        P(("dp", "tensor"), None),
        P("dp", "tensor"),
        P("dp", None),
        P(("dp", "tensor"), None),
        P("dp", "tensor"),
        P("dp", "tensor"),
        P("dp", "tensor"),
        P("tensor", "dp"),
        P("dp", "tensor"),
        P("dp", "tensor"),
        P("tensor", "dp"),
        P(),
        P(),
    )
    return jax.shard_map(
        fast_body if fits else general_body,
        mesh=mesh,
        in_specs=placed,
        out_specs=(
            P(("dp", "tensor"), None),
            P(("dp", "tensor"), None),
            P("dp", "tensor"),
            P("dp", "tensor"),
            P("dp", "tensor"),
            P("dp", "tensor"),
            P("tensor", "dp"),
            P("dp", "tensor"),
            P("dp", "tensor"),
            P("tensor", "dp"),
            P(),
            P(),
        ),
        check_vma=False,
    )
```

```python
import functools

import jax
import jax.numpy as jnp
from jax import lax
from jax.experimental import pallas as pl
from jax.experimental.pallas import tpu as pltpu
from jax.sharding import PartitionSpec as P

HEAD = 64
SEQ = 2048
DOCS = 8
EPSILON = 1e-05


def rms_norm(values, gain):
    factor = lax.rsqrt(jnp.mean(values * values, axis=1, keepdims=True) + EPSILON)
    return values * factor * gain


def documents(doc_lengths):
    ends = jnp.cumsum(doc_lengths, axis=1)
    starts = ends - doc_lengths
    places = jnp.arange(SEQ, dtype=jnp.int32)
    segment = jnp.sum((places[None, :, None] >= ends[:, None, :]).astype(jnp.int32), axis=2)
    member = segment[:, :, None] == jnp.arange(DOCS, dtype=jnp.int32)[None, None, :]
    offset = jnp.sum(jnp.where(member, starts[:, None, :], 0), axis=2)
    return (segment, (places[None, :] - offset).astype(jnp.float32))


def rotation(positions):
    half = HEAD // 2
    freqs = 10000.0 ** (-(jnp.arange(half, dtype=jnp.float32) * 2.0 / HEAD))
    angles = positions[:, None] * freqs[None, :]
    return (jnp.cos(angles), jnp.sin(angles))


def rotate(values, cosine, sine):
    shaped = values.reshape(values.shape[0], -1, HEAD)
    half = HEAD // 2
    first = shaped[:, :, :half]
    second = shaped[:, :, half:]
    cos_rows = cosine[:, None, :]
    sin_rows = sine[:, None, :]
    turned = jnp.concatenate(
        [first * cos_rows - second * sin_rows, second * cos_rows + first * sin_rows], axis=2
    )
    return turned.reshape(values.shape)


def rotate_back(grads, cosine, sine):
    shaped = grads.reshape(grads.shape[0], -1, HEAD)
    half = HEAD // 2
    first = shaped[:, :, :half]
    second = shaped[:, :, half:]
    cos_rows = cosine[:, None, :]
    sin_rows = sine[:, None, :]
    turned = jnp.concatenate(
        [first * cos_rows + second * sin_rows, second * cos_rows - first * sin_rows], axis=2
    )
    return turned.reshape(grads.shape)


def swiglu(gate, up_val):
    return jax.nn.silu(gate) * up_val


def product(left, right):
    return jnp.dot(left, right, preferred_element_type=jnp.float32)


def inner(left, right):
    return lax.dot_general(
        left, right, (((0,), (0,)), ((), ())), preferred_element_type=jnp.float32
    )


def outer(left, right):
    return lax.dot_general(
        left, right, (((1,), (1,)), ((), ())), preferred_element_type=jnp.float32
    )


def block_scores(queries, keys_all, segment, start, width):
    query_block = lax.dynamic_slice_in_dim(queries, start, width, 0)
    query_seg = lax.dynamic_slice_in_dim(segment, start, width, 0)
    scores = (
        jnp.einsum("qhd,khd->hqk", query_block, keys_all, preferred_element_type=jnp.float32)
        * 0.125
    )
    places = jnp.arange(SEQ, dtype=jnp.int32)
    rows_at = start + jnp.arange(width, dtype=jnp.int32)
    allowed = (query_seg[:, None] == segment[None, :]) & (places[None, :] <= rows_at[:, None])
    return (query_block, jnp.where(allowed[None], scores, -1e30))


def forward_row(pieces):
    queries, keys_all, values_all, segment = pieces
    width = min(512, SEQ)
    count = SEQ // width

    def forward_one_block(index):
        unused, scores = block_scores(queries, keys_all, segment, index * width, width)
        top = jnp.max(scores, axis=2, keepdims=True)
        expo = jnp.exp(scores - top)
        total = jnp.sum(expo, axis=2, keepdims=True)
        weights = (expo / total).astype(jnp.bfloat16)
        result = jnp.einsum("hqk,khd->qhd", weights, values_all, preferred_element_type=jnp.float32)
        return (result, (top + jnp.log(total))[:, :, 0])

    results, logsums = lax.map(forward_one_block, jnp.arange(count, dtype=jnp.int32))
    return (results.reshape(SEQ, queries.shape[1], HEAD), logsums)


def backward_row(pieces):
    queries, keys_all, values_all, segment, grad_rows, logsums = pieces
    width = min(512, SEQ)
    count = SEQ // width

    def backward_one_block(carry, extra):
        index, logsum = extra
        start = index * width
        query_block, scores = block_scores(queries, keys_all, segment, start, width)
        probs = jnp.exp(scores - logsum[:, :, None])
        grad_block = lax.dynamic_slice_in_dim(grad_rows, start, width, 0)
        grad_probs = jnp.einsum(
            "qhd,khd->hqk", grad_block, values_all, preferred_element_type=jnp.float32
        )
        delta = jnp.sum(probs * grad_probs, axis=2, keepdims=True)
        grad_scores = (probs * (grad_probs - delta)).astype(jnp.bfloat16)
        grad_query = (
            jnp.einsum("hqk,khd->qhd", grad_scores, keys_all, preferred_element_type=jnp.float32)
            * 0.125
        )
        grad_keys = (
            carry[0]
            + jnp.einsum(
                "hqk,qhd->khd", grad_scores, query_block, preferred_element_type=jnp.float32
            )
            * 0.125
        )
        grad_values = carry[1] + jnp.einsum(
            "hqk,qhd->khd",
            probs.astype(jnp.bfloat16),
            grad_block,
            preferred_element_type=jnp.float32,
        )
        return ((grad_keys, grad_values), grad_query)

    zeros = jnp.zeros(keys_all.shape, jnp.float32)
    sums, grad_queries = lax.scan(
        backward_one_block, (zeros, zeros), (jnp.arange(count, dtype=jnp.int32), logsums)
    )
    return (grad_queries.reshape(SEQ, queries.shape[1], HEAD), sums[0], sums[1])


def general_body(
    tokens,
    first_values,
    doc_lengths,
    cotangent,
    w_query,
    w_key,
    w_value,
    w_out,
    w_gate,
    w_up,
    w_down,
    gain_attn,
    gain_mlp,
):
    query_mat, key_mat, value_mat, out_mat, gate_mat, up_mat, down_mat = (
        lax.all_gather(w_query, "dp", axis=0, tiled=True),
        lax.all_gather(w_key, "dp", axis=0, tiled=True),
        lax.all_gather(w_value, "dp", axis=0, tiled=True),
        lax.all_gather(w_out, "dp", axis=1, tiled=True),
        lax.all_gather(w_gate, "dp", axis=0, tiled=True),
        lax.all_gather(w_up, "dp", axis=0, tiled=True),
        lax.all_gather(w_down, "dp", axis=1, tiled=True),
    )
    local_heads = query_mat.shape[1] // HEAD
    row_count = doc_lengths.shape[0]
    group = row_count * SEQ
    segment, positions = documents(doc_lengths)
    cosine, sine = rotation(positions.reshape(-1))

    def heads(matrix):
        return matrix.reshape(row_count, SEQ, local_heads, HEAD)

    inputs = tokens.astype(jnp.float32)
    normed_one, norm_one_back = jax.vjp(rms_norm, inputs, gain_attn)
    gathered_one = lax.all_gather(normed_one.astype(jnp.bfloat16), "tensor", axis=0, tiled=True)
    query_raw = product(gathered_one, query_mat)
    key_raw = product(gathered_one, key_mat)
    value_raw = product(gathered_one, value_mat)
    queries = rotate(query_raw, cosine, sine).astype(jnp.bfloat16)
    keys_low = rotate(key_raw, cosine, sine).astype(jnp.bfloat16)
    mixed_values = (0.5 * value_raw + 0.5 * first_values.astype(jnp.float32)).astype(jnp.bfloat16)
    attended, logsums = lax.map(
        forward_row, (heads(queries), heads(keys_low), heads(mixed_values), segment)
    )
    attended_low = attended.reshape(group, -1).astype(jnp.bfloat16)
    hidden_in = inputs + lax.psum_scatter(
        product(attended_low, out_mat), "tensor", scatter_dimension=0, tiled=True
    )
    normed_two, norm_two_back = jax.vjp(rms_norm, hidden_in, gain_mlp)
    normed_low_two = normed_two.astype(jnp.bfloat16)
    grad_out = cotangent.astype(jnp.float32)
    gathered_two = lax.all_gather(normed_low_two, "tensor", axis=0, tiled=True)
    activated, swiglu_back = jax.vjp(
        swiglu, product(gathered_two, gate_mat), product(gathered_two, up_mat)
    )
    act_low = activated.astype(jnp.bfloat16)
    layer_out = hidden_in + lax.psum_scatter(
        product(act_low, down_mat).astype(jnp.bfloat16), "tensor", scatter_dimension=0, tiled=True
    ).astype(jnp.float32)
    grad_rows = lax.all_gather(cotangent, "tensor", axis=0, tiled=True)
    grad_gate, grad_up = swiglu_back(outer(grad_rows, down_mat))
    gate_low = grad_gate.astype(jnp.bfloat16)
    up_low = grad_up.astype(jnp.bfloat16)
    grad_normed_two = lax.psum_scatter(
        outer(gate_low, gate_mat) + outer(up_low, up_mat), "tensor", scatter_dimension=0, tiled=True
    )
    grad_gate_mat = inner(gathered_two, gate_low)
    grad_up_mat = inner(gathered_two, up_low)
    grad_down_mat = inner(act_low, grad_rows)
    grad_hidden_two, grad_gain_two = norm_two_back(grad_normed_two)
    grad_hidden = grad_out + grad_hidden_two
    grad_branch = lax.all_gather(grad_hidden.astype(jnp.bfloat16), "tensor", axis=0, tiled=True)
    grad_attended = outer(grad_branch, out_mat).astype(jnp.bfloat16)
    grad_out_mat = inner(attended_low, grad_branch)
    grad_rot_query, grad_rot_key, grad_mixed = lax.map(
        backward_row,
        (
            heads(queries),
            heads(keys_low),
            heads(mixed_values),
            segment,
            heads(grad_attended),
            logsums,
        ),
    )
    grad_query_low = rotate_back(grad_rot_query.reshape(group, -1), cosine, sine).astype(
        jnp.bfloat16
    )
    grad_key_low = rotate_back(grad_rot_key.reshape(group, -1), cosine, sine).astype(jnp.bfloat16)
    grad_first = 0.5 * grad_mixed.reshape(group, -1)
    grad_value_low = grad_first.astype(jnp.bfloat16)
    grad_normed_one = lax.psum_scatter(
        outer(grad_query_low, query_mat)
        + outer(grad_key_low, key_mat)
        + outer(grad_value_low, value_mat),
        "tensor",
        scatter_dimension=0,
        tiled=True,
    )
    grad_query_mat = inner(gathered_one, grad_query_low)
    grad_key_mat = inner(gathered_one, grad_key_low)
    grad_value_mat = inner(gathered_one, grad_value_low)
    grad_inputs_one, grad_gain_one = norm_one_back(grad_normed_one)
    grad_tokens = grad_hidden + grad_inputs_one
    summed = (
        lax.psum_scatter(grad_query_mat, "dp", scatter_dimension=0, tiled=True),
        lax.psum_scatter(grad_key_mat, "dp", scatter_dimension=0, tiled=True),
        lax.psum_scatter(grad_value_mat, "dp", scatter_dimension=0, tiled=True),
        lax.psum_scatter(grad_out_mat, "dp", scatter_dimension=1, tiled=True),
        lax.psum_scatter(grad_gate_mat, "dp", scatter_dimension=0, tiled=True),
        lax.psum_scatter(grad_up_mat, "dp", scatter_dimension=0, tiled=True),
        lax.psum_scatter(grad_down_mat, "dp", scatter_dimension=1, tiled=True),
    )
    gain_sums = lax.psum((grad_gain_one, grad_gain_two), ("dp", "tensor"))
    return (
        layer_out.astype(jnp.bfloat16),
        grad_tokens,
        grad_first,
        summed[0],
        summed[1],
        summed[2],
        summed[3],
        summed[4],
        summed[5],
        summed[6],
        gain_sums[0],
        gain_sums[1],
    )


AXES = ("dp", "tensor")
MESH = pl.DeviceIdType.MESH
TILE = 256
NEG = -1e30
F32 = jnp.float32
BF16 = jnp.bfloat16


def flat(y, x, c, t):
    return ((y * 2 + x) * 2 + c) * 4 + t


def move(values, to):
    pairs = []
    for y in range(2):
        for x in range(2):
            for c in range(2):
                for t in range(4):
                    pair = (flat(y, x, c, t), flat(*to(y, x, c, t)))
                    if pair[0] != pair[1]:
                        pairs.append(pair)
    return lax.ppermute(values, AXES, pairs)


def across_x(values):
    return move(values, lambda y, x, c, t: (y, 1 - x, c, t))


def across_y(values):
    return move(values, lambda y, x, c, t: (1 - y, x, c, t))


def across_c(values):
    return move(values, lambda y, x, c, t: (y, x, 1 - c, t))


def along_t(values, step):
    return move(values, lambda y, x, c, t: (y, x, c, (t + step) % 4))


def swap_halves(values):
    return move(values, lambda y, x, c, t: (y, x, t % 2, (t // 2) * 2 + c))


def pack_kernel(wq, wk, wv, wo, wg, wu, wd, halves, small, big):
    small[0] = dot(wq[...], halves[...]).astype(BF16)
    small[1] = dot(wk[...], halves[...]).astype(BF16)
    small[2] = wv[...]
    small[3] = wo[...].T
    for n, units in enumerate((wg, wu, wd)):
        big[n] = units[...].reshape(big.shape[1:])


def pack(wq, wk, wv, wo, wg, wu, wd):
    wg, wu = wg.T, wu.T
    part, rows = wg.shape
    lane = jnp.arange(256, dtype=jnp.int32)
    source = ((lane & 127) >> 5) * 64 + (lane >> 7) * 32 + (lane & 31)
    halves = (lane[:, None] == source[None, :]).astype(BF16)
    return pl.pallas_call(
        pack_kernel,
        out_shape=[
            jax.ShapeDtypeStruct((4, rows, 256), BF16),
            jax.ShapeDtypeStruct((3, 2, part // 2, rows), BF16),
        ],
        compiler_params=params(),
        name="pack",
    )(wq, wk, wv, wo, wg, wu, wd, halves)


def meet(plane, c, t, dpx, dpy):
    barrier = pltpu.get_barrier_semaphore()
    for e in range(2):
        for d in range(4):
            if e or d:
                other = plane + lax.rem(c + e, 2)
                pl.semaphore_signal(barrier, inc=1, device_id=(other, lax.rem(t + d, 4)), device_id_type=MESH)
    pl.semaphore_signal(barrier, inc=1, device_id=(dpx, t), device_id_type=MESH)
    pl.semaphore_signal(barrier, inc=1, device_id=(dpy, t), device_id_type=MESH)
    pl.semaphore_wait(barrier, 9)


def gather_kernel(
    ends, tok, fv, small, big, gain, freqs, row_out, g_small, g_big, normed_out, q_out, k_out, v_out, cos_out, sin_out,
    row, first, w_s, n_s, q_s, k_s, v_s, raw_s, cos_s, sin_s,
    send, recv, relay_send, along_recv, next_send, next_recv, swap, fsend, frecv, here, tile_sem, end_sem,
):
    dp, t = lax.axis_index("dp"), lax.axis_index("tensor")
    c, x, y = lax.rem(dp, 2), lax.rem(lax.div(dp, 2), 2), lax.div(dp, 4)
    pair, side = lax.div(t, 2), lax.rem(t, 2)
    plane = dp - c
    dpx, dpy, dpc = dp + 2 - 4 * x, dp + 4 - 8 * y, dp + 1 - 2 * c
    dpxy = dpx + 4 - 8 * y

    meet(plane, c, t, dpx, dpy)
    def slot(k, at, owner, h):
        if k == 0:
            return g_small.at[pl.ds(2 * h, 2), at, pl.ds(owner * 128, 128), :]
        return g_big.at[k - 1, owner, h, at]

    def column(k, owner, h):
        if k == 0:
            return g_small.at[pl.ds(2 * h, 2), :, pl.ds(owner * 128, 128), :]
        return g_big.at[k - 1, owner, h]

    def both(k, at, owner):
        if k == 0:
            return g_small.at[:, at, pl.ds(owner * 128, 128), :]
        return g_big.at[k - 1, owner, :, at]

    def all_of(k, owner):
        if k == 0:
            return g_small.at[:, :, pl.ds(owner * 128, 128), :]
        return g_big.at[k - 1, owner]

    def shard(k):
        return small if k == 0 else big.at[k - 1]

    def part_of(k, h):
        return small.at[pl.ds(2 * h, 2)] if k == 0 else big.at[k - 1, h]

    def copy(k, n, src, dst, to, at):
        return pltpu.make_async_remote_copy(
            src_ref=src,
            dst_ref=dst,
            send_sem=send.at[k, n],
            recv_sem=recv.at[k, n],
            device_id=(to, at),
            device_id_type=MESH,
        )

    chunks = 4
    near, far = (dpx, dpy), (dpy, dpx)
    kept = [pltpu.make_async_copy(shard(k), both(k, t, dp), here.at[k]) for k in range(chunks)]

    def relay(k, at, side, src):
        return pltpu.make_async_remote_copy(
            src_ref=src,
            dst_ref=both(k, at, dp),
            send_sem=relay_send.at[k, at, side],
            recv_sem=along_recv.at[k, at],
            device_id=(dp, t + 2 * side - 1),
            device_id_type=MESH,
        )

    def onward(k, at, h, src):
        return pltpu.make_async_remote_copy(
            src_ref=src,
            dst_ref=slot(k, at, dp, h),
            send_sem=next_send.at[k, at, h],
            recv_sem=next_recv.at[k, at, h],
            device_id=(near[h], t),
            device_id_type=MESH,
        )

    def start_along(k):
        @pl.when(t < 3)
        def _():
            relay(k, t, 1, shard(k)).start()

        @pl.when(t > 0)
        def _():
            relay(k, t, 0, shard(k)).start()

    def pass_along(k, level):
        for side, at in ((1, t - level), (0, t + level)):

            @pl.when((at >= 0) & (at < 4))
            def _():
                block = both(k, at, dp)
                move = relay(k, at, side, block)
                move.wait_recv()

                @pl.when((t < 3) if side else (t > 0))
                def _():
                    move.start()

                for h in range(2):
                    onward(k, at, h, slot(k, at, dp, h)).start()

    def end_along(k):
        for level in range(4):
            for side, at in ((1, t - level), (0, t + level)):

                @pl.when((at >= 0) & (at < 4) & ((t < 3) if side else (t > 0)))
                def _():
                    relay(k, at, side, both(k, at, dp)).wait_send()

    across = [
        [
            copy(k, 2 * h + i, column(k, owner, h), column(k, owner, h), far[h], t)
            for h in range(2)
            for i, owner in enumerate((dp, near[h]))
        ]
        for k in range(chunks)
    ]
    over = [
        [copy(k, 4 + i, all_of(k, owner), all_of(k, owner), dpc, t) for i, owner in enumerate((dp, dpx, dpy, dpxy))]
        for k in range(chunks)
    ]

    order = (1, 0, 2, 3)
    start_along(order[0])
    for item in kept:
        item.start()
    for k in order:
        for h in range(2):
            onward(k, t, h, part_of(k, h)).start()
        if k == order[0]:
            start_along(order[1])

    moved = side != c
    to_own = pltpu.make_async_copy(tok, row.at[c], here.at[4])
    swapped = pltpu.make_async_remote_copy(
        src_ref=tok,
        dst_ref=row.at[side],
        send_sem=swap.at[0],
        recv_sem=swap.at[1],
        device_id=(plane + side, 2 * pair + c),
        device_id_type=MESH,
    )

    def start_tokens():
        @pl.when(moved)
        def _():
            swapped.start()

        @pl.when(jnp.logical_not(moved))
        def _():
            to_own.start()

    heads_core, slab = pair, side

    def first_copy(p):
        return pltpu.make_async_remote_copy(
            src_ref=fv.at[pl.ds(p * SEQ, SEQ), :],
            dst_ref=first.at[slab],
            send_sem=fsend.at[p],
            recv_sem=frecv.at[slab],
            device_id=(plane + heads_core, 2 * p + c),
            device_id_type=MESH,
        )

    def first_local(p):
        return pltpu.make_async_copy(fv.at[pl.ds(p * SEQ, SEQ), :], first.at[slab], here.at[5])

    stays = [(heads_core == c) & (t == 2 * p + c) for p in range(2)]

    def start_first():
        for p in range(2):

            @pl.when(stays[p])
            def _():
                first_local(p).start()

            @pl.when(jnp.logical_not(stays[p]))
            def _():
                first_copy(p).start()

    def pass_over(k):
        for item in across[k]:
            item.wait_recv()
        for item in over[k][1:]:
            item.start()

    def pass_next(k):
        for at in range(4):
            for h in range(2):
                onward(k, at, h, slot(k, at, dp, h)).wait_recv()
        for item in across[k]:
            item.start()

    for i in range(8):
        rows = slice(i * TILE, i * TILE + TILE)
        at_row = lax.broadcasted_iota(jnp.int32, (TILE, 128), 0) + i * TILE
        begin = jnp.zeros_like(at_row)
        for k in range(DOCS):
            begin = jnp.maximum(begin, jnp.where(at_row >= ends[k], ends[k], 0))
        angles = (at_row - begin).astype(F32) * freqs[...]
        cos_s[rows, :] = jnp.cos(angles)
        sin_s[rows, :] = jnp.sin(angles)
    tables = [pltpu.make_async_copy(cos_s, cos_out, end_sem.at[0]), pltpu.make_async_copy(sin_s, sin_out, end_sem.at[1])]

    for i, k in enumerate(order):
        pass_along(k, 1)
        if i + 2 < chunks:
            start_along(order[i + 2])
        if i:
            pass_next(order[i - 1])
        pass_along(k, 2)
        pass_along(k, 3)
        kept[k].wait()
        over[k][0].start()
        if i == 2:
            start_tokens()
        if i == 3:
            start_first()
        if i >= 2:
            pass_over(order[i - 2])
    pass_next(order[3])
    for item in tables:
        item.start()
    for item in over[0]:
        item.wait_recv()
    load_w = pltpu.make_async_copy(g_small.at[pl.ds(0, 3), pl.ds(2 * c, 2)], w_s, end_sem.at[2])
    load_w.start()

    @pl.when(moved)
    def _():
        swapped.wait_send()
        swapped.wait_recv()

    @pl.when(jnp.logical_not(moved))
    def _():
        to_own.wait()

    given = pltpu.make_async_remote_copy(
        src_ref=row.at[c],
        dst_ref=row.at[c],
        send_sem=swap.at[2],
        recv_sem=swap.at[3],
        device_id=(dpc, t),
        device_id_type=MESH,
    )
    given.start()
    load_w.wait()
    outs = []

    def project(half, n):
        low = pl.multiple_of(half * (SEQ // 2) + lax.rem(n, 2) * 512, 512)
        rows = pl.ds(low, 512)
        values = row[half, n % 2 * 512 : n % 2 * 512 + 512, :].astype(F32)
        factor = lax.rsqrt(jnp.mean(values * values, axis=1, keepdims=True) + EPSILON)
        normed = (values * factor * gain[...]).astype(BF16)
        n_s[rows, :] = normed
        cos, sin = cos_s[rows, :], sin_s[rows, :]
        for u in range(2):
            for m, out, scale in ((0, q_s, 0.125), (1, k_s, 1.0)):
                raw = dot(normed, w_s[m, u])
                a, b = raw[:, :128], raw[:, 128:]
                out[rows, u * 256 : u * 256 + 128] = ((a * cos - b * sin) * scale).astype(BF16)
                out[rows, u * 256 + 128 : u * 256 + 256] = ((b * cos + a * sin) * scale).astype(BF16)
            raw_s[rows, u * 256 : u * 256 + 256] = 0.5 * dot(normed, w_s[2, u])
        for m, (src, dst) in enumerate(((n_s, normed_out), (q_s, q_out), (k_s, k_out))):
            item = pltpu.make_async_copy(src.at[rows, :], dst.at[rows, :], tile_sem.at[n, m])
            item.start()
            outs.append(item)

    project(c, 0)
    project(c, 1)
    pass_over(order[2])
    given.wait_recv()
    row_copy = pltpu.make_async_copy(row, row_out, end_sem.at[3])
    row_copy.start()
    project(1 - c, 2)
    project(1 - c, 3)
    pass_over(order[3])

    for p in range(2):

        @pl.when(stays[p])
        def _():
            first_local(p).wait()

        @pl.when(jnp.logical_not(stays[p]))
        def _():
            first_copy(p).wait_send()

    for u in range(2):
        came = pltpu.make_async_remote_copy(
            src_ref=first.at[u],
            dst_ref=first.at[u],
            send_sem=fsend.at[u],
            recv_sem=frecv.at[u],
            device_id=(dpc, t),
            device_id_type=MESH,
        )

        @pl.when((side != c) | (t != 2 * c + u))
        def _():
            came.wait_recv()

    for n in range(4):
        rows = slice(n * 512, n * 512 + 512)
        for u in range(2):
            lanes = slice(u * 256, u * 256 + 256)
            v_s[rows, lanes] = (raw_s[rows, lanes] + 0.5 * first[u, rows, :].astype(F32)).astype(BF16)
        item = pltpu.make_async_copy(v_s.at[rows, :], v_out.at[rows, :], tile_sem.at[n, 3])
        item.start()
        outs.append(item)

    given.wait_send()
    for k in range(chunks):
        if k:
            for item in over[k]:
                item.wait_recv()
        end_along(k)
        for item in across[k] + over[k]:
            item.wait_send()
        for at in range(4):
            for h in range(2):
                onward(k, at, h, slot(k, at, dp, h)).wait_send()
    for item in outs + tables + [row_copy]:
        item.wait()


def gather(ends, tok, fv, small, big, gain, freqs):
    part, rows = big.shape[2:]
    wide = tok.shape[1]
    vmem = pl.BlockSpec(memory_space=pltpu.VMEM)
    sems = pltpu.SemaphoreType.DMA
    low = lambda *shape: pltpu.VMEM(shape, BF16)
    shapes = [(2, SEQ // 2, wide), (4, 4, wide, 256), (3, 8, 2, 4, part, rows), (SEQ, wide)] + [(SEQ, 512)] * 3
    return pl.pallas_call(
        gather_kernel,
        out_shape=[jax.ShapeDtypeStruct(shape, BF16) for shape in shapes]
        + [jax.ShapeDtypeStruct((SEQ, 128), F32)] * 2,
        in_specs=[pl.BlockSpec(memory_space=pltpu.SMEM)] + [vmem] * 6,
        out_specs=[any_spec()] * 9,
        scratch_shapes=[low(2, SEQ // 2, wide), low(2, SEQ, 256), low(3, 2, wide, 256), low(SEQ, wide)]
        + [low(SEQ, 512)] * 3
        + [pltpu.VMEM((SEQ, 512), F32)]
        + [pltpu.VMEM((SEQ, 128), F32)] * 2
        + [
            sems((4, 8)),
            sems((4, 8)),
            sems((4, 4, 2)),
            sems((4, 4)),
            sems((4, 4, 2)),
            sems((4, 4, 2)),
            sems((4,)),
            sems((2,)),
            sems((2,)),
            sems((6,)),
            sems((4, 4)),
            sems((4,)),
        ],
        compiler_params=params(collective_id=0, has_side_effects=True),
        name="gather",
    )(ends, tok, fv, small, big, gain, freqs)


def dot(left, right):
    return jnp.dot(left, right, preferred_element_type=F32)


def dot_nt(left, right):
    return lax.dot_general(left, right, (((1,), (1,)), ((), ())), preferred_element_type=F32)


def dot_tn(left, right):
    return lax.dot_general(left, right, (((0,), (0,)), ((), ())), preferred_element_type=F32)


def any_spec():
    return pl.BlockSpec(memory_space=pl.ANY)


def params(**more):
    return pltpu.CompilerParams(vmem_limit_bytes=62 * 1024 * 1024, **more)


def cost(flops, size, exps=0):
    return pl.CostEstimate(flops=int(flops), bytes_accessed=int(size), transcendentals=int(exps))


def once(shape, place):
    return pl.BlockSpec(shape, place, pipeline_mode=pl.Buffered(1))


def head_masks(rows):
    lane = lax.broadcasted_iota(jnp.int32, (rows, 256), 1)
    return (lane & 127) >> 5, lane >> 6


def attend_kernel(at, bounds, q_ref, k_ref, v_ref, starts, own_ref, send_ref, lse_ref, kept, turned, acc):
    tiles = SEQ // TILE
    of_qk, _ = head_masks(TILE)
    row = lax.broadcasted_iota(jnp.int32, (TILE, TILE), 0)
    lane = lax.broadcasted_iota(jnp.int32, (TILE, TILE), 1)
    slabs = [slice(0, 256), slice(256, 512)]

    def turn_values(j, carry):
        there = pl.ds(pl.multiple_of(j * TILE, TILE), TILE)
        turned[j] = v_ref[there, :].T
        return carry

    lax.fori_loop(0, tiles, turn_values, 0)

    def eighths(values, reduce):
        return reduce(values.reshape(TILE // 8, 8, 4 * TILE), axis=0)

    def query_tile(i, carry):
        here = pl.ds(pl.multiple_of(i * TILE, TILE), TILE)
        q4 = []
        for slab in slabs:
            q = q_ref[here, slab]
            zero = jnp.zeros_like(q)
            q4.append(jnp.concatenate([jnp.where(of_qk == h, q, zero) for h in range(4)], axis=0))
        low = bounds[i]
        begin = starts[pl.ds(i, 1), :]
        limit = lane + i * TILE

        def score(j, tops):
            there = pl.ds(pl.multiple_of(j * TILE, TILE), TILE)
            at_row = row + j * TILE
            ok = (at_row >= begin) & (at_row <= limit)
            ok = jnp.concatenate([ok] * 4, axis=1)
            new = []
            for u, slab in enumerate(slabs):
                s = jnp.where(ok, dot_nt(k_ref[there, slab], q4[u]), NEG)
                kept[j - low, u] = s
                new.append(jnp.maximum(tops[u], eighths(s, jnp.max)))
            return tuple(new)

        start = jnp.full((8, 4 * TILE), NEG, F32)
        tops = lax.fori_loop(low, i + 1, score, (start, start))
        tops = [jnp.max(top, axis=0, keepdims=True) for top in tops]
        acc[...] = jnp.zeros_like(acc)

        def weigh(j, totals):
            new = []
            for u in range(2):
                e = jnp.exp(kept[j - low, u] - tops[u])
                p = e.astype(BF16)
                for h in range(4):
                    part = slice(u * 256 + h * 64, u * 256 + h * 64 + 64)
                    acc[part] += dot(turned[j, part, :], p[:, h * TILE : (h + 1) * TILE])
                new.append(totals[u] + eighths(e, jnp.sum))
            return tuple(new)

        zero = jnp.zeros((8, 4 * TILE), F32)
        totals = lax.fori_loop(low, i + 1, weigh, (zero, zero))
        for u, slab in enumerate(slabs):
            total = jnp.sum(totals[u], axis=0, keepdims=True)
            inverse = 1.0 / total
            scaled = [
                acc[u * 256 + h * 64 : u * 256 + h * 64 + 64] * inverse[:, h * TILE : (h + 1) * TILE] for h in range(4)
            ]
            done = jnp.concatenate(scaled, axis=0).T.astype(BF16)
            local = pl.ds(pl.multiple_of(lax.rem(i, tiles // 2) * TILE, TILE), TILE)
            mine = lax.div(i, tiles // 2) == (at[0] & 1)

            @pl.when(mine)
            def _():
                own_ref[local, slab] = done

            @pl.when(jnp.logical_not(mine))
            def _():
                send_ref[local, slab] = done

            lse_ref[u, pl.ds(i, 1), :] = tops[u] + jnp.log(total)
        return carry

    lax.fori_loop(0, tiles, query_tile, 0)


def attend(at, bounds, q, k, v, starts):
    tiles = SEQ // TILE
    vmem = pl.BlockSpec(memory_space=pltpu.VMEM)
    return pl.pallas_call(
        attend_kernel,
        out_shape=[
            jax.ShapeDtypeStruct((SEQ // 2, 512), BF16),
            jax.ShapeDtypeStruct((SEQ // 2, 512), BF16),
            jax.ShapeDtypeStruct((2, tiles, 4 * TILE), F32),
        ],
        in_specs=[pl.BlockSpec(memory_space=pltpu.SMEM)] * 2 + [vmem] * 4,
        out_specs=[vmem] * 3,
        scratch_shapes=[
            pltpu.VMEM((tiles, 2, TILE, 4 * TILE), F32),
            pltpu.VMEM((tiles, 512, TILE), BF16),
            pltpu.VMEM((512, TILE), F32),
        ],
        compiler_params=params(),
        cost_estimate=cost(20e9, 12e6, 1e7),
        name="attend",
    )(at, bounds, q, k, v, starts)


def attend_back_kernel(
    at, bounds, q_hbm, k_hbm, v_hbm, do_own, do_other, o_own, o_other, lse_ref, starts, cosine, sine, dq_hbm, dk_hbm, dv_hbm,
    q_ref, k_ref, v_ref, do_ref, o_ref, dq_ref, dk_ref, dv_ref, dq_acc, delta, dk_acc, dv_acc, load, store,
):
    tiles = SEQ // TILE
    of_qk, of_v = head_masks(TILE)
    row = lax.broadcasted_iota(jnp.int32, (TILE, TILE), 0)
    lane = lax.broadcasted_iota(jnp.int32, (TILE, TILE), 1)
    slabs = [slice(0, 256), slice(256, 512)]
    pick = (lax.broadcasted_iota(jnp.int32, (8, 256), 1) >> 6) == lax.broadcasted_iota(
        jnp.int32, (8, 256), 0
    )
    pick = pick.astype(F32)
    half = SEQ // 2
    low = pl.multiple_of((at[0] & 1) * half, half)
    mine, others = pl.ds(low, half), pl.ds(half - low, half)
    loads = [
        pltpu.make_async_copy(src, dst, load.at[n])
        for n, (src, dst) in enumerate((
            (do_own, do_ref.at[mine, :]),
            (do_other, do_ref.at[others, :]),
            (o_own, o_ref.at[mine, :]),
            (o_other, o_ref.at[others, :]),
            (q_hbm, q_ref),
            (k_hbm, k_ref),
            (v_hbm, v_ref),
        ))
    ]
    for item in loads:
        item.start()
    dq_acc[...] = jnp.zeros_like(dq_acc)
    for item in loads[:4]:
        item.wait()

    def prepare(i, carry):
        here = pl.ds(pl.multiple_of(i * TILE, TILE), TILE)
        for u, slab in enumerate(slabs):
            both = do_ref[here, slab].astype(F32) * o_ref[here, slab].astype(F32)
            sums = lax.dot_general(
                pick, both, (((1,), (1,)), ((), ())), precision=lax.Precision.HIGHEST, preferred_element_type=F32
            )
            for h in range(4):
                delta[u, pl.ds(i, 1), h * TILE : (h + 1) * TILE] = sums[h : h + 1]
        return carry

    lax.fori_loop(0, tiles, prepare, 0)
    for item in loads[4:]:
        item.wait()

    def rotate_out(values, here, out, low, scale):
        a, b = values[:, :128], values[:, 128:]
        cos, sin = cosine[here, :], sine[here, :]
        out[here, low : low + 128] = ((a * cos + b * sin) * scale).astype(BF16)
        out[here, low + 128 : low + 256] = ((b * cos - a * sin) * scale).astype(BF16)

    def split(values, of):
        zero = jnp.zeros_like(values)
        return jnp.concatenate([jnp.where(of == h, values, zero) for h in range(4)], axis=0)

    def key_tile(j, carry):
        there = pl.ds(pl.multiple_of(j * TILE, TILE), TILE)
        at_row = row + j * TILE
        dk_acc[...] = jnp.zeros_like(dk_acc)
        dv_acc[...] = jnp.zeros_like(dv_acc)

        def query_tile(i, carry):
            here = pl.ds(pl.multiple_of(i * TILE, TILE), TILE)
            at_lane = lane + i * TILE
            ok = (at_row >= starts[pl.ds(i, 1), :]) & (at_row <= at_lane)
            ok = jnp.concatenate([ok] * 4, axis=1)
            for u, slab in enumerate(slabs):
                q4 = split(q_ref[here, slab], of_qk)
                do4 = split(do_ref[here, slab], of_v)
                s = dot_nt(k_ref[there, slab], q4)
                dp = dot_nt(v_ref[there, slab], do4)
                p = jnp.exp(jnp.where(ok, s - lse_ref[u, pl.ds(i, 1), :], NEG))
                ds = (p * (dp - delta[u, pl.ds(i, 1), :])).astype(BF16)
                dv_acc[u] += dot(p.astype(BF16), do4)
                dk_acc[u] += dot(ds, q4)
                ds4 = jnp.concatenate([ds[:, h * TILE : (h + 1) * TILE] for h in range(4)], axis=0)
                dq_acc[i, u] += dot_tn(ds4, split(k_ref[there, slab], of_qk))
            return carry

        lax.fori_loop(j, bounds[tiles + j] + 1, query_tile, 0)
        for u, slab in enumerate(slabs):
            rotate_out(dk_acc[u], there, dk_ref, u * 256, 1.0)
            dv_ref[there, slab] = (0.5 * dv_acc[u]).astype(BF16)
        pltpu.make_async_copy(dk_ref.at[there, :], dk_hbm.at[there, :], store.at[0]).start()
        pltpu.make_async_copy(dv_ref.at[there, :], dv_hbm.at[there, :], store.at[1]).start()
        return carry

    lax.fori_loop(0, tiles, key_tile, 0)

    def finish_tile(i, carry):
        here = pl.ds(pl.multiple_of(i * TILE, TILE), TILE)
        for u in range(2):
            rotate_out(dq_acc[i, u], here, dq_ref, u * 256, 0.125)
        pltpu.make_async_copy(dq_ref.at[here, :], dq_hbm.at[here, :], store.at[2]).start()
        return carry

    lax.fori_loop(0, tiles, finish_tile, 0)
    for n, (src, dst) in enumerate(((dk_ref, dk_hbm), (dv_ref, dv_hbm), (dq_ref, dq_hbm))):
        pltpu.make_async_copy(src, dst, store.at[n]).wait()


def attend_back(at, bounds, q, k, v, do_own, do_other, o_own, o_other, lse, starts, cosine, sine):
    tiles = SEQ // TILE
    vmem = pl.BlockSpec(memory_space=pltpu.VMEM)
    sems = pltpu.SemaphoreType.DMA
    return pl.pallas_call(
        attend_back_kernel,
        out_shape=[jax.ShapeDtypeStruct((SEQ, 512), BF16)] * 3,
        in_specs=[pl.BlockSpec(memory_space=pltpu.SMEM)] * 2 + [any_spec()] * 7 + [vmem] * 4,
        out_specs=[any_spec()] * 3,
        scratch_shapes=[pltpu.VMEM((SEQ, 512), BF16)] * 8
        + [
            pltpu.VMEM((tiles, 2, TILE, 256), F32),
            pltpu.VMEM((2, tiles, 4 * TILE), F32),
            pltpu.VMEM((2, TILE, 256), F32),
            pltpu.VMEM((2, TILE, 256), F32),
            sems((7,)),
            sems((3,)),
        ],
        compiler_params=params(),
        cost_estimate=cost(50e9, 20e6, 1e7),
        name="attend_back",
    )(at, bounds, q, k, v, do_own, do_other, o_own, o_other, lse, starts, cosine, sine)


def mlp_kernel(at, att_own, att_other, tok, cot_here, cot_moved, gain, wo, big, *rest):
    (out, gh_out, gb_out, n2_out, hid_out, ga_own, ga_other, gg_out, cot_out) = rest[:9]
    (wg, wu, wd, sems) = rest[9:]
    step = pl.program_id(0)
    c = at[0] & 1

    @pl.when(step == 0)
    def _():
        for n, held in enumerate((wg, wu, wd)):
            for owner in range(8):
                pltpu.make_async_copy(
                    big.at[n, owner], held.at[:, owner * 128 : owner * 128 + 128], sems.at[n]
                ).start()
        gg_out[...] = jnp.zeros_like(gg_out)

    hidden = tok[0].astype(F32)
    for e, att in enumerate((att_own, att_other)):
        for u in range(2):
            hidden += dot_nt(att[:, u * 256 : u * 256 + 256], wo[0, 2 * (c ^ e) + u])
    factor = lax.rsqrt(jnp.mean(hidden * hidden, axis=1, keepdims=True) + EPSILON)
    gains = gain[...]
    normed = (hidden * factor * gains).astype(BF16)
    n2_out[...] = normed
    g = jnp.where((at[1] & 1) == c, cot_here[...], cot_moved[...])
    cot_out[...] = g

    @pl.when(step == 0)
    def _():
        for n, held in enumerate((wg, wu, wd)):
            pltpu.make_async_copy(held, held, sems.at[n]).wait()

    down = jnp.zeros_like(hidden)
    back = jnp.zeros_like(hidden)
    units = wg.shape[0]
    for low in range(0, units, 768):
        part = slice(low, min(low + 768, units))
        gate, up, grad_act = dot_nt(normed, wg[part]), dot_nt(normed, wu[part]), dot_nt(g, wd[part])
        sig = 1.0 / (1.0 + jnp.exp(-gate))
        silu = gate * sig
        act = (silu * up).astype(BF16)
        grad_up = (grad_act * silu).astype(BF16)
        grad_gate = (grad_act * up * (sig * (1.0 + gate * (1.0 - sig)))).astype(BF16)
        hid_out[0, :, part], hid_out[1, :, part], hid_out[2, :, part] = grad_gate, grad_up, act
        down += dot(act, wd[part])
        back += dot(grad_gate, wg[part]) + dot(grad_up, wu[part])
    out[...] = (hidden + down).astype(BF16)
    gg_out[...] += jnp.sum((back * hidden * factor).reshape(-1, 8, back.shape[1]), axis=0)
    scaled = back * gains
    mean = jnp.mean(scaled * hidden, axis=1, keepdims=True)
    grad_hidden = g.astype(F32) + factor * scaled - hidden * (factor * factor * factor * mean)
    gh_out[...] = grad_hidden
    branch = grad_hidden.astype(BF16)
    gb_out[...] = branch
    for e, ga in enumerate((ga_own, ga_other)):
        for u in range(2):
            ga[:, u * 256 : u * 256 + 256] = dot(branch, wo[0, 2 * (c ^ e) + u]).astype(BF16)


def mlp(at, att_own, att_other, tok, cot_here, cot_moved, gain, small, big):
    _, count, wide = tok.shape
    big = big.reshape(3, 8, -1, 128)
    rows, units = 256, big.shape[2]
    row = lambda width: pl.BlockSpec((rows, width), lambda i, at: (i, 0))
    grid = pltpu.PrefetchScalarGridSpec(
        num_scalar_prefetch=1,
        grid=(count // rows,),
        in_specs=[
            row(512),
            row(512),
            pl.BlockSpec((1, rows, wide), lambda i, at: (at[0] & 1, i, 0)),
            row(wide),
            row(wide),
            pl.BlockSpec((1, wide), lambda i, at: (0, 0)),
            once((1, 4, wide, 256), lambda i, at: (3, 0, 0, 0)),
            any_spec(),
        ],
        out_specs=[
            row(wide),
            row(wide),
            row(wide),
            row(wide),
            pl.BlockSpec((3, rows, units), lambda i, at: (0, i, 0)),
            row(512),
            row(512),
            pl.BlockSpec((8, wide), lambda i, at: (0, 0)),
            row(wide),
        ],
        scratch_shapes=[pltpu.VMEM((units, wide), BF16)] * 3 + [pltpu.SemaphoreType.DMA((3,))],
    )
    tokens = lambda width, kind=BF16: jax.ShapeDtypeStruct((count, width), kind)
    return pl.pallas_call(
        mlp_kernel,
        out_shape=[
            tokens(wide),
            tokens(wide, F32),
            tokens(wide),
            tokens(wide),
            jax.ShapeDtypeStruct((3, count, units), BF16),
            tokens(512),
            tokens(512),
            jax.ShapeDtypeStruct((8, wide), F32),
            tokens(wide),
        ],
        grid_spec=grid,
        compiler_params=params(),
        cost_estimate=cost(2 * count * wide * (6 * units + 2 * wide), 60e6, 3e6),
        name="mlp",
    )(at, att_own, att_other, tok, cot_here, cot_moved, gain, small, big)


def turn_rows(source, plane, parity, held):
    for rel in range(4):
        block = ((plane ^ rel) * 2 + parity) * 128
        held[rel * 128 : rel * 128 + 128, :] = source[:, pl.ds(pl.multiple_of(block, 128), 128)].T


def place_first(send, keep, done, lanes):
    for yr in range(2):
        keep[yr, :, lanes] = done[2 * yr]
        send[yr, :, lanes] = done[2 * yr + 1]


def place_second(send, keep, done, lanes):
    for xr in range(2):
        keep[xr, :, lanes] = done[xr]
        send[xr, :, lanes] = done[2 + xr]


def weights_kernel(n2, g, branch, hid, own, other, send1, keep1, send2, keep2, turned, given, got, out_sem, in_sem):
    step = pl.program_id(0)
    dp, t = lax.axis_index("dp"), lax.axis_index("tensor")
    c = lax.rem(dp, 2)
    plane = lax.div(dp, 2)
    n = lax.rem(step, 4)
    units = hid.shape[2] // 2

    @pl.when(step == 0)
    def _():
        barrier = pltpu.get_barrier_semaphore()
        pl.semaphore_signal(barrier, inc=1, device_id=(dp + 1 - 2 * c, t), device_id_type=MESH)
        pl.semaphore_wait(barrier, 1)

    def exchange(k):
        lanes = pl.ds(k * units, units if k < 3 else 512)
        return pltpu.make_async_remote_copy(
            src_ref=given.at[:, :, :, lanes],
            dst_ref=got.at[:, :, :, lanes],
            send_sem=out_sem.at[k],
            recv_sem=in_sem.at[k],
            device_id=(dp + 1 - 2 * c, t),
            device_id_type=MESH,
        )

    for phase, parity in ((0, 1 - c), (1, c)):
        for at_n, source in ((0, n2), (2, g), (3, branch)):

            @pl.when(step == 4 * phase + at_n)
            def _():
                x = lax.rem(plane, 2)
                y = lax.div(plane, 2)
                for rel in range(4):
                    yy, xx = (y, 1 - y)[rel // 2], (x, 1 - x)[rel % 2]
                    block = pl.multiple_of((yy * 4 + xx * 2 + parity) * 128, 128)
                    turned[rel * 128 : rel * 128 + 128, :] = source[:, pl.ds(block, 128)].T

    def heads(h):
        return jnp.where(c == h, own[...], other[...])

    @pl.when(step < 3)
    def _():
        for h in range(2):
            product = dot(turned[...], hid[0, :, h * units : h * units + units]).astype(BF16)
            given[:, h, :, pl.ds(pl.multiple_of(n * units, 128), units)] = product.reshape(4, 128, units)

    @pl.when(step == 3)
    def _():
        for h in range(2):
            product = dot(turned[...], heads(h)).astype(BF16)
            given[:, h, :, 3 * units : 3 * units + 512] = product.reshape(4, 128, 512)

    for k in range(4):

        @pl.when(step == k + 1)
        def _():
            exchange(k).start()

        @pl.when(step == k + 4)
        def _():
            exchange(k).wait_recv()

    def keep(product, h, lanes):
        done = [(product[r * 128 : r * 128 + 128] + got[r, h, :, lanes].astype(F32)).astype(BF16) for r in range(4)]
        (place_first, place_second)[h](*((send1, keep1), (send2, keep2))[h], done, lanes)

    @pl.when((step >= 4) & (step < 7))
    def _():
        for h in range(2):
            product = dot(turned[...], hid[0, :, h * units : h * units + units])
            keep(product, h, pl.ds(pl.multiple_of(n * units, 128), units))

    @pl.when(step == 7)
    def _():
        for h in range(2):
            keep(dot(turned[...], heads(h)), h, pl.ds(3 * units, 512))
        for k in range(4):
            exchange(k).wait_send()


def weights(n2, g, branch, hid, own, other):
    count, wide = n2.shape
    units = hid.shape[2] // 2
    full = lambda *shape: pl.BlockSpec(shape, lambda s: (0,) * len(shape), pipeline_mode=pl.Buffered(1))
    length = 3 * units + 512
    grid = pl.GridSpec(
        grid=(8,),
        in_specs=[
            full(count, wide),
            full(count, wide),
            full(count, wide),
            pl.BlockSpec((1, count, 2 * units), lambda s: (jnp.minimum(lax.rem(s, 4), 2), 0, 0)),
            full(count, 512),
            full(count, 512),
        ],
        out_specs=[full(2, 128, length)] * 4,
        scratch_shapes=[
            pltpu.VMEM((512, count), BF16),
            pltpu.VMEM((4, 2, 128, length), BF16),
            pltpu.VMEM((4, 2, 128, length), BF16),
            pltpu.SemaphoreType.DMA((4,)),
            pltpu.SemaphoreType.DMA((4,)),
        ],
    )
    return pl.pallas_call(
        weights_kernel,
        out_shape=[jax.ShapeDtypeStruct((2, 128, length), BF16)] * 4,
        grid_spec=grid,
        compiler_params=params(collective_id=1, has_side_effects=True),
        cost_estimate=cost(2 * count * 1024 * length * 2, 50e6),
        name="weights",
    )(n2, g, branch, hid, own, other)


def add(left, right):
    return (left.astype(F32) + right.astype(F32)).astype(BF16)


def finish_kernel(at, own, got, own_heads, got_heads, tok, got_tok, first, layer, got_layer, gate, up, down, out, query, key, value, tok_out, first_out, layer_out):
    @pl.when(pl.program_id(0) == 0)
    def _():
        part = down.shape[0]
        for n, ref in enumerate((gate, up, down, out)):
            rows = slice(n * part, n * part + ref.shape[0])
            total = own[rows, :].astype(F32)
            for d in range(3):
                total += got[d, rows, :].astype(F32)
            ref[...] = total
        heads = own_heads[...].astype(F32)
        for d in range(3):
            heads += got_heads[d].astype(F32)
        for n, ref in enumerate((query, key)):
            parts = []
            for h in range(4):
                parts += [heads[n, :, h * 32 : h * 32 + 32], heads[n, :, 128 + h * 32 : 160 + h * 32]]
            ref[...] = jnp.concatenate(parts, axis=1)
        value[...] = heads[2]

    stays = (at[0] & 1) == (at[1] & 1)
    tok_out[...] = jnp.where(stays, tok[...], got_tok[...]).astype(F32)
    first_out[...] = first[...].astype(F32)
    layer_out[...] = jnp.where(stays, layer[...], got_layer[...])


def finish(at, pieces, got, own_heads, got_heads, tok, got_tok, first, layer, got_layer, part):
    count, wide = tok.shape
    rows = 256
    row = pl.BlockSpec((rows, wide), lambda i, at: (i, 0))
    wider = pl.BlockSpec((first.shape[0] * rows // count, first.shape[1]), lambda i, at: (i, 0))
    whole = lambda *shape: pl.BlockSpec(shape, lambda i, at: (0,) * len(shape))
    shapes = [(part, 128)] * 3 + [(256, 128)] + [(128, 256)] * 3
    grid = pltpu.PrefetchScalarGridSpec(
        num_scalar_prefetch=1,
        grid=(count // rows,),
        in_specs=[
            whole(*pieces.shape),
            whole(*got.shape),
            whole(*own_heads.shape),
            whole(*got_heads.shape),
            row,
            row,
            wider,
            row,
            row,
        ],
        out_specs=[whole(*shape) for shape in shapes] + [row, wider, row],
    )
    return pl.pallas_call(
        finish_kernel,
        out_shape=[jax.ShapeDtypeStruct(shape, F32) for shape in shapes + [(count, wide), first.shape]]
        + [jax.ShapeDtypeStruct((count, wide), BF16)],
        grid_spec=grid,
        compiler_params=params(),
        cost_estimate=cost(1e6, 18e6),
        name="finish",
    )(at, pieces, got, own_heads, got_heads, tok, got_tok, first, layer, got_layer)


def tail_kernel(
    dq, dk, dv, small, normed, row, grad_hidden, keep1, got1, keep2, got2, gain, gain_two,
    first, own_pieces, got_pieces, own_heads, got_heads, tok, got_tok, sums,
    q_s, k_s, v_s, w_s, n_s, x_s, gh_s, ks1, gs1, ks2, gs2, last1, last2, pieces, gn_send, gn_got, turned,
    h_send, h_got, s1, k1, a1, a2, part1, part2, rest1, rest2, heads, held, came,
    load, f_sem, m_sem, p_sem, n_sem, c_sem, one_sem, two_sem, h_sem, swap, g_sem,
):
    dp, t = lax.axis_index("dp"), lax.axis_index("tensor")
    c, x, y = lax.rem(dp, 2), lax.rem(lax.div(dp, 2), 2), lax.div(dp, 4)
    pair, side = lax.div(t, 2), lax.rem(t, 2)
    plane = dp - c
    dpx, dpy, dpc = dp + 2 - 4 * x, dp + 4 - 8 * y, dp + 1 - 2 * c
    half = SEQ // 2
    units = (ks1.shape[2] - 512) // 3

    def copy(src, dst, sems, n, to):
        return pltpu.make_async_remote_copy(
            src_ref=src,
            dst_ref=dst,
            send_sem=sems.at[0, n],
            recv_sem=sems.at[1, n],
            device_id=to,
            device_id_type=MESH,
        )

    sources = [(keep1, ks1), (got1, gs1), (keep2, ks2), (got2, gs2), (dq, q_s), (dk, k_s), (dv, v_s)]
    sources += [(small.at[pl.ds(0, 3), pl.ds(2 * c, 2)], w_s), (normed, n_s), (row.at[c], x_s), (grad_hidden, gh_s)]
    loads = [pltpu.make_async_copy(src, dst, load.at[n]) for n, (src, dst) in enumerate(sources)]
    for item in loads:
        item.start()
    meet(plane, c, t, dpx, dpy)

    def value_copy(u):
        src = dv.at[:, pl.ds(u * 256, 256)]
        return pltpu.make_async_remote_copy(
            src_ref=src,
            dst_ref=first.at[pair],
            send_sem=f_sem.at[0, u],
            recv_sem=f_sem.at[1, pair],
            device_id=(plane + side, 2 * c + u),
            device_id_type=MESH,
        )

    def value_local(u):
        return pltpu.make_async_copy(dv.at[:, pl.ds(u * 256, 256)], first.at[pair], load.at[11])

    for u in range(2):
        stay = (side == c) & (t == 2 * c + u)

        @pl.when(stay)
        def _():
            value_local(u).start()

        @pl.when(jnp.logical_not(stay))
        def _():
            value_copy(u).start()

    for item in loads[:4]:
        item.wait()
    gs1[1] = add(ks1[1], gs1[1])
    gs2[1] = add(ks2[1], gs2[1])
    seconds = [copy(gs1.at[1], last1, m_sem, 0, (dpy, t)), copy(gs2.at[1], last2, m_sem, 1, (dpx, t))]
    for item in loads[4:8]:
        item.wait()
    for item in seconds:
        item.start()

    def back_product(rows):
        total = None
        for u in range(2):
            for n, grad in enumerate((q_s, k_s, v_s)):
                term = dot_nt(grad[rows, u * 256 : u * 256 + 256], w_s[n, u])
                total = term if total is None else total + term
        return total

    ns = []
    for i in range(2):
        rows = pl.ds(pl.multiple_of((1 - c) * half + i * 512, 512), 512)
        gn_send[i] = back_product(rows).astype(BF16)
        ns.append(copy(gn_send.at[i], gn_got.at[i], n_sem, i, (dpc, t)))

    def turn(parity):
        for rel in range(4):
            yy, xx = (y, 1 - y)[rel // 2], (x, 1 - x)[rel % 2]
            block = pl.multiple_of((yy * 4 + xx * 2 + parity) * 128, 128)
            turned[rel * 128 : rel * 128 + 128, :] = n_s[:, pl.ds(block, 128)].T

    loads[8].wait()
    turn(1 - c)
    for item in ns:
        item.start()
    cs = []
    for n, right in enumerate((q_s, k_s, v_s)):
        product = dot(turned[...], right[...]).astype(BF16)
        lanes = slice(n * 512, n * 512 + 512)
        place_second(h_send.at[0], h_send.at[1], [product[r * 128 : r * 128 + 128] for r in range(4)], lanes)
        cs.append(copy(h_send.at[:, :, :, pl.ds(n * 512, 512)], h_got.at[:, :, :, pl.ds(n * 512, 512)], c_sem, n, (dpc, t)))
        if n:
            cs[n - 1].start()
    turn(c)
    cs[2].start()
    for n, right in enumerate((q_s, k_s, v_s)):
        product = dot(turned[...], right[...]).astype(BF16)
        lanes = slice(n * 512, n * 512 + 512)
        place_first(s1, k1, [product[r * 128 : r * 128 + 128] for r in range(4)], lanes)
    for item in cs:
        item.wait_recv()
    ones = [copy(h_got.at[0], a2, one_sem, 1, (dpy, t)), copy(s1, a1, one_sem, 0, (dpx, t))]
    for item in ones:
        item.start()

    for item in seconds:
        item.wait_recv()
    part = units // 4
    for h, (kept, got, last) in enumerate(((ks1, gs1, last1), (ks2, gs2, last2))):
        for n in range(4):
            lanes = slice(n * units, n * units + (units if n < 3 else 512))
            total = kept[0, :, lanes].astype(F32) + got[0, :, lanes].astype(F32) + last[:, lanes].astype(F32)
            flipped = total.T.astype(BF16)
            if n < 3:
                for i in range(4):
                    rows = slice((2 * n + h) * part, (2 * n + h + 1) * part)
                    pieces[lax.rem(i + 4 - t, 4), rows, :] = flipped[i * part : (i + 1) * part]
            else:
                for i in range(2):
                    pieces[lax.rem(2 * h + i + 4 - t, 4), 6 * part :, :] = flipped[i * 256 : i * 256 + 256]
    own_pieces[...] = pieces[0]
    zs = [copy(pieces.at[d], got_pieces.at[d - 1], p_sem, d - 1, (dp, lax.rem(t + d, 4))) for d in (1, 2, 3)]
    for item in zs:
        item.start()

    for item in loads[9:11]:
        item.wait()
    moved = side != c
    gained = jnp.zeros((8, tok.shape[2]), F32)
    for i in range(2):
        ns[i].wait_recv()
        rows = pl.ds(pl.multiple_of(c * half + i * 512, 512), 512)
        here = slice(i * 512, i * 512 + 512)
        grad = back_product(rows) + gn_got[i].astype(F32)
        values = x_s[here, :].astype(F32)
        factor = lax.rsqrt(jnp.mean(values * values, axis=1, keepdims=True) + EPSILON)
        gained += jnp.sum((grad * values * factor).reshape(-1, 8, grad.shape[1]), axis=0)
        scaled = grad * gain[...]
        mean = jnp.mean(scaled * values, axis=1, keepdims=True)
        tok[i] = (gh_s[here, :] + factor * scaled - values * (factor * factor * factor * mean)).astype(BF16)
    swaps = [copy(tok.at[i], got_tok.at[i], swap, i, (plane + side, 2 * pair + c)) for i in range(2)]

    for item in ones:
        item.wait_recv()
    part1[...] = add(k1[1], a1[1])
    part2[...] = add(h_got[1, 1], a2[1])

    @pl.when(moved)
    def _():
        for item in swaps:
            item.start()

    twos = [copy(part1, rest1, two_sem, 0, (dpy, t)), copy(part2, rest2, two_sem, 1, (dpx, t))]
    for item in twos:
        item.start()

    turns = (dpc, t), (dpx, t), (dpy, t), (dp, t + 1 - 2 * side), (dp, lax.rem(t + 2, 4))
    line = lax.broadcasted_iota(jnp.int32, gained.shape, 0)
    total_one = jnp.sum(gained, axis=0, keepdims=True)
    total_two = jnp.sum(gain_two[...], axis=0, keepdims=True)
    held[0] = jnp.where(line == 0, total_one, jnp.where(line == 1, total_two, 0.0))

    def gain_step(n):
        return copy(held.at[n], came.at[n], g_sem, n, turns[n])

    def gain_next(n):
        gain_step(n).wait_recv()
        held[n + 1] = held[n] + came[n]

    total1 = k1[0].astype(F32) + a1[0].astype(F32)
    total2 = h_got[1, 0].astype(F32) + a2[0].astype(F32)
    gain_step(0).start()
    gain_next(0)
    gain_step(1).start()
    gain_next(1)
    for item in twos:
        item.wait_recv()
    totals = ((total1 + rest1[...].astype(F32)).astype(BF16), (total2 + rest2[...].astype(F32)).astype(BF16))
    for e, total in enumerate(totals):
        core = (c, 1 - c)[e]
        for u in range(2):
            d = lax.rem(2 * core + u + 4 - t, 4)
            for n in range(3):
                heads[d, n] = total[:, n * 512 + u * 256 : n * 512 + u * 256 + 256]
    gain_step(2).start()
    gain_next(2)
    own_heads[...] = heads[0]
    hs = [copy(heads.at[d], got_heads.at[d - 1], h_sem, d - 1, (dp, lax.rem(t + d, 4))) for d in (1, 2, 3)]
    for item in hs:
        item.start()
    for n in (3, 4):
        gain_step(n).start()
        gain_next(n)
    sums[...] = held[5]

    for item in seconds + ns + cs + ones + twos:
        item.wait_send()
    for n in range(5):
        gain_step(n).wait_send()
    for u in range(2):
        stay = (side == c) & (t == 2 * c + u)

        @pl.when(stay)
        def _():
            value_local(u).wait()

        @pl.when(jnp.logical_not(stay))
        def _():
            value_copy(u).wait_send()

    for p in range(2):

        @pl.when((pair != c) | (t != 2 * p + c))
        def _():
            pltpu.make_async_remote_copy(
                src_ref=first.at[p],
                dst_ref=first.at[p],
                send_sem=f_sem.at[0, p],
                recv_sem=f_sem.at[1, p],
                device_id=(dpc, t),
                device_id_type=MESH,
            ).wait_recv()

    for item in zs + hs:
        item.wait()

    @pl.when(moved)
    def _():
        for item in swaps:
            item.wait()


def tail(dq, dk, dv, small, normed, row, grad_hidden, keep1, got1, keep2, got2, gain, gain_two):
    vmem = pl.BlockSpec(memory_space=pltpu.VMEM)
    sems = pltpu.SemaphoreType.DMA
    wide = normed.shape[1]
    length = keep1.shape[2]
    rows = (length - 512) // 2 + 256
    half = SEQ // 2
    low = lambda *shape: pltpu.VMEM(shape, BF16)
    return pl.pallas_call(
        tail_kernel,
        out_shape=[
            jax.ShapeDtypeStruct((2, SEQ, 256), BF16),
            jax.ShapeDtypeStruct((rows, 128), BF16),
            jax.ShapeDtypeStruct((3, rows, 128), BF16),
            jax.ShapeDtypeStruct((3, 128, 256), BF16),
            jax.ShapeDtypeStruct((3, 3, 128, 256), BF16),
            jax.ShapeDtypeStruct((2, half // 2, wide), BF16),
            jax.ShapeDtypeStruct((2, half // 2, wide), BF16),
            jax.ShapeDtypeStruct((8, wide), F32),
        ],
        in_specs=[any_spec()] * 11 + [vmem] * 2,
        out_specs=[any_spec(), vmem, any_spec(), vmem, any_spec(), vmem, any_spec(), vmem],
        scratch_shapes=[low(SEQ, 512)] * 3
        + [low(3, 2, wide, 256), low(SEQ, wide), low(half, wide), pltpu.VMEM((half, wide), F32)]
        + [low(2, 128, length)] * 4
        + [low(128, length)] * 2
        + [low(4, rows, 128), low(2, half // 2, wide), low(2, half // 2, wide), low(512, SEQ)]
        + [low(2, 2, 128, 1536)] * 2
        + [low(2, 128, 1536)] * 4
        + [low(128, 1536)] * 4
        + [low(4, 3, 128, 256), pltpu.VMEM((6, 8, wide), F32), pltpu.VMEM((5, 8, wide), F32)]
        + [sems((12,)), sems((2, 2)), sems((2, 2)), sems((2, 3)), sems((2, 2)), sems((2, 3)), sems((2, 2)), sems((2, 2))]
        + [sems((2, 3)), sems((2, 2)), sems((2, 5))],
        compiler_params=params(collective_id=2, has_side_effects=True),
        name="tail",
    )(dq, dk, dv, small, normed, row, grad_hidden, keep1, got1, keep2, got2, gain, gain_two)


def fast_body(tokens, first_values, doc_lengths, cotangent, w_query, w_key, w_value, w_out, w_gate, w_up, w_down, gain_attn, gain_mlp):
    me, t = lax.axis_index("dp"), lax.axis_index("tensor")
    c = me % 2
    pair, side = t // 2, t % 2
    wide = tokens.shape[1]
    tiles = SEQ // TILE
    at = jnp.where(jnp.arange(8, dtype=jnp.int32) == 0, me, t).astype(jnp.int32)

    small_shard, big_shard = pack(w_query, w_key, w_value, w_out, w_gate, w_up, w_down)
    lengths = jnp.where(c == side, doc_lengths, across_c(doc_lengths))
    lengths = lax.dynamic_index_in_dim(lengths, pair, 0, keepdims=False)
    order = jnp.arange(DOCS, dtype=jnp.int32)
    ends = jnp.sum(jnp.where(order[None, :] <= order[:, None], lengths[None, :], 0), axis=1)
    freqs = 10000.0 ** (-(jnp.arange(32, dtype=F32) * 2.0 / HEAD))
    row, small, big, normed_one, q, k, v, cosine, sine = gather(
        ends, tokens, first_values, small_shard, big_shard, gain_attn[None], jnp.tile(freqs, 4)[None]
    )
    places = jnp.arange(SEQ, dtype=jnp.int32)
    starts = jnp.max(jnp.where(ends[None, :] <= places[:, None], ends[None, :], 0), axis=1)
    last = jnp.arange(tiles, dtype=jnp.int32) * TILE + (TILE - 1)
    stop = jnp.min(jnp.where(ends[None, :] > last[:, None], ends[None, :], SEQ), axis=1)
    bounds = jnp.concatenate([starts.reshape(tiles, TILE)[:, 0] // TILE, (stop - 1) // TILE])
    starts_by_tile = starts.reshape(tiles, TILE)

    row, cotangent = lax.optimization_barrier((row, cotangent))
    moved_cot = swap_halves(cotangent)
    att_own, att_send, lse = attend(at, bounds, q, k, v, starts_by_tile)
    att_other = across_c(att_send)
    out, grad_hidden, branch, normed_two, hid, ga_own, ga_other, gain_two, cot = mlp(
        at, att_own, att_other, row, cotangent, moved_cot, gain_mlp[None], small, big
    )
    moved_out = swap_halves(out)

    ga_got = across_c(ga_other)

    kept = weights(normed_two, cot, branch, hid, att_own, att_other)
    kept, ga_got = lax.optimization_barrier((kept, ga_got))
    got1, got2 = across_x(kept[0]), across_y(kept[2])

    dq, dk, dv = attend_back(
        at, bounds, q, k, v, ga_own, ga_got, att_own, att_send, lse, starts_by_tile, cosine, sine
    )

    first_back, pieces, got, own_heads, got_heads, grad_tokens, got_tokens, gains = tail(
        dq, dk, dv, small, normed_one, row, grad_hidden, kept[1], got1, kept[3], got2, gain_attn[None], gain_two
    )
    shape = (SEQ // 2, wide)
    grad_gate, grad_up, grad_down, grad_out, gq, gk, gv, grad_tokens, grad_first, layer_out = finish(
        at, pieces, got, own_heads, got_heads, grad_tokens.reshape(shape), got_tokens.reshape(shape), first_back.reshape(2 * SEQ, 256), out, moved_out, w_gate.shape[1]
    )
    return (
        layer_out,
        grad_tokens,
        grad_first,
        gq,
        gk,
        gv,
        grad_out,
        grad_gate.T,
        grad_up.T,
        grad_down,
        gains[0],
        gains[1],
    )


def solution(mesh):
    fits = dict(mesh.shape) == {"dp": 8, "tensor": 4}
    placed = (
        P(("dp", "tensor"), None),
        P("dp", "tensor"),
        P("dp", None),
        P(("dp", "tensor"), None),
        P("dp", "tensor"),
        P("dp", "tensor"),
        P("dp", "tensor"),
        P("tensor", "dp"),
        P("dp", "tensor"),
        P("dp", "tensor"),
        P("tensor", "dp"),
        P(),
        P(),
    )
    return jax.shard_map(
        fast_body if fits else general_body,
        mesh=mesh,
        in_specs=placed,
        out_specs=(
            P(("dp", "tensor"), None),
            P(("dp", "tensor"), None),
            P("dp", "tensor"),
            P("dp", "tensor"),
            P("dp", "tensor"),
            P("dp", "tensor"),
            P("tensor", "dp"),
            P("dp", "tensor"),
            P("dp", "tensor"),
            P("tensor", "dp"),
            P(),
            P(),
        ),
        check_vma=False,
    )
```

```python
import functools

import jax
import jax.numpy as jnp
from jax import lax
from jax.experimental import pallas as pl
from jax.experimental.pallas import tpu as pltpu
from jax.sharding import PartitionSpec as P

HEAD = 64
SEQ = 2048
DOCS = 8
EPSILON = 1e-05


def rms_norm(values, gain):
    factor = lax.rsqrt(jnp.mean(values * values, axis=1, keepdims=True) + EPSILON)
    return values * factor * gain


def documents(doc_lengths):
    ends = jnp.cumsum(doc_lengths, axis=1)
    starts = ends - doc_lengths
    places = jnp.arange(SEQ, dtype=jnp.int32)
    segment = jnp.sum((places[None, :, None] >= ends[:, None, :]).astype(jnp.int32), axis=2)
    member = segment[:, :, None] == jnp.arange(DOCS, dtype=jnp.int32)[None, None, :]
    offset = jnp.sum(jnp.where(member, starts[:, None, :], 0), axis=2)
    return (segment, (places[None, :] - offset).astype(jnp.float32))


def rotation(positions):
    half = HEAD // 2
    freqs = 10000.0 ** (-(jnp.arange(half, dtype=jnp.float32) * 2.0 / HEAD))
    angles = positions[:, None] * freqs[None, :]
    return (jnp.cos(angles), jnp.sin(angles))


def rotate(values, cosine, sine):
    shaped = values.reshape(values.shape[0], -1, HEAD)
    half = HEAD // 2
    first = shaped[:, :, :half]
    second = shaped[:, :, half:]
    cos_rows = cosine[:, None, :]
    sin_rows = sine[:, None, :]
    turned = jnp.concatenate(
        [first * cos_rows - second * sin_rows, second * cos_rows + first * sin_rows], axis=2
    )
    return turned.reshape(values.shape)


def rotate_back(grads, cosine, sine):
    shaped = grads.reshape(grads.shape[0], -1, HEAD)
    half = HEAD // 2
    first = shaped[:, :, :half]
    second = shaped[:, :, half:]
    cos_rows = cosine[:, None, :]
    sin_rows = sine[:, None, :]
    turned = jnp.concatenate(
        [first * cos_rows + second * sin_rows, second * cos_rows - first * sin_rows], axis=2
    )
    return turned.reshape(grads.shape)


def swiglu(gate, up_val):
    return jax.nn.silu(gate) * up_val


def product(left, right):
    return jnp.dot(left, right, preferred_element_type=jnp.float32)


def inner(left, right):
    return lax.dot_general(
        left, right, (((0,), (0,)), ((), ())), preferred_element_type=jnp.float32
    )


def outer(left, right):
    return lax.dot_general(
        left, right, (((1,), (1,)), ((), ())), preferred_element_type=jnp.float32
    )


def block_scores(queries, keys_all, segment, start, width):
    query_block = lax.dynamic_slice_in_dim(queries, start, width, 0)
    query_seg = lax.dynamic_slice_in_dim(segment, start, width, 0)
    scores = (
        jnp.einsum("qhd,khd->hqk", query_block, keys_all, preferred_element_type=jnp.float32)
        * 0.125
    )
    places = jnp.arange(SEQ, dtype=jnp.int32)
    rows_at = start + jnp.arange(width, dtype=jnp.int32)
    allowed = (query_seg[:, None] == segment[None, :]) & (places[None, :] <= rows_at[:, None])
    return (query_block, jnp.where(allowed[None], scores, -1e30))


def forward_row(pieces):
    queries, keys_all, values_all, segment = pieces
    width = min(512, SEQ)
    count = SEQ // width

    def forward_one_block(index):
        unused, scores = block_scores(queries, keys_all, segment, index * width, width)
        top = jnp.max(scores, axis=2, keepdims=True)
        expo = jnp.exp(scores - top)
        total = jnp.sum(expo, axis=2, keepdims=True)
        weights = (expo / total).astype(jnp.bfloat16)
        result = jnp.einsum("hqk,khd->qhd", weights, values_all, preferred_element_type=jnp.float32)
        return (result, (top + jnp.log(total))[:, :, 0])

    results, logsums = lax.map(forward_one_block, jnp.arange(count, dtype=jnp.int32))
    return (results.reshape(SEQ, queries.shape[1], HEAD), logsums)


def backward_row(pieces):
    queries, keys_all, values_all, segment, grad_rows, logsums = pieces
    width = min(512, SEQ)
    count = SEQ // width

    def backward_one_block(carry, extra):
        index, logsum = extra
        start = index * width
        query_block, scores = block_scores(queries, keys_all, segment, start, width)
        probs = jnp.exp(scores - logsum[:, :, None])
        grad_block = lax.dynamic_slice_in_dim(grad_rows, start, width, 0)
        grad_probs = jnp.einsum(
            "qhd,khd->hqk", grad_block, values_all, preferred_element_type=jnp.float32
        )
        delta = jnp.sum(probs * grad_probs, axis=2, keepdims=True)
        grad_scores = (probs * (grad_probs - delta)).astype(jnp.bfloat16)
        grad_query = (
            jnp.einsum("hqk,khd->qhd", grad_scores, keys_all, preferred_element_type=jnp.float32)
            * 0.125
        )
        grad_keys = (
            carry[0]
            + jnp.einsum(
                "hqk,qhd->khd", grad_scores, query_block, preferred_element_type=jnp.float32
            )
            * 0.125
        )
        grad_values = carry[1] + jnp.einsum(
            "hqk,qhd->khd",
            probs.astype(jnp.bfloat16),
            grad_block,
            preferred_element_type=jnp.float32,
        )
        return ((grad_keys, grad_values), grad_query)

    zeros = jnp.zeros(keys_all.shape, jnp.float32)
    sums, grad_queries = lax.scan(
        backward_one_block, (zeros, zeros), (jnp.arange(count, dtype=jnp.int32), logsums)
    )
    return (grad_queries.reshape(SEQ, queries.shape[1], HEAD), sums[0], sums[1])


def general_body(
    tokens,
    first_values,
    doc_lengths,
    cotangent,
    w_query,
    w_key,
    w_value,
    w_out,
    w_gate,
    w_up,
    w_down,
    gain_attn,
    gain_mlp,
):
    query_mat, key_mat, value_mat, out_mat, gate_mat, up_mat, down_mat = (
        lax.all_gather(w_query, "dp", axis=0, tiled=True),
        lax.all_gather(w_key, "dp", axis=0, tiled=True),
        lax.all_gather(w_value, "dp", axis=0, tiled=True),
        lax.all_gather(w_out, "dp", axis=1, tiled=True),
        lax.all_gather(w_gate, "dp", axis=0, tiled=True),
        lax.all_gather(w_up, "dp", axis=0, tiled=True),
        lax.all_gather(w_down, "dp", axis=1, tiled=True),
    )
    local_heads = query_mat.shape[1] // HEAD
    row_count = doc_lengths.shape[0]
    group = row_count * SEQ
    segment, positions = documents(doc_lengths)
    cosine, sine = rotation(positions.reshape(-1))

    def heads(matrix):
        return matrix.reshape(row_count, SEQ, local_heads, HEAD)

    inputs = tokens.astype(jnp.float32)
    normed_one, norm_one_back = jax.vjp(rms_norm, inputs, gain_attn)
    gathered_one = lax.all_gather(normed_one.astype(jnp.bfloat16), "tensor", axis=0, tiled=True)
    query_raw = product(gathered_one, query_mat)
    key_raw = product(gathered_one, key_mat)
    value_raw = product(gathered_one, value_mat)
    queries = rotate(query_raw, cosine, sine).astype(jnp.bfloat16)
    keys_low = rotate(key_raw, cosine, sine).astype(jnp.bfloat16)
    mixed_values = (0.5 * value_raw + 0.5 * first_values.astype(jnp.float32)).astype(jnp.bfloat16)
    attended, logsums = lax.map(
        forward_row, (heads(queries), heads(keys_low), heads(mixed_values), segment)
    )
    attended_low = attended.reshape(group, -1).astype(jnp.bfloat16)
    hidden_in = inputs + lax.psum_scatter(
        product(attended_low, out_mat), "tensor", scatter_dimension=0, tiled=True
    )
    normed_two, norm_two_back = jax.vjp(rms_norm, hidden_in, gain_mlp)
    normed_low_two = normed_two.astype(jnp.bfloat16)
    grad_out = cotangent.astype(jnp.float32)
    gathered_two = lax.all_gather(normed_low_two, "tensor", axis=0, tiled=True)
    activated, swiglu_back = jax.vjp(
        swiglu, product(gathered_two, gate_mat), product(gathered_two, up_mat)
    )
    act_low = activated.astype(jnp.bfloat16)
    layer_out = hidden_in + lax.psum_scatter(
        product(act_low, down_mat).astype(jnp.bfloat16), "tensor", scatter_dimension=0, tiled=True
    ).astype(jnp.float32)
    grad_rows = lax.all_gather(cotangent, "tensor", axis=0, tiled=True)
    grad_gate, grad_up = swiglu_back(outer(grad_rows, down_mat))
    gate_low = grad_gate.astype(jnp.bfloat16)
    up_low = grad_up.astype(jnp.bfloat16)
    grad_normed_two = lax.psum_scatter(
        outer(gate_low, gate_mat) + outer(up_low, up_mat), "tensor", scatter_dimension=0, tiled=True
    )
    grad_gate_mat = inner(gathered_two, gate_low)
    grad_up_mat = inner(gathered_two, up_low)
    grad_down_mat = inner(act_low, grad_rows)
    grad_hidden_two, grad_gain_two = norm_two_back(grad_normed_two)
    grad_hidden = grad_out + grad_hidden_two
    grad_branch = lax.all_gather(grad_hidden.astype(jnp.bfloat16), "tensor", axis=0, tiled=True)
    grad_attended = outer(grad_branch, out_mat).astype(jnp.bfloat16)
    grad_out_mat = inner(attended_low, grad_branch)
    grad_rot_query, grad_rot_key, grad_mixed = lax.map(
        backward_row,
        (
            heads(queries),
            heads(keys_low),
            heads(mixed_values),
            segment,
            heads(grad_attended),
            logsums,
        ),
    )
    grad_query_low = rotate_back(grad_rot_query.reshape(group, -1), cosine, sine).astype(
        jnp.bfloat16
    )
    grad_key_low = rotate_back(grad_rot_key.reshape(group, -1), cosine, sine).astype(jnp.bfloat16)
    grad_first = 0.5 * grad_mixed.reshape(group, -1)
    grad_value_low = grad_first.astype(jnp.bfloat16)
    grad_normed_one = lax.psum_scatter(
        outer(grad_query_low, query_mat)
        + outer(grad_key_low, key_mat)
        + outer(grad_value_low, value_mat),
        "tensor",
        scatter_dimension=0,
        tiled=True,
    )
    grad_query_mat = inner(gathered_one, grad_query_low)
    grad_key_mat = inner(gathered_one, grad_key_low)
    grad_value_mat = inner(gathered_one, grad_value_low)
    grad_inputs_one, grad_gain_one = norm_one_back(grad_normed_one)
    grad_tokens = grad_hidden + grad_inputs_one
    summed = (
        lax.psum_scatter(grad_query_mat, "dp", scatter_dimension=0, tiled=True),
        lax.psum_scatter(grad_key_mat, "dp", scatter_dimension=0, tiled=True),
        lax.psum_scatter(grad_value_mat, "dp", scatter_dimension=0, tiled=True),
        lax.psum_scatter(grad_out_mat, "dp", scatter_dimension=1, tiled=True),
        lax.psum_scatter(grad_gate_mat, "dp", scatter_dimension=0, tiled=True),
        lax.psum_scatter(grad_up_mat, "dp", scatter_dimension=0, tiled=True),
        lax.psum_scatter(grad_down_mat, "dp", scatter_dimension=1, tiled=True),
    )
    gain_sums = lax.psum((grad_gain_one, grad_gain_two), ("dp", "tensor"))
    return (
        layer_out.astype(jnp.bfloat16),
        grad_tokens,
        grad_first,
        summed[0],
        summed[1],
        summed[2],
        summed[3],
        summed[4],
        summed[5],
        summed[6],
        gain_sums[0],
        gain_sums[1],
    )


AXES = ("dp", "tensor")
MESH = pl.DeviceIdType.MESH
TILE = 256
NEG = -1e30
F32 = jnp.float32
BF16 = jnp.bfloat16


def flat(y, x, c, t):
    return ((y * 2 + x) * 2 + c) * 4 + t


def move(values, to):
    pairs = []
    for y in range(2):
        for x in range(2):
            for c in range(2):
                for t in range(4):
                    pair = (flat(y, x, c, t), flat(*to(y, x, c, t)))
                    if pair[0] != pair[1]:
                        pairs.append(pair)
    return lax.ppermute(values, AXES, pairs)


def across_x(values):
    return move(values, lambda y, x, c, t: (y, 1 - x, c, t))


def across_y(values):
    return move(values, lambda y, x, c, t: (1 - y, x, c, t))


def across_c(values):
    return move(values, lambda y, x, c, t: (y, x, 1 - c, t))


def along_t(values, step):
    return move(values, lambda y, x, c, t: (y, x, c, (t + step) % 4))


def swap_halves(values):
    return move(values, lambda y, x, c, t: (y, x, t % 2, (t // 2) * 2 + c))


def pack_kernel(wq, wk, wv, wo, wg, wu, wd, halves, small, big):
    small[0] = dot(wq[...], halves[...]).astype(BF16)
    small[1] = dot(wk[...], halves[...]).astype(BF16)
    small[2] = wv[...]
    small[3] = wo[...].T
    for n, units in enumerate((wg, wu, wd)):
        big[n] = units[...].reshape(big.shape[1:])


def pack(wq, wk, wv, wo, wg, wu, wd):
    wg, wu = wg.T, wu.T
    part, rows = wg.shape
    lane = jnp.arange(256, dtype=jnp.int32)
    source = ((lane & 127) >> 5) * 64 + (lane >> 7) * 32 + (lane & 31)
    halves = (lane[:, None] == source[None, :]).astype(BF16)
    return pl.pallas_call(
        pack_kernel,
        out_shape=[
            jax.ShapeDtypeStruct((4, rows, 256), BF16),
            jax.ShapeDtypeStruct((3, 2, part // 2, rows), BF16),
        ],
        compiler_params=params(),
        name="pack",
    )(wq, wk, wv, wo, wg, wu, wd, halves)


def meet(plane, c, t, dpx, dpy):
    barrier = pltpu.get_barrier_semaphore()
    for e in range(2):
        for d in range(4):
            if e or d:
                other = plane + lax.rem(c + e, 2)
                pl.semaphore_signal(barrier, inc=1, device_id=(other, lax.rem(t + d, 4)), device_id_type=MESH)
    pl.semaphore_signal(barrier, inc=1, device_id=(dpx, t), device_id_type=MESH)
    pl.semaphore_signal(barrier, inc=1, device_id=(dpy, t), device_id_type=MESH)
    pl.semaphore_wait(barrier, 9)


def gather_kernel(
    ends, tok, fv, small, big, gain, freqs, row_out, g_small, g_big, normed_out, q_out, k_out, v_out, cos_out, sin_out,
    row, first, w_s, n_s, q_s, k_s, v_s, raw_s, cos_s, sin_s,
    send, recv, relay_send, along_recv, next_send, next_recv, swap, fsend, frecv, here, tile_sem, end_sem,
):
    dp, t = lax.axis_index("dp"), lax.axis_index("tensor")
    c, x, y = lax.rem(dp, 2), lax.rem(lax.div(dp, 2), 2), lax.div(dp, 4)
    pair, side = lax.div(t, 2), lax.rem(t, 2)
    plane = dp - c
    dpx, dpy, dpc = dp + 2 - 4 * x, dp + 4 - 8 * y, dp + 1 - 2 * c
    dpxy = dpx + 4 - 8 * y

    meet(plane, c, t, dpx, dpy)
    def slot(k, at, owner, h):
        if k == 0:
            return g_small.at[pl.ds(2 * h, 2), at, pl.ds(owner * 128, 128), :]
        return g_big.at[k - 1, owner, h, at]

    def column(k, owner, h):
        if k == 0:
            return g_small.at[pl.ds(2 * h, 2), :, pl.ds(owner * 128, 128), :]
        return g_big.at[k - 1, owner, h]

    def both(k, at, owner):
        if k == 0:
            return g_small.at[:, at, pl.ds(owner * 128, 128), :]
        return g_big.at[k - 1, owner, :, at]

    def all_of(k, owner):
        if k == 0:
            return g_small.at[:, :, pl.ds(owner * 128, 128), :]
        return g_big.at[k - 1, owner]

    def shard(k):
        return small if k == 0 else big.at[k - 1]

    def part_of(k, h):
        return small.at[pl.ds(2 * h, 2)] if k == 0 else big.at[k - 1, h]

    def copy(k, n, src, dst, to, at):
        return pltpu.make_async_remote_copy(
            src_ref=src,
            dst_ref=dst,
            send_sem=send.at[k, n],
            recv_sem=recv.at[k, n],
            device_id=(to, at),
            device_id_type=MESH,
        )

    chunks = 4
    near, far = (dpx, dpy), (dpy, dpx)
    kept = [pltpu.make_async_copy(shard(k), both(k, t, dp), here.at[k]) for k in range(chunks)]

    def relay(k, at, side, src):
        return pltpu.make_async_remote_copy(
            src_ref=src,
            dst_ref=both(k, at, dp),
            send_sem=relay_send.at[k, at, side],
            recv_sem=along_recv.at[k, at],
            device_id=(dp, t + 2 * side - 1),
            device_id_type=MESH,
        )

    def onward(k, at, h, src):
        return pltpu.make_async_remote_copy(
            src_ref=src,
            dst_ref=slot(k, at, dp, h),
            send_sem=next_send.at[k, at, h],
            recv_sem=next_recv.at[k, at, h],
            device_id=(near[h], t),
            device_id_type=MESH,
        )

    def start_along(k):
        @pl.when(t < 3)
        def _():
            relay(k, t, 1, shard(k)).start()

        @pl.when(t > 0)
        def _():
            relay(k, t, 0, shard(k)).start()

    def pass_along(k, level):
        for side, at in ((1, t - level), (0, t + level)):

            @pl.when((at >= 0) & (at < 4))
            def _():
                block = both(k, at, dp)
                move = relay(k, at, side, block)
                move.wait_recv()

                @pl.when((t < 3) if side else (t > 0))
                def _():
                    move.start()

                for h in range(2):
                    onward(k, at, h, slot(k, at, dp, h)).start()

    def end_along(k):
        for level in range(4):
            for side, at in ((1, t - level), (0, t + level)):

                @pl.when((at >= 0) & (at < 4) & ((t < 3) if side else (t > 0)))
                def _():
                    relay(k, at, side, both(k, at, dp)).wait_send()

    across = [
        [
            copy(k, 2 * h + i, column(k, owner, h), column(k, owner, h), far[h], t)
            for h in range(2)
            for i, owner in enumerate((dp, near[h]))
        ]
        for k in range(chunks)
    ]
    over = [
        [copy(k, 4 + i, all_of(k, owner), all_of(k, owner), dpc, t) for i, owner in enumerate((dp, dpx, dpy, dpxy))]
        for k in range(chunks)
    ]

    order = (1, 0, 2, 3)
    start_along(order[0])
    for item in kept:
        item.start()
    for k in order:
        for h in range(2):
            onward(k, t, h, part_of(k, h)).start()
        if k == order[0]:
            start_along(order[1])

    moved = side != c
    to_own = pltpu.make_async_copy(tok, row.at[c], here.at[4])
    swapped = pltpu.make_async_remote_copy(
        src_ref=tok,
        dst_ref=row.at[side],
        send_sem=swap.at[0],
        recv_sem=swap.at[1],
        device_id=(plane + side, 2 * pair + c),
        device_id_type=MESH,
    )

    def start_tokens():
        @pl.when(moved)
        def _():
            swapped.start()

        @pl.when(jnp.logical_not(moved))
        def _():
            to_own.start()

    heads_core, slab = pair, side

    def first_copy(p):
        return pltpu.make_async_remote_copy(
            src_ref=fv.at[pl.ds(p * SEQ, SEQ), :],
            dst_ref=first.at[slab],
            send_sem=fsend.at[p],
            recv_sem=frecv.at[slab],
            device_id=(plane + heads_core, 2 * p + c),
            device_id_type=MESH,
        )

    def first_local(p):
        return pltpu.make_async_copy(fv.at[pl.ds(p * SEQ, SEQ), :], first.at[slab], here.at[5])

    stays = [(heads_core == c) & (t == 2 * p + c) for p in range(2)]

    def start_first():
        for p in range(2):

            @pl.when(stays[p])
            def _():
                first_local(p).start()

            @pl.when(jnp.logical_not(stays[p]))
            def _():
                first_copy(p).start()

    def pass_over(k):
        for item in across[k]:
            item.wait_recv()
        for item in over[k][1:]:
            item.start()

    def pass_next(k):
        for at in range(4):
            for h in range(2):
                onward(k, at, h, slot(k, at, dp, h)).wait_recv()
        for item in across[k]:
            item.start()

    for i in range(8):
        rows = slice(i * TILE, i * TILE + TILE)
        at_row = lax.broadcasted_iota(jnp.int32, (TILE, 128), 0) + i * TILE
        begin = jnp.zeros_like(at_row)
        for k in range(DOCS):
            begin = jnp.maximum(begin, jnp.where(at_row >= ends[k], ends[k], 0))
        angles = (at_row - begin).astype(F32) * freqs[...]
        cos_s[rows, :] = jnp.cos(angles)
        sin_s[rows, :] = jnp.sin(angles)
    tables = [pltpu.make_async_copy(cos_s, cos_out, end_sem.at[0]), pltpu.make_async_copy(sin_s, sin_out, end_sem.at[1])]

    for i, k in enumerate(order):
        pass_along(k, 1)
        if i + 2 < chunks:
            start_along(order[i + 2])
        if i:
            pass_next(order[i - 1])
        pass_along(k, 2)
        pass_along(k, 3)
        kept[k].wait()
        over[k][0].start()
        if i == 2:
            start_tokens()
        if i == 3:
            start_first()
        if i >= 2:
            pass_over(order[i - 2])
    pass_next(order[3])
    for item in tables:
        item.start()
    for item in over[0]:
        item.wait_recv()
    load_w = pltpu.make_async_copy(g_small.at[pl.ds(0, 3), pl.ds(2 * c, 2)], w_s, end_sem.at[2])
    load_w.start()

    @pl.when(moved)
    def _():
        swapped.wait_send()
        swapped.wait_recv()

    @pl.when(jnp.logical_not(moved))
    def _():
        to_own.wait()

    given = pltpu.make_async_remote_copy(
        src_ref=row.at[c],
        dst_ref=row.at[c],
        send_sem=swap.at[2],
        recv_sem=swap.at[3],
        device_id=(dpc, t),
        device_id_type=MESH,
    )
    given.start()
    load_w.wait()

    def rows_of(half, n):
        return pl.ds(pl.multiple_of(half * (SEQ // 2) + n * 512, 512), 512)

    def done_copies(half, n):
        rows = rows_of(half, n)
        return [
            pltpu.make_async_copy(src.at[rows, :], dst.at[rows, :], tile_sem.at[2 * half + n, m])
            for m, (src, dst) in enumerate(((n_s, normed_out), (q_s, q_out), (k_s, k_out)))
        ]

    def project(half, n):
        rows = rows_of(half, n)
        values = row[half, pl.ds(pl.multiple_of(n * 512, 512), 512), :].astype(F32)
        factor = lax.rsqrt(jnp.mean(values * values, axis=1, keepdims=True) + EPSILON)
        normed = (values * factor * gain[...]).astype(BF16)
        n_s[rows, :] = normed
        cos, sin = cos_s[rows, :], sin_s[rows, :]
        for u in range(2):
            for m, out, scale in ((0, q_s, 0.125), (1, k_s, 1.0)):
                raw = dot(normed, w_s[m, u])
                a, b = raw[:, :128], raw[:, 128:]
                out[rows, u * 256 : u * 256 + 128] = ((a * cos - b * sin) * scale).astype(BF16)
                out[rows, u * 256 + 128 : u * 256 + 256] = ((b * cos + a * sin) * scale).astype(BF16)
            raw_s[rows, u * 256 : u * 256 + 256] = 0.5 * dot(normed, w_s[2, u])
        for item in done_copies(half, n):
            item.start()

    row_copy = pltpu.make_async_copy(row, row_out, end_sem.at[3])

    def half_row(i, carry):
        @pl.when(i == 1)
        def _():
            pass_over(order[2])
            given.wait_recv()
            row_copy.start()

        half = c + i - 2 * c * i
        project(half, 0)
        project(half, 1)
        return carry

    lax.fori_loop(0, 2, half_row, 0)
    pass_over(order[3])

    for p in range(2):

        @pl.when(stays[p])
        def _():
            first_local(p).wait()

        @pl.when(jnp.logical_not(stays[p]))
        def _():
            first_copy(p).wait_send()

    for u in range(2):
        came = pltpu.make_async_remote_copy(
            src_ref=first.at[u],
            dst_ref=first.at[u],
            send_sem=fsend.at[u],
            recv_sem=frecv.at[u],
            device_id=(dpc, t),
            device_id_type=MESH,
        )

        @pl.when((side != c) | (t != 2 * c + u))
        def _():
            came.wait_recv()

    outs = []
    for n in range(4):
        rows = slice(n * 512, n * 512 + 512)
        for u in range(2):
            lanes = slice(u * 256, u * 256 + 256)
            v_s[rows, lanes] = (raw_s[rows, lanes] + 0.5 * first[u, rows, :].astype(F32)).astype(BF16)
        item = pltpu.make_async_copy(v_s.at[rows, :], v_out.at[rows, :], tile_sem.at[n, 3])
        item.start()
        outs.append(item)

    for n in range(4):
        outs += done_copies(n // 2, n % 2)
    given.wait_send()
    for k in range(chunks):
        if k:
            for item in over[k]:
                item.wait_recv()
        end_along(k)
        for item in across[k] + over[k]:
            item.wait_send()
        for at in range(4):
            for h in range(2):
                onward(k, at, h, slot(k, at, dp, h)).wait_send()
    for item in outs + tables + [row_copy]:
        item.wait()


def gather(ends, tok, fv, small, big, gain, freqs):
    part, rows = big.shape[2:]
    wide = tok.shape[1]
    vmem = pl.BlockSpec(memory_space=pltpu.VMEM)
    sems = pltpu.SemaphoreType.DMA
    low = lambda *shape: pltpu.VMEM(shape, BF16)
    shapes = [(2, SEQ // 2, wide), (4, 4, wide, 256), (3, 8, 2, 4, part, rows), (SEQ, wide)] + [(SEQ, 512)] * 3
    return pl.pallas_call(
        gather_kernel,
        out_shape=[jax.ShapeDtypeStruct(shape, BF16) for shape in shapes]
        + [jax.ShapeDtypeStruct((SEQ, 128), F32)] * 2,
        in_specs=[pl.BlockSpec(memory_space=pltpu.SMEM)] + [vmem] * 6,
        out_specs=[any_spec()] * 9,
        scratch_shapes=[low(2, SEQ // 2, wide), low(2, SEQ, 256), low(3, 2, wide, 256), low(SEQ, wide)]
        + [low(SEQ, 512)] * 3
        + [pltpu.VMEM((SEQ, 512), F32)]
        + [pltpu.VMEM((SEQ, 128), F32)] * 2
        + [
            sems((4, 8)),
            sems((4, 8)),
            sems((4, 4, 2)),
            sems((4, 4)),
            sems((4, 4, 2)),
            sems((4, 4, 2)),
            sems((4,)),
            sems((2,)),
            sems((2,)),
            sems((6,)),
            sems((4, 4)),
            sems((4,)),
        ],
        compiler_params=params(collective_id=0, has_side_effects=True),
        name="gather",
    )(ends, tok, fv, small, big, gain, freqs)


def dot(left, right):
    return jnp.dot(left, right, preferred_element_type=F32)


def dot_nt(left, right):
    return lax.dot_general(left, right, (((1,), (1,)), ((), ())), preferred_element_type=F32)


def dot_tn(left, right):
    return lax.dot_general(left, right, (((0,), (0,)), ((), ())), preferred_element_type=F32)


def any_spec():
    return pl.BlockSpec(memory_space=pl.ANY)


def params(**more):
    return pltpu.CompilerParams(vmem_limit_bytes=62 * 1024 * 1024, **more)


def cost(flops, size, exps=0):
    return pl.CostEstimate(flops=int(flops), bytes_accessed=int(size), transcendentals=int(exps))


def once(shape, place):
    return pl.BlockSpec(shape, place, pipeline_mode=pl.Buffered(1))


def head_masks(rows):
    lane = lax.broadcasted_iota(jnp.int32, (rows, 256), 1)
    return (lane & 127) >> 5, lane >> 6


def attend_kernel(at, bounds, q_ref, k_ref, v_ref, starts, own_ref, send_ref, lse_ref, kept, turned, acc):
    tiles = SEQ // TILE
    of_qk, _ = head_masks(TILE)
    row = lax.broadcasted_iota(jnp.int32, (TILE, TILE), 0)
    lane = lax.broadcasted_iota(jnp.int32, (TILE, TILE), 1)
    slabs = [slice(0, 256), slice(256, 512)]

    def turn_values(j, carry):
        there = pl.ds(pl.multiple_of(j * TILE, TILE), TILE)
        turned[j] = v_ref[there, :].T
        return carry

    lax.fori_loop(0, tiles, turn_values, 0)

    def eighths(values, reduce):
        return reduce(values.reshape(TILE // 8, 8, 4 * TILE), axis=0)

    def query_tile(i, carry):
        here = pl.ds(pl.multiple_of(i * TILE, TILE), TILE)
        q4 = []
        for slab in slabs:
            q = q_ref[here, slab]
            zero = jnp.zeros_like(q)
            q4.append(jnp.concatenate([jnp.where(of_qk == h, q, zero) for h in range(4)], axis=0))
        low = bounds[i]
        begin = starts[pl.ds(i, 1), :]
        limit = lane + i * TILE

        def score(j, tops):
            there = pl.ds(pl.multiple_of(j * TILE, TILE), TILE)
            at_row = row + j * TILE
            ok = (at_row >= begin) & (at_row <= limit)
            ok = jnp.concatenate([ok] * 4, axis=1)
            new = []
            for u, slab in enumerate(slabs):
                s = jnp.where(ok, dot_nt(k_ref[there, slab], q4[u]), NEG)
                kept[j - low, u] = s
                new.append(jnp.maximum(tops[u], eighths(s, jnp.max)))
            return tuple(new)

        start = jnp.full((8, 4 * TILE), NEG, F32)
        tops = lax.fori_loop(low, i + 1, score, (start, start))
        tops = [jnp.max(top, axis=0, keepdims=True) for top in tops]
        acc[...] = jnp.zeros_like(acc)

        def weigh(j, totals):
            new = []
            for u in range(2):
                e = jnp.exp(kept[j - low, u] - tops[u])
                p = e.astype(BF16)
                for h in range(4):
                    part = slice(u * 256 + h * 64, u * 256 + h * 64 + 64)
                    acc[part] += dot(turned[j, part, :], p[:, h * TILE : (h + 1) * TILE])
                new.append(totals[u] + eighths(e, jnp.sum))
            return tuple(new)

        zero = jnp.zeros((8, 4 * TILE), F32)
        totals = lax.fori_loop(low, i + 1, weigh, (zero, zero))
        for u, slab in enumerate(slabs):
            total = jnp.sum(totals[u], axis=0, keepdims=True)
            inverse = 1.0 / total
            scaled = [
                acc[u * 256 + h * 64 : u * 256 + h * 64 + 64] * inverse[:, h * TILE : (h + 1) * TILE] for h in range(4)
            ]
            done = jnp.concatenate(scaled, axis=0).T.astype(BF16)
            local = pl.ds(pl.multiple_of(lax.rem(i, tiles // 2) * TILE, TILE), TILE)
            mine = lax.div(i, tiles // 2) == (at[0] & 1)

            @pl.when(mine)
            def _():
                own_ref[local, slab] = done

            @pl.when(jnp.logical_not(mine))
            def _():
                send_ref[local, slab] = done

            lse_ref[u, pl.ds(i, 1), :] = tops[u] + jnp.log(total)
        return carry

    lax.fori_loop(0, tiles, query_tile, 0)


def attend(at, bounds, q, k, v, starts):
    tiles = SEQ // TILE
    vmem = pl.BlockSpec(memory_space=pltpu.VMEM)
    return pl.pallas_call(
        attend_kernel,
        out_shape=[
            jax.ShapeDtypeStruct((SEQ // 2, 512), BF16),
            jax.ShapeDtypeStruct((SEQ // 2, 512), BF16),
            jax.ShapeDtypeStruct((2, tiles, 4 * TILE), F32),
        ],
        in_specs=[pl.BlockSpec(memory_space=pltpu.SMEM)] * 2 + [vmem] * 4,
        out_specs=[vmem] * 3,
        scratch_shapes=[
            pltpu.VMEM((tiles, 2, TILE, 4 * TILE), F32),
            pltpu.VMEM((tiles, 512, TILE), BF16),
            pltpu.VMEM((512, TILE), F32),
        ],
        compiler_params=params(),
        cost_estimate=cost(20e9, 12e6, 1e7),
        name="attend",
    )(at, bounds, q, k, v, starts)


def attend_back_kernel(
    at, bounds, q_hbm, k_hbm, v_hbm, do_own, do_other, o_own, o_other, lse_ref, starts, cosine, sine, *rest, part,
):
    if part:
        held_hbm, rest = rest[0], rest[1:]
        dq_hbm, dk_hbm, dv_hbm = rest[:3]
        rest = rest[3:]
    else:
        dq_hbm, dk_hbm, dv_hbm, held_hbm = rest[:4]
        rest = rest[4:]
    attend_back_part(
        at, bounds, q_hbm, k_hbm, v_hbm, do_own, do_other, o_own, o_other, lse_ref, starts, cosine, sine, held_hbm, dq_hbm, dk_hbm,
        dv_hbm, *rest, part=part
    )


def attend_back_part(
    at, bounds, q_hbm, k_hbm, v_hbm, do_own, do_other, o_own, o_other, lse_ref, starts, cosine, sine, held_hbm, dq_hbm, dk_hbm, dv_hbm,
    q_ref, k_ref, v_ref, do_ref, o_ref, dq_ref, dk_ref, dv_ref, dq_acc, delta, dk_acc, dv_acc, load, store, *, part,
):
    tiles = SEQ // TILE
    of_qk, of_v = head_masks(TILE)
    row = lax.broadcasted_iota(jnp.int32, (TILE, TILE), 0)
    lane = lax.broadcasted_iota(jnp.int32, (TILE, TILE), 1)
    slabs = [slice(0, 256), slice(256, 512)]
    pick = (lax.broadcasted_iota(jnp.int32, (8, 256), 1) >> 6) == lax.broadcasted_iota(
        jnp.int32, (8, 256), 0
    )
    pick = pick.astype(F32)
    half = SEQ // 2
    low = pl.multiple_of((at[0] & 1) * half, half)
    mine, others = pl.ds(low, half), pl.ds(half - low, half)
    first_half, second_half = pl.ds(0, half), pl.ds(half, half)
    mine_second = (at[0] & 1) == 1
    here_half = second_half if part else first_half
    q_rows = second_half if part else pl.ds(0, SEQ)
    plain = [
        (q_hbm.at[q_rows, :], q_ref.at[q_rows, :]),
        (k_hbm.at[here_half, :], k_ref.at[here_half, :]),
        (v_hbm.at[here_half, :], v_ref.at[here_half, :]),
    ]
    if part:
        plain.append((held_hbm, dq_acc.at[pl.ds(tiles // 2, tiles // 2)]))
    loads = [pltpu.make_async_copy(src, dst, load.at[4 + n]) for n, (src, dst) in enumerate(plain)]

    def half_loads(own, other, dst, n):
        pairs = [(own, mine, mine_second), (other, others, jnp.logical_not(mine_second))]
        for e, (src, rows, wanted) in enumerate(pairs):
            yield pltpu.make_async_copy(src, dst.at[rows, :], load.at[n + e]), wanted

    parts = list(half_loads(do_own, do_other, do_ref, 0)) + list(half_loads(o_own, o_other, o_ref, 2))

    def each(action):
        for item, wanted in parts:
            if part:
                pl.when(wanted)(functools.partial(action, item))
            else:
                action(item)

    each(lambda item: item.start())
    for item in loads:
        item.start()
    if not part:
        dq_acc[...] = jnp.zeros_like(dq_acc)
    each(lambda item: item.wait())

    def prepare(i, carry):
        here = pl.ds(pl.multiple_of(i * TILE, TILE), TILE)
        for u, slab in enumerate(slabs):
            both = do_ref[here, slab].astype(F32) * o_ref[here, slab].astype(F32)
            sums = lax.dot_general(
                pick, both, (((1,), (1,)), ((), ())), precision=lax.Precision.HIGHEST, preferred_element_type=F32
            )
            for h in range(4):
                delta[u, pl.ds(i, 1), h * TILE : (h + 1) * TILE] = sums[h : h + 1]
        return carry

    middle = tiles // 2
    lax.fori_loop(middle * part, tiles, prepare, 0)
    for item in loads:
        item.wait()

    def rotate_out(values, here, out, low, scale):
        a, b = values[:, :128], values[:, 128:]
        cos, sin = cosine[here, :], sine[here, :]
        out[here, low : low + 128] = ((a * cos + b * sin) * scale).astype(BF16)
        out[here, low + 128 : low + 256] = ((b * cos - a * sin) * scale).astype(BF16)

    def split(values, of):
        zero = jnp.zeros_like(values)
        return jnp.concatenate([jnp.where(of == h, values, zero) for h in range(4)], axis=0)

    def key_tile(j, carry):
        there = pl.ds(pl.multiple_of(j * TILE, TILE), TILE)
        at_row = row + j * TILE
        dk_acc[...] = jnp.zeros_like(dk_acc)
        dv_acc[...] = jnp.zeros_like(dv_acc)

        def query_tile(i, carry):
            here = pl.ds(pl.multiple_of(i * TILE, TILE), TILE)
            at_lane = lane + i * TILE
            ok = (at_row >= starts[pl.ds(i, 1), :]) & (at_row <= at_lane)
            ok = jnp.concatenate([ok] * 4, axis=1)
            for u, slab in enumerate(slabs):
                q4 = split(q_ref[here, slab], of_qk)
                do4 = split(do_ref[here, slab], of_v)
                s = dot_nt(k_ref[there, slab], q4)
                dp = dot_nt(v_ref[there, slab], do4)
                p = jnp.exp(jnp.where(ok, s - lse_ref[u, pl.ds(i, 1), :], NEG))
                ds = (p * (dp - delta[u, pl.ds(i, 1), :])).astype(BF16)
                dv_acc[u] += dot(p.astype(BF16), do4)
                dk_acc[u] += dot(ds, q4)
                ds4 = jnp.concatenate([ds[:, h * TILE : (h + 1) * TILE] for h in range(4)], axis=0)
                dq_acc[i, u] += dot_tn(ds4, split(k_ref[there, slab], of_qk))
            return carry

        lax.fori_loop(j, bounds[tiles + j] + 1, query_tile, 0)
        for u, slab in enumerate(slabs):
            rotate_out(dk_acc[u], there, dk_ref, u * 256, 1.0)
            dv_ref[there, slab] = (0.5 * dv_acc[u]).astype(BF16)
        local = pl.ds(pl.multiple_of((j - middle * part) * TILE, TILE), TILE)
        pltpu.make_async_copy(dk_ref.at[there, :], dk_hbm.at[local, :], store.at[0]).start()
        pltpu.make_async_copy(dv_ref.at[there, :], dv_hbm.at[local, :], store.at[1]).start()
        return carry

    lax.fori_loop(middle * part, middle * part + middle, key_tile, 0)
    if not part:
        held = pltpu.make_async_copy(dq_acc.at[pl.ds(middle, middle)], held_hbm, store.at[3])
        held.start()

    def finish_tile(i, carry):
        here = pl.ds(pl.multiple_of(i * TILE, TILE), TILE)
        for u in range(2):
            rotate_out(dq_acc[i, u], here, dq_ref, u * 256, 0.125)
        local = pl.ds(pl.multiple_of((i - middle * part) * TILE, TILE), TILE)
        pltpu.make_async_copy(dq_ref.at[here, :], dq_hbm.at[local, :], store.at[2]).start()
        return carry

    lax.fori_loop(middle * part, middle * part + middle, finish_tile, 0)
    for n, (src, dst) in enumerate(((dk_ref, dk_hbm), (dv_ref, dv_hbm), (dq_ref, dq_hbm))):
        pltpu.make_async_copy(src.at[here_half, :], dst, store.at[n]).wait()
    if not part:
        held.wait()


def attend_back(part, at, bounds, q, k, v, do_own, do_other, o_own, o_other, lse, starts, cosine, sine, *held):
    tiles = SEQ // TILE
    vmem = pl.BlockSpec(memory_space=pltpu.VMEM)
    sems = pltpu.SemaphoreType.DMA
    outs = [jax.ShapeDtypeStruct((SEQ // 2, 512), BF16)] * 3
    if not part:
        outs.append(jax.ShapeDtypeStruct((tiles // 2, 2, TILE, 256), F32))
    return pl.pallas_call(
        functools.partial(attend_back_kernel, part=part),
        out_shape=outs,
        in_specs=[pl.BlockSpec(memory_space=pltpu.SMEM)] * 2 + [any_spec()] * 7 + [vmem] * 4 + [any_spec()] * len(held),
        out_specs=[any_spec()] * len(outs),
        scratch_shapes=[pltpu.VMEM((SEQ, 512), BF16)] * 8
        + [
            pltpu.VMEM((tiles, 2, TILE, 256), F32),
            pltpu.VMEM((2, tiles, 4 * TILE), F32),
            pltpu.VMEM((2, TILE, 256), F32),
            pltpu.VMEM((2, TILE, 256), F32),
            sems((8,)),
            sems((4,)),
        ],
        compiler_params=params(),
        cost_estimate=cost(25e9, 12e6, 5e6),
        name="attend_back",
    )(at, bounds, q, k, v, do_own, do_other, o_own, o_other, lse, starts, cosine, sine, *held)


def mlp_kernel(at, att_own, att_other, tok, cot_here, cot_moved, gain, wo, big, *rest):
    (out, gh_out, gb_out, n2_out, hid_out, ga_own, ga_other, gg_out, cot_out) = rest[:9]
    (wg, wu, wd, sems) = rest[9:]
    step = pl.program_id(0)
    c = at[0] & 1

    @pl.when(step == 0)
    def _():
        for n, held in enumerate((wg, wu, wd)):
            for owner in range(8):
                pltpu.make_async_copy(
                    big.at[n, owner], held.at[:, owner * 128 : owner * 128 + 128], sems.at[n]
                ).start()
        gg_out[...] = jnp.zeros_like(gg_out)

    hidden = tok[0].astype(F32)
    for e, att in enumerate((att_own, att_other)):
        for u in range(2):
            hidden += dot_nt(att[:, u * 256 : u * 256 + 256], wo[0, 2 * (c ^ e) + u])
    factor = lax.rsqrt(jnp.mean(hidden * hidden, axis=1, keepdims=True) + EPSILON)
    gains = gain[...]
    normed = (hidden * factor * gains).astype(BF16)
    n2_out[...] = normed
    g = jnp.where((at[1] & 1) == c, cot_here[...], cot_moved[...])
    cot_out[...] = g

    @pl.when(step == 0)
    def _():
        for n, held in enumerate((wg, wu, wd)):
            pltpu.make_async_copy(held, held, sems.at[n]).wait()

    down = jnp.zeros_like(hidden)
    back = jnp.zeros_like(hidden)
    units = wg.shape[0]
    for low in range(0, units, 768):
        part = slice(low, min(low + 768, units))
        gate, up, grad_act = dot_nt(normed, wg[part]), dot_nt(normed, wu[part]), dot_nt(g, wd[part])
        sig = 1.0 / (1.0 + jnp.exp(-gate))
        silu = gate * sig
        act = (silu * up).astype(BF16)
        grad_up = (grad_act * silu).astype(BF16)
        grad_gate = (grad_act * up * (sig * (1.0 + gate * (1.0 - sig)))).astype(BF16)
        hid_out[0, :, part], hid_out[1, :, part], hid_out[2, :, part] = grad_gate, grad_up, act
        down += dot(act, wd[part])
        back += dot(grad_gate, wg[part]) + dot(grad_up, wu[part])
    out[...] = (hidden + down).astype(BF16)
    gg_out[...] += jnp.sum((back * hidden * factor).reshape(-1, 8, back.shape[1]), axis=0)
    scaled = back * gains
    mean = jnp.mean(scaled * hidden, axis=1, keepdims=True)
    grad_hidden = g.astype(F32) + factor * scaled - hidden * (factor * factor * factor * mean)
    gh_out[...] = grad_hidden
    branch = grad_hidden.astype(BF16)
    gb_out[...] = branch
    for e, ga in enumerate((ga_own, ga_other)):
        for u in range(2):
            ga[:, u * 256 : u * 256 + 256] = dot(branch, wo[0, 2 * (c ^ e) + u]).astype(BF16)


def mlp(at, att_own, att_other, tok, cot_here, cot_moved, gain, small, big):
    _, count, wide = tok.shape
    big = big.reshape(3, 8, -1, 128)
    rows, units = 256, big.shape[2]
    row = lambda width: pl.BlockSpec((rows, width), lambda i, at: (i, 0))
    grid = pltpu.PrefetchScalarGridSpec(
        num_scalar_prefetch=1,
        grid=(count // rows,),
        in_specs=[
            row(512),
            row(512),
            pl.BlockSpec((1, rows, wide), lambda i, at: (at[0] & 1, i, 0)),
            row(wide),
            row(wide),
            pl.BlockSpec((1, wide), lambda i, at: (0, 0)),
            once((1, 4, wide, 256), lambda i, at: (3, 0, 0, 0)),
            any_spec(),
        ],
        out_specs=[
            row(wide),
            row(wide),
            row(wide),
            row(wide),
            pl.BlockSpec((3, rows, units), lambda i, at: (0, i, 0)),
            row(512),
            row(512),
            pl.BlockSpec((8, wide), lambda i, at: (0, 0)),
            row(wide),
        ],
        scratch_shapes=[pltpu.VMEM((units, wide), BF16)] * 3 + [pltpu.SemaphoreType.DMA((3,))],
    )
    tokens = lambda width, kind=BF16: jax.ShapeDtypeStruct((count, width), kind)
    return pl.pallas_call(
        mlp_kernel,
        out_shape=[
            tokens(wide),
            tokens(wide, F32),
            tokens(wide),
            tokens(wide),
            jax.ShapeDtypeStruct((3, count, units), BF16),
            tokens(512),
            tokens(512),
            jax.ShapeDtypeStruct((8, wide), F32),
            tokens(wide),
        ],
        grid_spec=grid,
        compiler_params=params(),
        cost_estimate=cost(2 * count * wide * (6 * units + 2 * wide), 60e6, 3e6),
        name="mlp",
    )(at, att_own, att_other, tok, cot_here, cot_moved, gain, small, big)


def turn_rows(source, plane, parity, held):
    for rel in range(4):
        block = ((plane ^ rel) * 2 + parity) * 128
        held[rel * 128 : rel * 128 + 128, :] = source[:, pl.ds(pl.multiple_of(block, 128), 128)].T


def place_first(send, keep, done, lanes):
    for yr in range(2):
        keep[yr, :, lanes] = done[2 * yr]
        send[yr, :, lanes] = done[2 * yr + 1]


def place_second(send, keep, done, lanes):
    for xr in range(2):
        keep[xr, :, lanes] = done[xr]
        send[xr, :, lanes] = done[2 + xr]


def weights_kernel(n2, g, branch, hid, own, other, send1, keep1, send2, keep2, turned, given, got, out_sem, in_sem):
    step = pl.program_id(0)
    dp, t = lax.axis_index("dp"), lax.axis_index("tensor")
    c = lax.rem(dp, 2)
    plane = lax.div(dp, 2)
    n = lax.rem(step, 4)
    units = hid.shape[2] // 2

    @pl.when(step == 0)
    def _():
        barrier = pltpu.get_barrier_semaphore()
        pl.semaphore_signal(barrier, inc=1, device_id=(dp + 1 - 2 * c, t), device_id_type=MESH)
        pl.semaphore_wait(barrier, 1)

    def exchange(k):
        lanes = pl.ds(k * units, units if k < 3 else 512)
        return pltpu.make_async_remote_copy(
            src_ref=given.at[:, :, :, lanes],
            dst_ref=got.at[:, :, :, lanes],
            send_sem=out_sem.at[k],
            recv_sem=in_sem.at[k],
            device_id=(dp + 1 - 2 * c, t),
            device_id_type=MESH,
        )

    for phase, parity in ((0, 1 - c), (1, c)):
        for at_n, source in ((0, n2), (2, g), (3, branch)):

            @pl.when(step == 4 * phase + at_n)
            def _():
                x = lax.rem(plane, 2)
                y = lax.div(plane, 2)
                for rel in range(4):
                    yy, xx = (y, 1 - y)[rel // 2], (x, 1 - x)[rel % 2]
                    block = pl.multiple_of((yy * 4 + xx * 2 + parity) * 128, 128)
                    turned[rel * 128 : rel * 128 + 128, :] = source[:, pl.ds(block, 128)].T

    def heads(h):
        return jnp.where(c == h, own[...], other[...])

    @pl.when(step < 3)
    def _():
        for h in range(2):
            product = dot(turned[...], hid[0, :, h * units : h * units + units]).astype(BF16)
            given[:, h, :, pl.ds(pl.multiple_of(n * units, 128), units)] = product.reshape(4, 128, units)

    @pl.when(step == 3)
    def _():
        for h in range(2):
            product = dot(turned[...], heads(h)).astype(BF16)
            given[:, h, :, 3 * units : 3 * units + 512] = product.reshape(4, 128, 512)

    for k in range(4):

        @pl.when(step == k + 1)
        def _():
            exchange(k).start()

        @pl.when(step == k + 4)
        def _():
            exchange(k).wait_recv()

    def keep(product, h, lanes):
        done = [(product[r * 128 : r * 128 + 128] + got[r, h, :, lanes].astype(F32)).astype(BF16) for r in range(4)]
        (place_first, place_second)[h](*((send1, keep1), (send2, keep2))[h], done, lanes)

    @pl.when((step >= 4) & (step < 7))
    def _():
        for h in range(2):
            product = dot(turned[...], hid[0, :, h * units : h * units + units])
            keep(product, h, pl.ds(pl.multiple_of(n * units, 128), units))

    @pl.when(step == 7)
    def _():
        for h in range(2):
            keep(dot(turned[...], heads(h)), h, pl.ds(3 * units, 512))
        for k in range(4):
            exchange(k).wait_send()


def weights(n2, g, branch, hid, own, other):
    count, wide = n2.shape
    units = hid.shape[2] // 2
    full = lambda *shape: pl.BlockSpec(shape, lambda s: (0,) * len(shape), pipeline_mode=pl.Buffered(1))
    length = 3 * units + 512
    grid = pl.GridSpec(
        grid=(8,),
        in_specs=[
            full(count, wide),
            full(count, wide),
            full(count, wide),
            pl.BlockSpec((1, count, 2 * units), lambda s: (jnp.minimum(lax.rem(s, 4), 2), 0, 0)),
            full(count, 512),
            full(count, 512),
        ],
        out_specs=[full(2, 128, length)] * 4,
        scratch_shapes=[
            pltpu.VMEM((512, count), BF16),
            pltpu.VMEM((4, 2, 128, length), BF16),
            pltpu.VMEM((4, 2, 128, length), BF16),
            pltpu.SemaphoreType.DMA((4,)),
            pltpu.SemaphoreType.DMA((4,)),
        ],
    )
    return pl.pallas_call(
        weights_kernel,
        out_shape=[jax.ShapeDtypeStruct((2, 128, length), BF16)] * 4,
        grid_spec=grid,
        compiler_params=params(collective_id=1, has_side_effects=True),
        cost_estimate=cost(2 * count * 1024 * length * 2, 50e6),
        name="weights",
    )(n2, g, branch, hid, own, other)


def add(left, right):
    return (left.astype(F32) + right.astype(F32)).astype(BF16)


def finish_kernel(at, own, got, own_heads, got_heads, tok, got_tok, first, came0, came1, slab0, slab1, layer, got_layer, gate, up, down, out, query, key, value, tok_out, first_out, layer_out):
    @pl.when(pl.program_id(0) == 0)
    def _():
        part = down.shape[0]
        for n, ref in enumerate((gate, up, down, out)):
            rows = slice(n * part, n * part + ref.shape[0])
            total = own[rows, :].astype(F32)
            for d in range(3):
                total += got[d, rows, :].astype(F32)
            ref[...] = total
        heads = own_heads[...].astype(F32)
        for d in range(3):
            heads += got_heads[d].astype(F32)
        for n, ref in enumerate((query, key)):
            parts = []
            for h in range(4):
                parts += [heads[n, :, h * 32 : h * 32 + 32], heads[n, :, 128 + h * 32 : 160 + h * 32]]
            ref[...] = jnp.concatenate(parts, axis=1)
        value[...] = heads[2]

    stays = (at[0] & 1) == (at[1] & 1)
    tok_out[...] = jnp.where(stays, tok[...], got_tok[...]).astype(F32)
    step = pl.program_id(0)
    c, t = at[0] & 1, at[1]
    pair, side = t >> 1, t & 1
    r = (step >> 1) ^ side
    local = (c == side) & (t == 2 * c + (pair ^ r))

    @pl.when((step & 1) == 0)
    def _():
        came = jnp.where(r == 0, came0[...], came1[...])
        slab = jnp.where(r == 0, slab0[...], slab1[...])
        first_out[...] = jnp.where(local, slab, came).astype(F32)

    @pl.when((step & 1) == 1)
    def _():
        first_out[...] = first[0].astype(F32)

    layer_out[...] = jnp.where(stays, layer[...], got_layer[...])


def finish(at, pieces, got, own_heads, got_heads, tok, got_tok, first, early, layer, got_layer, part):
    count, wide = tok.shape
    rows = 256
    row = pl.BlockSpec((rows, wide), lambda i, at: (i, 0))
    wider = pl.BlockSpec((SEQ // 2, 256), lambda i, at: (i, 0))
    whole = lambda *shape: pl.BlockSpec(shape, lambda i, at: (0,) * len(shape))
    shapes = [(part, 128)] * 3 + [(256, 128)] + [(128, 256)] * 3
    grid = pltpu.PrefetchScalarGridSpec(
        num_scalar_prefetch=1,
        grid=(count // rows,),
        in_specs=[
            whole(*pieces.shape),
            whole(*got.shape),
            whole(*own_heads.shape),
            whole(*got_heads.shape),
            row,
            row,
            pl.BlockSpec((1, SEQ // 2, 256), lambda i, at: (i // 2, 0, 0)),
            *[whole(SEQ // 2, 256)] * 4,
            row,
            row,
        ],
        out_specs=[whole(*shape) for shape in shapes] + [row, wider, row],
    )
    return pl.pallas_call(
        finish_kernel,
        out_shape=[jax.ShapeDtypeStruct(shape, F32) for shape in shapes + [(count, wide), (2 * SEQ, 256)]]
        + [jax.ShapeDtypeStruct((count, wide), BF16)],
        grid_spec=grid,
        compiler_params=params(),
        cost_estimate=cost(1e6, 18e6),
        name="finish",
    )(at, pieces, got, own_heads, got_heads, tok, got_tok, first, *early, layer, got_layer)


def tail_kernel(
    dq0, dk0, dv0, dq1, dk1, dv1, small, normed, row, grad_hidden, keep1, got1, keep2, got2, gain, gain_two,
    first, own_pieces, got_pieces, own_heads, got_heads, tok, got_tok, sums,
    d_s, w_s, n_s, x_s, gh_s, ks1, gs1, ks2, gs2, last1, last2, pieces, gn_send, gn_got, turned,
    h_send, h_got, s1, k1, a1, a2, part1, part2, rest1, rest2, heads, held, came,
    load, f_sem, m_sem, p_sem, n_sem, c_sem, one_sem, two_sem, h_sem, swap, g_sem,
):
    dp, t = lax.axis_index("dp"), lax.axis_index("tensor")
    c, x, y = lax.rem(dp, 2), lax.rem(lax.div(dp, 2), 2), lax.div(dp, 4)
    pair, side = lax.div(t, 2), lax.rem(t, 2)
    plane = dp - c
    dpx, dpy, dpc = dp + 2 - 4 * x, dp + 4 - 8 * y, dp + 1 - 2 * c
    half = SEQ // 2
    units = (ks1.shape[2] - 512) // 3

    def copy(src, dst, sems, n, to):
        return pltpu.make_async_remote_copy(
            src_ref=src,
            dst_ref=dst,
            send_sem=sems.at[0, n],
            recv_sem=sems.at[1, n],
            device_id=to,
            device_id_type=MESH,
        )

    sources = [(keep1, ks1), (got1, gs1), (keep2, ks2), (got2, gs2)]
    for h, arrays in enumerate(((dq0, dk0, dv0), (dq1, dk1, dv1))):
        sources += [(src, d_s.at[n, pl.ds(h * half, half), :]) for n, src in enumerate(arrays)]
    sources += [(normed, n_s), (small.at[pl.ds(0, 3), pl.ds(2 * c, 2)], w_s), (row.at[c], x_s), (grad_hidden, gh_s)]
    loads = [pltpu.make_async_copy(src, dst, load.at[n]) for n, (src, dst) in enumerate(sources)]
    for item in loads:
        item.start()
    meet(plane, c, t, dpx, dpy)

    def value_copy(u):
        src = dv1.at[:, pl.ds(u * 256, 256)]
        return pltpu.make_async_remote_copy(
            src_ref=src,
            dst_ref=first.at[pair],
            send_sem=f_sem.at[0, u],
            recv_sem=f_sem.at[1, pair],
            device_id=(plane + side, 2 * c + u),
            device_id_type=MESH,
        )

    def value_local(u):
        return pltpu.make_async_copy(dv1.at[:, pl.ds(u * 256, 256)], first.at[pair], load.at[14])

    for u in range(2):
        stay = (side == c) & (t == 2 * c + u)

        @pl.when(stay)
        def _():
            value_local(u).start()

        @pl.when(jnp.logical_not(stay))
        def _():
            value_copy(u).start()

    for item in loads[:4]:
        item.wait()
    gs1[1] = add(ks1[1], gs1[1])
    gs2[1] = add(ks2[1], gs2[1])
    seconds = []
    for n, lanes in enumerate((pl.ds(0, 2 * units), pl.ds(2 * units, units + 512))):
        seconds.append(copy(gs1.at[1, :, lanes], last1.at[:, lanes], m_sem, 2 * n, (dpy, t)))
        seconds.append(copy(gs2.at[1, :, lanes], last2.at[:, lanes], m_sem, 2 * n + 1, (dpx, t)))
    for item in loads[4:11]:
        item.wait()
    for item in seconds:
        item.start()

    def turn(parity):
        for rel in range(4):
            yy, xx = (y, 1 - y)[rel // 2], (x, 1 - x)[rel % 2]
            block = pl.multiple_of((yy * 4 + xx * 2 + parity) * 128, 128)
            turned[rel * 128 : rel * 128 + 128, :] = n_s[:, pl.ds(block, 128)].T

    def heads_copy(n):
        lanes = pl.ds(pl.multiple_of(n * 512, 512), 512)
        return copy(h_send.at[:, :, :, lanes], h_got.at[:, :, :, lanes], c_sem, n, (dpc, t))

    def heads_product(n):
        product = dot(turned[...], d_s[n]).astype(BF16)
        return [product[r * 128 : r * 128 + 128] for r in range(4)], pl.ds(pl.multiple_of(n * 512, 512), 512)

    def heads_send(n, carry):
        place_second(h_send.at[0], h_send.at[1], *heads_product(n))

        @pl.when(n > 0)
        def _():
            heads_copy(n - 1).start()

        return carry

    def heads_keep(n, carry):
        place_first(s1, k1, *heads_product(n))
        return carry

    turn(1 - c)
    lax.fori_loop(0, 3, heads_send, 0)

    part = units // 4
    low_rows, high_rows = pl.ds(0, 4 * part), pl.ds(4 * part, 2 * part + 256)

    def fill_pieces(which):
        for h, (kept, got, last) in enumerate(((ks1, gs1, last1), (ks2, gs2, last2))):
            for n in which:
                lanes = slice(n * units, n * units + (units if n < 3 else 512))
                total = kept[0, :, lanes].astype(F32) + got[0, :, lanes].astype(F32) + last[:, lanes].astype(F32)
                flipped = total.T.astype(BF16)
                if n < 3:
                    for i in range(4):
                        rows = slice((2 * n + h) * part, (2 * n + h + 1) * part)
                        pieces[lax.rem(i + 4 - t, 4), rows, :] = flipped[i * part : (i + 1) * part]
                else:
                    for i in range(2):
                        pieces[lax.rem(2 * h + i + 4 - t, 4), 6 * part :, :] = flipped[i * 256 : i * 256 + 256]

    def piece_copies(rows, n):
        return [
            copy(pieces.at[d, rows, :], got_pieces.at[d - 1, rows, :], p_sem, 3 * n + d - 1, (dp, lax.rem(t + d, 4)))
            for d in (1, 2, 3)
        ]

    for item in seconds[:2]:
        item.wait_recv()
    fill_pieces((0, 1))
    turn(c)
    heads_copy(2).start()
    zs = piece_copies(low_rows, 0)
    for item in zs:
        item.start()
    lax.fori_loop(0, 3, heads_keep, 0)
    cs = [heads_copy(n) for n in range(3)]
    for item in cs:
        item.wait_recv()
    ones = [copy(h_got.at[0], a2, one_sem, 1, (dpy, t)), copy(s1, a1, one_sem, 0, (dpx, t))]
    for item in ones:
        item.start()
    for item in seconds[2:]:
        item.wait_recv()
    fill_pieces((2, 3))
    own_pieces[...] = pieces[0]
    last_zs = piece_copies(high_rows, 1)
    for item in last_zs:
        item.start()
    zs += last_zs

    def back_product(rows):
        total = None
        for u in range(2):
            for n in range(3):
                term = dot_nt(d_s[n, rows, u * 256 : u * 256 + 256], w_s[n, u])
                total = term if total is None else total + term
        return total

    ns = [copy(gn_send.at[i], gn_got.at[i], n_sem, i, (dpc, t)) for i in range(2)]

    def other_half(i, carry):
        rows = pl.ds(pl.multiple_of((1 - c) * half + i * 512, 512), 512)
        gn_send[i] = back_product(rows).astype(BF16)
        return carry

    loads[11].wait()
    lax.fori_loop(0, 2, other_half, 0)

    for item in ones:
        item.wait_recv()
    part1[...] = add(k1[1], a1[1])
    part2[...] = add(h_got[1, 1], a2[1])
    for item in ns:
        item.start()
    twos = [copy(part1, rest1, two_sem, 0, (dpy, t)), copy(part2, rest2, two_sem, 1, (dpx, t))]
    for item in twos:
        item.start()

    loads[12].wait()
    loads[13].wait()
    moved = side != c
    for item in ns:
        item.wait_recv()

    def own_half(i, gained):
        rows = pl.ds(pl.multiple_of(c * half + i * 512, 512), 512)
        here = pl.ds(pl.multiple_of(i * 512, 512), 512)
        grad = back_product(rows) + gn_got[i].astype(F32)
        values = x_s[here, :].astype(F32)
        factor = lax.rsqrt(jnp.mean(values * values, axis=1, keepdims=True) + EPSILON)
        gained += jnp.sum((grad * values * factor).reshape(-1, 8, grad.shape[1]), axis=0)
        scaled = grad * gain[...]
        mean = jnp.mean(scaled * values, axis=1, keepdims=True)
        tok[i] = (gh_s[here, :] + factor * scaled - values * (factor * factor * factor * mean)).astype(BF16)
        return gained

    gained = lax.fori_loop(0, 2, own_half, jnp.zeros((8, tok.shape[2]), F32))
    swaps = [copy(tok.at[i], got_tok.at[i], swap, i, (plane + side, 2 * pair + c)) for i in range(2)]

    total1 = k1[0].astype(F32) + a1[0].astype(F32)
    total2 = h_got[1, 0].astype(F32) + a2[0].astype(F32)

    @pl.when(moved)
    def _():
        for item in swaps:
            item.start()

    turns = (dpc, t), (dpx, t), (dpy, t), (dp, t + 1 - 2 * side), (dp, lax.rem(t + 2, 4))
    line = lax.broadcasted_iota(jnp.int32, gained.shape, 0)
    total_one = jnp.sum(gained, axis=0, keepdims=True)
    total_two = jnp.sum(gain_two[...], axis=0, keepdims=True)
    held[0] = jnp.where(line == 0, total_one, jnp.where(line == 1, total_two, 0.0))

    def gain_step(n):
        return copy(held.at[n], came.at[n], g_sem, n, turns[n])

    def gain_next(n):
        gain_step(n).wait_recv()
        held[n + 1] = held[n] + came[n]

    gain_step(0).start()
    gain_next(0)
    gain_step(1).start()
    gain_next(1)
    for item in twos:
        item.wait_recv()
    totals = ((total1 + rest1[...].astype(F32)).astype(BF16), (total2 + rest2[...].astype(F32)).astype(BF16))
    for e, total in enumerate(totals):
        core = (c, 1 - c)[e]
        for u in range(2):
            d = lax.rem(2 * core + u + 4 - t, 4)
            for n in range(3):
                heads[d, n] = total[:, n * 512 + u * 256 : n * 512 + u * 256 + 256]
    gain_step(2).start()
    gain_next(2)
    own_heads[...] = heads[0]
    hs = [copy(heads.at[d], got_heads.at[d - 1], h_sem, d - 1, (dp, lax.rem(t + d, 4))) for d in (1, 2, 3)]
    for item in hs:
        item.start()
    for n in (3, 4):
        gain_step(n).start()
        gain_next(n)
    sums[...] = held[5]

    for item in seconds + ns + cs + ones + twos:
        item.wait_send()
    for n in range(5):
        gain_step(n).wait_send()
    for u in range(2):
        stay = (side == c) & (t == 2 * c + u)

        @pl.when(stay)
        def _():
            value_local(u).wait()

        @pl.when(jnp.logical_not(stay))
        def _():
            value_copy(u).wait_send()

    for p in range(2):

        @pl.when((pair != c) | (t != 2 * p + c))
        def _():
            pltpu.make_async_remote_copy(
                src_ref=first.at[p],
                dst_ref=first.at[p],
                send_sem=f_sem.at[0, p],
                recv_sem=f_sem.at[1, p],
                device_id=(dpc, t),
                device_id_type=MESH,
            ).wait_recv()

    for item in zs + hs:
        item.wait()

    @pl.when(moved)
    def _():
        for item in swaps:
            item.wait()


def tail(back, small, normed, row, grad_hidden, keep1, got1, keep2, got2, gain, gain_two):
    vmem = pl.BlockSpec(memory_space=pltpu.VMEM)
    sems = pltpu.SemaphoreType.DMA
    wide = normed.shape[1]
    length = keep1.shape[2]
    rows = (length - 512) // 2 + 256
    half = SEQ // 2
    low = lambda *shape: pltpu.VMEM(shape, BF16)
    return pl.pallas_call(
        tail_kernel,
        out_shape=[
            jax.ShapeDtypeStruct((2, half, 256), BF16),
            jax.ShapeDtypeStruct((rows, 128), BF16),
            jax.ShapeDtypeStruct((3, rows, 128), BF16),
            jax.ShapeDtypeStruct((3, 128, 256), BF16),
            jax.ShapeDtypeStruct((3, 3, 128, 256), BF16),
            jax.ShapeDtypeStruct((2, half // 2, wide), BF16),
            jax.ShapeDtypeStruct((2, half // 2, wide), BF16),
            jax.ShapeDtypeStruct((8, wide), F32),
        ],
        in_specs=[any_spec()] * 14 + [vmem] * 2,
        out_specs=[any_spec(), vmem, any_spec(), vmem, any_spec(), vmem, any_spec(), vmem],
        scratch_shapes=[low(3, SEQ, 512)]
        + [low(3, 2, wide, 256), low(SEQ, wide), low(half, wide), pltpu.VMEM((half, wide), F32)]
        + [low(2, 128, length)] * 4
        + [low(128, length)] * 2
        + [low(4, rows, 128), low(2, half // 2, wide), low(2, half // 2, wide), low(512, SEQ)]
        + [low(2, 2, 128, 1536)] * 2
        + [low(2, 128, 1536)] * 4
        + [low(128, 1536)] * 4
        + [low(4, 3, 128, 256), pltpu.VMEM((6, 8, wide), F32), pltpu.VMEM((5, 8, wide), F32)]
        + [sems((15,)), sems((2, 2)), sems((2, 4)), sems((2, 6)), sems((2, 2)), sems((2, 3)), sems((2, 2)), sems((2, 2))]
        + [sems((2, 3)), sems((2, 2)), sems((2, 5))],
        compiler_params=params(collective_id=2, has_side_effects=True),
        name="tail",
    )(*back, small, normed, row, grad_hidden, keep1, got1, keep2, got2, gain, gain_two)


def fast_body(tokens, first_values, doc_lengths, cotangent, w_query, w_key, w_value, w_out, w_gate, w_up, w_down, gain_attn, gain_mlp):
    me, t = lax.axis_index("dp"), lax.axis_index("tensor")
    c = me % 2
    pair, side = t // 2, t % 2
    wide = tokens.shape[1]
    tiles = SEQ // TILE
    at = jnp.where(jnp.arange(8, dtype=jnp.int32) == 0, me, t).astype(jnp.int32)

    small_shard, big_shard = pack(w_query, w_key, w_value, w_out, w_gate, w_up, w_down)
    lengths = jnp.where(c == side, doc_lengths, across_c(doc_lengths))
    lengths = lax.dynamic_index_in_dim(lengths, pair, 0, keepdims=False)
    order = jnp.arange(DOCS, dtype=jnp.int32)
    ends = jnp.sum(jnp.where(order[None, :] <= order[:, None], lengths[None, :], 0), axis=1)
    freqs = 10000.0 ** (-(jnp.arange(32, dtype=F32) * 2.0 / HEAD))
    row, small, big, normed_one, q, k, v, cosine, sine = gather(
        ends, tokens, first_values, small_shard, big_shard, gain_attn[None], jnp.tile(freqs, 4)[None]
    )
    places = jnp.arange(SEQ, dtype=jnp.int32)
    starts = jnp.max(jnp.where(ends[None, :] <= places[:, None], ends[None, :], 0), axis=1)
    last = jnp.arange(tiles, dtype=jnp.int32) * TILE + (TILE - 1)
    stop = jnp.min(jnp.where(ends[None, :] > last[:, None], ends[None, :], SEQ), axis=1)
    bounds = jnp.concatenate([starts.reshape(tiles, TILE)[:, 0] // TILE, (stop - 1) // TILE])
    starts_by_tile = starts.reshape(tiles, TILE)

    row, cotangent = lax.optimization_barrier((row, cotangent))
    moved_cot = swap_halves(cotangent)
    att_own, att_send, lse = attend(at, bounds, q, k, v, starts_by_tile)
    att_other = across_c(att_send)
    out, grad_hidden, branch, normed_two, hid, ga_own, ga_other, gain_two, cot = mlp(
        at, att_own, att_other, row, cotangent, moved_cot, gain_mlp[None], small, big
    )
    moved_out = swap_halves(out)

    ga_got = across_c(ga_other)

    kept = weights(normed_two, cot, branch, hid, att_own, att_other)
    kept, ga_got = lax.optimization_barrier((kept, ga_got))
    got1, got2 = across_x(kept[0]), across_y(kept[2])

    rest = (att_own, att_send, lse, starts_by_tile, cosine, sine)
    dq0, dk0, dv0, held = attend_back(0, at, bounds, q, k, v, ga_own, ga_got, *rest)

    slabs = [jnp.where(pair == r, dv0[:, :256], dv0[:, 256:]) for r in range(2)]
    came = [
        move(slabs[r], lambda y, x, c, t, r=r: (y, x, t % 2, 2 * c + ((t // 2) ^ r))) for r in range(2)
    ]
    dq1, dk1, dv1 = attend_back(1, at, bounds, q, k, v, ga_own, ga_got, *rest, held)
    dv1, came = lax.optimization_barrier((dv1, came))

    first_back, pieces, got, own_heads, got_heads, grad_tokens, got_tokens, gains = tail(
        (dq0, dk0, dv0, dq1, dk1, dv1), small, normed_one, row, grad_hidden, kept[1], got1, kept[3], got2, gain_attn[None], gain_two
    )
    shape = (SEQ // 2, wide)
    grad_gate, grad_up, grad_down, grad_out, gq, gk, gv, grad_tokens, grad_first, layer_out = finish(
        at, pieces, got, own_heads, got_heads, grad_tokens.reshape(shape), got_tokens.reshape(shape), first_back, (*came, *slabs), out, moved_out, w_gate.shape[1]
    )
    return (
        layer_out,
        grad_tokens,
        grad_first,
        gq,
        gk,
        gv,
        grad_out,
        grad_gate.T,
        grad_up.T,
        grad_down,
        gains[0],
        gains[1],
    )


def solution(mesh):
    fits = dict(mesh.shape) == {"dp": 8, "tensor": 4}
    placed = (
        P(("dp", "tensor"), None),
        P("dp", "tensor"),
        P("dp", None),
        P(("dp", "tensor"), None),
        P("dp", "tensor"),
        P("dp", "tensor"),
        P("dp", "tensor"),
        P("tensor", "dp"),
        P("dp", "tensor"),
        P("dp", "tensor"),
        P("tensor", "dp"),
        P(),
        P(),
    )
    return jax.shard_map(
        fast_body if fits else general_body,
        mesh=mesh,
        in_specs=placed,
        out_specs=(
            P(("dp", "tensor"), None),
            P(("dp", "tensor"), None),
            P("dp", "tensor"),
            P("dp", "tensor"),
            P("dp", "tensor"),
            P("dp", "tensor"),
            P("tensor", "dp"),
            P("dp", "tensor"),
            P("dp", "tensor"),
            P("tensor", "dp"),
            P(),
            P(),
        ),
        check_vma=False,
    )
```

```python
import functools

import jax
import jax.numpy as jnp
from jax import lax
from jax.experimental import pallas as pl
from jax.experimental.pallas import tpu as pltpu
from jax.sharding import PartitionSpec as P

HEAD = 64
SEQ = 2048
DOCS = 8
EPSILON = 1e-05


def rms_norm(values, gain):
    factor = lax.rsqrt(jnp.mean(values * values, axis=1, keepdims=True) + EPSILON)
    return values * factor * gain


def documents(doc_lengths):
    ends = jnp.cumsum(doc_lengths, axis=1)
    starts = ends - doc_lengths
    places = jnp.arange(SEQ, dtype=jnp.int32)
    segment = jnp.sum((places[None, :, None] >= ends[:, None, :]).astype(jnp.int32), axis=2)
    member = segment[:, :, None] == jnp.arange(DOCS, dtype=jnp.int32)[None, None, :]
    offset = jnp.sum(jnp.where(member, starts[:, None, :], 0), axis=2)
    return (segment, (places[None, :] - offset).astype(jnp.float32))


def rotation(positions):
    half = HEAD // 2
    freqs = 10000.0 ** (-(jnp.arange(half, dtype=jnp.float32) * 2.0 / HEAD))
    angles = positions[:, None] * freqs[None, :]
    return (jnp.cos(angles), jnp.sin(angles))


def rotate(values, cosine, sine):
    shaped = values.reshape(values.shape[0], -1, HEAD)
    half = HEAD // 2
    first = shaped[:, :, :half]
    second = shaped[:, :, half:]
    cos_rows = cosine[:, None, :]
    sin_rows = sine[:, None, :]
    turned = jnp.concatenate(
        [first * cos_rows - second * sin_rows, second * cos_rows + first * sin_rows], axis=2
    )
    return turned.reshape(values.shape)


def rotate_back(grads, cosine, sine):
    shaped = grads.reshape(grads.shape[0], -1, HEAD)
    half = HEAD // 2
    first = shaped[:, :, :half]
    second = shaped[:, :, half:]
    cos_rows = cosine[:, None, :]
    sin_rows = sine[:, None, :]
    turned = jnp.concatenate(
        [first * cos_rows + second * sin_rows, second * cos_rows - first * sin_rows], axis=2
    )
    return turned.reshape(grads.shape)


def swiglu(gate, up_val):
    return jax.nn.silu(gate) * up_val


def product(left, right):
    return jnp.dot(left, right, preferred_element_type=jnp.float32)


def inner(left, right):
    return lax.dot_general(
        left, right, (((0,), (0,)), ((), ())), preferred_element_type=jnp.float32
    )


def outer(left, right):
    return lax.dot_general(
        left, right, (((1,), (1,)), ((), ())), preferred_element_type=jnp.float32
    )


def block_scores(queries, keys_all, segment, start, width):
    query_block = lax.dynamic_slice_in_dim(queries, start, width, 0)
    query_seg = lax.dynamic_slice_in_dim(segment, start, width, 0)
    scores = (
        jnp.einsum("qhd,khd->hqk", query_block, keys_all, preferred_element_type=jnp.float32)
        * 0.125
    )
    places = jnp.arange(SEQ, dtype=jnp.int32)
    rows_at = start + jnp.arange(width, dtype=jnp.int32)
    allowed = (query_seg[:, None] == segment[None, :]) & (places[None, :] <= rows_at[:, None])
    return (query_block, jnp.where(allowed[None], scores, -1e30))


def forward_row(pieces):
    queries, keys_all, values_all, segment = pieces
    width = min(512, SEQ)
    count = SEQ // width

    def forward_one_block(index):
        unused, scores = block_scores(queries, keys_all, segment, index * width, width)
        top = jnp.max(scores, axis=2, keepdims=True)
        expo = jnp.exp(scores - top)
        total = jnp.sum(expo, axis=2, keepdims=True)
        weights = (expo / total).astype(jnp.bfloat16)
        result = jnp.einsum("hqk,khd->qhd", weights, values_all, preferred_element_type=jnp.float32)
        return (result, (top + jnp.log(total))[:, :, 0])

    results, logsums = lax.map(forward_one_block, jnp.arange(count, dtype=jnp.int32))
    return (results.reshape(SEQ, queries.shape[1], HEAD), logsums)


def backward_row(pieces):
    queries, keys_all, values_all, segment, grad_rows, logsums = pieces
    width = min(512, SEQ)
    count = SEQ // width

    def backward_one_block(carry, extra):
        index, logsum = extra
        start = index * width
        query_block, scores = block_scores(queries, keys_all, segment, start, width)
        probs = jnp.exp(scores - logsum[:, :, None])
        grad_block = lax.dynamic_slice_in_dim(grad_rows, start, width, 0)
        grad_probs = jnp.einsum(
            "qhd,khd->hqk", grad_block, values_all, preferred_element_type=jnp.float32
        )
        delta = jnp.sum(probs * grad_probs, axis=2, keepdims=True)
        grad_scores = (probs * (grad_probs - delta)).astype(jnp.bfloat16)
        grad_query = (
            jnp.einsum("hqk,khd->qhd", grad_scores, keys_all, preferred_element_type=jnp.float32)
            * 0.125
        )
        grad_keys = (
            carry[0]
            + jnp.einsum(
                "hqk,qhd->khd", grad_scores, query_block, preferred_element_type=jnp.float32
            )
            * 0.125
        )
        grad_values = carry[1] + jnp.einsum(
            "hqk,qhd->khd",
            probs.astype(jnp.bfloat16),
            grad_block,
            preferred_element_type=jnp.float32,
        )
        return ((grad_keys, grad_values), grad_query)

    zeros = jnp.zeros(keys_all.shape, jnp.float32)
    sums, grad_queries = lax.scan(
        backward_one_block, (zeros, zeros), (jnp.arange(count, dtype=jnp.int32), logsums)
    )
    return (grad_queries.reshape(SEQ, queries.shape[1], HEAD), sums[0], sums[1])


def general_body(
    tokens,
    first_values,
    doc_lengths,
    cotangent,
    w_query,
    w_key,
    w_value,
    w_out,
    w_gate,
    w_up,
    w_down,
    gain_attn,
    gain_mlp,
):
    query_mat, key_mat, value_mat, out_mat, gate_mat, up_mat, down_mat = (
        lax.all_gather(w_query, "dp", axis=0, tiled=True),
        lax.all_gather(w_key, "dp", axis=0, tiled=True),
        lax.all_gather(w_value, "dp", axis=0, tiled=True),
        lax.all_gather(w_out, "dp", axis=1, tiled=True),
        lax.all_gather(w_gate, "dp", axis=0, tiled=True),
        lax.all_gather(w_up, "dp", axis=0, tiled=True),
        lax.all_gather(w_down, "dp", axis=1, tiled=True),
    )
    local_heads = query_mat.shape[1] // HEAD
    row_count = doc_lengths.shape[0]
    group = row_count * SEQ
    segment, positions = documents(doc_lengths)
    cosine, sine = rotation(positions.reshape(-1))

    def heads(matrix):
        return matrix.reshape(row_count, SEQ, local_heads, HEAD)

    inputs = tokens.astype(jnp.float32)
    normed_one, norm_one_back = jax.vjp(rms_norm, inputs, gain_attn)
    gathered_one = lax.all_gather(normed_one.astype(jnp.bfloat16), "tensor", axis=0, tiled=True)
    query_raw = product(gathered_one, query_mat)
    key_raw = product(gathered_one, key_mat)
    value_raw = product(gathered_one, value_mat)
    queries = rotate(query_raw, cosine, sine).astype(jnp.bfloat16)
    keys_low = rotate(key_raw, cosine, sine).astype(jnp.bfloat16)
    mixed_values = (0.5 * value_raw + 0.5 * first_values.astype(jnp.float32)).astype(jnp.bfloat16)
    attended, logsums = lax.map(
        forward_row, (heads(queries), heads(keys_low), heads(mixed_values), segment)
    )
    attended_low = attended.reshape(group, -1).astype(jnp.bfloat16)
    hidden_in = inputs + lax.psum_scatter(
        product(attended_low, out_mat), "tensor", scatter_dimension=0, tiled=True
    )
    normed_two, norm_two_back = jax.vjp(rms_norm, hidden_in, gain_mlp)
    normed_low_two = normed_two.astype(jnp.bfloat16)
    grad_out = cotangent.astype(jnp.float32)
    gathered_two = lax.all_gather(normed_low_two, "tensor", axis=0, tiled=True)
    activated, swiglu_back = jax.vjp(
        swiglu, product(gathered_two, gate_mat), product(gathered_two, up_mat)
    )
    act_low = activated.astype(jnp.bfloat16)
    layer_out = hidden_in + lax.psum_scatter(
        product(act_low, down_mat).astype(jnp.bfloat16), "tensor", scatter_dimension=0, tiled=True
    ).astype(jnp.float32)
    grad_rows = lax.all_gather(cotangent, "tensor", axis=0, tiled=True)
    grad_gate, grad_up = swiglu_back(outer(grad_rows, down_mat))
    gate_low = grad_gate.astype(jnp.bfloat16)
    up_low = grad_up.astype(jnp.bfloat16)
    grad_normed_two = lax.psum_scatter(
        outer(gate_low, gate_mat) + outer(up_low, up_mat), "tensor", scatter_dimension=0, tiled=True
    )
    grad_gate_mat = inner(gathered_two, gate_low)
    grad_up_mat = inner(gathered_two, up_low)
    grad_down_mat = inner(act_low, grad_rows)
    grad_hidden_two, grad_gain_two = norm_two_back(grad_normed_two)
    grad_hidden = grad_out + grad_hidden_two
    grad_branch = lax.all_gather(grad_hidden.astype(jnp.bfloat16), "tensor", axis=0, tiled=True)
    grad_attended = outer(grad_branch, out_mat).astype(jnp.bfloat16)
    grad_out_mat = inner(attended_low, grad_branch)
    grad_rot_query, grad_rot_key, grad_mixed = lax.map(
        backward_row,
        (
            heads(queries),
            heads(keys_low),
            heads(mixed_values),
            segment,
            heads(grad_attended),
            logsums,
        ),
    )
    grad_query_low = rotate_back(grad_rot_query.reshape(group, -1), cosine, sine).astype(
        jnp.bfloat16
    )
    grad_key_low = rotate_back(grad_rot_key.reshape(group, -1), cosine, sine).astype(jnp.bfloat16)
    grad_first = 0.5 * grad_mixed.reshape(group, -1)
    grad_value_low = grad_first.astype(jnp.bfloat16)
    grad_normed_one = lax.psum_scatter(
        outer(grad_query_low, query_mat)
        + outer(grad_key_low, key_mat)
        + outer(grad_value_low, value_mat),
        "tensor",
        scatter_dimension=0,
        tiled=True,
    )
    grad_query_mat = inner(gathered_one, grad_query_low)
    grad_key_mat = inner(gathered_one, grad_key_low)
    grad_value_mat = inner(gathered_one, grad_value_low)
    grad_inputs_one, grad_gain_one = norm_one_back(grad_normed_one)
    grad_tokens = grad_hidden + grad_inputs_one
    summed = (
        lax.psum_scatter(grad_query_mat, "dp", scatter_dimension=0, tiled=True),
        lax.psum_scatter(grad_key_mat, "dp", scatter_dimension=0, tiled=True),
        lax.psum_scatter(grad_value_mat, "dp", scatter_dimension=0, tiled=True),
        lax.psum_scatter(grad_out_mat, "dp", scatter_dimension=1, tiled=True),
        lax.psum_scatter(grad_gate_mat, "dp", scatter_dimension=0, tiled=True),
        lax.psum_scatter(grad_up_mat, "dp", scatter_dimension=0, tiled=True),
        lax.psum_scatter(grad_down_mat, "dp", scatter_dimension=1, tiled=True),
    )
    gain_sums = lax.psum((grad_gain_one, grad_gain_two), ("dp", "tensor"))
    return (
        layer_out.astype(jnp.bfloat16),
        grad_tokens,
        grad_first,
        summed[0],
        summed[1],
        summed[2],
        summed[3],
        summed[4],
        summed[5],
        summed[6],
        gain_sums[0],
        gain_sums[1],
    )


AXES = ("dp", "tensor")
MESH = pl.DeviceIdType.MESH
TILE = 256
NEG = -1e30
F32 = jnp.float32
BF16 = jnp.bfloat16


def flat(y, x, c, t):
    return ((y * 2 + x) * 2 + c) * 4 + t


def move(values, to):
    pairs = []
    for y in range(2):
        for x in range(2):
            for c in range(2):
                for t in range(4):
                    pair = (flat(y, x, c, t), flat(*to(y, x, c, t)))
                    if pair[0] != pair[1]:
                        pairs.append(pair)
    return lax.ppermute(values, AXES, pairs)


def across_x(values):
    return move(values, lambda y, x, c, t: (y, 1 - x, c, t))


def across_y(values):
    return move(values, lambda y, x, c, t: (1 - y, x, c, t))


def across_c(values):
    return move(values, lambda y, x, c, t: (y, x, 1 - c, t))


def along_t(values, step):
    return move(values, lambda y, x, c, t: (y, x, c, (t + step) % 4))


def swap_halves(values):
    return move(values, lambda y, x, c, t: (y, x, t % 2, (t // 2) * 2 + c))


def pack_kernel(wq, wk, wv, wo, wg, wu, wd, halves, small, big):
    small[0] = dot(wq[...], halves[...]).astype(BF16)
    small[1] = dot(wk[...], halves[...]).astype(BF16)
    small[2] = wv[...]
    small[3] = wo[...].T
    for n, units in enumerate((wg, wu, wd)):
        big[n] = units[...].reshape(big.shape[1:])


def pack(wq, wk, wv, wo, wg, wu, wd):
    wg, wu = wg.T, wu.T
    part, rows = wg.shape
    lane = jnp.arange(256, dtype=jnp.int32)
    source = ((lane & 127) >> 5) * 64 + (lane >> 7) * 32 + (lane & 31)
    halves = (lane[:, None] == source[None, :]).astype(BF16)
    return pl.pallas_call(
        pack_kernel,
        out_shape=[
            jax.ShapeDtypeStruct((4, rows, 256), BF16),
            jax.ShapeDtypeStruct((3, 2, part // 2, rows), BF16),
        ],
        compiler_params=params(),
        name="pack",
    )(wq, wk, wv, wo, wg, wu, wd, halves)


def meet(plane, c, t, dpx, dpy):
    barrier = pltpu.get_barrier_semaphore()
    for e in range(2):
        for d in range(4):
            if e or d:
                other = plane + lax.rem(c + e, 2)
                pl.semaphore_signal(barrier, inc=1, device_id=(other, lax.rem(t + d, 4)), device_id_type=MESH)
    pl.semaphore_signal(barrier, inc=1, device_id=(dpx, t), device_id_type=MESH)
    pl.semaphore_signal(barrier, inc=1, device_id=(dpy, t), device_id_type=MESH)
    pl.semaphore_wait(barrier, 9)


def gather_kernel(
    ends, tok, fv, small, big, gain, freqs, row_out, g_small, g_big, normed_out, q_out, k_out, v_out, cos_out, sin_out,
    row, first, w_s, n_s, q_s, k_s, v_s, raw_s, cos_s, sin_s,
    send, recv, relay_send, along_recv, next_send, next_recv, swap, fsend, frecv, here, tile_sem, end_sem,
):
    dp, t = lax.axis_index("dp"), lax.axis_index("tensor")
    c, x, y = lax.rem(dp, 2), lax.rem(lax.div(dp, 2), 2), lax.div(dp, 4)
    pair, side = lax.div(t, 2), lax.rem(t, 2)
    plane = dp - c
    dpx, dpy, dpc = dp + 2 - 4 * x, dp + 4 - 8 * y, dp + 1 - 2 * c
    dpxy = dpx + 4 - 8 * y

    meet(plane, c, t, dpx, dpy)
    def slot(k, at, owner, h):
        if k == 0:
            return g_small.at[pl.ds(2 * h, 2), at, pl.ds(owner * 128, 128), :]
        return g_big.at[k - 1, owner, h, at]

    def column(k, owner, h):
        if k == 0:
            return g_small.at[pl.ds(2 * h, 2), :, pl.ds(owner * 128, 128), :]
        return g_big.at[k - 1, owner, h]

    def both(k, at, owner):
        if k == 0:
            return g_small.at[:, at, pl.ds(owner * 128, 128), :]
        return g_big.at[k - 1, owner, :, at]

    def all_of(k, owner):
        if k == 0:
            return g_small.at[:, :, pl.ds(owner * 128, 128), :]
        return g_big.at[k - 1, owner]

    def shard(k):
        return small if k == 0 else big.at[k - 1]

    def part_of(k, h):
        return small.at[pl.ds(2 * h, 2)] if k == 0 else big.at[k - 1, h]

    def copy(k, n, src, dst, to, at):
        return pltpu.make_async_remote_copy(
            src_ref=src,
            dst_ref=dst,
            send_sem=send.at[k, n],
            recv_sem=recv.at[k, n],
            device_id=(to, at),
            device_id_type=MESH,
        )

    chunks = 4
    near, far = (dpx, dpy), (dpy, dpx)
    kept = [pltpu.make_async_copy(shard(k), both(k, t, dp), here.at[k]) for k in range(chunks)]

    def relay(k, at, side, src):
        return pltpu.make_async_remote_copy(
            src_ref=src,
            dst_ref=both(k, at, dp),
            send_sem=relay_send.at[k, at, side],
            recv_sem=along_recv.at[k, at],
            device_id=(dp, t + 2 * side - 1),
            device_id_type=MESH,
        )

    def onward(k, at, h, src):
        return pltpu.make_async_remote_copy(
            src_ref=src,
            dst_ref=slot(k, at, dp, h),
            send_sem=next_send.at[k, at, h],
            recv_sem=next_recv.at[k, at, h],
            device_id=(near[h], t),
            device_id_type=MESH,
        )

    def start_along(k):
        @pl.when(t < 3)
        def _():
            relay(k, t, 1, shard(k)).start()

        @pl.when(t > 0)
        def _():
            relay(k, t, 0, shard(k)).start()

    def pass_along(k, level):
        for side, at in ((1, t - level), (0, t + level)):

            @pl.when((at >= 0) & (at < 4))
            def _():
                block = both(k, at, dp)
                move = relay(k, at, side, block)
                move.wait_recv()

                @pl.when((t < 3) if side else (t > 0))
                def _():
                    move.start()

                for h in range(2):
                    onward(k, at, h, slot(k, at, dp, h)).start()

    def end_along(k):
        for level in range(4):
            for side, at in ((1, t - level), (0, t + level)):

                @pl.when((at >= 0) & (at < 4) & ((t < 3) if side else (t > 0)))
                def _():
                    relay(k, at, side, both(k, at, dp)).wait_send()

    across = [
        [
            copy(k, 2 * h + i, column(k, owner, h), column(k, owner, h), far[h], t)
            for h in range(2)
            for i, owner in enumerate((dp, near[h]))
        ]
        for k in range(chunks)
    ]
    over = [
        [copy(k, 4 + i, all_of(k, owner), all_of(k, owner), dpc, t) for i, owner in enumerate((dp, dpx, dpy, dpxy))]
        for k in range(chunks)
    ]

    order = (1, 0, 2, 3)
    start_along(order[0])
    for item in kept:
        item.start()
    for k in order:
        for h in range(2):
            onward(k, t, h, part_of(k, h)).start()
        if k == order[0]:
            start_along(order[1])

    moved = side != c
    to_own = pltpu.make_async_copy(tok, row.at[c], here.at[4])
    swapped = pltpu.make_async_remote_copy(
        src_ref=tok,
        dst_ref=row.at[side],
        send_sem=swap.at[0],
        recv_sem=swap.at[1],
        device_id=(plane + side, 2 * pair + c),
        device_id_type=MESH,
    )

    def start_tokens():
        @pl.when(moved)
        def _():
            swapped.start()

        @pl.when(jnp.logical_not(moved))
        def _():
            to_own.start()

    heads_core, slab = pair, side

    def first_copy(p):
        return pltpu.make_async_remote_copy(
            src_ref=fv.at[pl.ds(p * SEQ, SEQ), :],
            dst_ref=first.at[slab],
            send_sem=fsend.at[p],
            recv_sem=frecv.at[slab],
            device_id=(plane + heads_core, 2 * p + c),
            device_id_type=MESH,
        )

    def first_local(p):
        return pltpu.make_async_copy(fv.at[pl.ds(p * SEQ, SEQ), :], first.at[slab], here.at[5])

    stays = [(heads_core == c) & (t == 2 * p + c) for p in range(2)]

    def start_first():
        for p in range(2):

            @pl.when(stays[p])
            def _():
                first_local(p).start()

            @pl.when(jnp.logical_not(stays[p]))
            def _():
                first_copy(p).start()

    def pass_over(k):
        for item in across[k]:
            item.wait_recv()
        for item in over[k][1:]:
            item.start()

    def pass_next(k):
        for at in range(4):
            for h in range(2):
                onward(k, at, h, slot(k, at, dp, h)).wait_recv()
        for item in across[k]:
            item.start()

    def table(i, carry):
        rows = pl.ds(pl.multiple_of(i * TILE, TILE), TILE)
        at_row = lax.broadcasted_iota(jnp.int32, (TILE, 128), 0) + i * TILE
        begin = jnp.zeros_like(at_row)
        for k in range(DOCS):
            begin = jnp.maximum(begin, jnp.where(at_row >= ends[k], ends[k], 0))
        angles = (at_row - begin).astype(F32) * freqs[...]
        cos_s[rows, :] = jnp.cos(angles)
        sin_s[rows, :] = jnp.sin(angles)
        return carry

    lax.fori_loop(0, SEQ // TILE, table, 0)
    tables = [pltpu.make_async_copy(cos_s, cos_out, end_sem.at[0]), pltpu.make_async_copy(sin_s, sin_out, end_sem.at[1])]

    for i, k in enumerate(order):
        pass_along(k, 1)
        if i + 2 < chunks:
            start_along(order[i + 2])
        if i:
            pass_next(order[i - 1])
        pass_along(k, 2)
        pass_along(k, 3)
        kept[k].wait()
        over[k][0].start()
        if i == 2:
            start_tokens()
        if i == 3:
            start_first()
        if i >= 2:
            pass_over(order[i - 2])
    pass_next(order[3])
    for item in tables:
        item.start()
    for item in over[0]:
        item.wait_recv()
    load_w = pltpu.make_async_copy(g_small.at[pl.ds(0, 3), pl.ds(2 * c, 2)], w_s, end_sem.at[2])
    load_w.start()

    @pl.when(moved)
    def _():
        swapped.wait_send()
        swapped.wait_recv()

    @pl.when(jnp.logical_not(moved))
    def _():
        to_own.wait()

    given = pltpu.make_async_remote_copy(
        src_ref=row.at[c],
        dst_ref=row.at[c],
        send_sem=swap.at[2],
        recv_sem=swap.at[3],
        device_id=(dpc, t),
        device_id_type=MESH,
    )
    given.start()
    load_w.wait()

    def rows_of(half, n):
        return pl.ds(pl.multiple_of(half * (SEQ // 2) + n * 512, 512), 512)

    def done_copies(half, n):
        rows = rows_of(half, n)
        return [
            pltpu.make_async_copy(src.at[rows, :], dst.at[rows, :], tile_sem.at[2 * half + n, m])
            for m, (src, dst) in enumerate(((n_s, normed_out), (q_s, q_out), (k_s, k_out)))
        ]

    def project(half, n):
        rows = rows_of(half, n)
        values = row[half, pl.ds(pl.multiple_of(n * 512, 512), 512), :].astype(F32)
        factor = lax.rsqrt(jnp.mean(values * values, axis=1, keepdims=True) + EPSILON)
        normed = (values * factor * gain[...]).astype(BF16)
        n_s[rows, :] = normed
        cos, sin = cos_s[rows, :], sin_s[rows, :]
        for u in range(2):
            for m, out, scale in ((0, q_s, 0.125), (1, k_s, 1.0)):
                raw = dot(normed, w_s[m, u])
                a, b = raw[:, :128], raw[:, 128:]
                out[rows, u * 256 : u * 256 + 128] = ((a * cos - b * sin) * scale).astype(BF16)
                out[rows, u * 256 + 128 : u * 256 + 256] = ((b * cos + a * sin) * scale).astype(BF16)
            raw_s[rows, u * 256 : u * 256 + 256] = 0.5 * dot(normed, w_s[2, u])
        for item in done_copies(half, n):
            item.start()
        return 0

    row_copy = pltpu.make_async_copy(row, row_out, end_sem.at[3])

    def half_row(i, carry):
        @pl.when(i == 1)
        def _():
            pass_over(order[2])
            given.wait_recv()
            row_copy.start()

        half = c + i - 2 * c * i
        lax.fori_loop(0, 2, lambda n, _: project(half, n), 0)
        return carry

    lax.fori_loop(0, 2, half_row, 0)
    pass_over(order[3])

    for p in range(2):

        @pl.when(stays[p])
        def _():
            first_local(p).wait()

        @pl.when(jnp.logical_not(stays[p]))
        def _():
            first_copy(p).wait_send()

    for u in range(2):
        came = pltpu.make_async_remote_copy(
            src_ref=first.at[u],
            dst_ref=first.at[u],
            send_sem=fsend.at[u],
            recv_sem=frecv.at[u],
            device_id=(dpc, t),
            device_id_type=MESH,
        )

        @pl.when((side != c) | (t != 2 * c + u))
        def _():
            came.wait_recv()

    def mixed_copy(n):
        rows = pl.ds(pl.multiple_of(n * 512, 512), 512)
        return rows, pltpu.make_async_copy(v_s.at[rows, :], v_out.at[rows, :], tile_sem.at[n, 3])

    def mix(n, carry):
        rows, item = mixed_copy(n)
        for u in range(2):
            lanes = slice(u * 256, u * 256 + 256)
            v_s[rows, lanes] = (raw_s[rows, lanes] + 0.5 * first[u, rows, :].astype(F32)).astype(BF16)
        item.start()
        return carry

    lax.fori_loop(0, 4, mix, 0)
    outs = []
    for n in range(4):
        outs += done_copies(n // 2, n % 2) + [mixed_copy(n)[1]]
    given.wait_send()
    for k in range(chunks):
        if k:
            for item in over[k]:
                item.wait_recv()
        end_along(k)
        for item in across[k] + over[k]:
            item.wait_send()
        for at in range(4):
            for h in range(2):
                onward(k, at, h, slot(k, at, dp, h)).wait_send()
    for item in outs + tables + [row_copy]:
        item.wait()


def gather(ends, tok, fv, small, big, gain, freqs):
    part, rows = big.shape[2:]
    wide = tok.shape[1]
    vmem = pl.BlockSpec(memory_space=pltpu.VMEM)
    sems = pltpu.SemaphoreType.DMA
    low = lambda *shape: pltpu.VMEM(shape, BF16)
    shapes = [(2, SEQ // 2, wide), (4, 4, wide, 256), (3, 8, 2, 4, part, rows), (SEQ, wide)] + [(SEQ, 512)] * 3
    return pl.pallas_call(
        gather_kernel,
        out_shape=[jax.ShapeDtypeStruct(shape, BF16) for shape in shapes]
        + [jax.ShapeDtypeStruct((SEQ, 128), F32)] * 2,
        in_specs=[pl.BlockSpec(memory_space=pltpu.SMEM)] + [vmem] * 6,
        out_specs=[any_spec()] * 9,
        scratch_shapes=[low(2, SEQ // 2, wide), low(2, SEQ, 256), low(3, 2, wide, 256), low(SEQ, wide)]
        + [low(SEQ, 512)] * 3
        + [pltpu.VMEM((SEQ, 512), F32)]
        + [pltpu.VMEM((SEQ, 128), F32)] * 2
        + [
            sems((4, 8)),
            sems((4, 8)),
            sems((4, 4, 2)),
            sems((4, 4)),
            sems((4, 4, 2)),
            sems((4, 4, 2)),
            sems((4,)),
            sems((2,)),
            sems((2,)),
            sems((6,)),
            sems((4, 4)),
            sems((4,)),
        ],
        compiler_params=params(collective_id=0, has_side_effects=True),
        name="gather",
    )(ends, tok, fv, small, big, gain, freqs)


def dot(left, right):
    return jnp.dot(left, right, preferred_element_type=F32)


def dot_nt(left, right):
    return lax.dot_general(left, right, (((1,), (1,)), ((), ())), preferred_element_type=F32)


def dot_tn(left, right):
    return lax.dot_general(left, right, (((0,), (0,)), ((), ())), preferred_element_type=F32)


def any_spec():
    return pl.BlockSpec(memory_space=pl.ANY)


def params(**more):
    return pltpu.CompilerParams(vmem_limit_bytes=62 * 1024 * 1024, **more)


def cost(flops, size, exps=0):
    return pl.CostEstimate(flops=int(flops), bytes_accessed=int(size), transcendentals=int(exps))


def once(shape, place):
    return pl.BlockSpec(shape, place, pipeline_mode=pl.Buffered(1))


def head_masks(rows):
    lane = lax.broadcasted_iota(jnp.int32, (rows, 256), 1)
    return (lane & 127) >> 5, lane >> 6


def attend_kernel(at, bounds, q_ref, k_ref, v_ref, starts, own_ref, send_ref, lse_ref, kept, turned, acc):
    tiles = SEQ // TILE
    of_qk, _ = head_masks(TILE)
    row = lax.broadcasted_iota(jnp.int32, (TILE, TILE), 0)
    lane = lax.broadcasted_iota(jnp.int32, (TILE, TILE), 1)
    slabs = [slice(0, 256), slice(256, 512)]

    def turn_values(j, carry):
        there = pl.ds(pl.multiple_of(j * TILE, TILE), TILE)
        turned[j] = v_ref[there, :].T
        return carry

    lax.fori_loop(0, tiles, turn_values, 0)

    def eighths(values, reduce):
        return reduce(values.reshape(TILE // 8, 8, 4 * TILE), axis=0)

    def query_tile(i, carry):
        here = pl.ds(pl.multiple_of(i * TILE, TILE), TILE)
        q4 = []
        for slab in slabs:
            q = q_ref[here, slab]
            zero = jnp.zeros_like(q)
            q4.append(jnp.concatenate([jnp.where(of_qk == h, q, zero) for h in range(4)], axis=0))
        low = bounds[i]
        begin = starts[pl.ds(i, 1), :]
        limit = lane + i * TILE

        def score(j, tops):
            there = pl.ds(pl.multiple_of(j * TILE, TILE), TILE)
            at_row = row + j * TILE
            ok = (at_row >= begin) & (at_row <= limit)
            ok = jnp.concatenate([ok] * 4, axis=1)
            new = []
            for u, slab in enumerate(slabs):
                s = jnp.where(ok, dot_nt(k_ref[there, slab], q4[u]), NEG)
                kept[j - low, u] = s
                new.append(jnp.maximum(tops[u], eighths(s, jnp.max)))
            return tuple(new)

        start = jnp.full((8, 4 * TILE), NEG, F32)
        tops = lax.fori_loop(low, i + 1, score, (start, start))
        tops = [jnp.max(top, axis=0, keepdims=True) for top in tops]
        acc[...] = jnp.zeros_like(acc)

        def weigh(j, totals):
            new = []
            for u in range(2):
                e = jnp.exp(kept[j - low, u] - tops[u])
                p = e.astype(BF16)
                for h in range(4):
                    part = slice(u * 256 + h * 64, u * 256 + h * 64 + 64)
                    acc[part] += dot(turned[j, part, :], p[:, h * TILE : (h + 1) * TILE])
                new.append(totals[u] + eighths(e, jnp.sum))
            return tuple(new)

        zero = jnp.zeros((8, 4 * TILE), F32)
        totals = lax.fori_loop(low, i + 1, weigh, (zero, zero))
        for u, slab in enumerate(slabs):
            total = jnp.sum(totals[u], axis=0, keepdims=True)
            inverse = 1.0 / total
            scaled = [
                acc[u * 256 + h * 64 : u * 256 + h * 64 + 64] * inverse[:, h * TILE : (h + 1) * TILE] for h in range(4)
            ]
            done = jnp.concatenate(scaled, axis=0).T.astype(BF16)
            local = pl.ds(pl.multiple_of(lax.rem(i, tiles // 2) * TILE, TILE), TILE)
            mine = lax.div(i, tiles // 2) == (at[0] & 1)

            @pl.when(mine)
            def _():
                own_ref[local, slab] = done

            @pl.when(jnp.logical_not(mine))
            def _():
                send_ref[local, slab] = done

            lse_ref[u, pl.ds(i, 1), :] = tops[u] + jnp.log(total)
        return carry

    lax.fori_loop(0, tiles, query_tile, 0)


def attend(at, bounds, q, k, v, starts):
    tiles = SEQ // TILE
    vmem = pl.BlockSpec(memory_space=pltpu.VMEM)
    return pl.pallas_call(
        attend_kernel,
        out_shape=[
            jax.ShapeDtypeStruct((SEQ // 2, 512), BF16),
            jax.ShapeDtypeStruct((SEQ // 2, 512), BF16),
            jax.ShapeDtypeStruct((2, tiles, 4 * TILE), F32),
        ],
        in_specs=[pl.BlockSpec(memory_space=pltpu.SMEM)] * 2 + [vmem] * 4,
        out_specs=[vmem] * 3,
        scratch_shapes=[
            pltpu.VMEM((tiles, 2, TILE, 4 * TILE), F32),
            pltpu.VMEM((tiles, 512, TILE), BF16),
            pltpu.VMEM((512, TILE), F32),
        ],
        compiler_params=params(),
        cost_estimate=cost(20e9, 12e6, 1e7),
        name="attend",
    )(at, bounds, q, k, v, starts)


def attend_back_kernel(
    at, bounds, q_hbm, k_hbm, v_hbm, do_own, do_other, o_own, o_other, lse_ref, starts, cosine, sine, *rest, part,
):
    if part:
        held_hbm, rest = rest[0], rest[1:]
        dq_hbm, dk_hbm, dv_hbm = rest[:3]
        rest = rest[3:]
    else:
        dq_hbm, dk_hbm, dv_hbm, held_hbm = rest[:4]
        rest = rest[4:]
    attend_back_part(
        at, bounds, q_hbm, k_hbm, v_hbm, do_own, do_other, o_own, o_other, lse_ref, starts, cosine, sine, held_hbm, dq_hbm, dk_hbm,
        dv_hbm, *rest, part=part
    )


def attend_back_part(
    at, bounds, q_hbm, k_hbm, v_hbm, do_own, do_other, o_own, o_other, lse_ref, starts, cosine, sine, held_hbm, dq_hbm, dk_hbm, dv_hbm,
    q_ref, k_ref, v_ref, do_ref, o_ref, dq_ref, dk_ref, dv_ref, dq_acc, delta, dk_acc, dv_acc, load, store, *, part,
):
    tiles = SEQ // TILE
    of_qk, of_v = head_masks(TILE)
    row = lax.broadcasted_iota(jnp.int32, (TILE, TILE), 0)
    lane = lax.broadcasted_iota(jnp.int32, (TILE, TILE), 1)
    slabs = [slice(0, 256), slice(256, 512)]
    pick = (lax.broadcasted_iota(jnp.int32, (8, 256), 1) >> 6) == lax.broadcasted_iota(
        jnp.int32, (8, 256), 0
    )
    pick = pick.astype(F32)
    half = SEQ // 2
    low = pl.multiple_of((at[0] & 1) * half, half)
    mine, others = pl.ds(low, half), pl.ds(half - low, half)
    first_half, second_half = pl.ds(0, half), pl.ds(half, half)
    mine_second = (at[0] & 1) == 1
    here_half = second_half if part else first_half
    q_rows = second_half if part else pl.ds(0, SEQ)
    plain = [
        (q_hbm.at[q_rows, :], q_ref.at[q_rows, :]),
        (k_hbm.at[here_half, :], k_ref.at[here_half, :]),
        (v_hbm.at[here_half, :], v_ref.at[here_half, :]),
    ]
    if part:
        plain.append((held_hbm, dq_acc.at[pl.ds(tiles // 2, tiles // 2)]))
    loads = [pltpu.make_async_copy(src, dst, load.at[4 + n]) for n, (src, dst) in enumerate(plain)]

    def half_loads(own, other, dst, n):
        pairs = [(own, mine, mine_second), (other, others, jnp.logical_not(mine_second))]
        for e, (src, rows, wanted) in enumerate(pairs):
            yield pltpu.make_async_copy(src, dst.at[rows, :], load.at[n + e]), wanted

    parts = list(half_loads(do_own, do_other, do_ref, 0)) + list(half_loads(o_own, o_other, o_ref, 2))

    def each(action):
        for item, wanted in parts:
            if part:
                pl.when(wanted)(functools.partial(action, item))
            else:
                action(item)

    each(lambda item: item.start())
    for item in loads:
        item.start()
    if not part:
        dq_acc[...] = jnp.zeros_like(dq_acc)
    each(lambda item: item.wait())

    def prepare(i, carry):
        here = pl.ds(pl.multiple_of(i * TILE, TILE), TILE)
        for u, slab in enumerate(slabs):
            both = do_ref[here, slab].astype(F32) * o_ref[here, slab].astype(F32)
            sums = lax.dot_general(
                pick, both, (((1,), (1,)), ((), ())), precision=lax.Precision.HIGHEST, preferred_element_type=F32
            )
            for h in range(4):
                delta[u, pl.ds(i, 1), h * TILE : (h + 1) * TILE] = sums[h : h + 1]
        return carry

    middle = tiles // 2
    lax.fori_loop(middle * part, tiles, prepare, 0)
    for item in loads:
        item.wait()

    def rotate_out(values, here, out, low, scale):
        a, b = values[:, :128], values[:, 128:]
        cos, sin = cosine[here, :], sine[here, :]
        out[here, low : low + 128] = ((a * cos + b * sin) * scale).astype(BF16)
        out[here, low + 128 : low + 256] = ((b * cos - a * sin) * scale).astype(BF16)

    def split(values, of):
        zero = jnp.zeros_like(values)
        return jnp.concatenate([jnp.where(of == h, values, zero) for h in range(4)], axis=0)

    def key_tile(j, carry):
        there = pl.ds(pl.multiple_of(j * TILE, TILE), TILE)
        at_row = row + j * TILE
        dk_acc[...] = jnp.zeros_like(dk_acc)
        dv_acc[...] = jnp.zeros_like(dv_acc)

        def query_tile(i, carry):
            here = pl.ds(pl.multiple_of(i * TILE, TILE), TILE)
            at_lane = lane + i * TILE
            ok = (at_row >= starts[pl.ds(i, 1), :]) & (at_row <= at_lane)
            ok = jnp.concatenate([ok] * 4, axis=1)
            for u, slab in enumerate(slabs):
                q4 = split(q_ref[here, slab], of_qk)
                do4 = split(do_ref[here, slab], of_v)
                s = dot_nt(k_ref[there, slab], q4)
                dp = dot_nt(v_ref[there, slab], do4)
                p = jnp.exp(jnp.where(ok, s - lse_ref[u, pl.ds(i, 1), :], NEG))
                ds = (p * (dp - delta[u, pl.ds(i, 1), :])).astype(BF16)
                dv_acc[u] += dot(p.astype(BF16), do4)
                dk_acc[u] += dot(ds, q4)
                ds4 = jnp.concatenate([ds[:, h * TILE : (h + 1) * TILE] for h in range(4)], axis=0)
                dq_acc[i, u] += dot_tn(ds4, split(k_ref[there, slab], of_qk))
            return carry

        lax.fori_loop(j, bounds[tiles + j] + 1, query_tile, 0)
        for u, slab in enumerate(slabs):
            rotate_out(dk_acc[u], there, dk_ref, u * 256, 1.0)
            dv_ref[there, slab] = (0.5 * dv_acc[u]).astype(BF16)
        local = pl.ds(pl.multiple_of((j - middle * part) * TILE, TILE), TILE)
        pltpu.make_async_copy(dk_ref.at[there, :], dk_hbm.at[local, :], store.at[0]).start()
        pltpu.make_async_copy(dv_ref.at[there, :], dv_hbm.at[local, :], store.at[1]).start()
        return carry

    lax.fori_loop(middle * part, middle * part + middle, key_tile, 0)
    if not part:
        held = pltpu.make_async_copy(dq_acc.at[pl.ds(middle, middle)], held_hbm, store.at[3])
        held.start()

    def finish_tile(i, carry):
        here = pl.ds(pl.multiple_of(i * TILE, TILE), TILE)
        for u in range(2):
            rotate_out(dq_acc[i, u], here, dq_ref, u * 256, 0.125)
        local = pl.ds(pl.multiple_of((i - middle * part) * TILE, TILE), TILE)
        pltpu.make_async_copy(dq_ref.at[here, :], dq_hbm.at[local, :], store.at[2]).start()
        return carry

    lax.fori_loop(middle * part, middle * part + middle, finish_tile, 0)
    for n, (src, dst) in enumerate(((dk_ref, dk_hbm), (dv_ref, dv_hbm), (dq_ref, dq_hbm))):
        pltpu.make_async_copy(src.at[here_half, :], dst, store.at[n]).wait()
    if not part:
        held.wait()


def attend_back(part, at, bounds, q, k, v, do_own, do_other, o_own, o_other, lse, starts, cosine, sine, *held):
    tiles = SEQ // TILE
    vmem = pl.BlockSpec(memory_space=pltpu.VMEM)
    sems = pltpu.SemaphoreType.DMA
    outs = [jax.ShapeDtypeStruct((SEQ // 2, 512), BF16)] * 3
    if not part:
        outs.append(jax.ShapeDtypeStruct((tiles // 2, 2, TILE, 256), F32))
    return pl.pallas_call(
        functools.partial(attend_back_kernel, part=part),
        out_shape=outs,
        in_specs=[pl.BlockSpec(memory_space=pltpu.SMEM)] * 2 + [any_spec()] * 7 + [vmem] * 4 + [any_spec()] * len(held),
        out_specs=[any_spec()] * len(outs),
        scratch_shapes=[pltpu.VMEM((SEQ, 512), BF16)] * 8
        + [
            pltpu.VMEM((tiles, 2, TILE, 256), F32),
            pltpu.VMEM((2, tiles, 4 * TILE), F32),
            pltpu.VMEM((2, TILE, 256), F32),
            pltpu.VMEM((2, TILE, 256), F32),
            sems((8,)),
            sems((4,)),
        ],
        compiler_params=params(),
        cost_estimate=cost(25e9, 12e6, 5e6),
        name="attend_back",
    )(at, bounds, q, k, v, do_own, do_other, o_own, o_other, lse, starts, cosine, sine, *held)


def mlp_kernel(at, att_own, att_other, tok, cot_here, cot_moved, gain, wo, big, *rest):
    (out, gh_out, gb_out, n2_out, hid_out, ga_own, ga_other, gg_out, cot_out) = rest[:9]
    (wg, wu, wd, down, back, sems) = rest[9:]
    step = pl.program_id(0)
    c = at[0] & 1

    @pl.when(step == 0)
    def _():
        for n, held in enumerate((wg, wu, wd)):
            for owner in range(8):
                pltpu.make_async_copy(
                    big.at[n, owner], held.at[:, owner * 128 : owner * 128 + 128], sems.at[n]
                ).start()
        gg_out[...] = jnp.zeros_like(gg_out)

    hidden = tok[0].astype(F32)
    for e, att in enumerate((att_own, att_other)):
        for u in range(2):
            hidden += dot_nt(att[:, u * 256 : u * 256 + 256], wo[0, 2 * (c ^ e) + u])
    factor = lax.rsqrt(jnp.mean(hidden * hidden, axis=1, keepdims=True) + EPSILON)
    gains = gain[...]
    normed = (hidden * factor * gains).astype(BF16)
    n2_out[...] = normed
    g = jnp.where((at[1] & 1) == c, cot_here[...], cot_moved[...])
    cot_out[...] = g

    @pl.when(step == 0)
    def _():
        for n, held in enumerate((wg, wu, wd)):
            pltpu.make_async_copy(held, held, sems.at[n]).wait()

    down[...] = hidden
    back[...] = jnp.zeros_like(back)
    units, block = wg.shape[0], 768

    def unit_block(low, width):
        part = pl.ds(low, width)
        gate, up, grad_act = dot_nt(normed, wg[part, :]), dot_nt(normed, wu[part, :]), dot_nt(g, wd[part, :])
        sig = 1.0 / (1.0 + jnp.exp(-gate))
        silu = gate * sig
        act = (silu * up).astype(BF16)
        grad_up = (grad_act * silu).astype(BF16)
        grad_gate = (grad_act * up * (sig * (1.0 + gate * (1.0 - sig)))).astype(BF16)
        hid_out[0, :, part], hid_out[1, :, part], hid_out[2, :, part] = grad_gate, grad_up, act
        down[...] += dot(act, wd[part, :])
        back[...] += dot(grad_gate, wg[part, :]) + dot(grad_up, wu[part, :])

    def whole_block(k, carry):
        unit_block(pl.multiple_of(k * block, block), block)
        return carry

    lax.fori_loop(0, units // block, whole_block, 0)
    if units % block:
        unit_block(units - units % block, units % block)
    grad = back[...]
    out[...] = down[...].astype(BF16)
    gg_out[...] += jnp.sum((grad * hidden * factor).reshape(-1, 8, grad.shape[1]), axis=0)
    scaled = grad * gains
    mean = jnp.mean(scaled * hidden, axis=1, keepdims=True)
    grad_hidden = g.astype(F32) + factor * scaled - hidden * (factor * factor * factor * mean)
    gh_out[...] = grad_hidden
    branch = grad_hidden.astype(BF16)
    gb_out[...] = branch
    for e, ga in enumerate((ga_own, ga_other)):
        for u in range(2):
            ga[:, u * 256 : u * 256 + 256] = dot(branch, wo[0, 2 * (c ^ e) + u]).astype(BF16)


def mlp(at, att_own, att_other, tok, cot_here, cot_moved, gain, small, big):
    _, count, wide = tok.shape
    big = big.reshape(3, 8, -1, 128)
    rows, units = 256, big.shape[2]
    row = lambda width: pl.BlockSpec((rows, width), lambda i, at: (i, 0))
    grid = pltpu.PrefetchScalarGridSpec(
        num_scalar_prefetch=1,
        grid=(count // rows,),
        in_specs=[
            row(512),
            row(512),
            pl.BlockSpec((1, rows, wide), lambda i, at: (at[0] & 1, i, 0)),
            row(wide),
            row(wide),
            pl.BlockSpec((1, wide), lambda i, at: (0, 0)),
            once((1, 4, wide, 256), lambda i, at: (3, 0, 0, 0)),
            any_spec(),
        ],
        out_specs=[
            row(wide),
            row(wide),
            row(wide),
            row(wide),
            pl.BlockSpec((3, rows, units), lambda i, at: (0, i, 0)),
            row(512),
            row(512),
            pl.BlockSpec((8, wide), lambda i, at: (0, 0)),
            row(wide),
        ],
        scratch_shapes=[pltpu.VMEM((units, wide), BF16)] * 3
        + [pltpu.VMEM((rows, wide), F32)] * 2
        + [pltpu.SemaphoreType.DMA((3,))],
    )
    tokens = lambda width, kind=BF16: jax.ShapeDtypeStruct((count, width), kind)
    return pl.pallas_call(
        mlp_kernel,
        out_shape=[
            tokens(wide),
            tokens(wide, F32),
            tokens(wide),
            tokens(wide),
            jax.ShapeDtypeStruct((3, count, units), BF16),
            tokens(512),
            tokens(512),
            jax.ShapeDtypeStruct((8, wide), F32),
            tokens(wide),
        ],
        grid_spec=grid,
        compiler_params=params(),
        cost_estimate=cost(2 * count * wide * (6 * units + 2 * wide), 60e6, 3e6),
        name="mlp",
    )(at, att_own, att_other, tok, cot_here, cot_moved, gain, small, big)


def turn_rows(source, plane, parity, held):
    for rel in range(4):
        block = ((plane ^ rel) * 2 + parity) * 128
        held[rel * 128 : rel * 128 + 128, :] = source[:, pl.ds(pl.multiple_of(block, 128), 128)].T


def place_first(send, keep, done, lanes):
    for yr in range(2):
        keep[yr, :, lanes] = done[2 * yr]
        send[yr, :, lanes] = done[2 * yr + 1]


def place_second(send, keep, done, lanes):
    for xr in range(2):
        keep[xr, :, lanes] = done[xr]
        send[xr, :, lanes] = done[2 + xr]


def weights_kernel(
    n2, g_hbm, branch_hbm, hid, own_hbm, other_hbm, send1_out, keep1_out, send2_out, keep2_out,
    turned, g, branch, own, other, send1, keep1, send2, keep2, given, got, out_sem, in_sem, load, store,
):
    step = pl.program_id(0)
    dp, t = lax.axis_index("dp"), lax.axis_index("tensor")
    c = lax.rem(dp, 2)
    plane = lax.div(dp, 2)
    n = lax.rem(step, 4)
    units = hid.shape[2] // 2
    loads = [
        pltpu.make_async_copy(src, dst, load.at[m])
        for m, (src, dst) in enumerate(((g_hbm, g), (branch_hbm, branch), (own_hbm, own), (other_hbm, other)))
    ]

    @pl.when(step == 0)
    def _():
        for item in loads:
            item.start()
        barrier = pltpu.get_barrier_semaphore()
        pl.semaphore_signal(barrier, inc=1, device_id=(dp + 1 - 2 * c, t), device_id_type=MESH)
        pl.semaphore_wait(barrier, 1)

    @pl.when(step == 2)
    def _():
        for item in loads:
            item.wait()

    def lanes_of(k):
        return pl.ds(k * units, units if k < 3 else 512)

    def exchange(k):
        return pltpu.make_async_remote_copy(
            src_ref=given.at[:, :, :, lanes_of(k)],
            dst_ref=got.at[:, :, :, lanes_of(k)],
            send_sem=out_sem.at[k],
            recv_sem=in_sem.at[k],
            device_id=(dp + 1 - 2 * c, t),
            device_id_type=MESH,
        )

    def stores(k):
        arrays = ((send1, send1_out), (keep1, keep1_out), (send2, send2_out), (keep2, keep2_out))
        return [
            pltpu.make_async_copy(src.at[:, :, lanes_of(k)], dst.at[:, :, lanes_of(k)], store.at[m, k])
            for m, (src, dst) in enumerate(arrays)
        ]

    def turn(source, parity):
        x = lax.rem(plane, 2)
        y = lax.div(plane, 2)
        for rel in range(4):
            yy, xx = (y, 1 - y)[rel // 2], (x, 1 - x)[rel % 2]
            block = pl.multiple_of((yy * 4 + xx * 2 + parity) * 128, 128)
            turned[rel * 128 : rel * 128 + 128, :] = source[:, pl.ds(block, 128)].T

    parity = jnp.where(step < 4, 1 - c, c)
    for at_n, source in ((0, n2), (2, g), (3, branch)):

        @pl.when(n == at_n)
        def _():
            turn(source, parity)

    for k in range(4):

        @pl.when(step == k + 1)
        def _():
            exchange(k).start()

        @pl.when(step == k + 4)
        def _():
            exchange(k).wait_recv()

        if k < 3:

            @pl.when(step == k + 5)
            def _():
                for item in stores(k):
                    item.start()

    def give_or_keep(product, h, lanes):
        @pl.when(step < 4)
        def _():
            given[:, h, :, lanes] = product.astype(BF16).reshape(4, 128, product.shape[1])

        for e, (place, send, keep) in enumerate(((place_first, send1, keep1), (place_second, send2, keep2))):

            @pl.when((step >= 4) & (h == e))
            def _():
                done = [
                    (product[r * 128 : r * 128 + 128] + got[r, h, :, lanes].astype(F32)).astype(BF16) for r in range(4)
                ]
                place(send, keep, done, lanes)

    @pl.when(n < 3)
    def _():
        def one(h, carry):
            right = hid[0, :, pl.ds(pl.multiple_of(h * units, 128), units)]
            give_or_keep(dot(turned[...], right), h, pl.ds(pl.multiple_of(n * units, 128), units))
            return carry

        lax.fori_loop(0, 2, one, 0)

    @pl.when(n == 3)
    def _():
        def one(h, carry):
            right = jnp.where(c == h, own[...], other[...])
            give_or_keep(dot(turned[...], right), h, lanes_of(3))
            return carry

        lax.fori_loop(0, 2, one, 0)

    @pl.when(step == 7)
    def _():
        for item in stores(3):
            item.start()
        for k in range(4):
            exchange(k).wait_send()
            for item in stores(k):
                item.wait()


def weights(n2, g, branch, hid, own, other):
    count, wide = n2.shape
    units = hid.shape[2] // 2
    length = 3 * units + 512
    low = lambda *shape: pltpu.VMEM(shape, BF16)
    sems = pltpu.SemaphoreType.DMA
    grid = pl.GridSpec(
        grid=(8,),
        in_specs=[
            pl.BlockSpec((count, wide), lambda s: (0, 0), pipeline_mode=pl.Buffered(1)),
            any_spec(),
            any_spec(),
            pl.BlockSpec((1, count, 2 * units), lambda s: (jnp.minimum(lax.rem(s, 4), 2), 0, 0)),
            any_spec(),
            any_spec(),
        ],
        out_specs=[any_spec()] * 4,
        scratch_shapes=[low(512, count), low(count, wide), low(count, wide), low(count, 512), low(count, 512)]
        + [low(2, 128, length)] * 4
        + [low(4, 2, 128, length)] * 2
        + [sems((4,)), sems((4,)), sems((4,)), sems((4, 4))],
    )
    return pl.pallas_call(
        weights_kernel,
        out_shape=[jax.ShapeDtypeStruct((2, 128, length), BF16)] * 4,
        grid_spec=grid,
        compiler_params=params(collective_id=1, has_side_effects=True),
        cost_estimate=cost(2 * count * 1024 * length * 2, 50e6),
        name="weights",
    )(n2, g, branch, hid, own, other)


def add(left, right):
    return (left.astype(F32) + right.astype(F32)).astype(BF16)


def finish_kernel(at, own, got, own_heads, got_heads, tok, got_tok, first, came0, came1, slab0, slab1, layer, got_layer, gate, up, down, out, query, key, value, tok_out, first_out, layer_out):
    @pl.when(pl.program_id(0) == 0)
    def _():
        part = down.shape[0]
        for n, ref in enumerate((gate, up, down, out)):
            rows = slice(n * part, n * part + ref.shape[0])
            total = own[rows, :].astype(F32)
            for d in range(3):
                total += got[d, rows, :].astype(F32)
            ref[...] = total
        heads = own_heads[...].astype(F32)
        for d in range(3):
            heads += got_heads[d].astype(F32)
        for n, ref in enumerate((query, key)):
            parts = []
            for h in range(4):
                parts += [heads[n, :, h * 32 : h * 32 + 32], heads[n, :, 128 + h * 32 : 160 + h * 32]]
            ref[...] = jnp.concatenate(parts, axis=1)
        value[...] = heads[2]

    stays = (at[0] & 1) == (at[1] & 1)
    tok_out[...] = jnp.where(stays, tok[...], got_tok[...]).astype(F32)
    step = pl.program_id(0)
    c, t = at[0] & 1, at[1]
    pair, side = t >> 1, t & 1
    r = (step >> 1) ^ side
    local = (c == side) & (t == 2 * c + (pair ^ r))

    @pl.when((step & 1) == 0)
    def _():
        came = jnp.where(r == 0, came0[...], came1[...])
        slab = jnp.where(r == 0, slab0[...], slab1[...])
        first_out[...] = jnp.where(local, slab, came).astype(F32)

    @pl.when((step & 1) == 1)
    def _():
        first_out[...] = first[0].astype(F32)

    layer_out[...] = jnp.where(stays, layer[...], got_layer[...])


def finish(at, pieces, got, own_heads, got_heads, tok, got_tok, first, early, layer, got_layer, part):
    count, wide = tok.shape
    rows = 256
    row = pl.BlockSpec((rows, wide), lambda i, at: (i, 0))
    wider = pl.BlockSpec((SEQ // 2, 256), lambda i, at: (i, 0))
    whole = lambda *shape: pl.BlockSpec(shape, lambda i, at: (0,) * len(shape))
    shapes = [(part, 128)] * 3 + [(256, 128)] + [(128, 256)] * 3
    grid = pltpu.PrefetchScalarGridSpec(
        num_scalar_prefetch=1,
        grid=(count // rows,),
        in_specs=[
            whole(*pieces.shape),
            whole(*got.shape),
            whole(*own_heads.shape),
            whole(*got_heads.shape),
            row,
            row,
            pl.BlockSpec((1, SEQ // 2, 256), lambda i, at: (i // 2, 0, 0)),
            *[whole(SEQ // 2, 256)] * 4,
            row,
            row,
        ],
        out_specs=[whole(*shape) for shape in shapes] + [row, wider, row],
    )
    return pl.pallas_call(
        finish_kernel,
        out_shape=[jax.ShapeDtypeStruct(shape, F32) for shape in shapes + [(count, wide), (2 * SEQ, 256)]]
        + [jax.ShapeDtypeStruct((count, wide), BF16)],
        grid_spec=grid,
        compiler_params=params(),
        cost_estimate=cost(1e6, 18e6),
        name="finish",
    )(at, pieces, got, own_heads, got_heads, tok, got_tok, first, *early, layer, got_layer)


def tail_kernel(
    dq0, dk0, dv0, dq1, dk1, dv1, small, normed, row, grad_hidden, keep1, got1, keep2, got2, gain, gain_two,
    first, own_pieces, got_pieces, own_heads, got_heads, tok, got_tok, sums,
    d_s, w_s, n_s, x_s, gh_s, ks1, gs1, ks2, gs2, last1, last2, pieces, gn_send, gn_got, turned,
    h_send, h_got, s1, k1, a1, a2, part1, part2, rest1, rest2, heads, held, came,
    load, f_sem, m_sem, p_sem, n_sem, c_sem, one_sem, two_sem, h_sem, swap, g_sem,
):
    dp, t = lax.axis_index("dp"), lax.axis_index("tensor")
    c, x, y = lax.rem(dp, 2), lax.rem(lax.div(dp, 2), 2), lax.div(dp, 4)
    pair, side = lax.div(t, 2), lax.rem(t, 2)
    plane = dp - c
    dpx, dpy, dpc = dp + 2 - 4 * x, dp + 4 - 8 * y, dp + 1 - 2 * c
    half = SEQ // 2
    units = (ks1.shape[2] - 512) // 3

    def copy(src, dst, sems, n, to):
        return pltpu.make_async_remote_copy(
            src_ref=src,
            dst_ref=dst,
            send_sem=sems.at[0, n],
            recv_sem=sems.at[1, n],
            device_id=to,
            device_id_type=MESH,
        )

    sources = [(keep1, ks1), (got1, gs1), (keep2, ks2), (got2, gs2)]
    for h, arrays in enumerate(((dq0, dk0, dv0), (dq1, dk1, dv1))):
        sources += [(src, d_s.at[n, pl.ds(h * half, half), :]) for n, src in enumerate(arrays)]
    sources += [(normed, n_s), (small.at[pl.ds(0, 3), pl.ds(2 * c, 2)], w_s), (row.at[c], x_s), (grad_hidden, gh_s)]
    loads = [pltpu.make_async_copy(src, dst, load.at[n]) for n, (src, dst) in enumerate(sources)]
    for item in loads:
        item.start()
    meet(plane, c, t, dpx, dpy)

    def value_copy(u):
        src = dv1.at[:, pl.ds(u * 256, 256)]
        return pltpu.make_async_remote_copy(
            src_ref=src,
            dst_ref=first.at[pair],
            send_sem=f_sem.at[0, u],
            recv_sem=f_sem.at[1, pair],
            device_id=(plane + side, 2 * c + u),
            device_id_type=MESH,
        )

    def value_local(u):
        return pltpu.make_async_copy(dv1.at[:, pl.ds(u * 256, 256)], first.at[pair], load.at[14])

    for u in range(2):
        stay = (side == c) & (t == 2 * c + u)

        @pl.when(stay)
        def _():
            value_local(u).start()

        @pl.when(jnp.logical_not(stay))
        def _():
            value_copy(u).start()

    for item in loads[:4]:
        item.wait()
    gs1[1] = add(ks1[1], gs1[1])
    gs2[1] = add(ks2[1], gs2[1])
    seconds = []
    for n, lanes in enumerate((pl.ds(0, 2 * units), pl.ds(2 * units, units + 512))):
        seconds.append(copy(gs1.at[1, :, lanes], last1.at[:, lanes], m_sem, 2 * n, (dpy, t)))
        seconds.append(copy(gs2.at[1, :, lanes], last2.at[:, lanes], m_sem, 2 * n + 1, (dpx, t)))
    for item in loads[4:11]:
        item.wait()
    for item in seconds:
        item.start()

    def turn(parity):
        for rel in range(4):
            yy, xx = (y, 1 - y)[rel // 2], (x, 1 - x)[rel % 2]
            block = pl.multiple_of((yy * 4 + xx * 2 + parity) * 128, 128)
            turned[rel * 128 : rel * 128 + 128, :] = n_s[:, pl.ds(block, 128)].T

    def heads_copy(n):
        lanes = pl.ds(pl.multiple_of(n * 512, 512), 512)
        return copy(h_send.at[:, :, :, lanes], h_got.at[:, :, :, lanes], c_sem, n, (dpc, t))

    def heads_product(n):
        product = dot(turned[...], d_s[n]).astype(BF16)
        return [product[r * 128 : r * 128 + 128] for r in range(4)], pl.ds(pl.multiple_of(n * 512, 512), 512)

    def heads_send(n, carry):
        place_second(h_send.at[0], h_send.at[1], *heads_product(n))

        @pl.when(n > 0)
        def _():
            heads_copy(n - 1).start()

        return carry

    def heads_keep(n, carry):
        place_first(s1, k1, *heads_product(n))
        return carry

    turn(1 - c)
    lax.fori_loop(0, 3, heads_send, 0)

    part = units // 4
    low_rows, high_rows = pl.ds(0, 4 * part), pl.ds(4 * part, 2 * part + 256)

    def fill_pieces(which):
        for h, (kept, got, last) in enumerate(((ks1, gs1, last1), (ks2, gs2, last2))):
            for n in which:
                lanes = slice(n * units, n * units + (units if n < 3 else 512))
                total = kept[0, :, lanes].astype(F32) + got[0, :, lanes].astype(F32) + last[:, lanes].astype(F32)
                flipped = total.T.astype(BF16)
                if n < 3:
                    for i in range(4):
                        rows = slice((2 * n + h) * part, (2 * n + h + 1) * part)
                        pieces[lax.rem(i + 4 - t, 4), rows, :] = flipped[i * part : (i + 1) * part]
                else:
                    for i in range(2):
                        pieces[lax.rem(2 * h + i + 4 - t, 4), 6 * part :, :] = flipped[i * 256 : i * 256 + 256]

    def piece_copies(rows, n):
        return [
            copy(pieces.at[d, rows, :], got_pieces.at[d - 1, rows, :], p_sem, 3 * n + d - 1, (dp, lax.rem(t + d, 4)))
            for d in (1, 2, 3)
        ]

    for item in seconds[:2]:
        item.wait_recv()
    fill_pieces((0, 1))
    turn(c)
    heads_copy(2).start()
    zs = piece_copies(low_rows, 0)
    for item in zs:
        item.start()
    lax.fori_loop(0, 3, heads_keep, 0)
    cs = [heads_copy(n) for n in range(3)]
    for item in cs:
        item.wait_recv()
    ones = [copy(h_got.at[0], a2, one_sem, 1, (dpy, t)), copy(s1, a1, one_sem, 0, (dpx, t))]
    for item in ones:
        item.start()
    for item in seconds[2:]:
        item.wait_recv()
    fill_pieces((2, 3))
    own_pieces[...] = pieces[0]
    last_zs = piece_copies(high_rows, 1)
    for item in last_zs:
        item.start()
    zs += last_zs

    def back_product(rows):
        total = None
        for u in range(2):
            for n in range(3):
                term = dot_nt(d_s[n, rows, u * 256 : u * 256 + 256], w_s[n, u])
                total = term if total is None else total + term
        return total

    ns = [copy(gn_send.at[i], gn_got.at[i], n_sem, i, (dpc, t)) for i in range(2)]

    def other_half(i, carry):
        rows = pl.ds(pl.multiple_of((1 - c) * half + i * 512, 512), 512)
        gn_send[i] = back_product(rows).astype(BF16)
        return carry

    loads[11].wait()
    lax.fori_loop(0, 2, other_half, 0)

    for item in ones:
        item.wait_recv()
    part1[...] = add(k1[1], a1[1])
    part2[...] = add(h_got[1, 1], a2[1])
    for item in ns:
        item.start()
    twos = [copy(part1, rest1, two_sem, 0, (dpy, t)), copy(part2, rest2, two_sem, 1, (dpx, t))]
    for item in twos:
        item.start()

    loads[12].wait()
    loads[13].wait()
    moved = side != c
    for item in ns:
        item.wait_recv()

    def own_half(i, gained):
        rows = pl.ds(pl.multiple_of(c * half + i * 512, 512), 512)
        here = pl.ds(pl.multiple_of(i * 512, 512), 512)
        grad = back_product(rows) + gn_got[i].astype(F32)
        values = x_s[here, :].astype(F32)
        factor = lax.rsqrt(jnp.mean(values * values, axis=1, keepdims=True) + EPSILON)
        gained += jnp.sum((grad * values * factor).reshape(-1, 8, grad.shape[1]), axis=0)
        scaled = grad * gain[...]
        mean = jnp.mean(scaled * values, axis=1, keepdims=True)
        tok[i] = (gh_s[here, :] + factor * scaled - values * (factor * factor * factor * mean)).astype(BF16)
        return gained

    gained = lax.fori_loop(0, 2, own_half, jnp.zeros((8, tok.shape[2]), F32))
    swaps = [copy(tok.at[i], got_tok.at[i], swap, i, (plane + side, 2 * pair + c)) for i in range(2)]

    total1 = k1[0].astype(F32) + a1[0].astype(F32)
    total2 = h_got[1, 0].astype(F32) + a2[0].astype(F32)

    @pl.when(moved)
    def _():
        for item in swaps:
            item.start()

    turns = (dpc, t), (dpx, t), (dpy, t), (dp, t + 1 - 2 * side), (dp, lax.rem(t + 2, 4))
    line = lax.broadcasted_iota(jnp.int32, gained.shape, 0)
    total_one = jnp.sum(gained, axis=0, keepdims=True)
    total_two = jnp.sum(gain_two[...], axis=0, keepdims=True)
    held[0] = jnp.where(line == 0, total_one, jnp.where(line == 1, total_two, 0.0))

    def gain_step(n):
        return copy(held.at[n], came.at[n], g_sem, n, turns[n])

    def gain_next(n):
        gain_step(n).wait_recv()
        held[n + 1] = held[n] + came[n]

    gain_step(0).start()
    gain_next(0)
    gain_step(1).start()
    gain_next(1)
    for item in twos:
        item.wait_recv()
    totals = ((total1 + rest1[...].astype(F32)).astype(BF16), (total2 + rest2[...].astype(F32)).astype(BF16))
    for e, total in enumerate(totals):
        core = (c, 1 - c)[e]
        for u in range(2):
            d = lax.rem(2 * core + u + 4 - t, 4)
            for n in range(3):
                heads[d, n] = total[:, n * 512 + u * 256 : n * 512 + u * 256 + 256]
    gain_step(2).start()
    gain_next(2)
    own_heads[...] = heads[0]
    hs = [copy(heads.at[d], got_heads.at[d - 1], h_sem, d - 1, (dp, lax.rem(t + d, 4))) for d in (1, 2, 3)]
    for item in hs:
        item.start()
    for n in (3, 4):
        gain_step(n).start()
        gain_next(n)
    sums[...] = held[5]

    for item in seconds + ns + cs + ones + twos:
        item.wait_send()
    for n in range(5):
        gain_step(n).wait_send()
    for u in range(2):
        stay = (side == c) & (t == 2 * c + u)

        @pl.when(stay)
        def _():
            value_local(u).wait()

        @pl.when(jnp.logical_not(stay))
        def _():
            value_copy(u).wait_send()

    for p in range(2):

        @pl.when((pair != c) | (t != 2 * p + c))
        def _():
            pltpu.make_async_remote_copy(
                src_ref=first.at[p],
                dst_ref=first.at[p],
                send_sem=f_sem.at[0, p],
                recv_sem=f_sem.at[1, p],
                device_id=(dpc, t),
                device_id_type=MESH,
            ).wait_recv()

    for item in zs + hs:
        item.wait()

    @pl.when(moved)
    def _():
        for item in swaps:
            item.wait()


def tail(back, small, normed, row, grad_hidden, keep1, got1, keep2, got2, gain, gain_two):
    vmem = pl.BlockSpec(memory_space=pltpu.VMEM)
    sems = pltpu.SemaphoreType.DMA
    wide = normed.shape[1]
    length = keep1.shape[2]
    rows = (length - 512) // 2 + 256
    half = SEQ // 2
    low = lambda *shape: pltpu.VMEM(shape, BF16)
    return pl.pallas_call(
        tail_kernel,
        out_shape=[
            jax.ShapeDtypeStruct((2, half, 256), BF16),
            jax.ShapeDtypeStruct((rows, 128), BF16),
            jax.ShapeDtypeStruct((3, rows, 128), BF16),
            jax.ShapeDtypeStruct((3, 128, 256), BF16),
            jax.ShapeDtypeStruct((3, 3, 128, 256), BF16),
            jax.ShapeDtypeStruct((2, half // 2, wide), BF16),
            jax.ShapeDtypeStruct((2, half // 2, wide), BF16),
            jax.ShapeDtypeStruct((8, wide), F32),
        ],
        in_specs=[any_spec()] * 14 + [vmem] * 2,
        out_specs=[any_spec(), vmem, any_spec(), vmem, any_spec(), vmem, any_spec(), vmem],
        scratch_shapes=[low(3, SEQ, 512)]
        + [low(3, 2, wide, 256), low(SEQ, wide), low(half, wide), pltpu.VMEM((half, wide), F32)]
        + [low(2, 128, length)] * 4
        + [low(128, length)] * 2
        + [low(4, rows, 128), low(2, half // 2, wide), low(2, half // 2, wide), low(512, SEQ)]
        + [low(2, 2, 128, 1536)] * 2
        + [low(2, 128, 1536)] * 4
        + [low(128, 1536)] * 4
        + [low(4, 3, 128, 256), pltpu.VMEM((6, 8, wide), F32), pltpu.VMEM((5, 8, wide), F32)]
        + [sems((15,)), sems((2, 2)), sems((2, 4)), sems((2, 6)), sems((2, 2)), sems((2, 3)), sems((2, 2)), sems((2, 2))]
        + [sems((2, 3)), sems((2, 2)), sems((2, 5))],
        compiler_params=params(collective_id=2, has_side_effects=True),
        name="tail",
    )(*back, small, normed, row, grad_hidden, keep1, got1, keep2, got2, gain, gain_two)


def fast_body(tokens, first_values, doc_lengths, cotangent, w_query, w_key, w_value, w_out, w_gate, w_up, w_down, gain_attn, gain_mlp):
    me, t = lax.axis_index("dp"), lax.axis_index("tensor")
    c = me % 2
    pair, side = t // 2, t % 2
    wide = tokens.shape[1]
    tiles = SEQ // TILE
    at = jnp.where(jnp.arange(8, dtype=jnp.int32) == 0, me, t).astype(jnp.int32)

    small_shard, big_shard = pack(w_query, w_key, w_value, w_out, w_gate, w_up, w_down)
    lengths = jnp.where(c == side, doc_lengths, across_c(doc_lengths))
    lengths = lax.dynamic_index_in_dim(lengths, pair, 0, keepdims=False)
    order = jnp.arange(DOCS, dtype=jnp.int32)
    ends = jnp.sum(jnp.where(order[None, :] <= order[:, None], lengths[None, :], 0), axis=1)
    freqs = 10000.0 ** (-(jnp.arange(32, dtype=F32) * 2.0 / HEAD))
    row, small, big, normed_one, q, k, v, cosine, sine = gather(
        ends, tokens, first_values, small_shard, big_shard, gain_attn[None], jnp.tile(freqs, 4)[None]
    )
    places = jnp.arange(SEQ, dtype=jnp.int32)
    starts = jnp.max(jnp.where(ends[None, :] <= places[:, None], ends[None, :], 0), axis=1)
    last = jnp.arange(tiles, dtype=jnp.int32) * TILE + (TILE - 1)
    stop = jnp.min(jnp.where(ends[None, :] > last[:, None], ends[None, :], SEQ), axis=1)
    bounds = jnp.concatenate([starts.reshape(tiles, TILE)[:, 0] // TILE, (stop - 1) // TILE])
    starts_by_tile = starts.reshape(tiles, TILE)

    row, cotangent = lax.optimization_barrier((row, cotangent))
    moved_cot = swap_halves(cotangent)
    att_own, att_send, lse = attend(at, bounds, q, k, v, starts_by_tile)
    att_other = across_c(att_send)
    out, grad_hidden, branch, normed_two, hid, ga_own, ga_other, gain_two, cot = mlp(
        at, att_own, att_other, row, cotangent, moved_cot, gain_mlp[None], small, big
    )
    moved_out = swap_halves(out)

    ga_got = across_c(ga_other)

    kept = weights(normed_two, cot, branch, hid, att_own, att_other)
    kept, ga_got = lax.optimization_barrier((kept, ga_got))
    got1, got2 = across_x(kept[0]), across_y(kept[2])

    rest = (att_own, att_send, lse, starts_by_tile, cosine, sine)
    dq0, dk0, dv0, held = attend_back(0, at, bounds, q, k, v, ga_own, ga_got, *rest)

    slabs = [jnp.where(pair == r, dv0[:, :256], dv0[:, 256:]) for r in range(2)]
    came = [
        move(slabs[r], lambda y, x, c, t, r=r: (y, x, t % 2, 2 * c + ((t // 2) ^ r))) for r in range(2)
    ]
    dq1, dk1, dv1 = attend_back(1, at, bounds, q, k, v, ga_own, ga_got, *rest, held)
    dv1, came = lax.optimization_barrier((dv1, came))

    first_back, pieces, got, own_heads, got_heads, grad_tokens, got_tokens, gains = tail(
        (dq0, dk0, dv0, dq1, dk1, dv1), small, normed_one, row, grad_hidden, kept[1], got1, kept[3], got2, gain_attn[None], gain_two
    )
    shape = (SEQ // 2, wide)
    grad_gate, grad_up, grad_down, grad_out, gq, gk, gv, grad_tokens, grad_first, layer_out = finish(
        at, pieces, got, own_heads, got_heads, grad_tokens.reshape(shape), got_tokens.reshape(shape), first_back, (*came, *slabs), out, moved_out, w_gate.shape[1]
    )
    return (
        layer_out,
        grad_tokens,
        grad_first,
        gq,
        gk,
        gv,
        grad_out,
        grad_gate.T,
        grad_up.T,
        grad_down,
        gains[0],
        gains[1],
    )


def solution(mesh):
    fits = dict(mesh.shape) == {"dp": 8, "tensor": 4}
    placed = (
        P(("dp", "tensor"), None),
        P("dp", "tensor"),
        P("dp", None),
        P(("dp", "tensor"), None),
        P("dp", "tensor"),
        P("dp", "tensor"),
        P("dp", "tensor"),
        P("tensor", "dp"),
        P("dp", "tensor"),
        P("dp", "tensor"),
        P("tensor", "dp"),
        P(),
        P(),
    )
    return jax.shard_map(
        fast_body if fits else general_body,
        mesh=mesh,
        in_specs=placed,
        out_specs=(
            P(("dp", "tensor"), None),
            P(("dp", "tensor"), None),
            P("dp", "tensor"),
            P("dp", "tensor"),
            P("dp", "tensor"),
            P("dp", "tensor"),
            P("tensor", "dp"),
            P("dp", "tensor"),
            P("dp", "tensor"),
            P("tensor", "dp"),
            P(),
            P(),
        ),
        check_vma=False,
    )
```

```python
import functools

import jax
import jax.numpy as jnp
from jax import lax
from jax.experimental import pallas as pl
from jax.experimental.pallas import tpu as pltpu
from jax.sharding import PartitionSpec as P

HEAD = 64
SEQ = 2048
DOCS = 8
EPSILON = 1e-05


def rms_norm(values, gain):
    factor = lax.rsqrt(jnp.mean(values * values, axis=1, keepdims=True) + EPSILON)
    return values * factor * gain


def documents(doc_lengths):
    ends = jnp.cumsum(doc_lengths, axis=1)
    starts = ends - doc_lengths
    places = jnp.arange(SEQ, dtype=jnp.int32)
    segment = jnp.sum((places[None, :, None] >= ends[:, None, :]).astype(jnp.int32), axis=2)
    member = segment[:, :, None] == jnp.arange(DOCS, dtype=jnp.int32)[None, None, :]
    offset = jnp.sum(jnp.where(member, starts[:, None, :], 0), axis=2)
    return (segment, (places[None, :] - offset).astype(jnp.float32))


def rotation(positions):
    half = HEAD // 2
    freqs = 10000.0 ** (-(jnp.arange(half, dtype=jnp.float32) * 2.0 / HEAD))
    angles = positions[:, None] * freqs[None, :]
    return (jnp.cos(angles), jnp.sin(angles))


def rotate(values, cosine, sine):
    shaped = values.reshape(values.shape[0], -1, HEAD)
    half = HEAD // 2
    first = shaped[:, :, :half]
    second = shaped[:, :, half:]
    cos_rows = cosine[:, None, :]
    sin_rows = sine[:, None, :]
    turned = jnp.concatenate(
        [first * cos_rows - second * sin_rows, second * cos_rows + first * sin_rows], axis=2
    )
    return turned.reshape(values.shape)


def rotate_back(grads, cosine, sine):
    shaped = grads.reshape(grads.shape[0], -1, HEAD)
    half = HEAD // 2
    first = shaped[:, :, :half]
    second = shaped[:, :, half:]
    cos_rows = cosine[:, None, :]
    sin_rows = sine[:, None, :]
    turned = jnp.concatenate(
        [first * cos_rows + second * sin_rows, second * cos_rows - first * sin_rows], axis=2
    )
    return turned.reshape(grads.shape)


def swiglu(gate, up_val):
    return jax.nn.silu(gate) * up_val


def product(left, right):
    return jnp.dot(left, right, preferred_element_type=jnp.float32)


def inner(left, right):
    return lax.dot_general(
        left, right, (((0,), (0,)), ((), ())), preferred_element_type=jnp.float32
    )


def outer(left, right):
    return lax.dot_general(
        left, right, (((1,), (1,)), ((), ())), preferred_element_type=jnp.float32
    )


def block_scores(queries, keys_all, segment, start, width):
    query_block = lax.dynamic_slice_in_dim(queries, start, width, 0)
    query_seg = lax.dynamic_slice_in_dim(segment, start, width, 0)
    scores = (
        jnp.einsum("qhd,khd->hqk", query_block, keys_all, preferred_element_type=jnp.float32)
        * 0.125
    )
    places = jnp.arange(SEQ, dtype=jnp.int32)
    rows_at = start + jnp.arange(width, dtype=jnp.int32)
    allowed = (query_seg[:, None] == segment[None, :]) & (places[None, :] <= rows_at[:, None])
    return (query_block, jnp.where(allowed[None], scores, -1e30))


def forward_row(pieces):
    queries, keys_all, values_all, segment = pieces
    width = min(512, SEQ)
    count = SEQ // width

    def forward_one_block(index):
        unused, scores = block_scores(queries, keys_all, segment, index * width, width)
        top = jnp.max(scores, axis=2, keepdims=True)
        expo = jnp.exp(scores - top)
        total = jnp.sum(expo, axis=2, keepdims=True)
        weights = (expo / total).astype(jnp.bfloat16)
        result = jnp.einsum("hqk,khd->qhd", weights, values_all, preferred_element_type=jnp.float32)
        return (result, (top + jnp.log(total))[:, :, 0])

    results, logsums = lax.map(forward_one_block, jnp.arange(count, dtype=jnp.int32))
    return (results.reshape(SEQ, queries.shape[1], HEAD), logsums)


def backward_row(pieces):
    queries, keys_all, values_all, segment, grad_rows, logsums = pieces
    width = min(512, SEQ)
    count = SEQ // width

    def backward_one_block(carry, extra):
        index, logsum = extra
        start = index * width
        query_block, scores = block_scores(queries, keys_all, segment, start, width)
        probs = jnp.exp(scores - logsum[:, :, None])
        grad_block = lax.dynamic_slice_in_dim(grad_rows, start, width, 0)
        grad_probs = jnp.einsum(
            "qhd,khd->hqk", grad_block, values_all, preferred_element_type=jnp.float32
        )
        delta = jnp.sum(probs * grad_probs, axis=2, keepdims=True)
        grad_scores = (probs * (grad_probs - delta)).astype(jnp.bfloat16)
        grad_query = (
            jnp.einsum("hqk,khd->qhd", grad_scores, keys_all, preferred_element_type=jnp.float32)
            * 0.125
        )
        grad_keys = (
            carry[0]
            + jnp.einsum(
                "hqk,qhd->khd", grad_scores, query_block, preferred_element_type=jnp.float32
            )
            * 0.125
        )
        grad_values = carry[1] + jnp.einsum(
            "hqk,qhd->khd",
            probs.astype(jnp.bfloat16),
            grad_block,
            preferred_element_type=jnp.float32,
        )
        return ((grad_keys, grad_values), grad_query)

    zeros = jnp.zeros(keys_all.shape, jnp.float32)
    sums, grad_queries = lax.scan(
        backward_one_block, (zeros, zeros), (jnp.arange(count, dtype=jnp.int32), logsums)
    )
    return (grad_queries.reshape(SEQ, queries.shape[1], HEAD), sums[0], sums[1])


def general_body(
    tokens,
    first_values,
    doc_lengths,
    cotangent,
    w_query,
    w_key,
    w_value,
    w_out,
    w_gate,
    w_up,
    w_down,
    gain_attn,
    gain_mlp,
):
    query_mat, key_mat, value_mat, out_mat, gate_mat, up_mat, down_mat = (
        lax.all_gather(w_query, "dp", axis=0, tiled=True),
        lax.all_gather(w_key, "dp", axis=0, tiled=True),
        lax.all_gather(w_value, "dp", axis=0, tiled=True),
        lax.all_gather(w_out, "dp", axis=1, tiled=True),
        lax.all_gather(w_gate, "dp", axis=0, tiled=True),
        lax.all_gather(w_up, "dp", axis=0, tiled=True),
        lax.all_gather(w_down, "dp", axis=1, tiled=True),
    )
    local_heads = query_mat.shape[1] // HEAD
    row_count = doc_lengths.shape[0]
    group = row_count * SEQ
    segment, positions = documents(doc_lengths)
    cosine, sine = rotation(positions.reshape(-1))

    def heads(matrix):
        return matrix.reshape(row_count, SEQ, local_heads, HEAD)

    inputs = tokens.astype(jnp.float32)
    normed_one, norm_one_back = jax.vjp(rms_norm, inputs, gain_attn)
    gathered_one = lax.all_gather(normed_one.astype(jnp.bfloat16), "tensor", axis=0, tiled=True)
    query_raw = product(gathered_one, query_mat)
    key_raw = product(gathered_one, key_mat)
    value_raw = product(gathered_one, value_mat)
    queries = rotate(query_raw, cosine, sine).astype(jnp.bfloat16)
    keys_low = rotate(key_raw, cosine, sine).astype(jnp.bfloat16)
    mixed_values = (0.5 * value_raw + 0.5 * first_values.astype(jnp.float32)).astype(jnp.bfloat16)
    attended, logsums = lax.map(
        forward_row, (heads(queries), heads(keys_low), heads(mixed_values), segment)
    )
    attended_low = attended.reshape(group, -1).astype(jnp.bfloat16)
    hidden_in = inputs + lax.psum_scatter(
        product(attended_low, out_mat), "tensor", scatter_dimension=0, tiled=True
    )
    normed_two, norm_two_back = jax.vjp(rms_norm, hidden_in, gain_mlp)
    normed_low_two = normed_two.astype(jnp.bfloat16)
    grad_out = cotangent.astype(jnp.float32)
    gathered_two = lax.all_gather(normed_low_two, "tensor", axis=0, tiled=True)
    activated, swiglu_back = jax.vjp(
        swiglu, product(gathered_two, gate_mat), product(gathered_two, up_mat)
    )
    act_low = activated.astype(jnp.bfloat16)
    layer_out = hidden_in + lax.psum_scatter(
        product(act_low, down_mat).astype(jnp.bfloat16), "tensor", scatter_dimension=0, tiled=True
    ).astype(jnp.float32)
    grad_rows = lax.all_gather(cotangent, "tensor", axis=0, tiled=True)
    grad_gate, grad_up = swiglu_back(outer(grad_rows, down_mat))
    gate_low = grad_gate.astype(jnp.bfloat16)
    up_low = grad_up.astype(jnp.bfloat16)
    grad_normed_two = lax.psum_scatter(
        outer(gate_low, gate_mat) + outer(up_low, up_mat), "tensor", scatter_dimension=0, tiled=True
    )
    grad_gate_mat = inner(gathered_two, gate_low)
    grad_up_mat = inner(gathered_two, up_low)
    grad_down_mat = inner(act_low, grad_rows)
    grad_hidden_two, grad_gain_two = norm_two_back(grad_normed_two)
    grad_hidden = grad_out + grad_hidden_two
    grad_branch = lax.all_gather(grad_hidden.astype(jnp.bfloat16), "tensor", axis=0, tiled=True)
    grad_attended = outer(grad_branch, out_mat).astype(jnp.bfloat16)
    grad_out_mat = inner(attended_low, grad_branch)
    grad_rot_query, grad_rot_key, grad_mixed = lax.map(
        backward_row,
        (
            heads(queries),
            heads(keys_low),
            heads(mixed_values),
            segment,
            heads(grad_attended),
            logsums,
        ),
    )
    grad_query_low = rotate_back(grad_rot_query.reshape(group, -1), cosine, sine).astype(
        jnp.bfloat16
    )
    grad_key_low = rotate_back(grad_rot_key.reshape(group, -1), cosine, sine).astype(jnp.bfloat16)
    grad_first = 0.5 * grad_mixed.reshape(group, -1)
    grad_value_low = grad_first.astype(jnp.bfloat16)
    grad_normed_one = lax.psum_scatter(
        outer(grad_query_low, query_mat)
        + outer(grad_key_low, key_mat)
        + outer(grad_value_low, value_mat),
        "tensor",
        scatter_dimension=0,
        tiled=True,
    )
    grad_query_mat = inner(gathered_one, grad_query_low)
    grad_key_mat = inner(gathered_one, grad_key_low)
    grad_value_mat = inner(gathered_one, grad_value_low)
    grad_inputs_one, grad_gain_one = norm_one_back(grad_normed_one)
    grad_tokens = grad_hidden + grad_inputs_one
    summed = (
        lax.psum_scatter(grad_query_mat, "dp", scatter_dimension=0, tiled=True),
        lax.psum_scatter(grad_key_mat, "dp", scatter_dimension=0, tiled=True),
        lax.psum_scatter(grad_value_mat, "dp", scatter_dimension=0, tiled=True),
        lax.psum_scatter(grad_out_mat, "dp", scatter_dimension=1, tiled=True),
        lax.psum_scatter(grad_gate_mat, "dp", scatter_dimension=0, tiled=True),
        lax.psum_scatter(grad_up_mat, "dp", scatter_dimension=0, tiled=True),
        lax.psum_scatter(grad_down_mat, "dp", scatter_dimension=1, tiled=True),
    )
    gain_sums = lax.psum((grad_gain_one, grad_gain_two), ("dp", "tensor"))
    return (
        layer_out.astype(jnp.bfloat16),
        grad_tokens,
        grad_first,
        summed[0],
        summed[1],
        summed[2],
        summed[3],
        summed[4],
        summed[5],
        summed[6],
        gain_sums[0],
        gain_sums[1],
    )


AXES = ("dp", "tensor")
MESH = pl.DeviceIdType.MESH
TILE = 256
NEG = -1e30
F32 = jnp.float32
BF16 = jnp.bfloat16


def flat(y, x, c, t):
    return ((y * 2 + x) * 2 + c) * 4 + t


def move(values, to):
    pairs = []
    for y in range(2):
        for x in range(2):
            for c in range(2):
                for t in range(4):
                    pair = (flat(y, x, c, t), flat(*to(y, x, c, t)))
                    if pair[0] != pair[1]:
                        pairs.append(pair)
    return lax.ppermute(values, AXES, pairs)


def across_x(values):
    return move(values, lambda y, x, c, t: (y, 1 - x, c, t))


def across_y(values):
    return move(values, lambda y, x, c, t: (1 - y, x, c, t))


def across_c(values):
    return move(values, lambda y, x, c, t: (y, x, 1 - c, t))


def along_t(values, step):
    return move(values, lambda y, x, c, t: (y, x, c, (t + step) % 4))


def swap_halves(values):
    return move(values, lambda y, x, c, t: (y, x, t % 2, (t // 2) * 2 + c))


def pack_kernel(wq, wk, wv, wo, wg, wu, wd, halves, small, big):
    small[0] = dot(wq[...], halves[...]).astype(BF16)
    small[1] = dot(wk[...], halves[...]).astype(BF16)
    small[2] = wv[...]
    small[3] = wo[...].T
    for n, units in enumerate((wg, wu, wd)):
        big[n] = units[...].reshape(big.shape[1:])


def pack(wq, wk, wv, wo, wg, wu, wd):
    wg, wu = wg.T, wu.T
    part, rows = wg.shape
    lane = jnp.arange(256, dtype=jnp.int32)
    source = ((lane & 127) >> 5) * 64 + (lane >> 7) * 32 + (lane & 31)
    halves = (lane[:, None] == source[None, :]).astype(BF16)
    return pl.pallas_call(
        pack_kernel,
        out_shape=[
            jax.ShapeDtypeStruct((4, rows, 256), BF16),
            jax.ShapeDtypeStruct((3, 2, part // 2, rows), BF16),
        ],
        compiler_params=params(),
        name="pack",
    )(wq, wk, wv, wo, wg, wu, wd, halves)


def meet(plane, c, t, dpx, dpy):
    barrier = pltpu.get_barrier_semaphore()
    for e in range(2):
        for d in range(4):
            if e or d:
                other = plane + lax.rem(c + e, 2)
                pl.semaphore_signal(barrier, inc=1, device_id=(other, lax.rem(t + d, 4)), device_id_type=MESH)
    pl.semaphore_signal(barrier, inc=1, device_id=(dpx, t), device_id_type=MESH)
    pl.semaphore_signal(barrier, inc=1, device_id=(dpy, t), device_id_type=MESH)
    pl.semaphore_wait(barrier, 9)


def gather_kernel(
    ends, tok, fv, small, big, gain, freqs, row_out, g_small, g_big, normed_out, q_out, k_out, v_out, cos_out, sin_out,
    row, first, w_s, n_s, q_s, k_s, v_s, raw_s, cos_s, sin_s,
    send, recv, relay_send, along_recv, next_send, next_recv, swap, fsend, frecv, here, tile_sem, end_sem,
):
    dp, t = lax.axis_index("dp"), lax.axis_index("tensor")
    c, x, y = lax.rem(dp, 2), lax.rem(lax.div(dp, 2), 2), lax.div(dp, 4)
    pair, side = lax.div(t, 2), lax.rem(t, 2)
    plane = dp - c
    dpx, dpy, dpc = dp + 2 - 4 * x, dp + 4 - 8 * y, dp + 1 - 2 * c
    dpxy = dpx + 4 - 8 * y

    meet(plane, c, t, dpx, dpy)
    def slot(k, at, owner, h):
        if k == 0:
            return g_small.at[pl.ds(2 * h, 2), at, pl.ds(owner * 128, 128), :]
        return g_big.at[k - 1, owner, h, at]

    def column(k, owner, h):
        if k == 0:
            return g_small.at[pl.ds(2 * h, 2), :, pl.ds(owner * 128, 128), :]
        return g_big.at[k - 1, owner, h]

    def both(k, at, owner):
        if k == 0:
            return g_small.at[:, at, pl.ds(owner * 128, 128), :]
        return g_big.at[k - 1, owner, :, at]

    def all_of(k, owner):
        if k == 0:
            return g_small.at[:, :, pl.ds(owner * 128, 128), :]
        return g_big.at[k - 1, owner]

    def shard(k):
        return small if k == 0 else big.at[k - 1]

    def part_of(k, h):
        return small.at[pl.ds(2 * h, 2)] if k == 0 else big.at[k - 1, h]

    def copy(k, n, src, dst, to, at):
        return pltpu.make_async_remote_copy(
            src_ref=src,
            dst_ref=dst,
            send_sem=send.at[k, n],
            recv_sem=recv.at[k, n],
            device_id=(to, at),
            device_id_type=MESH,
        )

    chunks = 4
    near, far = (dpx, dpy), (dpy, dpx)
    kept = [pltpu.make_async_copy(shard(k), both(k, t, dp), here.at[k]) for k in range(chunks)]

    def relay(k, at, side, src):
        return pltpu.make_async_remote_copy(
            src_ref=src,
            dst_ref=both(k, at, dp),
            send_sem=relay_send.at[k, at, side],
            recv_sem=along_recv.at[k, at],
            device_id=(dp, t + 2 * side - 1),
            device_id_type=MESH,
        )

    def onward(k, at, h, src):
        return pltpu.make_async_remote_copy(
            src_ref=src,
            dst_ref=slot(k, at, dp, h),
            send_sem=next_send.at[k, at, h],
            recv_sem=next_recv.at[k, at, h],
            device_id=(near[h], t),
            device_id_type=MESH,
        )

    def start_along(k):
        @pl.when(t < 3)
        def _():
            relay(k, t, 1, shard(k)).start()

        @pl.when(t > 0)
        def _():
            relay(k, t, 0, shard(k)).start()

    def pass_along(k, level):
        for side, at in ((1, t - level), (0, t + level)):

            @pl.when((at >= 0) & (at < 4))
            def _():
                block = both(k, at, dp)
                move = relay(k, at, side, block)
                move.wait_recv()

                @pl.when((t < 3) if side else (t > 0))
                def _():
                    move.start()

                for h in range(2):
                    onward(k, at, h, slot(k, at, dp, h)).start()

    def end_along(k):
        for level in range(4):
            for side, at in ((1, t - level), (0, t + level)):

                @pl.when((at >= 0) & (at < 4) & ((t < 3) if side else (t > 0)))
                def _():
                    relay(k, at, side, both(k, at, dp)).wait_send()

    across = [
        [
            copy(k, 2 * h + i, column(k, owner, h), column(k, owner, h), far[h], t)
            for h in range(2)
            for i, owner in enumerate((dp, near[h]))
        ]
        for k in range(chunks)
    ]
    over = [
        [copy(k, 4 + i, all_of(k, owner), all_of(k, owner), dpc, t) for i, owner in enumerate((dp, dpx, dpy, dpxy))]
        for k in range(chunks)
    ]

    order = (1, 0, 2, 3)
    start_along(order[0])
    for item in kept:
        item.start()
    for k in order:
        for h in range(2):
            onward(k, t, h, part_of(k, h)).start()
        if k == order[0]:
            start_along(order[1])

    moved = side != c
    to_own = pltpu.make_async_copy(tok, row.at[c], here.at[4])
    swapped = pltpu.make_async_remote_copy(
        src_ref=tok,
        dst_ref=row.at[side],
        send_sem=swap.at[0],
        recv_sem=swap.at[1],
        device_id=(plane + side, 2 * pair + c),
        device_id_type=MESH,
    )

    def start_tokens():
        @pl.when(moved)
        def _():
            swapped.start()

        @pl.when(jnp.logical_not(moved))
        def _():
            to_own.start()

    heads_core, slab = pair, side

    def first_copy(p):
        return pltpu.make_async_remote_copy(
            src_ref=fv.at[pl.ds(p * SEQ, SEQ), :],
            dst_ref=first.at[slab],
            send_sem=fsend.at[p],
            recv_sem=frecv.at[slab],
            device_id=(plane + heads_core, 2 * p + c),
            device_id_type=MESH,
        )

    def first_local(p):
        return pltpu.make_async_copy(fv.at[pl.ds(p * SEQ, SEQ), :], first.at[slab], here.at[5])

    stays = [(heads_core == c) & (t == 2 * p + c) for p in range(2)]

    def start_first():
        for p in range(2):

            @pl.when(stays[p])
            def _():
                first_local(p).start()

            @pl.when(jnp.logical_not(stays[p]))
            def _():
                first_copy(p).start()

    def pass_over(k):
        for item in across[k]:
            item.wait_recv()
        for item in over[k][1:]:
            item.start()

    def pass_next(k):
        for at in range(4):
            for h in range(2):
                onward(k, at, h, slot(k, at, dp, h)).wait_recv()
        for item in across[k]:
            item.start()

    def table(i, carry):
        rows = pl.ds(pl.multiple_of(i * TILE, TILE), TILE)
        at_row = lax.broadcasted_iota(jnp.int32, (TILE, 128), 0) + i * TILE
        begin = jnp.zeros_like(at_row)
        for k in range(DOCS):
            begin = jnp.maximum(begin, jnp.where(at_row >= ends[k], ends[k], 0))
        angles = (at_row - begin).astype(F32) * freqs[...]
        cos_s[rows, :] = jnp.cos(angles)
        sin_s[rows, :] = jnp.sin(angles)
        return carry

    lax.fori_loop(0, SEQ // TILE, table, 0)
    tables = [pltpu.make_async_copy(cos_s, cos_out, end_sem.at[0]), pltpu.make_async_copy(sin_s, sin_out, end_sem.at[1])]

    for i, k in enumerate(order):
        pass_along(k, 1)
        if i + 2 < chunks:
            start_along(order[i + 2])
        if i:
            pass_next(order[i - 1])
        pass_along(k, 2)
        pass_along(k, 3)
        kept[k].wait()
        over[k][0].start()
        if i == 2:
            start_tokens()
        if i == 3:
            start_first()
        if i >= 2:
            pass_over(order[i - 2])
    pass_next(order[3])
    for item in tables:
        item.start()
    for item in over[0]:
        item.wait_recv()
    load_w = pltpu.make_async_copy(g_small.at[pl.ds(0, 3), pl.ds(2 * c, 2)], w_s, end_sem.at[2])
    load_w.start()

    @pl.when(moved)
    def _():
        swapped.wait_send()
        swapped.wait_recv()

    @pl.when(jnp.logical_not(moved))
    def _():
        to_own.wait()

    given = pltpu.make_async_remote_copy(
        src_ref=row.at[c],
        dst_ref=row.at[c],
        send_sem=swap.at[2],
        recv_sem=swap.at[3],
        device_id=(dpc, t),
        device_id_type=MESH,
    )
    given.start()
    load_w.wait()

    def rows_of(half, n):
        return pl.ds(pl.multiple_of(half * (SEQ // 2) + n * 512, 512), 512)

    def done_copies(half, n):
        rows = rows_of(half, n)
        return [
            pltpu.make_async_copy(src.at[rows, :], dst.at[rows, :], tile_sem.at[2 * half + n, m])
            for m, (src, dst) in enumerate(((n_s, normed_out), (q_s, q_out), (k_s, k_out)))
        ]

    def project(half, n):
        rows = rows_of(half, n)
        values = row[half, pl.ds(pl.multiple_of(n * 512, 512), 512), :].astype(F32)
        factor = lax.rsqrt(jnp.mean(values * values, axis=1, keepdims=True) + EPSILON)
        normed = (values * factor * gain[...]).astype(BF16)
        n_s[rows, :] = normed
        cos, sin = cos_s[rows, :], sin_s[rows, :]
        for u in range(2):
            for m, out, scale in ((0, q_s, 0.125), (1, k_s, 1.0)):
                raw = dot(normed, w_s[m, u])
                a, b = raw[:, :128], raw[:, 128:]
                out[rows, u * 256 : u * 256 + 128] = ((a * cos - b * sin) * scale).astype(BF16)
                out[rows, u * 256 + 128 : u * 256 + 256] = ((b * cos + a * sin) * scale).astype(BF16)
            raw_s[rows, u * 256 : u * 256 + 256] = 0.5 * dot(normed, w_s[2, u])
        for item in done_copies(half, n):
            item.start()
        return 0

    row_copy = pltpu.make_async_copy(row, row_out, end_sem.at[3])

    def half_row(i, carry):
        @pl.when(i == 1)
        def _():
            pass_over(order[2])
            given.wait_recv()
            row_copy.start()

        half = c + i - 2 * c * i
        lax.fori_loop(0, 2, lambda n, _: project(half, n), 0)
        return carry

    lax.fori_loop(0, 2, half_row, 0)
    pass_over(order[3])

    for p in range(2):

        @pl.when(stays[p])
        def _():
            first_local(p).wait()

        @pl.when(jnp.logical_not(stays[p]))
        def _():
            first_copy(p).wait_send()

    for u in range(2):
        came = pltpu.make_async_remote_copy(
            src_ref=first.at[u],
            dst_ref=first.at[u],
            send_sem=fsend.at[u],
            recv_sem=frecv.at[u],
            device_id=(dpc, t),
            device_id_type=MESH,
        )

        @pl.when((side != c) | (t != 2 * c + u))
        def _():
            came.wait_recv()

    def mixed_copy(n):
        rows = pl.ds(pl.multiple_of(n * 512, 512), 512)
        return rows, pltpu.make_async_copy(v_s.at[rows, :], v_out.at[rows, :], tile_sem.at[n, 3])

    def mix(n, carry):
        rows, item = mixed_copy(n)
        for u in range(2):
            lanes = slice(u * 256, u * 256 + 256)
            v_s[rows, lanes] = (raw_s[rows, lanes] + 0.5 * first[u, rows, :].astype(F32)).astype(BF16)
        item.start()
        return carry

    lax.fori_loop(0, 4, mix, 0)
    outs = []
    for n in range(4):
        outs += done_copies(n // 2, n % 2) + [mixed_copy(n)[1]]
    given.wait_send()
    for k in range(chunks):
        if k:
            for item in over[k]:
                item.wait_recv()
        end_along(k)
        for item in across[k] + over[k]:
            item.wait_send()
        for at in range(4):
            for h in range(2):
                onward(k, at, h, slot(k, at, dp, h)).wait_send()
    for item in outs + tables + [row_copy]:
        item.wait()


def gather(ends, tok, fv, small, big, gain, freqs):
    part, rows = big.shape[2:]
    wide = tok.shape[1]
    vmem = pl.BlockSpec(memory_space=pltpu.VMEM)
    sems = pltpu.SemaphoreType.DMA
    low = lambda *shape: pltpu.VMEM(shape, BF16)
    shapes = [(2, SEQ // 2, wide), (4, 4, wide, 256), (3, 8, 2, 4, part, rows), (SEQ, wide)] + [(SEQ, 512)] * 3
    return pl.pallas_call(
        gather_kernel,
        out_shape=[jax.ShapeDtypeStruct(shape, BF16) for shape in shapes]
        + [jax.ShapeDtypeStruct((SEQ, 128), F32)] * 2,
        in_specs=[pl.BlockSpec(memory_space=pltpu.SMEM)] + [vmem] * 6,
        out_specs=[any_spec()] * 9,
        scratch_shapes=[low(2, SEQ // 2, wide), low(2, SEQ, 256), low(3, 2, wide, 256), low(SEQ, wide)]
        + [low(SEQ, 512)] * 3
        + [pltpu.VMEM((SEQ, 512), F32)]
        + [pltpu.VMEM((SEQ, 128), F32)] * 2
        + [
            sems((4, 8)),
            sems((4, 8)),
            sems((4, 4, 2)),
            sems((4, 4)),
            sems((4, 4, 2)),
            sems((4, 4, 2)),
            sems((4,)),
            sems((2,)),
            sems((2,)),
            sems((6,)),
            sems((4, 4)),
            sems((4,)),
        ],
        compiler_params=params(collective_id=0, has_side_effects=True),
        name="gather",
    )(ends, tok, fv, small, big, gain, freqs)


def dot(left, right):
    return jnp.dot(left, right, preferred_element_type=F32)


def dot_nt(left, right):
    return lax.dot_general(left, right, (((1,), (1,)), ((), ())), preferred_element_type=F32)


def dot_tn(left, right):
    return lax.dot_general(left, right, (((0,), (0,)), ((), ())), preferred_element_type=F32)


def any_spec():
    return pl.BlockSpec(memory_space=pl.ANY)


def params(**more):
    return pltpu.CompilerParams(vmem_limit_bytes=62 * 1024 * 1024, **more)


def cost(flops, size, exps=0):
    return pl.CostEstimate(flops=int(flops), bytes_accessed=int(size), transcendentals=int(exps))


def once(shape, place):
    return pl.BlockSpec(shape, place, pipeline_mode=pl.Buffered(1))


def head_masks(rows):
    lane = lax.broadcasted_iota(jnp.int32, (rows, 256), 1)
    return (lane & 127) >> 5, lane >> 6


def attend_kernel(at, bounds, q_ref, k_ref, v_ref, starts, own_ref, send_ref, lse_ref, kept, turned, acc):
    tiles = SEQ // TILE
    of_qk, _ = head_masks(TILE)
    row = lax.broadcasted_iota(jnp.int32, (TILE, TILE), 0)
    lane = lax.broadcasted_iota(jnp.int32, (TILE, TILE), 1)
    slabs = [slice(0, 256), slice(256, 512)]

    def turn_values(j, carry):
        there = pl.ds(pl.multiple_of(j * TILE, TILE), TILE)
        turned[j] = v_ref[there, :].T
        return carry

    lax.fori_loop(0, tiles, turn_values, 0)

    def eighths(values, reduce):
        return reduce(values.reshape(TILE // 8, 8, 4 * TILE), axis=0)

    def query_tile(i, carry):
        here = pl.ds(pl.multiple_of(i * TILE, TILE), TILE)
        q4 = []
        for slab in slabs:
            q = q_ref[here, slab]
            zero = jnp.zeros_like(q)
            q4.append(jnp.concatenate([jnp.where(of_qk == h, q, zero) for h in range(4)], axis=0))
        low = bounds[i]
        begin = starts[pl.ds(i, 1), :]
        limit = lane + i * TILE

        def score(j, tops):
            there = pl.ds(pl.multiple_of(j * TILE, TILE), TILE)
            at_row = row + j * TILE
            ok = (at_row >= begin) & (at_row <= limit)
            ok = jnp.concatenate([ok] * 4, axis=1)
            new = []
            for u, slab in enumerate(slabs):
                s = jnp.where(ok, dot_nt(k_ref[there, slab], q4[u]), NEG)
                kept[j - low, u] = s
                new.append(jnp.maximum(tops[u], eighths(s, jnp.max)))
            return tuple(new)

        start = jnp.full((8, 4 * TILE), NEG, F32)
        tops = lax.fori_loop(low, i + 1, score, (start, start))
        tops = [jnp.max(top, axis=0, keepdims=True) for top in tops]
        acc[...] = jnp.zeros_like(acc)

        def weigh(j, totals):
            new = []
            for u in range(2):
                e = jnp.exp(kept[j - low, u] - tops[u])
                p = e.astype(BF16)
                for h in range(4):
                    part = slice(u * 256 + h * 64, u * 256 + h * 64 + 64)
                    acc[part] += dot(turned[j, part, :], p[:, h * TILE : (h + 1) * TILE])
                new.append(totals[u] + eighths(e, jnp.sum))
            return tuple(new)

        zero = jnp.zeros((8, 4 * TILE), F32)
        totals = lax.fori_loop(low, i + 1, weigh, (zero, zero))
        for u, slab in enumerate(slabs):
            total = jnp.sum(totals[u], axis=0, keepdims=True)
            inverse = 1.0 / total
            scaled = [
                acc[u * 256 + h * 64 : u * 256 + h * 64 + 64] * inverse[:, h * TILE : (h + 1) * TILE] for h in range(4)
            ]
            done = jnp.concatenate(scaled, axis=0).T.astype(BF16)
            local = pl.ds(pl.multiple_of(lax.rem(i, tiles // 2) * TILE, TILE), TILE)
            mine = lax.div(i, tiles // 2) == (at[0] & 1)

            @pl.when(mine)
            def _():
                own_ref[local, slab] = done

            @pl.when(jnp.logical_not(mine))
            def _():
                send_ref[local, slab] = done

            lse_ref[u, pl.ds(i, 1), :] = tops[u] + jnp.log(total)
        return carry

    lax.fori_loop(0, tiles, query_tile, 0)


def attend(at, bounds, q, k, v, starts):
    tiles = SEQ // TILE
    vmem = pl.BlockSpec(memory_space=pltpu.VMEM)
    return pl.pallas_call(
        attend_kernel,
        out_shape=[
            jax.ShapeDtypeStruct((SEQ // 2, 512), BF16),
            jax.ShapeDtypeStruct((SEQ // 2, 512), BF16),
            jax.ShapeDtypeStruct((2, tiles, 4 * TILE), F32),
        ],
        in_specs=[pl.BlockSpec(memory_space=pltpu.SMEM)] * 2 + [vmem] * 4,
        out_specs=[vmem] * 3,
        scratch_shapes=[
            pltpu.VMEM((tiles, 2, TILE, 4 * TILE), F32),
            pltpu.VMEM((tiles, 512, TILE), BF16),
            pltpu.VMEM((512, TILE), F32),
        ],
        compiler_params=params(),
        cost_estimate=cost(20e9, 12e6, 1e7),
        name="attend",
    )(at, bounds, q, k, v, starts)


def attend_back_kernel(
    at, bounds, q_hbm, k_hbm, v_hbm, do_own, do_other, o_own, o_other, lse_ref, starts, cosine, sine, *rest, part,
):
    if part:
        held_hbm, rest = rest[0], rest[1:]
        dq_hbm, dk_hbm, dv_hbm = rest[:3]
        rest = rest[3:]
    else:
        dq_hbm, dk_hbm, dv_hbm, held_hbm = rest[:4]
        rest = rest[4:]
    attend_back_part(
        at, bounds, q_hbm, k_hbm, v_hbm, do_own, do_other, o_own, o_other, lse_ref, starts, cosine, sine, held_hbm, dq_hbm, dk_hbm,
        dv_hbm, *rest, part=part
    )


def attend_back_part(
    at, bounds, q_hbm, k_hbm, v_hbm, do_own, do_other, o_own, o_other, lse_ref, starts, cosine, sine, held_hbm, dq_hbm, dk_hbm, dv_hbm,
    q_ref, k_ref, v_ref, do_ref, o_ref, dq_ref, dk_ref, dv_ref, dq_acc, delta, dk_acc, dv_acc, load, store, *, part,
):
    tiles = SEQ // TILE
    of_qk, of_v = head_masks(TILE)
    row = lax.broadcasted_iota(jnp.int32, (TILE, TILE), 0)
    lane = lax.broadcasted_iota(jnp.int32, (TILE, TILE), 1)
    slabs = [slice(0, 256), slice(256, 512)]
    pick = (lax.broadcasted_iota(jnp.int32, (8, 256), 1) >> 6) == lax.broadcasted_iota(
        jnp.int32, (8, 256), 0
    )
    pick = pick.astype(F32)
    half = SEQ // 2
    low = pl.multiple_of((at[0] & 1) * half, half)
    mine, others = pl.ds(low, half), pl.ds(half - low, half)
    first_half, second_half = pl.ds(0, half), pl.ds(half, half)
    mine_second = (at[0] & 1) == 1
    here_half = second_half if part else first_half
    q_rows = second_half if part else pl.ds(0, SEQ)
    plain = [
        (q_hbm.at[q_rows, :], q_ref.at[q_rows, :]),
        (k_hbm.at[here_half, :], k_ref.at[here_half, :]),
        (v_hbm.at[here_half, :], v_ref.at[here_half, :]),
    ]
    if part:
        plain.append((held_hbm, dq_acc.at[pl.ds(tiles // 2, tiles // 2)]))
    loads = [pltpu.make_async_copy(src, dst, load.at[4 + n]) for n, (src, dst) in enumerate(plain)]

    def half_loads(own, other, dst, n):
        pairs = [(own, mine, mine_second), (other, others, jnp.logical_not(mine_second))]
        for e, (src, rows, wanted) in enumerate(pairs):
            yield pltpu.make_async_copy(src, dst.at[rows, :], load.at[n + e]), wanted

    parts = list(half_loads(do_own, do_other, do_ref, 0)) + list(half_loads(o_own, o_other, o_ref, 2))

    def each(action):
        for item, wanted in parts:
            if part:
                pl.when(wanted)(functools.partial(action, item))
            else:
                action(item)

    each(lambda item: item.start())
    for item in loads:
        item.start()
    if not part:
        dq_acc[...] = jnp.zeros_like(dq_acc)
    each(lambda item: item.wait())

    def prepare(i, carry):
        here = pl.ds(pl.multiple_of(i * TILE, TILE), TILE)
        for u, slab in enumerate(slabs):
            both = do_ref[here, slab].astype(F32) * o_ref[here, slab].astype(F32)
            sums = lax.dot_general(
                pick, both, (((1,), (1,)), ((), ())), precision=lax.Precision.HIGHEST, preferred_element_type=F32
            )
            for h in range(4):
                delta[u, pl.ds(i, 1), h * TILE : (h + 1) * TILE] = sums[h : h + 1]
        return carry

    middle = tiles // 2
    lax.fori_loop(middle * part, tiles, prepare, 0)
    for item in loads:
        item.wait()

    def rotate_out(values, here, out, low, scale):
        a, b = values[:, :128], values[:, 128:]
        cos, sin = cosine[here, :], sine[here, :]
        out[here, low : low + 128] = ((a * cos + b * sin) * scale).astype(BF16)
        out[here, low + 128 : low + 256] = ((b * cos - a * sin) * scale).astype(BF16)

    def split(values, of):
        zero = jnp.zeros_like(values)
        return jnp.concatenate([jnp.where(of == h, values, zero) for h in range(4)], axis=0)

    def key_tile(j, carry):
        there = pl.ds(pl.multiple_of(j * TILE, TILE), TILE)
        at_row = row + j * TILE
        dk_acc[...] = jnp.zeros_like(dk_acc)
        dv_acc[...] = jnp.zeros_like(dv_acc)

        def query_tile(i, carry):
            here = pl.ds(pl.multiple_of(i * TILE, TILE), TILE)
            at_lane = lane + i * TILE
            ok = (at_row >= starts[pl.ds(i, 1), :]) & (at_row <= at_lane)
            ok = jnp.concatenate([ok] * 4, axis=1)
            for u, slab in enumerate(slabs):
                q4 = split(q_ref[here, slab], of_qk)
                do4 = split(do_ref[here, slab], of_v)
                s = dot_nt(k_ref[there, slab], q4)
                dp = dot_nt(v_ref[there, slab], do4)
                p = jnp.exp(jnp.where(ok, s - lse_ref[u, pl.ds(i, 1), :], NEG))
                ds = (p * (dp - delta[u, pl.ds(i, 1), :])).astype(BF16)
                dv_acc[u] += dot(p.astype(BF16), do4)
                dk_acc[u] += dot(ds, q4)
                ds4 = jnp.concatenate([ds[:, h * TILE : (h + 1) * TILE] for h in range(4)], axis=0)
                dq_acc[i, u] += dot_tn(ds4, split(k_ref[there, slab], of_qk))
            return carry

        lax.fori_loop(j, bounds[tiles + j] + 1, query_tile, 0)
        for u, slab in enumerate(slabs):
            rotate_out(dk_acc[u], there, dk_ref, u * 256, 1.0)
            dv_ref[there, slab] = (0.5 * dv_acc[u]).astype(BF16)
        local = pl.ds(pl.multiple_of((j - middle * part) * TILE, TILE), TILE)
        pltpu.make_async_copy(dk_ref.at[there, :], dk_hbm.at[local, :], store.at[0]).start()
        pltpu.make_async_copy(dv_ref.at[there, :], dv_hbm.at[local, :], store.at[1]).start()
        return carry

    lax.fori_loop(middle * part, middle * part + middle, key_tile, 0)
    if not part:
        held = pltpu.make_async_copy(dq_acc.at[pl.ds(middle, middle)], held_hbm, store.at[3])
        held.start()

    def finish_tile(i, carry):
        here = pl.ds(pl.multiple_of(i * TILE, TILE), TILE)
        for u in range(2):
            rotate_out(dq_acc[i, u], here, dq_ref, u * 256, 0.125)
        local = pl.ds(pl.multiple_of((i - middle * part) * TILE, TILE), TILE)
        pltpu.make_async_copy(dq_ref.at[here, :], dq_hbm.at[local, :], store.at[2]).start()
        return carry

    lax.fori_loop(middle * part, middle * part + middle, finish_tile, 0)
    for n, (src, dst) in enumerate(((dk_ref, dk_hbm), (dv_ref, dv_hbm), (dq_ref, dq_hbm))):
        pltpu.make_async_copy(src.at[here_half, :], dst, store.at[n]).wait()
    if not part:
        held.wait()


def attend_back(part, at, bounds, q, k, v, do_own, do_other, o_own, o_other, lse, starts, cosine, sine, *held):
    tiles = SEQ // TILE
    vmem = pl.BlockSpec(memory_space=pltpu.VMEM)
    sems = pltpu.SemaphoreType.DMA
    outs = [jax.ShapeDtypeStruct((SEQ // 2, 512), BF16)] * 3
    if not part:
        outs.append(jax.ShapeDtypeStruct((tiles // 2, 2, TILE, 256), F32))
    return pl.pallas_call(
        functools.partial(attend_back_kernel, part=part),
        out_shape=outs,
        in_specs=[pl.BlockSpec(memory_space=pltpu.SMEM)] * 2 + [any_spec()] * 7 + [vmem] * 4 + [any_spec()] * len(held),
        out_specs=[any_spec()] * len(outs),
        scratch_shapes=[pltpu.VMEM((SEQ, 512), BF16)] * 8
        + [
            pltpu.VMEM((tiles, 2, TILE, 256), F32),
            pltpu.VMEM((2, tiles, 4 * TILE), F32),
            pltpu.VMEM((2, TILE, 256), F32),
            pltpu.VMEM((2, TILE, 256), F32),
            sems((8,)),
            sems((4,)),
        ],
        compiler_params=params(),
        cost_estimate=cost(25e9, 12e6, 5e6),
        name="attend_back",
    )(at, bounds, q, k, v, do_own, do_other, o_own, o_other, lse, starts, cosine, sine, *held)


def mlp_kernel(at, att_own, att_other, tok, cot_here, cot_moved, gain, wo, big, *rest):
    (out, gh_out, gb_out, n2_out, hid_out, ga_own, ga_other, gg_out, cot_out) = rest[:9]
    (wg, wu, wd, down, back, sems) = rest[9:]
    step = pl.program_id(0)
    c = at[0] & 1

    @pl.when(step == 0)
    def _():
        for n, held in enumerate((wg, wu, wd)):
            for owner in range(8):
                pltpu.make_async_copy(
                    big.at[n, owner], held.at[:, owner * 128 : owner * 128 + 128], sems.at[n]
                ).start()
        gg_out[...] = jnp.zeros_like(gg_out)

    hidden = tok[0].astype(F32)
    for e, att in enumerate((att_own, att_other)):
        for u in range(2):
            hidden += dot_nt(att[:, u * 256 : u * 256 + 256], wo[0, 2 * (c ^ e) + u])
    factor = lax.rsqrt(jnp.mean(hidden * hidden, axis=1, keepdims=True) + EPSILON)
    gains = gain[...]
    normed = (hidden * factor * gains).astype(BF16)
    n2_out[...] = normed.T
    g = jnp.where((at[1] & 1) == c, cot_here[...], cot_moved[...])
    cot_out[...] = g.T

    @pl.when(step == 0)
    def _():
        for n, held in enumerate((wg, wu, wd)):
            pltpu.make_async_copy(held, held, sems.at[n]).wait()

    down[...] = hidden
    back[...] = jnp.zeros_like(back)
    units, block = wg.shape[0], 768

    def unit_block(low, width):
        part = pl.ds(low, width)
        gate, up, grad_act = dot_nt(normed, wg[part, :]), dot_nt(normed, wu[part, :]), dot_nt(g, wd[part, :])
        sig = 1.0 / (1.0 + jnp.exp(-gate))
        silu = gate * sig
        act = (silu * up).astype(BF16)
        grad_up = (grad_act * silu).astype(BF16)
        grad_gate = (grad_act * up * (sig * (1.0 + gate * (1.0 - sig)))).astype(BF16)
        hid_out[0, :, part], hid_out[1, :, part], hid_out[2, :, part] = grad_gate, grad_up, act
        down[...] += dot(act, wd[part, :])
        back[...] += dot(grad_gate, wg[part, :]) + dot(grad_up, wu[part, :])

    def whole_block(k, carry):
        unit_block(pl.multiple_of(k * block, block), block)
        return carry

    lax.fori_loop(0, units // block, whole_block, 0)
    if units % block:
        unit_block(units - units % block, units % block)
    grad = back[...]
    out[...] = down[...].astype(BF16)
    gg_out[...] += jnp.sum((grad * hidden * factor).reshape(-1, 8, grad.shape[1]), axis=0)
    scaled = grad * gains
    mean = jnp.mean(scaled * hidden, axis=1, keepdims=True)
    grad_hidden = g.astype(F32) + factor * scaled - hidden * (factor * factor * factor * mean)
    gh_out[...] = grad_hidden
    branch = grad_hidden.astype(BF16)
    gb_out[...] = branch.T
    for e, ga in enumerate((ga_own, ga_other)):
        for u in range(2):
            ga[:, u * 256 : u * 256 + 256] = dot(branch, wo[0, 2 * (c ^ e) + u]).astype(BF16)


def mlp(at, att_own, att_other, tok, cot_here, cot_moved, gain, small, big):
    _, count, wide = tok.shape
    big = big.reshape(3, 8, -1, 128)
    rows, units = 256, big.shape[2]
    row = lambda width: pl.BlockSpec((rows, width), lambda i, at: (i, 0))
    turned = pl.BlockSpec((wide, rows), lambda i, at: (0, i))
    grid = pltpu.PrefetchScalarGridSpec(
        num_scalar_prefetch=1,
        grid=(count // rows,),
        in_specs=[
            row(512),
            row(512),
            pl.BlockSpec((1, rows, wide), lambda i, at: (at[0] & 1, i, 0)),
            row(wide),
            row(wide),
            pl.BlockSpec((1, wide), lambda i, at: (0, 0)),
            once((1, 4, wide, 256), lambda i, at: (3, 0, 0, 0)),
            any_spec(),
        ],
        out_specs=[
            row(wide),
            row(wide),
            turned,
            turned,
            pl.BlockSpec((3, rows, units), lambda i, at: (0, i, 0)),
            row(512),
            row(512),
            pl.BlockSpec((8, wide), lambda i, at: (0, 0)),
            turned,
        ],
        scratch_shapes=[pltpu.VMEM((units, wide), BF16)] * 3
        + [pltpu.VMEM((rows, wide), F32)] * 2
        + [pltpu.SemaphoreType.DMA((3,))],
    )
    tokens = lambda width, kind=BF16: jax.ShapeDtypeStruct((count, width), kind)
    return pl.pallas_call(
        mlp_kernel,
        out_shape=[
            tokens(wide),
            tokens(wide, F32),
            jax.ShapeDtypeStruct((wide, count), BF16),
            jax.ShapeDtypeStruct((wide, count), BF16),
            jax.ShapeDtypeStruct((3, count, units), BF16),
            tokens(512),
            tokens(512),
            jax.ShapeDtypeStruct((8, wide), F32),
            jax.ShapeDtypeStruct((wide, count), BF16),
        ],
        grid_spec=grid,
        compiler_params=params(),
        cost_estimate=cost(2 * count * wide * (6 * units + 2 * wide), 60e6, 3e6),
        name="mlp",
    )(at, att_own, att_other, tok, cot_here, cot_moved, gain, small, big)


def turn_rows(source, plane, parity, held):
    for rel in range(4):
        block = ((plane ^ rel) * 2 + parity) * 128
        held[rel * 128 : rel * 128 + 128, :] = source[:, pl.ds(pl.multiple_of(block, 128), 128)].T


def place_first(send, keep, done, lanes):
    for yr in range(2):
        keep[yr, :, lanes] = done[2 * yr]
        send[yr, :, lanes] = done[2 * yr + 1]


def place_second(send, keep, done, lanes):
    for xr in range(2):
        keep[xr, :, lanes] = done[xr]
        send[xr, :, lanes] = done[2 + xr]


def weights_kernel(
    n2, g_hbm, branch_hbm, hid, own_hbm, other_hbm, send1_out, keep1_out, send2_out, keep2_out,
    turned, g, branch, own, other, send1, keep1, send2, keep2, given, got, out_sem, in_sem, load, store,
):
    step = pl.program_id(0)
    dp, t = lax.axis_index("dp"), lax.axis_index("tensor")
    c = lax.rem(dp, 2)
    plane = lax.div(dp, 2)
    units = hid.shape[2] // 2
    loads = [
        pltpu.make_async_copy(src, dst, load.at[m])
        for m, (src, dst) in enumerate(((g_hbm, g), (branch_hbm, branch), (own_hbm, own), (other_hbm, other)))
    ]

    @pl.when(step == 0)
    def _():
        for item in loads:
            item.start()
        barrier = pltpu.get_barrier_semaphore()
        pl.semaphore_signal(barrier, inc=1, device_id=(dp + 1 - 2 * c, t), device_id_type=MESH)
        pl.semaphore_wait(barrier, 1)

    @pl.when(step == 2)
    def _():
        for item in loads:
            item.wait()

    def lanes_of(k):
        return pl.ds(k * units, units if k < 3 else 512)

    def exchange(k):
        return pltpu.make_async_remote_copy(
            src_ref=given.at[:, :, :, lanes_of(k)],
            dst_ref=got.at[:, :, :, lanes_of(k)],
            send_sem=out_sem.at[k],
            recv_sem=in_sem.at[k],
            device_id=(dp + 1 - 2 * c, t),
            device_id_type=MESH,
        )

    def stores(k):
        arrays = ((send1, send1_out), (keep1, keep1_out), (send2, send2_out), (keep2, keep2_out))
        return [
            pltpu.make_async_copy(src.at[:, :, lanes_of(k)], dst.at[:, :, lanes_of(k)], store.at[m, k])
            for m, (src, dst) in enumerate(arrays)
        ]

    def turn(source):
        x = lax.rem(plane, 2)
        y = lax.div(plane, 2)
        for e, parity in enumerate((1 - c, c)):
            for rel in range(4):
                yy, xx = (y, 1 - y)[rel // 2], (x, 1 - x)[rel % 2]
                block = pl.multiple_of((yy * 4 + xx * 2 + parity) * 128, 128)
                low = e * 512 + rel * 128
                turned[low : low + 128, :] = source[pl.ds(block, 128), :]

    for at_step, source in ((0, n2), (2, g), (3, branch)):

        @pl.when(step == at_step)
        def _():
            turn(source)

    places = ((place_first, send1, keep1), (place_second, send2, keep2))

    def take(product, h, lanes):
        rows = product.astype(BF16)
        given[:, h, :, lanes] = rows[:512].reshape(4, 128, rows.shape[1])
        for e, (place, send, keep) in enumerate(places):

            @pl.when(h == e)
            def _():
                place(send, keep, [rows[512 + r * 128 : 640 + r * 128] for r in range(4)], lanes)

    def add_got(lanes):
        for yr in range(2):
            keep1[yr, :, lanes] = add(keep1[yr, :, lanes], got[2 * yr, 0, :, lanes])
            send1[yr, :, lanes] = add(send1[yr, :, lanes], got[2 * yr + 1, 0, :, lanes])
            keep2[yr, :, lanes] = add(keep2[yr, :, lanes], got[yr, 1, :, lanes])
            send2[yr, :, lanes] = add(send2[yr, :, lanes], got[2 + yr, 1, :, lanes])

    for k in range(4):

        @pl.when(step == k + 1)
        def _():
            exchange(k).start()

    @pl.when(step < 3)
    def _():
        def one(h, carry):
            right = hid[0, :, pl.ds(pl.multiple_of(h * units, 128), units)]
            take(dot(turned[...], right), h, pl.ds(pl.multiple_of(step * units, 128), units))
            return carry

        lax.fori_loop(0, 2, one, 0)

    @pl.when(step == 3)
    def _():
        def one(h, carry):
            take(dot(turned[...], jnp.where(c == h, own[...], other[...])), h, lanes_of(3))
            return carry

        lax.fori_loop(0, 2, one, 0)

    for k in range(4):

        @pl.when(step == k + 2)
        def _():
            exchange(k).wait_recv()
            add_got(lanes_of(k))
            for item in stores(k):
                item.start()

    @pl.when(step == 5)
    def _():
        for k in range(4):
            exchange(k).wait_send()
            for item in stores(k):
                item.wait()


def weights(n2, g, branch, hid, own, other):
    wide, count = n2.shape
    units = hid.shape[2] // 2
    length = 3 * units + 512
    low = lambda *shape: pltpu.VMEM(shape, BF16)
    sems = pltpu.SemaphoreType.DMA
    grid = pl.GridSpec(
        grid=(6,),
        in_specs=[
            pl.BlockSpec((wide, count), lambda s: (0, 0), pipeline_mode=pl.Buffered(1)),
            any_spec(),
            any_spec(),
            pl.BlockSpec((1, count, 2 * units), lambda s: (jnp.minimum(s, 2), 0, 0)),
            any_spec(),
            any_spec(),
        ],
        out_specs=[any_spec()] * 4,
        scratch_shapes=[low(wide, count), low(wide, count), low(wide, count), low(count, 512), low(count, 512)]
        + [low(2, 128, length)] * 4
        + [low(4, 2, 128, length)] * 2
        + [sems((4,)), sems((4,)), sems((4,)), sems((4, 4))],
    )
    return pl.pallas_call(
        weights_kernel,
        out_shape=[jax.ShapeDtypeStruct((2, 128, length), BF16)] * 4,
        grid_spec=grid,
        compiler_params=params(collective_id=1, has_side_effects=True),
        cost_estimate=cost(2 * count * 1024 * length * 2, 50e6),
        name="weights",
    )(n2, g, branch, hid, own, other)


def add(left, right):
    return (left.astype(F32) + right.astype(F32)).astype(BF16)


def finish_kernel(at, own, got, own_heads, got_heads, tok, got_tok, first, came0, came1, slab0, slab1, layer, got_layer, gate, up, down, out, query, key, value, tok_out, first_out, layer_out):
    part = down.shape[0]
    for n, ref in enumerate((gate, up, down, out)):

        @pl.when(pl.program_id(0) == n)
        def _():
            rows = slice(n * part, n * part + ref.shape[0])
            total = own[rows, :].astype(F32)
            for d in range(3):
                total += got[d, rows, :].astype(F32)
            ref[...] = total

    @pl.when(pl.program_id(0) == 3)
    def _():
        heads = own_heads[...].astype(F32)
        for d in range(3):
            heads += got_heads[d].astype(F32)
        for n, ref in enumerate((query, key)):
            parts = []
            for h in range(4):
                parts += [heads[n, :, h * 32 : h * 32 + 32], heads[n, :, 128 + h * 32 : 160 + h * 32]]
            ref[...] = jnp.concatenate(parts, axis=1)
        value[...] = heads[2]

    stays = (at[0] & 1) == (at[1] & 1)
    tok_out[...] = jnp.where(stays, tok[...], got_tok[...]).astype(F32)
    step = pl.program_id(0)
    c, t = at[0] & 1, at[1]
    pair, side = t >> 1, t & 1
    r = (step >> 1) ^ side
    local = (c == side) & (t == 2 * c + (pair ^ r))

    @pl.when((step & 1) == 0)
    def _():
        came = jnp.where(r == 0, came0[...], came1[...])
        slab = jnp.where(r == 0, slab0[...], slab1[...])
        first_out[...] = jnp.where(local, slab, came).astype(F32)

    @pl.when((step & 1) == 1)
    def _():
        first_out[...] = first[0].astype(F32)

    layer_out[...] = jnp.where(stays, layer[...], got_layer[...])


def finish(at, pieces, got, own_heads, got_heads, tok, got_tok, first, early, layer, got_layer, part):
    count, wide = tok.shape
    rows = 256
    row = pl.BlockSpec((rows, wide), lambda i, at: (i, 0))
    wider = pl.BlockSpec((SEQ // 2, 256), lambda i, at: (i, 0))
    whole = lambda *shape: pl.BlockSpec(shape, lambda i, at: (0,) * len(shape))
    shapes = [(part, 128)] * 3 + [(256, 128)] + [(128, 256)] * 3
    grid = pltpu.PrefetchScalarGridSpec(
        num_scalar_prefetch=1,
        grid=(count // rows,),
        in_specs=[
            whole(*pieces.shape),
            whole(*got.shape),
            whole(*own_heads.shape),
            whole(*got_heads.shape),
            row,
            row,
            pl.BlockSpec((1, SEQ // 2, 256), lambda i, at: (i // 2, 0, 0)),
            *[whole(SEQ // 2, 256)] * 4,
            row,
            row,
        ],
        out_specs=[whole(*shape) for shape in shapes] + [row, wider, row],
    )
    return pl.pallas_call(
        finish_kernel,
        out_shape=[jax.ShapeDtypeStruct(shape, F32) for shape in shapes + [(count, wide), (2 * SEQ, 256)]]
        + [jax.ShapeDtypeStruct((count, wide), BF16)],
        grid_spec=grid,
        compiler_params=params(),
        cost_estimate=cost(1e6, 18e6),
        name="finish",
    )(at, pieces, got, own_heads, got_heads, tok, got_tok, first, *early, layer, got_layer)


def tail_kernel(
    dq0, dk0, dv0, dq1, dk1, dv1, small, normed, row, grad_hidden, keep1, got1, keep2, got2, gain, gain_two,
    first, own_pieces, got_pieces, own_heads, got_heads, tok, got_tok, sums,
    d_s, w_s, n_s, x_s, gh_s, ks1, gs1, ks2, gs2, last1, last2, pieces, gn_send, gn_got, turned,
    h_send, h_got, s1, k1, a1, a2, part1, part2, rest1, rest2, heads, held, came,
    load, f_sem, m_sem, p_sem, n_sem, c_sem, one_sem, two_sem, h_sem, swap, g_sem,
):
    dp, t = lax.axis_index("dp"), lax.axis_index("tensor")
    c, x, y = lax.rem(dp, 2), lax.rem(lax.div(dp, 2), 2), lax.div(dp, 4)
    pair, side = lax.div(t, 2), lax.rem(t, 2)
    plane = dp - c
    dpx, dpy, dpc = dp + 2 - 4 * x, dp + 4 - 8 * y, dp + 1 - 2 * c
    half = SEQ // 2
    units = (ks1.shape[2] - 512) // 3

    def copy(src, dst, sems, n, to):
        return pltpu.make_async_remote_copy(
            src_ref=src,
            dst_ref=dst,
            send_sem=sems.at[0, n],
            recv_sem=sems.at[1, n],
            device_id=to,
            device_id_type=MESH,
        )

    sources = [(keep1, ks1), (got1, gs1), (keep2, ks2), (got2, gs2)]
    for h, arrays in enumerate(((dq0, dk0, dv0), (dq1, dk1, dv1))):
        sources += [(src, d_s.at[n, pl.ds(h * half, half), :]) for n, src in enumerate(arrays)]
    sources += [(normed, n_s), (small.at[pl.ds(0, 3), pl.ds(2 * c, 2)], w_s), (row.at[c], x_s), (grad_hidden, gh_s)]
    loads = [pltpu.make_async_copy(src, dst, load.at[n]) for n, (src, dst) in enumerate(sources)]
    for item in loads:
        item.start()
    meet(plane, c, t, dpx, dpy)

    def value_copy(u):
        src = dv1.at[:, pl.ds(u * 256, 256)]
        return pltpu.make_async_remote_copy(
            src_ref=src,
            dst_ref=first.at[pair],
            send_sem=f_sem.at[0, u],
            recv_sem=f_sem.at[1, pair],
            device_id=(plane + side, 2 * c + u),
            device_id_type=MESH,
        )

    def value_local(u):
        return pltpu.make_async_copy(dv1.at[:, pl.ds(u * 256, 256)], first.at[pair], load.at[14])

    for u in range(2):
        stay = (side == c) & (t == 2 * c + u)

        @pl.when(stay)
        def _():
            value_local(u).start()

        @pl.when(jnp.logical_not(stay))
        def _():
            value_copy(u).start()

    for item in loads[:4]:
        item.wait()
    gs1[1] = add(ks1[1], gs1[1])
    gs2[1] = add(ks2[1], gs2[1])
    seconds = []
    for n, lanes in enumerate((pl.ds(0, 2 * units), pl.ds(2 * units, units + 512))):
        seconds.append(copy(gs1.at[1, :, lanes], last1.at[:, lanes], m_sem, 2 * n, (dpy, t)))
        seconds.append(copy(gs2.at[1, :, lanes], last2.at[:, lanes], m_sem, 2 * n + 1, (dpx, t)))
    for item in loads[4:11]:
        item.wait()
    for item in seconds:
        item.start()

    def turn(parity):
        for rel in range(4):
            yy, xx = (y, 1 - y)[rel // 2], (x, 1 - x)[rel % 2]
            block = pl.multiple_of((yy * 4 + xx * 2 + parity) * 128, 128)
            turned[rel * 128 : rel * 128 + 128, :] = n_s[:, pl.ds(block, 128)].T

    def heads_copy(n):
        lanes = pl.ds(pl.multiple_of(n * 512, 512), 512)
        return copy(h_send.at[:, :, :, lanes], h_got.at[:, :, :, lanes], c_sem, n, (dpc, t))

    def heads_product(n):
        product = dot(turned[...], d_s[n]).astype(BF16)
        return [product[r * 128 : r * 128 + 128] for r in range(4)], pl.ds(pl.multiple_of(n * 512, 512), 512)

    def heads_send(n, carry):
        place_second(h_send.at[0], h_send.at[1], *heads_product(n))

        @pl.when(n > 0)
        def _():
            heads_copy(n - 1).start()

        return carry

    def heads_keep(n, carry):
        place_first(s1, k1, *heads_product(n))
        return carry

    turn(1 - c)
    lax.fori_loop(0, 3, heads_send, 0)

    part = units // 4
    low_rows, high_rows = pl.ds(0, 4 * part), pl.ds(4 * part, 2 * part + 256)

    def fill_pieces(which):
        for h, (kept, got, last) in enumerate(((ks1, gs1, last1), (ks2, gs2, last2))):
            for n in which:
                lanes = slice(n * units, n * units + (units if n < 3 else 512))
                total = kept[0, :, lanes].astype(F32) + got[0, :, lanes].astype(F32) + last[:, lanes].astype(F32)
                flipped = total.T.astype(BF16)
                if n < 3:
                    for i in range(4):
                        rows = slice((2 * n + h) * part, (2 * n + h + 1) * part)
                        pieces[lax.rem(i + 4 - t, 4), rows, :] = flipped[i * part : (i + 1) * part]
                else:
                    for i in range(2):
                        pieces[lax.rem(2 * h + i + 4 - t, 4), 6 * part :, :] = flipped[i * 256 : i * 256 + 256]

    def piece_copies(rows, n):
        return [
            copy(pieces.at[d, rows, :], got_pieces.at[d - 1, rows, :], p_sem, 3 * n + d - 1, (dp, lax.rem(t + d, 4)))
            for d in (1, 2, 3)
        ]

    for item in seconds[:2]:
        item.wait_recv()
    fill_pieces((0, 1))
    turn(c)
    heads_copy(2).start()
    zs = piece_copies(low_rows, 0)
    for item in zs:
        item.start()
    lax.fori_loop(0, 3, heads_keep, 0)
    cs = [heads_copy(n) for n in range(3)]
    for item in cs:
        item.wait_recv()
    ones = [copy(h_got.at[0], a2, one_sem, 1, (dpy, t)), copy(s1, a1, one_sem, 0, (dpx, t))]
    for item in ones:
        item.start()
    for item in seconds[2:]:
        item.wait_recv()
    fill_pieces((2, 3))
    own_pieces[...] = pieces[0]
    last_zs = piece_copies(high_rows, 1)
    for item in last_zs:
        item.start()
    zs += last_zs

    def back_product(rows):
        total = None
        for u in range(2):
            for n in range(3):
                term = dot_nt(d_s[n, rows, u * 256 : u * 256 + 256], w_s[n, u])
                total = term if total is None else total + term
        return total

    ns = [copy(gn_send.at[i], gn_got.at[i], n_sem, i, (dpc, t)) for i in range(2)]

    def other_half(i, carry):
        rows = pl.ds(pl.multiple_of((1 - c) * half + i * 512, 512), 512)
        gn_send[i] = back_product(rows).astype(BF16)
        return carry

    loads[11].wait()
    lax.fori_loop(0, 2, other_half, 0)

    for item in ones:
        item.wait_recv()
    part1[...] = add(k1[1], a1[1])
    part2[...] = add(h_got[1, 1], a2[1])
    for item in ns:
        item.start()
    twos = [copy(part1, rest1, two_sem, 0, (dpy, t)), copy(part2, rest2, two_sem, 1, (dpx, t))]
    for item in twos:
        item.start()

    loads[12].wait()
    loads[13].wait()
    moved = side != c
    for item in ns:
        item.wait_recv()

    def own_half(i, gained):
        rows = pl.ds(pl.multiple_of(c * half + i * 512, 512), 512)
        here = pl.ds(pl.multiple_of(i * 512, 512), 512)
        grad = back_product(rows) + gn_got[i].astype(F32)
        values = x_s[here, :].astype(F32)
        factor = lax.rsqrt(jnp.mean(values * values, axis=1, keepdims=True) + EPSILON)
        gained += jnp.sum((grad * values * factor).reshape(-1, 8, grad.shape[1]), axis=0)
        scaled = grad * gain[...]
        mean = jnp.mean(scaled * values, axis=1, keepdims=True)
        tok[i] = (gh_s[here, :] + factor * scaled - values * (factor * factor * factor * mean)).astype(BF16)
        return gained

    gained = lax.fori_loop(0, 2, own_half, jnp.zeros((8, tok.shape[2]), F32))
    swaps = [copy(tok.at[i], got_tok.at[i], swap, i, (plane + side, 2 * pair + c)) for i in range(2)]

    total1 = k1[0].astype(F32) + a1[0].astype(F32)
    total2 = h_got[1, 0].astype(F32) + a2[0].astype(F32)

    @pl.when(moved)
    def _():
        for item in swaps:
            item.start()

    turns = (dpc, t), (dpx, t), (dpy, t), (dp, t + 1 - 2 * side), (dp, lax.rem(t + 2, 4))
    line = lax.broadcasted_iota(jnp.int32, gained.shape, 0)
    total_one = jnp.sum(gained, axis=0, keepdims=True)
    total_two = jnp.sum(gain_two[...], axis=0, keepdims=True)
    held[0] = jnp.where(line == 0, total_one, jnp.where(line == 1, total_two, 0.0))

    def gain_step(n):
        return copy(held.at[n], came.at[n], g_sem, n, turns[n])

    def gain_next(n):
        gain_step(n).wait_recv()
        held[n + 1] = held[n] + came[n]

    gain_step(0).start()
    gain_next(0)
    gain_step(1).start()
    gain_next(1)
    for item in twos:
        item.wait_recv()
    totals = ((total1 + rest1[...].astype(F32)).astype(BF16), (total2 + rest2[...].astype(F32)).astype(BF16))
    for e, total in enumerate(totals):
        core = (c, 1 - c)[e]
        for u in range(2):
            d = lax.rem(2 * core + u + 4 - t, 4)
            for n in range(3):
                heads[d, n] = total[:, n * 512 + u * 256 : n * 512 + u * 256 + 256]
    gain_step(2).start()
    gain_next(2)
    own_heads[...] = heads[0]
    hs = [copy(heads.at[d], got_heads.at[d - 1], h_sem, d - 1, (dp, lax.rem(t + d, 4))) for d in (1, 2, 3)]
    for item in hs:
        item.start()
    for n in (3, 4):
        gain_step(n).start()
        gain_next(n)
    sums[...] = held[5]

    for item in seconds + ns + cs + ones + twos:
        item.wait_send()
    for n in range(5):
        gain_step(n).wait_send()
    for u in range(2):
        stay = (side == c) & (t == 2 * c + u)

        @pl.when(stay)
        def _():
            value_local(u).wait()

        @pl.when(jnp.logical_not(stay))
        def _():
            value_copy(u).wait_send()

    for p in range(2):

        @pl.when((pair != c) | (t != 2 * p + c))
        def _():
            pltpu.make_async_remote_copy(
                src_ref=first.at[p],
                dst_ref=first.at[p],
                send_sem=f_sem.at[0, p],
                recv_sem=f_sem.at[1, p],
                device_id=(dpc, t),
                device_id_type=MESH,
            ).wait_recv()

    for item in zs + hs:
        item.wait()

    @pl.when(moved)
    def _():
        for item in swaps:
            item.wait()


def tail(back, small, normed, row, grad_hidden, keep1, got1, keep2, got2, gain, gain_two):
    vmem = pl.BlockSpec(memory_space=pltpu.VMEM)
    sems = pltpu.SemaphoreType.DMA
    wide = normed.shape[1]
    length = keep1.shape[2]
    rows = (length - 512) // 2 + 256
    half = SEQ // 2
    low = lambda *shape: pltpu.VMEM(shape, BF16)
    return pl.pallas_call(
        tail_kernel,
        out_shape=[
            jax.ShapeDtypeStruct((2, half, 256), BF16),
            jax.ShapeDtypeStruct((rows, 128), BF16),
            jax.ShapeDtypeStruct((3, rows, 128), BF16),
            jax.ShapeDtypeStruct((3, 128, 256), BF16),
            jax.ShapeDtypeStruct((3, 3, 128, 256), BF16),
            jax.ShapeDtypeStruct((2, half // 2, wide), BF16),
            jax.ShapeDtypeStruct((2, half // 2, wide), BF16),
            jax.ShapeDtypeStruct((8, wide), F32),
        ],
        in_specs=[any_spec()] * 14 + [vmem] * 2,
        out_specs=[any_spec(), vmem, any_spec(), vmem, any_spec(), vmem, any_spec(), vmem],
        scratch_shapes=[low(3, SEQ, 512)]
        + [low(3, 2, wide, 256), low(SEQ, wide), low(half, wide), pltpu.VMEM((half, wide), F32)]
        + [low(2, 128, length)] * 4
        + [low(128, length)] * 2
        + [low(4, rows, 128), low(2, half // 2, wide), low(2, half // 2, wide), low(512, SEQ)]
        + [low(2, 2, 128, 1536)] * 2
        + [low(2, 128, 1536)] * 4
        + [low(128, 1536)] * 4
        + [low(4, 3, 128, 256), pltpu.VMEM((6, 8, wide), F32), pltpu.VMEM((5, 8, wide), F32)]
        + [sems((15,)), sems((2, 2)), sems((2, 4)), sems((2, 6)), sems((2, 2)), sems((2, 3)), sems((2, 2)), sems((2, 2))]
        + [sems((2, 3)), sems((2, 2)), sems((2, 5))],
        compiler_params=params(collective_id=2, has_side_effects=True),
        name="tail",
    )(*back, small, normed, row, grad_hidden, keep1, got1, keep2, got2, gain, gain_two)


def fast_body(tokens, first_values, doc_lengths, cotangent, w_query, w_key, w_value, w_out, w_gate, w_up, w_down, gain_attn, gain_mlp):
    me, t = lax.axis_index("dp"), lax.axis_index("tensor")
    c = me % 2
    pair, side = t // 2, t % 2
    wide = tokens.shape[1]
    tiles = SEQ // TILE
    at = jnp.where(jnp.arange(8, dtype=jnp.int32) == 0, me, t).astype(jnp.int32)

    small_shard, big_shard = pack(w_query, w_key, w_value, w_out, w_gate, w_up, w_down)
    lengths = jnp.where(c == side, doc_lengths, across_c(doc_lengths))
    lengths = lax.dynamic_index_in_dim(lengths, pair, 0, keepdims=False)
    order = jnp.arange(DOCS, dtype=jnp.int32)
    ends = jnp.sum(jnp.where(order[None, :] <= order[:, None], lengths[None, :], 0), axis=1)
    freqs = 10000.0 ** (-(jnp.arange(32, dtype=F32) * 2.0 / HEAD))
    row, small, big, normed_one, q, k, v, cosine, sine = gather(
        ends, tokens, first_values, small_shard, big_shard, gain_attn[None], jnp.tile(freqs, 4)[None]
    )
    places = jnp.arange(SEQ, dtype=jnp.int32)
    starts = jnp.max(jnp.where(ends[None, :] <= places[:, None], ends[None, :], 0), axis=1)
    last = jnp.arange(tiles, dtype=jnp.int32) * TILE + (TILE - 1)
    stop = jnp.min(jnp.where(ends[None, :] > last[:, None], ends[None, :], SEQ), axis=1)
    bounds = jnp.concatenate([starts.reshape(tiles, TILE)[:, 0] // TILE, (stop - 1) // TILE])
    starts_by_tile = starts.reshape(tiles, TILE)

    row, cotangent = lax.optimization_barrier((row, cotangent))
    moved_cot = swap_halves(cotangent)
    att_own, att_send, lse = attend(at, bounds, q, k, v, starts_by_tile)
    att_other = across_c(att_send)
    out, grad_hidden, branch, normed_two, hid, ga_own, ga_other, gain_two, cot = mlp(
        at, att_own, att_other, row, cotangent, moved_cot, gain_mlp[None], small, big
    )
    moved_out = swap_halves(out)

    ga_got = across_c(ga_other)

    kept = weights(normed_two, cot, branch, hid, att_own, att_other)
    kept, ga_got = lax.optimization_barrier((kept, ga_got))
    got1, got2 = across_x(kept[0]), across_y(kept[2])

    rest = (att_own, att_send, lse, starts_by_tile, cosine, sine)
    dq0, dk0, dv0, held = attend_back(0, at, bounds, q, k, v, ga_own, ga_got, *rest)

    slabs = [jnp.where(pair == r, dv0[:, :256], dv0[:, 256:]) for r in range(2)]
    came = [
        move(slabs[r], lambda y, x, c, t, r=r: (y, x, t % 2, 2 * c + ((t // 2) ^ r))) for r in range(2)
    ]
    dq1, dk1, dv1 = attend_back(1, at, bounds, q, k, v, ga_own, ga_got, *rest, held)
    dv1, came = lax.optimization_barrier((dv1, came))

    first_back, pieces, got, own_heads, got_heads, grad_tokens, got_tokens, gains = tail(
        (dq0, dk0, dv0, dq1, dk1, dv1), small, normed_one, row, grad_hidden, kept[1], got1, kept[3], got2, gain_attn[None], gain_two
    )
    shape = (SEQ // 2, wide)
    grad_gate, grad_up, grad_down, grad_out, gq, gk, gv, grad_tokens, grad_first, layer_out = finish(
        at, pieces, got, own_heads, got_heads, grad_tokens.reshape(shape), got_tokens.reshape(shape), first_back, (*came, *slabs), out, moved_out, w_gate.shape[1]
    )
    return (
        layer_out,
        grad_tokens,
        grad_first,
        gq,
        gk,
        gv,
        grad_out,
        grad_gate.T,
        grad_up.T,
        grad_down,
        gains[0],
        gains[1],
    )


def solution(mesh):
    fits = dict(mesh.shape) == {"dp": 8, "tensor": 4}
    placed = (
        P(("dp", "tensor"), None),
        P("dp", "tensor"),
        P("dp", None),
        P(("dp", "tensor"), None),
        P("dp", "tensor"),
        P("dp", "tensor"),
        P("dp", "tensor"),
        P("tensor", "dp"),
        P("dp", "tensor"),
        P("dp", "tensor"),
        P("tensor", "dp"),
        P(),
        P(),
    )
    return jax.shard_map(
        fast_body if fits else general_body,
        mesh=mesh,
        in_specs=placed,
        out_specs=(
            P(("dp", "tensor"), None),
            P(("dp", "tensor"), None),
            P("dp", "tensor"),
            P("dp", "tensor"),
            P("dp", "tensor"),
            P("dp", "tensor"),
            P("tensor", "dp"),
            P("dp", "tensor"),
            P("dp", "tensor"),
            P("tensor", "dp"),
            P(),
            P(),
        ),
        check_vma=False,
    )
```

```python
import functools

import jax
import jax.numpy as jnp
from jax import lax
from jax.experimental import pallas as pl
from jax.experimental.pallas import tpu as pltpu
from jax.sharding import PartitionSpec as P

HEAD = 64
SEQ = 2048
DOCS = 8
EPSILON = 1e-05


def rms_norm(values, gain):
    factor = lax.rsqrt(jnp.mean(values * values, axis=1, keepdims=True) + EPSILON)
    return values * factor * gain


def documents(doc_lengths):
    ends = jnp.cumsum(doc_lengths, axis=1)
    starts = ends - doc_lengths
    places = jnp.arange(SEQ, dtype=jnp.int32)
    segment = jnp.sum((places[None, :, None] >= ends[:, None, :]).astype(jnp.int32), axis=2)
    member = segment[:, :, None] == jnp.arange(DOCS, dtype=jnp.int32)[None, None, :]
    offset = jnp.sum(jnp.where(member, starts[:, None, :], 0), axis=2)
    return (segment, (places[None, :] - offset).astype(jnp.float32))


def rotation(positions):
    half = HEAD // 2
    freqs = 10000.0 ** (-(jnp.arange(half, dtype=jnp.float32) * 2.0 / HEAD))
    angles = positions[:, None] * freqs[None, :]
    return (jnp.cos(angles), jnp.sin(angles))


def rotate(values, cosine, sine):
    shaped = values.reshape(values.shape[0], -1, HEAD)
    half = HEAD // 2
    first = shaped[:, :, :half]
    second = shaped[:, :, half:]
    cos_rows = cosine[:, None, :]
    sin_rows = sine[:, None, :]
    turned = jnp.concatenate(
        [first * cos_rows - second * sin_rows, second * cos_rows + first * sin_rows], axis=2
    )
    return turned.reshape(values.shape)


def rotate_back(grads, cosine, sine):
    shaped = grads.reshape(grads.shape[0], -1, HEAD)
    half = HEAD // 2
    first = shaped[:, :, :half]
    second = shaped[:, :, half:]
    cos_rows = cosine[:, None, :]
    sin_rows = sine[:, None, :]
    turned = jnp.concatenate(
        [first * cos_rows + second * sin_rows, second * cos_rows - first * sin_rows], axis=2
    )
    return turned.reshape(grads.shape)


def swiglu(gate, up_val):
    return jax.nn.silu(gate) * up_val


def product(left, right):
    return jnp.dot(left, right, preferred_element_type=jnp.float32)


def inner(left, right):
    return lax.dot_general(
        left, right, (((0,), (0,)), ((), ())), preferred_element_type=jnp.float32
    )


def outer(left, right):
    return lax.dot_general(
        left, right, (((1,), (1,)), ((), ())), preferred_element_type=jnp.float32
    )


def block_scores(queries, keys_all, segment, start, width):
    query_block = lax.dynamic_slice_in_dim(queries, start, width, 0)
    query_seg = lax.dynamic_slice_in_dim(segment, start, width, 0)
    scores = (
        jnp.einsum("qhd,khd->hqk", query_block, keys_all, preferred_element_type=jnp.float32)
        * 0.125
    )
    places = jnp.arange(SEQ, dtype=jnp.int32)
    rows_at = start + jnp.arange(width, dtype=jnp.int32)
    allowed = (query_seg[:, None] == segment[None, :]) & (places[None, :] <= rows_at[:, None])
    return (query_block, jnp.where(allowed[None], scores, -1e30))


def forward_row(pieces):
    queries, keys_all, values_all, segment = pieces
    width = min(512, SEQ)
    count = SEQ // width

    def forward_one_block(index):
        unused, scores = block_scores(queries, keys_all, segment, index * width, width)
        top = jnp.max(scores, axis=2, keepdims=True)
        expo = jnp.exp(scores - top)
        total = jnp.sum(expo, axis=2, keepdims=True)
        weights = (expo / total).astype(jnp.bfloat16)
        result = jnp.einsum("hqk,khd->qhd", weights, values_all, preferred_element_type=jnp.float32)
        return (result, (top + jnp.log(total))[:, :, 0])

    results, logsums = lax.map(forward_one_block, jnp.arange(count, dtype=jnp.int32))
    return (results.reshape(SEQ, queries.shape[1], HEAD), logsums)


def backward_row(pieces):
    queries, keys_all, values_all, segment, grad_rows, logsums = pieces
    width = min(512, SEQ)
    count = SEQ // width

    def backward_one_block(carry, extra):
        index, logsum = extra
        start = index * width
        query_block, scores = block_scores(queries, keys_all, segment, start, width)
        probs = jnp.exp(scores - logsum[:, :, None])
        grad_block = lax.dynamic_slice_in_dim(grad_rows, start, width, 0)
        grad_probs = jnp.einsum(
            "qhd,khd->hqk", grad_block, values_all, preferred_element_type=jnp.float32
        )
        delta = jnp.sum(probs * grad_probs, axis=2, keepdims=True)
        grad_scores = (probs * (grad_probs - delta)).astype(jnp.bfloat16)
        grad_query = (
            jnp.einsum("hqk,khd->qhd", grad_scores, keys_all, preferred_element_type=jnp.float32)
            * 0.125
        )
        grad_keys = (
            carry[0]
            + jnp.einsum(
                "hqk,qhd->khd", grad_scores, query_block, preferred_element_type=jnp.float32
            )
            * 0.125
        )
        grad_values = carry[1] + jnp.einsum(
            "hqk,qhd->khd",
            probs.astype(jnp.bfloat16),
            grad_block,
            preferred_element_type=jnp.float32,
        )
        return ((grad_keys, grad_values), grad_query)

    zeros = jnp.zeros(keys_all.shape, jnp.float32)
    sums, grad_queries = lax.scan(
        backward_one_block, (zeros, zeros), (jnp.arange(count, dtype=jnp.int32), logsums)
    )
    return (grad_queries.reshape(SEQ, queries.shape[1], HEAD), sums[0], sums[1])


def general_body(
    tokens,
    first_values,
    doc_lengths,
    cotangent,
    w_query,
    w_key,
    w_value,
    w_out,
    w_gate,
    w_up,
    w_down,
    gain_attn,
    gain_mlp,
):
    query_mat, key_mat, value_mat, out_mat, gate_mat, up_mat, down_mat = (
        lax.all_gather(w_query, "dp", axis=0, tiled=True),
        lax.all_gather(w_key, "dp", axis=0, tiled=True),
        lax.all_gather(w_value, "dp", axis=0, tiled=True),
        lax.all_gather(w_out, "dp", axis=1, tiled=True),
        lax.all_gather(w_gate, "dp", axis=0, tiled=True),
        lax.all_gather(w_up, "dp", axis=0, tiled=True),
        lax.all_gather(w_down, "dp", axis=1, tiled=True),
    )
    local_heads = query_mat.shape[1] // HEAD
    row_count = doc_lengths.shape[0]
    group = row_count * SEQ
    segment, positions = documents(doc_lengths)
    cosine, sine = rotation(positions.reshape(-1))

    def heads(matrix):
        return matrix.reshape(row_count, SEQ, local_heads, HEAD)

    inputs = tokens.astype(jnp.float32)
    normed_one, norm_one_back = jax.vjp(rms_norm, inputs, gain_attn)
    gathered_one = lax.all_gather(normed_one.astype(jnp.bfloat16), "tensor", axis=0, tiled=True)
    query_raw = product(gathered_one, query_mat)
    key_raw = product(gathered_one, key_mat)
    value_raw = product(gathered_one, value_mat)
    queries = rotate(query_raw, cosine, sine).astype(jnp.bfloat16)
    keys_low = rotate(key_raw, cosine, sine).astype(jnp.bfloat16)
    mixed_values = (0.5 * value_raw + 0.5 * first_values.astype(jnp.float32)).astype(jnp.bfloat16)
    attended, logsums = lax.map(
        forward_row, (heads(queries), heads(keys_low), heads(mixed_values), segment)
    )
    attended_low = attended.reshape(group, -1).astype(jnp.bfloat16)
    hidden_in = inputs + lax.psum_scatter(
        product(attended_low, out_mat), "tensor", scatter_dimension=0, tiled=True
    )
    normed_two, norm_two_back = jax.vjp(rms_norm, hidden_in, gain_mlp)
    normed_low_two = normed_two.astype(jnp.bfloat16)
    grad_out = cotangent.astype(jnp.float32)
    gathered_two = lax.all_gather(normed_low_two, "tensor", axis=0, tiled=True)
    activated, swiglu_back = jax.vjp(
        swiglu, product(gathered_two, gate_mat), product(gathered_two, up_mat)
    )
    act_low = activated.astype(jnp.bfloat16)
    layer_out = hidden_in + lax.psum_scatter(
        product(act_low, down_mat).astype(jnp.bfloat16), "tensor", scatter_dimension=0, tiled=True
    ).astype(jnp.float32)
    grad_rows = lax.all_gather(cotangent, "tensor", axis=0, tiled=True)
    grad_gate, grad_up = swiglu_back(outer(grad_rows, down_mat))
    gate_low = grad_gate.astype(jnp.bfloat16)
    up_low = grad_up.astype(jnp.bfloat16)
    grad_normed_two = lax.psum_scatter(
        outer(gate_low, gate_mat) + outer(up_low, up_mat), "tensor", scatter_dimension=0, tiled=True
    )
    grad_gate_mat = inner(gathered_two, gate_low)
    grad_up_mat = inner(gathered_two, up_low)
    grad_down_mat = inner(act_low, grad_rows)
    grad_hidden_two, grad_gain_two = norm_two_back(grad_normed_two)
    grad_hidden = grad_out + grad_hidden_two
    grad_branch = lax.all_gather(grad_hidden.astype(jnp.bfloat16), "tensor", axis=0, tiled=True)
    grad_attended = outer(grad_branch, out_mat).astype(jnp.bfloat16)
    grad_out_mat = inner(attended_low, grad_branch)
    grad_rot_query, grad_rot_key, grad_mixed = lax.map(
        backward_row,
        (
            heads(queries),
            heads(keys_low),
            heads(mixed_values),
            segment,
            heads(grad_attended),
            logsums,
        ),
    )
    grad_query_low = rotate_back(grad_rot_query.reshape(group, -1), cosine, sine).astype(
        jnp.bfloat16
    )
    grad_key_low = rotate_back(grad_rot_key.reshape(group, -1), cosine, sine).astype(jnp.bfloat16)
    grad_first = 0.5 * grad_mixed.reshape(group, -1)
    grad_value_low = grad_first.astype(jnp.bfloat16)
    grad_normed_one = lax.psum_scatter(
        outer(grad_query_low, query_mat)
        + outer(grad_key_low, key_mat)
        + outer(grad_value_low, value_mat),
        "tensor",
        scatter_dimension=0,
        tiled=True,
    )
    grad_query_mat = inner(gathered_one, grad_query_low)
    grad_key_mat = inner(gathered_one, grad_key_low)
    grad_value_mat = inner(gathered_one, grad_value_low)
    grad_inputs_one, grad_gain_one = norm_one_back(grad_normed_one)
    grad_tokens = grad_hidden + grad_inputs_one
    summed = (
        lax.psum_scatter(grad_query_mat, "dp", scatter_dimension=0, tiled=True),
        lax.psum_scatter(grad_key_mat, "dp", scatter_dimension=0, tiled=True),
        lax.psum_scatter(grad_value_mat, "dp", scatter_dimension=0, tiled=True),
        lax.psum_scatter(grad_out_mat, "dp", scatter_dimension=1, tiled=True),
        lax.psum_scatter(grad_gate_mat, "dp", scatter_dimension=0, tiled=True),
        lax.psum_scatter(grad_up_mat, "dp", scatter_dimension=0, tiled=True),
        lax.psum_scatter(grad_down_mat, "dp", scatter_dimension=1, tiled=True),
    )
    gain_sums = lax.psum((grad_gain_one, grad_gain_two), ("dp", "tensor"))
    return (
        layer_out.astype(jnp.bfloat16),
        grad_tokens,
        grad_first,
        summed[0],
        summed[1],
        summed[2],
        summed[3],
        summed[4],
        summed[5],
        summed[6],
        gain_sums[0],
        gain_sums[1],
    )


AXES = ("dp", "tensor")
MESH = pl.DeviceIdType.MESH
TILE = 256
NEG = -1e30
F32 = jnp.float32
BF16 = jnp.bfloat16


def flat(y, x, c, t):
    return ((y * 2 + x) * 2 + c) * 4 + t


def move(values, to):
    pairs = []
    for y in range(2):
        for x in range(2):
            for c in range(2):
                for t in range(4):
                    pair = (flat(y, x, c, t), flat(*to(y, x, c, t)))
                    if pair[0] != pair[1]:
                        pairs.append(pair)
    return lax.ppermute(values, AXES, pairs)


def across_x(values):
    return move(values, lambda y, x, c, t: (y, 1 - x, c, t))


def across_y(values):
    return move(values, lambda y, x, c, t: (1 - y, x, c, t))


def across_c(values):
    return move(values, lambda y, x, c, t: (y, x, 1 - c, t))


def along_t(values, step):
    return move(values, lambda y, x, c, t: (y, x, c, (t + step) % 4))


def swap_halves(values):
    return move(values, lambda y, x, c, t: (y, x, t % 2, (t // 2) * 2 + c))


def pack_kernel(wq, wk, wv, wo, wg, wu, wd, halves, small, big):
    small[0] = dot(wq[...], halves[...]).astype(BF16)
    small[1] = dot(wk[...], halves[...]).astype(BF16)
    small[2] = wv[...]
    small[3] = wo[...].T
    for n, units in enumerate((wg, wu, wd)):
        big[n] = units[...].reshape(big.shape[1:])


def pack(wq, wk, wv, wo, wg, wu, wd):
    wg, wu = wg.T, wu.T
    part, rows = wg.shape
    lane = jnp.arange(256, dtype=jnp.int32)
    source = ((lane & 127) >> 5) * 64 + (lane >> 7) * 32 + (lane & 31)
    halves = (lane[:, None] == source[None, :]).astype(BF16)
    return pl.pallas_call(
        pack_kernel,
        out_shape=[
            jax.ShapeDtypeStruct((4, rows, 256), BF16),
            jax.ShapeDtypeStruct((3, 2, part // 2, rows), BF16),
        ],
        compiler_params=params(),
        name="pack",
    )(wq, wk, wv, wo, wg, wu, wd, halves)


def meet(plane, c, t, dpx, dpy):
    barrier = pltpu.get_barrier_semaphore()
    for e in range(2):
        for d in range(4):
            if e or d:
                other = plane + lax.rem(c + e, 2)
                pl.semaphore_signal(barrier, inc=1, device_id=(other, lax.rem(t + d, 4)), device_id_type=MESH)
    pl.semaphore_signal(barrier, inc=1, device_id=(dpx, t), device_id_type=MESH)
    pl.semaphore_signal(barrier, inc=1, device_id=(dpy, t), device_id_type=MESH)
    pl.semaphore_wait(barrier, 9)


def gather_kernel(
    ends, tok, fv, small, big, gain, freqs, row_out, g_small, g_big, normed_out, q_out, k_out, v_out, cos_out, sin_out,
    row, first, w_s, n_s, q_s, k_s, v_s, raw_s, cos_s, sin_s,
    send, recv, relay_send, along_recv, next_send, next_recv, swap, fsend, frecv, here, tile_sem, end_sem,
):
    dp, t = lax.axis_index("dp"), lax.axis_index("tensor")
    c, x, y = lax.rem(dp, 2), lax.rem(lax.div(dp, 2), 2), lax.div(dp, 4)
    pair, side = lax.div(t, 2), lax.rem(t, 2)
    plane = dp - c
    dpx, dpy, dpc = dp + 2 - 4 * x, dp + 4 - 8 * y, dp + 1 - 2 * c
    dpxy = dpx + 4 - 8 * y

    meet(plane, c, t, dpx, dpy)
    def slot(k, at, owner, h):
        if k == 0:
            return g_small.at[pl.ds(2 * h, 2), at, pl.ds(owner * 128, 128), :]
        return g_big.at[k - 1, owner, h, at]

    def column(k, owner, h):
        if k == 0:
            return g_small.at[pl.ds(2 * h, 2), :, pl.ds(owner * 128, 128), :]
        return g_big.at[k - 1, owner, h]

    def both(k, at, owner):
        if k == 0:
            return g_small.at[:, at, pl.ds(owner * 128, 128), :]
        return g_big.at[k - 1, owner, :, at]

    def all_of(k, owner):
        if k == 0:
            return g_small.at[:, :, pl.ds(owner * 128, 128), :]
        return g_big.at[k - 1, owner]

    def shard(k):
        return small if k == 0 else big.at[k - 1]

    def part_of(k, h):
        return small.at[pl.ds(2 * h, 2)] if k == 0 else big.at[k - 1, h]

    def copy(k, n, src, dst, to, at):
        return pltpu.make_async_remote_copy(
            src_ref=src,
            dst_ref=dst,
            send_sem=send.at[k, n],
            recv_sem=recv.at[k, n],
            device_id=(to, at),
            device_id_type=MESH,
        )

    chunks = 4
    near, far = (dpx, dpy), (dpy, dpx)
    kept = [pltpu.make_async_copy(shard(k), both(k, t, dp), here.at[k]) for k in range(chunks)]

    def relay(k, at, side, src):
        return pltpu.make_async_remote_copy(
            src_ref=src,
            dst_ref=both(k, at, dp),
            send_sem=relay_send.at[k, at, side],
            recv_sem=along_recv.at[k, at],
            device_id=(dp, t + 2 * side - 1),
            device_id_type=MESH,
        )

    def onward(k, at, h, src):
        return pltpu.make_async_remote_copy(
            src_ref=src,
            dst_ref=slot(k, at, dp, h),
            send_sem=next_send.at[k, at, h],
            recv_sem=next_recv.at[k, at, h],
            device_id=(near[h], t),
            device_id_type=MESH,
        )

    def start_along(k):
        @pl.when(t < 3)
        def _():
            relay(k, t, 1, shard(k)).start()

        @pl.when(t > 0)
        def _():
            relay(k, t, 0, shard(k)).start()

    def pass_along(k, level):
        for side, at in ((1, t - level), (0, t + level)):

            @pl.when((at >= 0) & (at < 4))
            def _():
                block = both(k, at, dp)
                move = relay(k, at, side, block)
                move.wait_recv()

                @pl.when((t < 3) if side else (t > 0))
                def _():
                    move.start()

                for h in range(2):
                    onward(k, at, h, slot(k, at, dp, h)).start()

    def end_along(k):
        for level in range(4):
            for side, at in ((1, t - level), (0, t + level)):

                @pl.when((at >= 0) & (at < 4) & ((t < 3) if side else (t > 0)))
                def _():
                    relay(k, at, side, both(k, at, dp)).wait_send()

    across = [
        [
            copy(k, 2 * h + i, column(k, owner, h), column(k, owner, h), far[h], t)
            for h in range(2)
            for i, owner in enumerate((dp, near[h]))
        ]
        for k in range(chunks)
    ]
    over = [
        [copy(k, 4 + i, all_of(k, owner), all_of(k, owner), dpc, t) for i, owner in enumerate((dp, dpx, dpy, dpxy))]
        for k in range(chunks)
    ]

    order = (1, 0, 2, 3)
    start_along(order[0])
    for item in kept:
        item.start()
    for k in order:
        for h in range(2):
            onward(k, t, h, part_of(k, h)).start()
        if k == order[0]:
            start_along(order[1])

    moved = side != c
    to_own = pltpu.make_async_copy(tok, row.at[c], here.at[4])
    swapped = pltpu.make_async_remote_copy(
        src_ref=tok,
        dst_ref=row.at[side],
        send_sem=swap.at[0],
        recv_sem=swap.at[1],
        device_id=(plane + side, 2 * pair + c),
        device_id_type=MESH,
    )

    def start_tokens():
        @pl.when(moved)
        def _():
            swapped.start()

        @pl.when(jnp.logical_not(moved))
        def _():
            to_own.start()

    heads_core, slab = pair, side

    def first_copy(p):
        return pltpu.make_async_remote_copy(
            src_ref=fv.at[pl.ds(p * SEQ, SEQ), :],
            dst_ref=first.at[slab],
            send_sem=fsend.at[p],
            recv_sem=frecv.at[slab],
            device_id=(plane + heads_core, 2 * p + c),
            device_id_type=MESH,
        )

    def first_local(p):
        return pltpu.make_async_copy(fv.at[pl.ds(p * SEQ, SEQ), :], first.at[slab], here.at[5])

    stays = [(heads_core == c) & (t == 2 * p + c) for p in range(2)]

    def start_first():
        for p in range(2):

            @pl.when(stays[p])
            def _():
                first_local(p).start()

            @pl.when(jnp.logical_not(stays[p]))
            def _():
                first_copy(p).start()

    def pass_over(k):
        for item in across[k]:
            item.wait_recv()
        for item in over[k][1:]:
            item.start()

    def pass_next(k):
        for at in range(4):
            for h in range(2):
                onward(k, at, h, slot(k, at, dp, h)).wait_recv()
        for item in across[k]:
            item.start()

    def table(i, carry):
        rows = pl.ds(pl.multiple_of(i * TILE, TILE), TILE)
        at_row = lax.broadcasted_iota(jnp.int32, (TILE, 128), 0) + i * TILE
        begin = jnp.zeros_like(at_row)
        for k in range(DOCS):
            begin = jnp.maximum(begin, jnp.where(at_row >= ends[k], ends[k], 0))
        angles = (at_row - begin).astype(F32) * freqs[...]
        cos_s[rows, :] = jnp.cos(angles)
        sin_s[rows, :] = jnp.sin(angles)
        return carry

    lax.fori_loop(0, SEQ // TILE, table, 0)
    tables = [pltpu.make_async_copy(cos_s, cos_out, end_sem.at[0]), pltpu.make_async_copy(sin_s, sin_out, end_sem.at[1])]

    for i, k in enumerate(order):
        pass_along(k, 1)
        if i + 2 < chunks:
            start_along(order[i + 2])
        if i:
            pass_next(order[i - 1])
        pass_along(k, 2)
        pass_along(k, 3)
        kept[k].wait()
        over[k][0].start()
        if i == 2:
            start_tokens()
        if i == 3:
            start_first()
        if i >= 2:
            pass_over(order[i - 2])
    pass_next(order[3])
    for item in tables:
        item.start()
    for item in over[0]:
        item.wait_recv()
    load_w = pltpu.make_async_copy(g_small.at[pl.ds(0, 3), pl.ds(2 * c, 2)], w_s, end_sem.at[2])
    load_w.start()

    @pl.when(moved)
    def _():
        swapped.wait_send()
        swapped.wait_recv()

    @pl.when(jnp.logical_not(moved))
    def _():
        to_own.wait()

    given = pltpu.make_async_remote_copy(
        src_ref=row.at[c],
        dst_ref=row.at[c],
        send_sem=swap.at[2],
        recv_sem=swap.at[3],
        device_id=(dpc, t),
        device_id_type=MESH,
    )
    given.start()
    load_w.wait()

    def rows_of(half, n):
        return pl.ds(pl.multiple_of(half * (SEQ // 2) + n * 512, 512), 512)

    def done_copies(half, n):
        rows = rows_of(half, n)
        return [
            pltpu.make_async_copy(src.at[rows, :], dst.at[rows, :], tile_sem.at[2 * half + n, m])
            for m, (src, dst) in enumerate(((n_s, normed_out), (q_s, q_out), (k_s, k_out)))
        ]

    def project(half, n):
        rows = rows_of(half, n)
        values = row[half, pl.ds(pl.multiple_of(n * 512, 512), 512), :].astype(F32)
        factor = lax.rsqrt(jnp.mean(values * values, axis=1, keepdims=True) + EPSILON)
        normed = (values * factor * gain[...]).astype(BF16)
        n_s[rows, :] = normed
        cos, sin = cos_s[rows, :], sin_s[rows, :]
        for u in range(2):
            for m, out, scale in ((0, q_s, 0.125), (1, k_s, 1.0)):
                raw = dot(normed, w_s[m, u])
                a, b = raw[:, :128], raw[:, 128:]
                out[rows, u * 256 : u * 256 + 128] = ((a * cos - b * sin) * scale).astype(BF16)
                out[rows, u * 256 + 128 : u * 256 + 256] = ((b * cos + a * sin) * scale).astype(BF16)
            raw_s[rows, u * 256 : u * 256 + 256] = 0.5 * dot(normed, w_s[2, u])
        for item in done_copies(half, n):
            item.start()
        return 0

    row_copy = pltpu.make_async_copy(row, row_out, end_sem.at[3])

    def half_row(i, carry):
        @pl.when(i == 1)
        def _():
            pass_over(order[2])
            given.wait_recv()
            row_copy.start()

        half = c + i - 2 * c * i
        lax.fori_loop(0, 2, lambda n, _: project(half, n), 0)
        return carry

    lax.fori_loop(0, 2, half_row, 0)
    pass_over(order[3])

    for p in range(2):

        @pl.when(stays[p])
        def _():
            first_local(p).wait()

        @pl.when(jnp.logical_not(stays[p]))
        def _():
            first_copy(p).wait_send()

    for u in range(2):
        came = pltpu.make_async_remote_copy(
            src_ref=first.at[u],
            dst_ref=first.at[u],
            send_sem=fsend.at[u],
            recv_sem=frecv.at[u],
            device_id=(dpc, t),
            device_id_type=MESH,
        )

        @pl.when((side != c) | (t != 2 * c + u))
        def _():
            came.wait_recv()

    def mixed_copy(n):
        rows = pl.ds(pl.multiple_of(n * 512, 512), 512)
        return rows, pltpu.make_async_copy(v_s.at[rows, :], v_out.at[rows, :], tile_sem.at[n, 3])

    def mix(n, carry):
        rows, item = mixed_copy(n)
        for u in range(2):
            lanes = slice(u * 256, u * 256 + 256)
            v_s[rows, lanes] = (raw_s[rows, lanes] + 0.5 * first[u, rows, :].astype(F32)).astype(BF16)
        item.start()
        return carry

    lax.fori_loop(0, 4, mix, 0)
    outs = []
    for n in range(4):
        outs += done_copies(n // 2, n % 2) + [mixed_copy(n)[1]]
    given.wait_send()
    for k in range(chunks):
        if k:
            for item in over[k]:
                item.wait_recv()
        end_along(k)
        for item in across[k] + over[k]:
            item.wait_send()
        for at in range(4):
            for h in range(2):
                onward(k, at, h, slot(k, at, dp, h)).wait_send()
    for item in outs + tables + [row_copy]:
        item.wait()


def gather(ends, tok, fv, small, big, gain, freqs):
    part, rows = big.shape[2:]
    wide = tok.shape[1]
    vmem = pl.BlockSpec(memory_space=pltpu.VMEM)
    sems = pltpu.SemaphoreType.DMA
    low = lambda *shape: pltpu.VMEM(shape, BF16)
    shapes = [(2, SEQ // 2, wide), (4, 4, wide, 256), (3, 8, 2, 4, part, rows), (SEQ, wide)] + [(SEQ, 512)] * 3
    return pl.pallas_call(
        gather_kernel,
        out_shape=[jax.ShapeDtypeStruct(shape, BF16) for shape in shapes]
        + [jax.ShapeDtypeStruct((SEQ, 128), F32)] * 2,
        in_specs=[pl.BlockSpec(memory_space=pltpu.SMEM)] + [vmem] * 6,
        out_specs=[any_spec()] * 9,
        scratch_shapes=[low(2, SEQ // 2, wide), low(2, SEQ, 256), low(3, 2, wide, 256), low(SEQ, wide)]
        + [low(SEQ, 512)] * 3
        + [pltpu.VMEM((SEQ, 512), F32)]
        + [pltpu.VMEM((SEQ, 128), F32)] * 2
        + [
            sems((4, 8)),
            sems((4, 8)),
            sems((4, 4, 2)),
            sems((4, 4)),
            sems((4, 4, 2)),
            sems((4, 4, 2)),
            sems((4,)),
            sems((2,)),
            sems((2,)),
            sems((6,)),
            sems((4, 4)),
            sems((4,)),
        ],
        compiler_params=params(collective_id=0, has_side_effects=True),
        name="gather",
    )(ends, tok, fv, small, big, gain, freqs)


def dot(left, right):
    return jnp.dot(left, right, preferred_element_type=F32)


def dot_nt(left, right):
    return lax.dot_general(left, right, (((1,), (1,)), ((), ())), preferred_element_type=F32)


def dot_tn(left, right):
    return lax.dot_general(left, right, (((0,), (0,)), ((), ())), preferred_element_type=F32)


def any_spec():
    return pl.BlockSpec(memory_space=pl.ANY)


def params(**more):
    return pltpu.CompilerParams(vmem_limit_bytes=62 * 1024 * 1024, **more)


def cost(flops, size, exps=0):
    return pl.CostEstimate(flops=int(flops), bytes_accessed=int(size), transcendentals=int(exps))


def once(shape, place):
    return pl.BlockSpec(shape, place, pipeline_mode=pl.Buffered(1))


def head_masks(rows):
    lane = lax.broadcasted_iota(jnp.int32, (rows, 256), 1)
    return (lane & 127) >> 5, lane >> 6


def attend_kernel(at, bounds, q_ref, k_ref, v_ref, starts, own_ref, send_ref, lse_ref, kept, turned, acc):
    tiles = SEQ // TILE
    of_qk, _ = head_masks(TILE)
    row = lax.broadcasted_iota(jnp.int32, (TILE, TILE), 0)
    lane = lax.broadcasted_iota(jnp.int32, (TILE, TILE), 1)
    slabs = [slice(0, 256), slice(256, 512)]

    def turn_values(j, carry):
        there = pl.ds(pl.multiple_of(j * TILE, TILE), TILE)
        turned[j] = v_ref[there, :].T
        return carry

    lax.fori_loop(0, tiles, turn_values, 0)

    def eighths(values, reduce):
        return reduce(values.reshape(TILE // 8, 8, 4 * TILE), axis=0)

    def query_tile(i, carry):
        here = pl.ds(pl.multiple_of(i * TILE, TILE), TILE)
        q4 = []
        for slab in slabs:
            q = q_ref[here, slab]
            zero = jnp.zeros_like(q)
            q4.append(jnp.concatenate([jnp.where(of_qk == h, q, zero) for h in range(4)], axis=0))
        low = bounds[i]
        begin = starts[pl.ds(i, 1), :]
        limit = lane + i * TILE

        def score(j, tops):
            there = pl.ds(pl.multiple_of(j * TILE, TILE), TILE)
            at_row = row + j * TILE
            ok = (at_row >= begin) & (at_row <= limit)
            ok = jnp.concatenate([ok] * 4, axis=1)
            new = []
            for u, slab in enumerate(slabs):
                s = jnp.where(ok, dot_nt(k_ref[there, slab], q4[u]), NEG)
                kept[j - low, u] = s
                new.append(jnp.maximum(tops[u], eighths(s, jnp.max)))
            return tuple(new)

        start = jnp.full((8, 4 * TILE), NEG, F32)
        tops = lax.fori_loop(low, i + 1, score, (start, start))
        tops = [jnp.max(top, axis=0, keepdims=True) for top in tops]
        acc[...] = jnp.zeros_like(acc)

        def weigh(j, totals):
            new = []
            for u in range(2):
                e = jnp.exp(kept[j - low, u] - tops[u])
                p = e.astype(BF16)
                for h in range(4):
                    part = slice(u * 256 + h * 64, u * 256 + h * 64 + 64)
                    acc[part] += dot(turned[j, part, :], p[:, h * TILE : (h + 1) * TILE])
                new.append(totals[u] + eighths(e, jnp.sum))
            return tuple(new)

        zero = jnp.zeros((8, 4 * TILE), F32)
        totals = lax.fori_loop(low, i + 1, weigh, (zero, zero))
        for u, slab in enumerate(slabs):
            total = jnp.sum(totals[u], axis=0, keepdims=True)
            inverse = 1.0 / total
            scaled = [
                acc[u * 256 + h * 64 : u * 256 + h * 64 + 64] * inverse[:, h * TILE : (h + 1) * TILE] for h in range(4)
            ]
            done = jnp.concatenate(scaled, axis=0).T.astype(BF16)
            local = pl.ds(pl.multiple_of(lax.rem(i, tiles // 2) * TILE, TILE), TILE)
            mine = lax.div(i, tiles // 2) == (at[0] & 1)

            @pl.when(mine)
            def _():
                own_ref[local, slab] = done

            @pl.when(jnp.logical_not(mine))
            def _():
                send_ref[local, slab] = done

            lse_ref[u, pl.ds(i, 1), :] = tops[u] + jnp.log(total)
        return carry

    lax.fori_loop(0, tiles, query_tile, 0)


def attend(at, bounds, q, k, v, starts):
    tiles = SEQ // TILE
    vmem = pl.BlockSpec(memory_space=pltpu.VMEM)
    return pl.pallas_call(
        attend_kernel,
        out_shape=[
            jax.ShapeDtypeStruct((SEQ // 2, 512), BF16),
            jax.ShapeDtypeStruct((SEQ // 2, 512), BF16),
            jax.ShapeDtypeStruct((2, tiles, 4 * TILE), F32),
        ],
        in_specs=[pl.BlockSpec(memory_space=pltpu.SMEM)] * 2 + [vmem] * 4,
        out_specs=[vmem] * 3,
        scratch_shapes=[
            pltpu.VMEM((tiles, 2, TILE, 4 * TILE), F32),
            pltpu.VMEM((tiles, 512, TILE), BF16),
            pltpu.VMEM((512, TILE), F32),
        ],
        compiler_params=params(),
        cost_estimate=cost(20e9, 12e6, 1e7),
        name="attend",
    )(at, bounds, q, k, v, starts)


def attend_back_kernel(
    at, bounds, q_hbm, k_hbm, v_hbm, do_own, do_other, o_own, o_other, lse_ref, starts, cosine, sine, *rest, part,
):
    if part:
        held_hbm, rest = rest[0], rest[1:]
        dq_hbm, dk_hbm, dv_hbm = rest[:3]
        rest = rest[3:]
    else:
        dq_hbm, dk_hbm, dv_hbm, held_hbm = rest[:4]
        rest = rest[4:]
    attend_back_part(
        at, bounds, q_hbm, k_hbm, v_hbm, do_own, do_other, o_own, o_other, lse_ref, starts, cosine, sine, held_hbm, dq_hbm, dk_hbm,
        dv_hbm, *rest, part=part
    )


def attend_back_part(
    at, bounds, q_hbm, k_hbm, v_hbm, do_own, do_other, o_own, o_other, lse_ref, starts, cosine, sine, held_hbm, dq_hbm, dk_hbm, dv_hbm,
    q_ref, k_ref, v_ref, do_ref, o_ref, dq_ref, dk_ref, dv_ref, dq_acc, delta, dk_acc, dv_acc, load, store, *, part,
):
    tiles = SEQ // TILE
    of_qk, of_v = head_masks(TILE)
    row = lax.broadcasted_iota(jnp.int32, (TILE, TILE), 0)
    lane = lax.broadcasted_iota(jnp.int32, (TILE, TILE), 1)
    slabs = [slice(0, 256), slice(256, 512)]
    pick = (lax.broadcasted_iota(jnp.int32, (8, 256), 1) >> 6) == lax.broadcasted_iota(
        jnp.int32, (8, 256), 0
    )
    pick = pick.astype(F32)
    half = SEQ // 2
    low = pl.multiple_of((at[0] & 1) * half, half)
    mine, others = pl.ds(low, half), pl.ds(half - low, half)
    first_half, second_half = pl.ds(0, half), pl.ds(half, half)
    mine_second = (at[0] & 1) == 1
    here_half = second_half if part else first_half
    q_rows = second_half if part else pl.ds(0, SEQ)
    plain = [
        (q_hbm.at[q_rows, :], q_ref.at[q_rows, :]),
        (k_hbm.at[here_half, :], k_ref.at[here_half, :]),
        (v_hbm.at[here_half, :], v_ref.at[here_half, :]),
    ]
    if part:
        plain.append((held_hbm, dq_acc.at[pl.ds(tiles // 2, tiles // 2)]))
    loads = [pltpu.make_async_copy(src, dst, load.at[4 + n]) for n, (src, dst) in enumerate(plain)]

    def half_loads(own, other, dst, n):
        pairs = [(own, mine, mine_second), (other, others, jnp.logical_not(mine_second))]
        for e, (src, rows, wanted) in enumerate(pairs):
            yield pltpu.make_async_copy(src, dst.at[rows, :], load.at[n + e]), wanted

    parts = list(half_loads(do_own, do_other, do_ref, 0)) + list(half_loads(o_own, o_other, o_ref, 2))

    def each(action):
        for item, wanted in parts:
            if part:
                pl.when(wanted)(functools.partial(action, item))
            else:
                action(item)

    each(lambda item: item.start())
    for item in loads:
        item.start()
    if not part:
        dq_acc[...] = jnp.zeros_like(dq_acc)
    each(lambda item: item.wait())

    def prepare(i, carry):
        here = pl.ds(pl.multiple_of(i * TILE, TILE), TILE)
        for u, slab in enumerate(slabs):
            both = do_ref[here, slab].astype(F32) * o_ref[here, slab].astype(F32)
            sums = lax.dot_general(
                pick, both, (((1,), (1,)), ((), ())), precision=lax.Precision.HIGHEST, preferred_element_type=F32
            )
            for h in range(4):
                delta[u, pl.ds(i, 1), h * TILE : (h + 1) * TILE] = sums[h : h + 1]
        return carry

    middle = tiles // 2
    lax.fori_loop(middle * part, tiles, prepare, 0)
    for item in loads:
        item.wait()

    def rotate_out(values, here, out, low, scale):
        a, b = values[:, :128], values[:, 128:]
        cos, sin = cosine[here, :], sine[here, :]
        out[here, low : low + 128] = ((a * cos + b * sin) * scale).astype(BF16)
        out[here, low + 128 : low + 256] = ((b * cos - a * sin) * scale).astype(BF16)

    def split(values, of):
        zero = jnp.zeros_like(values)
        return jnp.concatenate([jnp.where(of == h, values, zero) for h in range(4)], axis=0)

    def key_tile(j, carry):
        there = pl.ds(pl.multiple_of(j * TILE, TILE), TILE)
        at_row = row + j * TILE
        dk_acc[...] = jnp.zeros_like(dk_acc)
        dv_acc[...] = jnp.zeros_like(dv_acc)

        def query_tile(i, carry):
            here = pl.ds(pl.multiple_of(i * TILE, TILE), TILE)
            at_lane = lane + i * TILE
            ok = (at_row >= starts[pl.ds(i, 1), :]) & (at_row <= at_lane)
            ok = jnp.concatenate([ok] * 4, axis=1)
            for u, slab in enumerate(slabs):
                q4 = split(q_ref[here, slab], of_qk)
                do4 = split(do_ref[here, slab], of_v)
                s = dot_nt(k_ref[there, slab], q4)
                dp = dot_nt(v_ref[there, slab], do4)
                p = jnp.exp(jnp.where(ok, s - lse_ref[u, pl.ds(i, 1), :], NEG))
                ds = (p * (dp - delta[u, pl.ds(i, 1), :])).astype(BF16)
                dv_acc[u] += dot(p.astype(BF16), do4)
                dk_acc[u] += dot(ds, q4)
                ds4 = jnp.concatenate([ds[:, h * TILE : (h + 1) * TILE] for h in range(4)], axis=0)
                dq_acc[i, u] += dot_tn(ds4, split(k_ref[there, slab], of_qk))
            return carry

        lax.fori_loop(j, bounds[tiles + j] + 1, query_tile, 0)
        for u, slab in enumerate(slabs):
            rotate_out(dk_acc[u], there, dk_ref, u * 256, 1.0)
            dv_ref[there, slab] = (0.5 * dv_acc[u]).astype(BF16)
        local = pl.ds(pl.multiple_of((j - middle * part) * TILE, TILE), TILE)
        pltpu.make_async_copy(dk_ref.at[there, :], dk_hbm.at[local, :], store.at[0]).start()
        pltpu.make_async_copy(dv_ref.at[there, :], dv_hbm.at[local, :], store.at[1]).start()
        return carry

    lax.fori_loop(middle * part, middle * part + middle, key_tile, 0)
    if not part:
        held = pltpu.make_async_copy(dq_acc.at[pl.ds(middle, middle)], held_hbm, store.at[3])
        held.start()

    def finish_tile(i, carry):
        here = pl.ds(pl.multiple_of(i * TILE, TILE), TILE)
        for u in range(2):
            rotate_out(dq_acc[i, u], here, dq_ref, u * 256, 0.125)
        local = pl.ds(pl.multiple_of((i - middle * part) * TILE, TILE), TILE)
        pltpu.make_async_copy(dq_ref.at[here, :], dq_hbm.at[local, :], store.at[2]).start()
        return carry

    lax.fori_loop(middle * part, middle * part + middle, finish_tile, 0)
    for n, (src, dst) in enumerate(((dk_ref, dk_hbm), (dv_ref, dv_hbm), (dq_ref, dq_hbm))):
        pltpu.make_async_copy(src.at[here_half, :], dst, store.at[n]).wait()
    if not part:
        held.wait()


def attend_back(part, at, bounds, q, k, v, do_own, do_other, o_own, o_other, lse, starts, cosine, sine, *held):
    tiles = SEQ // TILE
    vmem = pl.BlockSpec(memory_space=pltpu.VMEM)
    sems = pltpu.SemaphoreType.DMA
    outs = [jax.ShapeDtypeStruct((SEQ // 2, 512), BF16)] * 3
    if not part:
        outs.append(jax.ShapeDtypeStruct((tiles // 2, 2, TILE, 256), F32))
    return pl.pallas_call(
        functools.partial(attend_back_kernel, part=part),
        out_shape=outs,
        in_specs=[pl.BlockSpec(memory_space=pltpu.SMEM)] * 2 + [any_spec()] * 7 + [vmem] * 4 + [any_spec()] * len(held),
        out_specs=[any_spec()] * len(outs),
        scratch_shapes=[pltpu.VMEM((SEQ, 512), BF16)] * 8
        + [
            pltpu.VMEM((tiles, 2, TILE, 256), F32),
            pltpu.VMEM((2, tiles, 4 * TILE), F32),
            pltpu.VMEM((2, TILE, 256), F32),
            pltpu.VMEM((2, TILE, 256), F32),
            sems((8,)),
            sems((4,)),
        ],
        compiler_params=params(),
        cost_estimate=cost(25e9, 12e6, 5e6),
        name="attend_back",
    )(at, bounds, q, k, v, do_own, do_other, o_own, o_other, lse, starts, cosine, sine, *held)


def mlp_kernel(at, att_own, att_other, tok, cot_here, cot_moved, gain, wo, big, *rest):
    (out, gh_out, gb_out, n2_out, hid_out, ga_own, ga_other, gg_out, cot_out) = rest[:9]
    (wg, wu, wd, down, back, sems) = rest[9:]
    step = pl.program_id(0)
    c = at[0] & 1

    @pl.when(step == 0)
    def _():
        for n, held in enumerate((wg, wu, wd)):
            for owner in range(8):
                pltpu.make_async_copy(
                    big.at[n, owner], held.at[:, owner * 128 : owner * 128 + 128], sems.at[n]
                ).start()
        gg_out[...] = jnp.zeros_like(gg_out)

    hidden = tok[0].astype(F32)
    for e, att in enumerate((att_own, att_other)):
        for u in range(2):
            hidden += dot_nt(att[:, u * 256 : u * 256 + 256], wo[0, 2 * (c ^ e) + u])
    factor = lax.rsqrt(jnp.mean(hidden * hidden, axis=1, keepdims=True) + EPSILON)
    gains = gain[...]
    normed = (hidden * factor * gains).astype(BF16)
    n2_out[...] = normed.T
    g = jnp.where((at[1] & 1) == c, cot_here[...], cot_moved[...])
    cot_out[...] = g.T

    @pl.when(step == 0)
    def _():
        for n, held in enumerate((wg, wu, wd)):
            pltpu.make_async_copy(held, held, sems.at[n]).wait()

    down[...] = hidden
    back[...] = jnp.zeros_like(back)
    units, block = wg.shape[0], 768

    def unit_block(low, width):
        part = pl.ds(low, width)
        gate, up, grad_act = dot_nt(normed, wg[part, :]), dot_nt(normed, wu[part, :]), dot_nt(g, wd[part, :])
        sig = 1.0 / (1.0 + jnp.exp(-gate))
        silu = gate * sig
        act = (silu * up).astype(BF16)
        grad_up = (grad_act * silu).astype(BF16)
        grad_gate = (grad_act * up * (sig * (1.0 + gate * (1.0 - sig)))).astype(BF16)
        hid_out[0, :, part], hid_out[1, :, part], hid_out[2, :, part] = grad_gate, grad_up, act
        down[...] += dot(act, wd[part, :])
        back[...] += dot(grad_gate, wg[part, :]) + dot(grad_up, wu[part, :])

    def whole_block(k, carry):
        unit_block(pl.multiple_of(k * block, block), block)
        return carry

    lax.fori_loop(0, units // block, whole_block, 0)
    if units % block:
        unit_block(units - units % block, units % block)
    grad = back[...]
    out[...] = down[...].astype(BF16)
    gg_out[...] += jnp.sum((grad * hidden * factor).reshape(-1, 8, grad.shape[1]), axis=0)
    scaled = grad * gains
    mean = jnp.mean(scaled * hidden, axis=1, keepdims=True)
    grad_hidden = g.astype(F32) + factor * scaled - hidden * (factor * factor * factor * mean)
    gh_out[...] = grad_hidden
    branch = grad_hidden.astype(BF16)
    gb_out[...] = branch.T
    for e, ga in enumerate((ga_own, ga_other)):
        for u in range(2):
            ga[:, u * 256 : u * 256 + 256] = dot(branch, wo[0, 2 * (c ^ e) + u]).astype(BF16)


def mlp(at, att_own, att_other, tok, cot_here, cot_moved, gain, small, big):
    _, count, wide = tok.shape
    big = big.reshape(3, 8, -1, 128)
    rows, units = 256, big.shape[2]
    row = lambda width: pl.BlockSpec((rows, width), lambda i, at: (i, 0))
    turned = pl.BlockSpec((wide, rows), lambda i, at: (0, i))
    grid = pltpu.PrefetchScalarGridSpec(
        num_scalar_prefetch=1,
        grid=(count // rows,),
        in_specs=[
            row(512),
            row(512),
            pl.BlockSpec((1, rows, wide), lambda i, at: (at[0] & 1, i, 0)),
            row(wide),
            row(wide),
            pl.BlockSpec((1, wide), lambda i, at: (0, 0)),
            once((1, 4, wide, 256), lambda i, at: (3, 0, 0, 0)),
            any_spec(),
        ],
        out_specs=[
            row(wide),
            row(wide),
            turned,
            turned,
            pl.BlockSpec((3, rows, units), lambda i, at: (0, i, 0)),
            row(512),
            row(512),
            pl.BlockSpec((8, wide), lambda i, at: (0, 0)),
            turned,
        ],
        scratch_shapes=[pltpu.VMEM((units, wide), BF16)] * 3
        + [pltpu.VMEM((rows, wide), F32)] * 2
        + [pltpu.SemaphoreType.DMA((3,))],
    )
    tokens = lambda width, kind=BF16: jax.ShapeDtypeStruct((count, width), kind)
    return pl.pallas_call(
        mlp_kernel,
        out_shape=[
            tokens(wide),
            tokens(wide, F32),
            jax.ShapeDtypeStruct((wide, count), BF16),
            jax.ShapeDtypeStruct((wide, count), BF16),
            jax.ShapeDtypeStruct((3, count, units), BF16),
            tokens(512),
            tokens(512),
            jax.ShapeDtypeStruct((8, wide), F32),
            jax.ShapeDtypeStruct((wide, count), BF16),
        ],
        grid_spec=grid,
        compiler_params=params(),
        cost_estimate=cost(2 * count * wide * (6 * units + 2 * wide), 60e6, 3e6),
        name="mlp",
    )(at, att_own, att_other, tok, cot_here, cot_moved, gain, small, big)


def turn_rows(source, plane, parity, held):
    for rel in range(4):
        block = ((plane ^ rel) * 2 + parity) * 128
        held[rel * 128 : rel * 128 + 128, :] = source[:, pl.ds(pl.multiple_of(block, 128), 128)].T


def place_first(send, keep, done, lanes):
    for yr in range(2):
        keep[yr, :, lanes] = done[2 * yr]
        send[yr, :, lanes] = done[2 * yr + 1]


def place_second(send, keep, done, lanes):
    for xr in range(2):
        keep[xr, :, lanes] = done[xr]
        send[xr, :, lanes] = done[2 + xr]


def weights_kernel(
    n2, g_hbm, branch_hbm, hid, own_hbm, other_hbm, send1_out, keep1_out, send2_out, keep2_out,
    turned, g, branch, own, other, send1, keep1, send2, keep2, given, got, out_sem, in_sem, load, store,
):
    step = pl.program_id(0)
    dp, t = lax.axis_index("dp"), lax.axis_index("tensor")
    c = lax.rem(dp, 2)
    plane = lax.div(dp, 2)
    units = hid.shape[2] // 2
    loads = [
        pltpu.make_async_copy(src, dst, load.at[m])
        for m, (src, dst) in enumerate(((g_hbm, g), (branch_hbm, branch), (own_hbm, own), (other_hbm, other)))
    ]

    @pl.when(step == 0)
    def _():
        for item in loads:
            item.start()
        barrier = pltpu.get_barrier_semaphore()
        pl.semaphore_signal(barrier, inc=1, device_id=(dp + 1 - 2 * c, t), device_id_type=MESH)
        pl.semaphore_wait(barrier, 1)

    @pl.when(step == 2)
    def _():
        for item in loads:
            item.wait()

    def lanes_of(k):
        return pl.ds(k * units, units if k < 3 else 512)

    def exchange(k):
        return pltpu.make_async_remote_copy(
            src_ref=given.at[:, :, :, lanes_of(k)],
            dst_ref=got.at[:, :, :, lanes_of(k)],
            send_sem=out_sem.at[k],
            recv_sem=in_sem.at[k],
            device_id=(dp + 1 - 2 * c, t),
            device_id_type=MESH,
        )

    def stores(k):
        arrays = ((send1, send1_out), (keep1, keep1_out), (send2, send2_out), (keep2, keep2_out))
        return [
            pltpu.make_async_copy(src.at[:, :, lanes_of(k)], dst.at[:, :, lanes_of(k)], store.at[m, k])
            for m, (src, dst) in enumerate(arrays)
        ]

    def turn(source):
        x = lax.rem(plane, 2)
        y = lax.div(plane, 2)
        for e, parity in enumerate((1 - c, c)):
            for rel in range(4):
                yy, xx = (y, 1 - y)[rel // 2], (x, 1 - x)[rel % 2]
                block = pl.multiple_of((yy * 4 + xx * 2 + parity) * 128, 128)
                low = e * 512 + rel * 128
                turned[low : low + 128, :] = source[pl.ds(block, 128), :]

    for at_step, source in ((0, n2), (2, g), (3, branch)):

        @pl.when(step == at_step)
        def _():
            turn(source)

    places = ((place_first, send1, keep1), (place_second, send2, keep2))

    def take(product, h, lanes):
        rows = product.astype(BF16)
        given[:, h, :, lanes] = rows[:512].reshape(4, 128, rows.shape[1])
        for e, (place, send, keep) in enumerate(places):

            @pl.when(h == e)
            def _():
                place(send, keep, [rows[512 + r * 128 : 640 + r * 128] for r in range(4)], lanes)

    def add_got(lanes):
        for yr in range(2):
            keep1[yr, :, lanes] = add(keep1[yr, :, lanes], got[2 * yr, 0, :, lanes])
            send1[yr, :, lanes] = add(send1[yr, :, lanes], got[2 * yr + 1, 0, :, lanes])
            keep2[yr, :, lanes] = add(keep2[yr, :, lanes], got[yr, 1, :, lanes])
            send2[yr, :, lanes] = add(send2[yr, :, lanes], got[2 + yr, 1, :, lanes])

    for k in range(4):

        @pl.when(step == k + 1)
        def _():
            exchange(k).start()

    @pl.when(step < 3)
    def _():
        def one(h, carry):
            right = hid[0, :, pl.ds(pl.multiple_of(h * units, 128), units)]
            take(dot(turned[...], right), h, pl.ds(pl.multiple_of(step * units, 128), units))
            return carry

        lax.fori_loop(0, 2, one, 0)

    @pl.when(step == 3)
    def _():
        def one(h, carry):
            take(dot(turned[...], jnp.where(c == h, own[...], other[...])), h, lanes_of(3))
            return carry

        lax.fori_loop(0, 2, one, 0)

    for k in range(4):

        @pl.when(step == k + 2)
        def _():
            exchange(k).wait_recv()
            add_got(lanes_of(k))
            for item in stores(k):
                item.start()

    @pl.when(step == 5)
    def _():
        for k in range(4):
            exchange(k).wait_send()
            for item in stores(k):
                item.wait()


def weights(n2, g, branch, hid, own, other):
    wide, count = n2.shape
    units = hid.shape[2] // 2
    length = 3 * units + 512
    low = lambda *shape: pltpu.VMEM(shape, BF16)
    sems = pltpu.SemaphoreType.DMA
    grid = pl.GridSpec(
        grid=(6,),
        in_specs=[
            pl.BlockSpec((wide, count), lambda s: (0, 0), pipeline_mode=pl.Buffered(1)),
            any_spec(),
            any_spec(),
            pl.BlockSpec((1, count, 2 * units), lambda s: (jnp.minimum(s, 2), 0, 0)),
            any_spec(),
            any_spec(),
        ],
        out_specs=[any_spec()] * 4,
        scratch_shapes=[low(wide, count), low(wide, count), low(wide, count), low(count, 512), low(count, 512)]
        + [low(2, 128, length)] * 4
        + [low(4, 2, 128, length)] * 2
        + [sems((4,)), sems((4,)), sems((4,)), sems((4, 4))],
    )
    return pl.pallas_call(
        weights_kernel,
        out_shape=[jax.ShapeDtypeStruct((2, 128, length), BF16)] * 4,
        grid_spec=grid,
        compiler_params=params(collective_id=1, has_side_effects=True),
        cost_estimate=cost(2 * count * 1024 * length * 2, 50e6),
        name="weights",
    )(n2, g, branch, hid, own, other)


def add(left, right):
    return (left.astype(F32) + right.astype(F32)).astype(BF16)


def finish_kernel(at, own, got, own_heads, got_heads, tok, got_tok, first, came0, came1, slab0, slab1, layer, got_layer, gate, up, down, out, query, key, value, tok_out, first_out, layer_out):
    part = down.shape[0]
    for n, ref in enumerate((gate, up, down, out)):

        @pl.when(pl.program_id(0) == n)
        def _():
            rows = slice(n * part, n * part + ref.shape[0])
            total = own[rows, :].astype(F32)
            for d in range(3):
                total += got[d, rows, :].astype(F32)
            ref[...] = total

    @pl.when(pl.program_id(0) == 3)
    def _():
        heads = own_heads[...].astype(F32)
        for d in range(3):
            heads += got_heads[d].astype(F32)
        for n, ref in enumerate((query, key)):
            parts = []
            for h in range(4):
                parts += [heads[n, :, h * 32 : h * 32 + 32], heads[n, :, 128 + h * 32 : 160 + h * 32]]
            ref[...] = jnp.concatenate(parts, axis=1)
        value[...] = heads[2]

    stays = (at[0] & 1) == (at[1] & 1)
    tok_out[...] = jnp.where(stays, tok[...], got_tok[...]).astype(F32)
    step = pl.program_id(0)
    c, t = at[0] & 1, at[1]
    pair, side = t >> 1, t & 1
    r = (step >> 1) ^ side
    local = (c == side) & (t == 2 * c + (pair ^ r))

    @pl.when((step & 1) == 0)
    def _():
        came = jnp.where(r == 0, came0[...], came1[...])
        slab = jnp.where(r == 0, slab0[...], slab1[...])
        first_out[...] = jnp.where(local, slab, came).astype(F32)

    @pl.when((step & 1) == 1)
    def _():
        first_out[...] = first[0].astype(F32)

    layer_out[...] = jnp.where(stays, layer[...], got_layer[...])


def finish(at, pieces, got, own_heads, got_heads, tok, got_tok, first, early, layer, got_layer, part):
    count, wide = tok.shape
    rows = 256
    row = pl.BlockSpec((rows, wide), lambda i, at: (i, 0))
    wider = pl.BlockSpec((SEQ // 2, 256), lambda i, at: (i, 0))
    whole = lambda *shape: pl.BlockSpec(shape, lambda i, at: (0,) * len(shape))
    shapes = [(part, 128)] * 3 + [(256, 128)] + [(128, 256)] * 3
    grid = pltpu.PrefetchScalarGridSpec(
        num_scalar_prefetch=1,
        grid=(count // rows,),
        in_specs=[
            whole(*pieces.shape),
            whole(*got.shape),
            whole(*own_heads.shape),
            whole(*got_heads.shape),
            row,
            row,
            pl.BlockSpec((1, SEQ // 2, 256), lambda i, at: (i // 2, 0, 0)),
            *[whole(SEQ // 2, 256)] * 4,
            row,
            row,
        ],
        out_specs=[whole(*shape) for shape in shapes] + [row, wider, row],
    )
    return pl.pallas_call(
        finish_kernel,
        out_shape=[jax.ShapeDtypeStruct(shape, F32) for shape in shapes + [(count, wide), (2 * SEQ, 256)]]
        + [jax.ShapeDtypeStruct((count, wide), BF16)],
        grid_spec=grid,
        compiler_params=params(),
        cost_estimate=cost(1e6, 18e6),
        name="finish",
    )(at, pieces, got, own_heads, got_heads, tok, got_tok, first, *early, layer, got_layer)


def tail_kernel(
    dq0, dk0, dv0, dq1, dk1, dv1, small, normed, row, grad_hidden, keep1, got1, keep2, got2, gain, gain_two,
    first, own_pieces, got_pieces, own_heads, got_heads, tok, got_tok, sums,
    d_s, w_s, n_s, x_s, gh_s, ks1, gs1, ks2, gs2, last1, last2, pieces, gn_send, gn_got, turned,
    h_send, h_got, s1, k1, a1, a2, part1, part2, rest1, rest2, heads, held, came,
    load, f_sem, m_sem, p_sem, n_sem, c_sem, one_sem, two_sem, h_sem, swap, g_sem,
):
    dp, t = lax.axis_index("dp"), lax.axis_index("tensor")
    c, x, y = lax.rem(dp, 2), lax.rem(lax.div(dp, 2), 2), lax.div(dp, 4)
    pair, side = lax.div(t, 2), lax.rem(t, 2)
    plane = dp - c
    dpx, dpy, dpc = dp + 2 - 4 * x, dp + 4 - 8 * y, dp + 1 - 2 * c
    half = SEQ // 2
    units = (ks1.shape[2] - 512) // 3

    def copy(src, dst, sems, n, to):
        return pltpu.make_async_remote_copy(
            src_ref=src,
            dst_ref=dst,
            send_sem=sems.at[0, n],
            recv_sem=sems.at[1, n],
            device_id=to,
            device_id_type=MESH,
        )

    sources = [(keep1, ks1), (got1, gs1), (keep2, ks2), (got2, gs2)]
    for h, arrays in enumerate(((dq0, dk0, dv0), (dq1, dk1, dv1))):
        sources += [(src, d_s.at[n, pl.ds(h * half, half), :]) for n, src in enumerate(arrays)]
    sources += [(normed, n_s), (small.at[pl.ds(0, 3), pl.ds(2 * c, 2)], w_s), (row.at[c], x_s), (grad_hidden, gh_s)]
    loads = [pltpu.make_async_copy(src, dst, load.at[n]) for n, (src, dst) in enumerate(sources)]
    for item in loads:
        item.start()
    meet(plane, c, t, dpx, dpy)

    def value_copy(u):
        src = dv1.at[:, pl.ds(u * 256, 256)]
        return pltpu.make_async_remote_copy(
            src_ref=src,
            dst_ref=first.at[pair],
            send_sem=f_sem.at[0, u],
            recv_sem=f_sem.at[1, pair],
            device_id=(plane + side, 2 * c + u),
            device_id_type=MESH,
        )

    def value_local(u):
        return pltpu.make_async_copy(dv1.at[:, pl.ds(u * 256, 256)], first.at[pair], load.at[14])

    for u in range(2):
        stay = (side == c) & (t == 2 * c + u)

        @pl.when(stay)
        def _():
            value_local(u).start()

        @pl.when(jnp.logical_not(stay))
        def _():
            value_copy(u).start()

    for item in loads[:4]:
        item.wait()
    gs1[1] = add(ks1[1], gs1[1])
    gs2[1] = add(ks2[1], gs2[1])
    seconds = []
    for n, lanes in enumerate((pl.ds(0, 2 * units), pl.ds(2 * units, units + 512))):
        seconds.append(copy(gs1.at[1, :, lanes], last1.at[:, lanes], m_sem, 2 * n, (dpy, t)))
        seconds.append(copy(gs2.at[1, :, lanes], last2.at[:, lanes], m_sem, 2 * n + 1, (dpx, t)))
    for item in loads[4:11]:
        item.wait()
    for item in seconds:
        item.start()

    def turn(parity):
        for rel in range(4):
            yy, xx = (y, 1 - y)[rel // 2], (x, 1 - x)[rel % 2]
            block = pl.multiple_of((yy * 4 + xx * 2 + parity) * 128, 128)
            turned[rel * 128 : rel * 128 + 128, :] = n_s[:, pl.ds(block, 128)].T

    def heads_copy(n):
        lanes = pl.ds(pl.multiple_of(n * 512, 512), 512)
        return copy(h_send.at[:, :, :, lanes], h_got.at[:, :, :, lanes], c_sem, n, (dpc, t))

    def heads_product(n):
        product = dot(turned[...], d_s[n]).astype(BF16)
        return [product[r * 128 : r * 128 + 128] for r in range(4)], pl.ds(pl.multiple_of(n * 512, 512), 512)

    def heads_send(n, carry):
        place_second(h_send.at[0], h_send.at[1], *heads_product(n))

        @pl.when(n > 0)
        def _():
            heads_copy(n - 1).start()

        return carry

    def heads_keep(n, carry):
        place_first(s1, k1, *heads_product(n))
        return carry

    turn(1 - c)
    lax.fori_loop(0, 3, heads_send, 0)

    part = units // 4
    low_rows, high_rows = pl.ds(0, 4 * part), pl.ds(4 * part, 2 * part + 256)

    def fill_pieces(which):
        for h, (kept, got, last) in enumerate(((ks1, gs1, last1), (ks2, gs2, last2))):
            for n in which:
                lanes = slice(n * units, n * units + (units if n < 3 else 512))
                total = kept[0, :, lanes].astype(F32) + got[0, :, lanes].astype(F32) + last[:, lanes].astype(F32)
                flipped = total.T.astype(BF16)
                if n < 3:
                    for i in range(4):
                        rows = slice((2 * n + h) * part, (2 * n + h + 1) * part)
                        pieces[lax.rem(i + 4 - t, 4), rows, :] = flipped[i * part : (i + 1) * part]
                else:
                    for i in range(2):
                        pieces[lax.rem(2 * h + i + 4 - t, 4), 6 * part :, :] = flipped[i * 256 : i * 256 + 256]

    def piece_copies(rows, n):
        return [
            copy(pieces.at[d, rows, :], got_pieces.at[d - 1, rows, :], p_sem, 3 * n + d - 1, (dp, lax.rem(t + d, 4)))
            for d in (1, 2, 3)
        ]

    for item in seconds[:2]:
        item.wait_recv()
    fill_pieces((0, 1))
    turn(c)
    heads_copy(2).start()
    zs = piece_copies(low_rows, 0)
    for item in zs:
        item.start()
    lax.fori_loop(0, 3, heads_keep, 0)
    cs = [heads_copy(n) for n in range(3)]
    for item in cs:
        item.wait_recv()
    ones = [copy(h_got.at[0], a2, one_sem, 1, (dpy, t)), copy(s1, a1, one_sem, 0, (dpx, t))]
    for item in ones:
        item.start()
    for item in seconds[2:]:
        item.wait_recv()
    fill_pieces((2, 3))
    own_pieces[...] = pieces[0]
    last_zs = piece_copies(high_rows, 1)
    for item in last_zs:
        item.start()
    zs += last_zs

    def back_product(rows):
        total = None
        for u in range(2):
            for n in range(3):
                term = dot_nt(d_s[n, rows, u * 256 : u * 256 + 256], w_s[n, u])
                total = term if total is None else total + term
        return total

    ns = [copy(gn_send.at[i], gn_got.at[i], n_sem, i, (dpc, t)) for i in range(2)]

    def other_half(i, carry):
        rows = pl.ds(pl.multiple_of((1 - c) * half + i * 512, 512), 512)
        gn_send[i] = back_product(rows).astype(BF16)
        return carry

    loads[11].wait()
    lax.fori_loop(0, 2, other_half, 0)

    for item in ones:
        item.wait_recv()
    part1[...] = add(k1[1], a1[1])
    part2[...] = add(h_got[1, 1], a2[1])
    for item in ns:
        item.start()
    twos = [copy(part1, rest1, two_sem, 0, (dpy, t)), copy(part2, rest2, two_sem, 1, (dpx, t))]
    for item in twos:
        item.start()

    loads[12].wait()
    loads[13].wait()
    moved = side != c
    for item in ns:
        item.wait_recv()

    def own_half(i, gained):
        rows = pl.ds(pl.multiple_of(c * half + i * 512, 512), 512)
        here = pl.ds(pl.multiple_of(i * 512, 512), 512)
        grad = back_product(rows) + gn_got[i].astype(F32)
        values = x_s[here, :].astype(F32)
        factor = lax.rsqrt(jnp.mean(values * values, axis=1, keepdims=True) + EPSILON)
        gained += jnp.sum((grad * values * factor).reshape(-1, 8, grad.shape[1]), axis=0)
        scaled = grad * gain[...]
        mean = jnp.mean(scaled * values, axis=1, keepdims=True)
        tok[i] = (gh_s[here, :] + factor * scaled - values * (factor * factor * factor * mean)).astype(BF16)
        return gained

    gained = lax.fori_loop(0, 2, own_half, jnp.zeros((8, tok.shape[2]), F32))
    swaps = [copy(tok.at[i], got_tok.at[i], swap, i, (plane + side, 2 * pair + c)) for i in range(2)]

    total1 = k1[0].astype(F32) + a1[0].astype(F32)
    total2 = h_got[1, 0].astype(F32) + a2[0].astype(F32)

    @pl.when(moved)
    def _():
        for item in swaps:
            item.start()

    turns = (dpc, t), (dpx, t), (dpy, t), (dp, t + 1 - 2 * side), (dp, lax.rem(t + 2, 4))
    line = lax.broadcasted_iota(jnp.int32, gained.shape, 0)
    total_one = jnp.sum(gained, axis=0, keepdims=True)
    total_two = jnp.sum(gain_two[...], axis=0, keepdims=True)
    held[0] = jnp.where(line == 0, total_one, jnp.where(line == 1, total_two, 0.0))

    def gain_step(n):
        return copy(held.at[n], came.at[n], g_sem, n, turns[n])

    def gain_next(n):
        gain_step(n).wait_recv()
        held[n + 1] = held[n] + came[n]

    gain_step(0).start()
    gain_next(0)
    gain_step(1).start()
    gain_next(1)
    for item in twos:
        item.wait_recv()
    totals = ((total1 + rest1[...].astype(F32)).astype(BF16), (total2 + rest2[...].astype(F32)).astype(BF16))
    for e, total in enumerate(totals):
        core = (c, 1 - c)[e]
        for u in range(2):
            d = lax.rem(2 * core + u + 4 - t, 4)
            for n in range(3):
                heads[d, n] = total[:, n * 512 + u * 256 : n * 512 + u * 256 + 256]
    gain_step(2).start()
    gain_next(2)
    own_heads[...] = heads[0]
    hs = [copy(heads.at[d], got_heads.at[d - 1], h_sem, d - 1, (dp, lax.rem(t + d, 4))) for d in (1, 2, 3)]
    for item in hs:
        item.start()
    for n in (3, 4):
        gain_step(n).start()
        gain_next(n)
    sums[...] = held[5]

    for item in seconds + ns + cs + ones + twos:
        item.wait_send()
    for n in range(5):
        gain_step(n).wait_send()
    for u in range(2):
        stay = (side == c) & (t == 2 * c + u)

        @pl.when(stay)
        def _():
            value_local(u).wait()

        @pl.when(jnp.logical_not(stay))
        def _():
            value_copy(u).wait_send()

    for p in range(2):

        @pl.when((pair != c) | (t != 2 * p + c))
        def _():
            pltpu.make_async_remote_copy(
                src_ref=first.at[p],
                dst_ref=first.at[p],
                send_sem=f_sem.at[0, p],
                recv_sem=f_sem.at[1, p],
                device_id=(dpc, t),
                device_id_type=MESH,
            ).wait_recv()

    for item in zs + hs:
        item.wait()

    @pl.when(moved)
    def _():
        for item in swaps:
            item.wait()


def tail(back, small, normed, row, grad_hidden, keep1, got1, keep2, got2, gain, gain_two):
    vmem = pl.BlockSpec(memory_space=pltpu.VMEM)
    sems = pltpu.SemaphoreType.DMA
    wide = normed.shape[1]
    length = keep1.shape[2]
    rows = (length - 512) // 2 + 256
    half = SEQ // 2
    low = lambda *shape: pltpu.VMEM(shape, BF16)
    return pl.pallas_call(
        tail_kernel,
        out_shape=[
            jax.ShapeDtypeStruct((2, half, 256), BF16),
            jax.ShapeDtypeStruct((rows, 128), BF16),
            jax.ShapeDtypeStruct((3, rows, 128), BF16),
            jax.ShapeDtypeStruct((3, 128, 256), BF16),
            jax.ShapeDtypeStruct((3, 3, 128, 256), BF16),
            jax.ShapeDtypeStruct((2, half // 2, wide), BF16),
            jax.ShapeDtypeStruct((2, half // 2, wide), BF16),
            jax.ShapeDtypeStruct((8, wide), F32),
        ],
        in_specs=[any_spec()] * 14 + [vmem] * 2,
        out_specs=[any_spec(), vmem, any_spec(), vmem, any_spec(), vmem, any_spec(), vmem],
        scratch_shapes=[low(3, SEQ, 512)]
        + [low(3, 2, wide, 256), low(SEQ, wide), low(half, wide), pltpu.VMEM((half, wide), F32)]
        + [low(2, 128, length)] * 4
        + [low(128, length)] * 2
        + [low(4, rows, 128), low(2, half // 2, wide), low(2, half // 2, wide), low(512, SEQ)]
        + [low(2, 2, 128, 1536)] * 2
        + [low(2, 128, 1536)] * 4
        + [low(128, 1536)] * 4
        + [low(4, 3, 128, 256), pltpu.VMEM((6, 8, wide), F32), pltpu.VMEM((5, 8, wide), F32)]
        + [sems((15,)), sems((2, 2)), sems((2, 4)), sems((2, 6)), sems((2, 2)), sems((2, 3)), sems((2, 2)), sems((2, 2))]
        + [sems((2, 3)), sems((2, 2)), sems((2, 5))],
        compiler_params=params(collective_id=2, has_side_effects=True),
        name="tail",
    )(*back, small, normed, row, grad_hidden, keep1, got1, keep2, got2, gain, gain_two)


def fast_body(tokens, first_values, doc_lengths, cotangent, w_query, w_key, w_value, w_out, w_gate, w_up, w_down, gain_attn, gain_mlp):
    me, t = lax.axis_index("dp"), lax.axis_index("tensor")
    c = me % 2
    pair, side = t // 2, t % 2
    wide = tokens.shape[1]
    tiles = SEQ // TILE
    at = jnp.where(jnp.arange(8, dtype=jnp.int32) == 0, me, t).astype(jnp.int32)

    small_shard, big_shard = pack(w_query, w_key, w_value, w_out, w_gate, w_up, w_down)
    lengths = jnp.where(c == side, doc_lengths, across_c(doc_lengths))
    lengths = lax.dynamic_index_in_dim(lengths, pair, 0, keepdims=False)
    order = jnp.arange(DOCS, dtype=jnp.int32)
    ends = jnp.sum(jnp.where(order[None, :] <= order[:, None], lengths[None, :], 0), axis=1)
    freqs = 10000.0 ** (-(jnp.arange(32, dtype=F32) * 2.0 / HEAD))
    row, small, big, normed_one, q, k, v, cosine, sine = gather(
        ends, tokens, first_values, small_shard, big_shard, gain_attn[None], jnp.tile(freqs, 4)[None]
    )
    places = jnp.arange(SEQ, dtype=jnp.int32)
    starts = jnp.max(jnp.where(ends[None, :] <= places[:, None], ends[None, :], 0), axis=1)
    last = jnp.arange(tiles, dtype=jnp.int32) * TILE + (TILE - 1)
    stop = jnp.min(jnp.where(ends[None, :] > last[:, None], ends[None, :], SEQ), axis=1)
    bounds = jnp.concatenate([starts.reshape(tiles, TILE)[:, 0] // TILE, (stop - 1) // TILE])
    starts_by_tile = starts.reshape(tiles, TILE)

    row, cotangent = lax.optimization_barrier((row, cotangent))
    moved_cot = swap_halves(cotangent)
    att_own, att_send, lse = attend(at, bounds, q, k, v, starts_by_tile)
    att_other = across_c(att_send)
    out, grad_hidden, branch, normed_two, hid, ga_own, ga_other, gain_two, cot = mlp(
        at, att_own, att_other, row, cotangent, moved_cot, gain_mlp[None], small, big
    )
    moved_out = swap_halves(out)

    ga_got = across_c(ga_other)

    kept = weights(normed_two, cot, branch, hid, att_own, att_other)
    kept, ga_got = lax.optimization_barrier((kept, ga_got))
    got1, got2 = across_x(kept[0]), across_y(kept[2])

    rest = (att_own, att_send, lse, starts_by_tile, cosine, sine)
    dq0, dk0, dv0, held = attend_back(0, at, bounds, q, k, v, ga_own, ga_got, *rest)

    slabs = [jnp.where(pair == r, dv0[:, :256], dv0[:, 256:]) for r in range(2)]
    came = [
        move(slabs[r], lambda y, x, c, t, r=r: (y, x, t % 2, 2 * c + ((t // 2) ^ r))) for r in range(2)
    ]
    dq1, dk1, dv1 = attend_back(1, at, bounds, q, k, v, ga_own, ga_got, *rest, held)

    first_back, pieces, got, own_heads, got_heads, grad_tokens, got_tokens, gains = tail(
        (dq0, dk0, dv0, dq1, dk1, dv1), small, normed_one, row, grad_hidden, kept[1], got1, kept[3], got2, gain_attn[None], gain_two
    )
    shape = (SEQ // 2, wide)
    grad_gate, grad_up, grad_down, grad_out, gq, gk, gv, grad_tokens, grad_first, layer_out = finish(
        at, pieces, got, own_heads, got_heads, grad_tokens.reshape(shape), got_tokens.reshape(shape), first_back, (*came, *slabs), out, moved_out, w_gate.shape[1]
    )
    return (
        layer_out,
        grad_tokens,
        grad_first,
        gq,
        gk,
        gv,
        grad_out,
        grad_gate.T,
        grad_up.T,
        grad_down,
        gains[0],
        gains[1],
    )


def solution(mesh):
    fits = dict(mesh.shape) == {"dp": 8, "tensor": 4}
    placed = (
        P(("dp", "tensor"), None),
        P("dp", "tensor"),
        P("dp", None),
        P(("dp", "tensor"), None),
        P("dp", "tensor"),
        P("dp", "tensor"),
        P("dp", "tensor"),
        P("tensor", "dp"),
        P("dp", "tensor"),
        P("dp", "tensor"),
        P("tensor", "dp"),
        P(),
        P(),
    )
    return jax.shard_map(
        fast_body if fits else general_body,
        mesh=mesh,
        in_specs=placed,
        out_specs=(
            P(("dp", "tensor"), None),
            P(("dp", "tensor"), None),
            P("dp", "tensor"),
            P("dp", "tensor"),
            P("dp", "tensor"),
            P("dp", "tensor"),
            P("tensor", "dp"),
            P("dp", "tensor"),
            P("dp", "tensor"),
            P("tensor", "dp"),
            P(),
            P(),
        ),
        check_vma=False,
    )
```
